32 devices in a mesh: seq: 4 (over y, x), fsdp: 8 (over z, core).
Axes of the slice: x: 2, y: 2, z: 4, core: 2. Of those that a mesh axis runs over, the one named last changes fastest.
Arguments:
- tokens: bfloat16 [3, 8, 1536, 512], P(None, 'fsdp', 'seq'), may hold values from -6 to 6
- time_embed: bfloat16 [3, 8, 1536, 512], P(None, 'fsdp', 'seq'), may hold values from -3 to 3
- doc_ids: int32 [3, 8, 1536], P(None, 'fsdp', 'seq'), may hold values from 0 to 7, never falling along the last dimension, each value on 1 to 768 neighbouring positions
- out_grad: bfloat16 [3, 8, 1536, 512], P(None, 'fsdp', 'seq'), may hold values from -6 to 6
- norm1_gain: bfloat16 [512], P('fsdp'), may hold values from 0.25 to 1.75
- norm1_shift: bfloat16 [512], P('fsdp'), may hold values from -3 to 3
- qkv_weight: bfloat16 [512, 1536], P('fsdp'), may hold values from -0.25 to 0.25
- out_weight: bfloat16 [512, 512], P('fsdp'), may hold values from -1 to 1
- norm2_gain: bfloat16 [512], P('fsdp'), may hold values from 0.25 to 1.75
- norm2_shift: bfloat16 [512], P('fsdp'), may hold values from -3 to 3
- up_weight: bfloat16 [512, 2048], P('fsdp'), may hold values from -0.25 to 0.25
- up_bias: bfloat16 [2048], P('fsdp'), may hold values from -3 to 3
- down_weight: bfloat16 [2048, 512], P('fsdp'), may hold values from -0.125 to 0.125
- down_bias: bfloat16 [512], P('fsdp'), may hold values from -3 to 3
Outputs:
- layer_output: bfloat16 [3, 8, 1536, 512], P(None, 'fsdp', 'seq')
- input_grad: float32 [3, 8, 1536, 512], P(None, 'fsdp', 'seq')
- grad_norm1_gain: float32 [512], P('fsdp')
- grad_norm1_shift: float32 [512], P('fsdp')
- grad_qkv_weight: float32 [512, 1536], P('fsdp')
- grad_out_weight: float32 [512, 512], P('fsdp')
- grad_norm2_gain: float32 [512], P('fsdp')
- grad_norm2_shift: float32 [512], P('fsdp')
- grad_up_weight: float32 [512, 2048], P('fsdp')
- grad_up_bias: float32 [2048], P('fsdp')
- grad_down_weight: float32 [2048, 512], P('fsdp')
- grad_down_bias: float32 [512], P('fsdp')
The draws below stay inside these ranges and needn't reach their ends.
Inputs may be any that keep to these rules, and one draw needn't show every extreme that they name: `doc_ids`: in each sequence the ids never fall along the positions; each of the 8 ids is used by 1 to 768 positions, and one document holds exactly 768.
All inputs are finite; a program needn't handle non-finite values.
Results may differ from the reference program's by a relative error of at most 0.011.
Values may be sent and summed in bfloat16 or wider, within the bound.
No kernel may reach another device: no remote copies, remote signals or barrier semaphores. Data moves between devices by JAX's collectives and lax.ppermute only.
A program may use at most 128 MiB of HBM per device.

```python
import math
import jax
import jax.numpy as jnp
import numpy as np
from jax import lax

D = 512
FF = 2048
HEADS = 8
MB = 3
SEQS = 8
LEN = 1536
DOCS = 8
DOC_MOST = 768
N_FSDP = 8


def shard_levels(rng, dims, pieces, smallest, top_value):
    level, own = 1.0, jax.random.fold_in(rng, 6)
    for position, shards_of in pieces:
        steps = jnp.exp(jax.random.uniform(jax.random.fold_in(own, position), (shards_of,), jnp.float32, smallest / len(pieces), top_value / len(pieces)))
        level = level * jnp.repeat(steps, dims[position] // shards_of).reshape([-1 if axis == position else 1 for axis in range(len(dims))])
    return level


def profile(count, total, reach, lean):
    weights = [(1 << 20) // math.isqrt(rank ** lean) + 1 for rank in range(2, count + 1)]
    rest, counts = total - reach - (count - 1), [1] * (count - 1)
    while rest > 0:
        candidates = [i for i in range(count - 1) if counts[i] < reach]
        whole, budget = sum([weights[i] for i in candidates]), rest
        for i in candidates:
            addition = min(reach - counts[i], max(1, budget * weights[i] // whole), rest)
            counts[i] = counts[i] + addition
            rest = rest - addition
    return np.array([reach] + counts)


def uneven(stream_key, number_of, total, bound, skew):
    if number_of == 2:
        one = jax.random.randint(stream_key, (), max(1, total - bound), min(bound, total - 1) + 1)
        return jnp.stack([one, total - one])
    tallies = jnp.asarray(profile(number_of, total, bound, skew), jnp.int32)
    twos = (number_of - 1) // 2
    donor, receiver = tallies[1:1 + 2 * twos:2], tallies[2:2 + 2 * twos:2]
    room = jnp.minimum(donor - 1, bound - receiver)
    moved = jax.random.randint(jax.random.fold_in(stream_key, 1), (twos,), 0, 1 << 20) % (room + 1)
    tallies = tallies.at[1:1 + 2 * twos:2].set(donor - moved).at[2:2 + 2 * twos:2].set(receiver + moved)
    return tallies[jax.random.permutation(jax.random.fold_in(stream_key, 2), number_of)]


def scatter_about(rng, shape, deviation, bound, shards=(), dtype=jnp.bfloat16):
    loudness = shard_levels(rng, shape, shards, -0.22, 0.18) if shards else 1.0
    drawn = jax.random.normal(rng, shape, jnp.float32) * deviation * loudness
    return jnp.minimum(jnp.maximum(drawn, -bound), bound).astype(dtype)


def setup_inputs(seed: int = 0) -> dict:
    arg_keys = jax.random.split(jax.random.key(seed), 15)
    return {
        "tokens": scatter_about(arg_keys[0], (MB, SEQS, LEN, D), 1.0, 6.0, ((1, 8), (2, 4))),
        "time_embed": scatter_about(arg_keys[1], (MB, SEQS, LEN, D), 0.5, 3.0, ((1, 8), (2, 4))),
        "doc_ids": jax.vmap(lambda own: jnp.searchsorted(jnp.cumsum(uneven(own, DOCS, LEN, DOC_MOST, 2)), jnp.arange(LEN), side="right"))(jax.random.split(arg_keys[2], MB * SEQS)).reshape((MB, SEQS, LEN)).astype(jnp.int32),
        "out_grad": scatter_about(arg_keys[3], (MB, SEQS, LEN, D), 1.0, 6.0, ((1, 8), (2, 4))),
        "norm1_gain": jnp.clip(1.0 + 0.15 * jax.random.normal(arg_keys[4], (D,), jnp.float32), 0.25, 1.75).astype(jnp.bfloat16),
        "norm1_shift": scatter_about(arg_keys[5], (D,), 0.5, 3.0, ((0, 8),)),
        "qkv_weight": scatter_about(arg_keys[6], (D, 3 * D), D ** -0.5, 0.25, ((0, 8),)),
        "out_weight": scatter_about(arg_keys[7], (D, D), (D // 16) ** -0.5, 1.0, ((0, 8),)),
        "norm2_gain": jnp.clip(1.0 + 0.15 * jax.random.normal(arg_keys[8], (D,), jnp.float32), 0.25, 1.75).astype(jnp.bfloat16),
        "norm2_shift": scatter_about(arg_keys[9], (D,), 0.5, 3.0, ((0, 8),)),
        "up_weight": scatter_about(arg_keys[10], (D, FF), D ** -0.5, 0.25, ((0, 8),)),
        "up_bias": scatter_about(arg_keys[11], (FF,), 0.5, 3.0, ((0, 8),)),
        "down_weight": scatter_about(arg_keys[12], (FF, D), FF ** -0.5, 0.125, ((0, 8),)),
        "down_bias": scatter_about(arg_keys[13], (D,), 0.5, 3.0, ((0, 8),)),
    }


highest = lax.Precision.HIGHEST

@jax.custom_vjp
def low(v):
    return lax.optimization_barrier(v.astype(jnp.bfloat16)).astype(jnp.float32)

@jax.custom_vjp
def low_back(v):
    return v

def low_keep(v):
    return (low(v), None)

def low_pass(kept, grad):
    return (grad,)

def back_keep(v):
    return (v, None)

def back_low(kept, grad):
    return (low(grad),)
low.defvjp(low_keep, low_pass)
low_back.defvjp(back_keep, back_low)

def normalize(inputs, gain, shift):
    mean_row = lax.optimization_barrier(jnp.mean(inputs, axis=-1, keepdims=True))
    centred = inputs - mean_row
    variance = lax.optimization_barrier(jnp.mean(centred * centred, axis=-1, keepdims=True))
    return centred * lax.rsqrt(variance + 1e-05) * gain + shift

def attend(queries, key_rows, value_rows, doc_row):
    length = queries.shape[0]
    head_dim = D // HEADS
    score_scale = head_dim ** (-0.5)
    block_rows = min(512, length)
    query_blocks = queries.reshape(length // block_rows, block_rows, HEADS, head_dim)
    doc_blocks = doc_row.reshape(length // block_rows, block_rows)
    key_heads = key_rows.reshape(length, HEADS, head_dim)
    value_heads = value_rows.reshape(length, HEADS, head_dim)

    def one_block(block_pair):
        query_part, doc_part = block_pair
        scores = jnp.einsum('qhd,khd->hqk', query_part, key_heads, precision=highest) * score_scale
        scores = low_back(scores)
        same_doc = (doc_part[:, None] == doc_row[None, :])[None]
        scores = jnp.where(same_doc, scores, -jnp.inf)
        probs = low(jax.nn.softmax(scores, axis=-1))
        return jnp.einsum('hqk,khd->qhd', probs, value_heads, precision=highest)
    block_out = lax.map(jax.checkpoint(one_block), (query_blocks, doc_blocks))
    return block_out.reshape(length, D)

def layer(rows_in, doc_row, params):
    gain_one, shift_one, w_qkv, w_out, gain_two, shift_two, w_up, bias_up, w_down, bias_down = params
    hidden_one = low(normalize(rows_in, gain_one, shift_one))
    triple = low(low_back(jnp.dot(hidden_one, w_qkv, precision=highest)))
    mixed_rows = low(low_back(attend(triple[:, :D], triple[:, D:2 * D], triple[:, 2 * D:], doc_row)))
    branch = low_back(jnp.dot(mixed_rows, w_out, precision=highest))
    middle = rows_in + branch
    hidden_two = low(normalize(middle, gain_two, shift_two))
    pre_act = low_back(jnp.dot(hidden_two, w_up, precision=highest) + bias_up)
    activated = low(jax.nn.gelu(pre_act, approximate=True))
    return middle + jnp.dot(activated, w_down, precision=highest) + bias_down

def reference(tokens, time_embed, doc_ids, out_grad, norm1_gain, norm1_shift, qkv_weight, out_weight, norm2_gain, norm2_shift, up_weight, up_bias, down_weight, down_bias):
    params = tuple((item.astype(jnp.float32) for item in (norm1_gain, norm1_shift, qkv_weight, out_weight, norm2_gain, norm2_shift, up_weight, up_bias, down_weight, down_bias)))
    count = MB * N_FSDP
    rows_all = (tokens.astype(jnp.float32) + time_embed.astype(jnp.float32)).reshape(count, LEN, D)
    docs_all = doc_ids.reshape(count, LEN).astype(jnp.int32)
    cotangents = out_grad.astype(jnp.float32).reshape(count, LEN, D)
    zero_state = tuple((jnp.zeros(item.shape, jnp.float32) for item in params))

    def one_sequence(totals, sequence_item):
        rows_in, doc_row, cotangent = sequence_item

        def forward(rows, *weights):
            return layer(rows, doc_row, weights)
        result, pull = jax.vjp(forward, rows_in, *params)
        grads = pull(cotangent)
        totals = tuple((earlier + current for earlier, current in zip(totals, grads[1:])))
        return (totals, (result.astype(jnp.bfloat16), grads[0]))
    totals, (outputs, in_grads) = lax.scan(one_sequence, zero_state, (rows_all, docs_all, cotangents))
    return (outputs.reshape(MB, N_FSDP, LEN, D), in_grads.reshape(MB, N_FSDP, LEN, D), totals[0], totals[1], totals[2], totals[3], totals[4], totals[5], totals[6], totals[7], totals[8], totals[9])
```

```python
from functools import partial

import jax
import jax.numpy as jnp
from jax import lax
from jax.experimental import pallas as pl
from jax.experimental.pallas import tpu as pltpu
from jax.sharding import PartitionSpec as P

HEADS = 8
EPS = 1e-05
LOG2E = 1.4426950408889634
BLOCK = 256
VMEM_LIMIT = 56 * 1024 * 1024
BF = jnp.bfloat16
F32 = jnp.float32


def dot(a, b, dims=((1,), (0,))):
    return lax.dot_general(a, b, (dims, ((), ())), preferred_element_type=F32)


def dot_t(a, b):
    return dot(a, b, ((1,), (1,)))


def params(limit=VMEM_LIMIT):
    return pltpu.CompilerParams(vmem_limit_bytes=limit)


def cost(flops, read, transcendentals=0):
    return pl.CostEstimate(
        flops=int(flops), bytes_accessed=int(read), transcendentals=int(transcendentals)
    )


VM = pl.BlockSpec(memory_space=pltpu.VMEM)
SM = pl.BlockSpec(memory_space=pltpu.SMEM)


def swap(value, axis, bit):
    size = lax.axis_size(axis)
    return lax.ppermute(value, axis, [(i, i ^ bit) for i in range(size)])


def gather_pieces(value, axis):
    size = lax.axis_size(axis)
    held = {0: value}
    bit = size // 2
    while bit:
        held.update({j | bit: swap(item, axis, bit) for j, item in list(held.items())})
        bit //= 2
    return [held[j] for j in range(size)]


def exchange(pieces, axis):
    return [pieces[0]] + [swap(pieces[k], axis, k) for k in range(1, len(pieces))]


def assemble_qkv_kernel(count, seq_parts, part_width, me_ref, *refs):
    pieces, (wq_ref, vec_ref, col_ref) = refs[:count], refs[count:]
    rows, width = pieces[0].shape
    model = wq_ref.shape[1]
    for j in range(count):
        start = pl.multiple_of((me_ref[0] ^ j) * rows, rows)
        for d in range(seq_parts):
            for t in range(3):
                lane = t * model + d * part_width
                wq_ref[d, pl.ds(start, rows), t * part_width : (t + 1) * part_width] = pieces[j][
                    :, lane : lane + part_width
                ]
        col_ref[pl.ds(start, rows), :] = pieces[j][:, 3 * model :].astype(F32)
    vec_ref[...] = col_ref[...].T[: vec_ref.shape[0]]


def assemble_qkv(pieces, me, model, seq_parts):
    part_width = model // seq_parts
    count = len(pieces)
    return pl.pallas_call(
        partial(assemble_qkv_kernel, count, seq_parts, part_width),
        name="assemble_qkv",
        out_shape=(
            jax.ShapeDtypeStruct((seq_parts, model, 3 * part_width), BF),
            jax.ShapeDtypeStruct((16, model), F32),
        ),
        in_specs=[SM] + [VM] * count,
        out_specs=(VM, VM),
        scratch_shapes=[pltpu.VMEM((model, 128), F32)],
        compiler_params=params(),
        cost_estimate=cost(0, 4 * 3 * model * model),
    )(me, *pieces)


def assemble_rest_kernel(count, me_ref, *refs):
    pieces, (out_ref, up_ref, down_ref) = refs[:count], refs[count:]
    model = out_ref.shape[0]
    rows = model // count
    ratio = up_ref.shape[1] // model
    down_rows = ratio * rows
    for j in range(count):
        owner = me_ref[0] ^ j
        start = pl.multiple_of(owner * rows, rows)
        out_ref[pl.ds(start, rows), :] = pieces[j][:rows]
        for t in range(ratio):
            up_ref[pl.ds(start, rows), t * model : (t + 1) * model] = pieces[j][
                (1 + t) * rows : (2 + t) * rows
            ]
        down_ref[pl.ds(pl.multiple_of(owner * down_rows, down_rows), down_rows), :] = pieces[j][
            (1 + ratio) * rows :
        ]


def assemble_rest(pieces, me, model, hidden):
    count = len(pieces)
    return pl.pallas_call(
        partial(assemble_rest_kernel, count),
        name="assemble_rest",
        out_shape=(
            jax.ShapeDtypeStruct((model, model), BF),
            jax.ShapeDtypeStruct((model, hidden), BF),
            jax.ShapeDtypeStruct((hidden, model), BF),
        ),
        in_specs=[SM] + [VM] * count,
        out_specs=(VM, VM, VM),
        compiler_params=params(),
        cost_estimate=cost(0, 4 * (model * model + 2 * model * hidden)),
    )(me, *pieces)


def norm_parts(rows):
    mean_row = jnp.mean(rows, axis=-1, keepdims=True)
    centred = rows - mean_row
    inverse = lax.rsqrt(jnp.mean(centred * centred, axis=-1, keepdims=True) + EPS)
    return centred * inverse, inverse


def norm_back(grad_normed, scaled, inverse, gain):
    grad_scaled = grad_normed * gain
    centre = jnp.mean(grad_scaled, axis=-1, keepdims=True)
    along = jnp.mean(grad_scaled * scaled, axis=-1, keepdims=True)
    return inverse * (grad_scaled - centre - scaled * along)


def project_kernel(parts, me_ref, tokens_ref, embed_ref, wq_ref, vec_ref, hidden_ref, *outs):
    rows = tokens_ref[0].astype(F32) + embed_ref[0].astype(F32)
    scaled, _ = norm_parts(rows)
    hidden = (scaled * vec_ref[0:1] + vec_ref[1:2]).astype(BF)
    hidden_ref[...] = hidden
    for k in range(parts):
        outs[k][...] = dot(hidden, wq_ref[me_ref[0] ^ k]).astype(BF)


def project(tokens, embed, micro_index, wq, vec, me):
    _, rows, model = tokens.shape
    parts, _, width = wq.shape
    row_spec = pl.BlockSpec((1, rows, model), lambda i: (micro_index, 0, 0))
    whole = lambda shape: pl.BlockSpec(shape, lambda i: (0,) * len(shape))
    return pl.pallas_call(
        partial(project_kernel, parts),
        name="project",
        grid=(1,),
        out_shape=[jax.ShapeDtypeStruct((rows, model), BF)]
        + [jax.ShapeDtypeStruct((rows, width), BF)] * parts,
        in_specs=[SM, row_spec, row_spec, whole(wq.shape), whole(vec.shape)],
        out_specs=[whole((rows, model))] + [whole((rows, width))] * parts,
        compiler_params=params(),
        cost_estimate=cost(2 * rows * model * width * parts, 4e6),
    )(me, tokens, embed, wq, vec)


def head_mask(value, head, heads, head_dim):
    if heads == 1:
        return value
    lane = lax.broadcasted_iota(jnp.int32, value.shape, 1)
    keep = (lane >= head * head_dim) & (lane < (head + 1) * head_dim)
    return jnp.where(keep, value, jnp.zeros_like(value))


def attend_kernel(
    parts, heads, head_dim, me_ref, low_ref, high_ref, col_ref, row_ref, *refs
):
    pieces = refs[:parts]
    outs = refs[parts : 2 * parts]
    log_ref = refs[2 * parts]
    query_s, key_s, value_s, out_s = refs[2 * parts + 1 :]
    rows, width = pieces[0].shape
    here = width // 3
    length = rows * parts
    for k in range(parts):
        place = pl.ds(pl.multiple_of((me_ref[0] ^ k) * rows, rows), rows)
        query_s[place, :] = pieces[k][:, 0:here]
        key_s[place, :] = pieces[k][:, here : 2 * here]
        value_s[place, :] = pieces[k][:, 2 * here :]
    scale = head_dim ** (-0.5) * LOG2E

    def one_block(i, _):
        place = pl.ds(pl.multiple_of(i * BLOCK, BLOCK), BLOCK)
        query = query_s[place, :]
        queries = [head_mask(query, h, heads, head_dim) for h in range(heads)]
        doc_row = row_ref[i]

        def one_key(j, carry):
            key_place = pl.ds(pl.multiple_of(j * BLOCK, BLOCK), BLOCK)
            keys = key_s[key_place, :]
            values_t = value_s[key_place, :].astype(F32).T.astype(BF)
            same = col_ref[key_place, :] == doc_row
            result = []
            for h in range(heads):
                top, total, acc = carry[h]
                scores = jnp.where(same, dot_t(keys, queries[h]) * scale, -jnp.inf)
                new_top = jnp.maximum(top, jnp.max(scores, axis=0, keepdims=True))
                safe = jnp.where(new_top == -jnp.inf, 0.0, new_top)
                shrink = jnp.exp2(top - safe)
                weight = jnp.exp2(scores - safe)
                total = total * shrink + jnp.sum(weight, axis=0, keepdims=True)
                part = dot(values_t[h * head_dim : (h + 1) * head_dim], weight.astype(BF))
                result.append((new_top, total, acc * shrink + part))
            return tuple(result)

        start = tuple(
            (
                jnp.full((1, BLOCK), -jnp.inf, F32),
                jnp.zeros((1, BLOCK), F32),
                jnp.zeros((head_dim, BLOCK), F32),
            )
            for _ in range(heads)
        )
        done = lax.fori_loop(low_ref[i], high_ref[i], one_key, start)
        mixed = []
        for h in range(heads):
            top, total, acc = done[h]
            mixed.append(acc / total)
            log_ref[h, i] = top + jnp.log2(total)
        mixed = jnp.concatenate(mixed, axis=0) if heads > 1 else mixed[0]
        out_s[place, :] = mixed.T.astype(BF)
        return 0

    lax.fori_loop(0, length // BLOCK, one_block, 0)
    for k in range(parts):
        place = pl.ds(pl.multiple_of((me_ref[0] ^ k) * rows, rows), rows)
        outs[k][...] = out_s[place, :]


def attend(pieces, me, low, high, doc_col, doc_row, heads, head_dim):
    parts = len(pieces)
    rows, width = pieces[0].shape
    here = width // 3
    length = rows * parts
    blocks = length // BLOCK
    found = pl.pallas_call(
        partial(attend_kernel, parts, heads, head_dim),
        name="attend",
        out_shape=[jax.ShapeDtypeStruct((rows, here), BF)] * parts
        + [jax.ShapeDtypeStruct((heads, blocks, 1, BLOCK), F32)],
        in_specs=[SM, SM, SM, VM, VM] + [VM] * parts,
        out_specs=[VM] * (parts + 1),
        scratch_shapes=[pltpu.VMEM((length, here), BF)] * 4,
        compiler_params=params(),
        cost_estimate=cost(4e9, 3e6, 2e6),
    )(me, low, high, doc_col, doc_row, *pieces)
    return found[:parts], found[parts]


def attend_back_kernel(
    parts, heads, head_dim, me_ref, low_ref, high_ref, col_ref, row_ref, log_ref, *refs
):
    pieces = refs[:parts]
    mixes = refs[parts : 2 * parts]
    grads = refs[2 * parts : 3 * parts]
    outs = refs[3 * parts : 4 * parts]
    query_s, key_s, value_s, grad_s, centre_s, query_t, triple_s = refs[4 * parts :]
    rows, width = pieces[0].shape
    here = width // 3
    length = rows * parts
    blocks = length // BLOCK
    for k in range(parts):
        place = pl.ds(pl.multiple_of((me_ref[0] ^ k) * rows, rows), rows)
        query_s[place, :] = pieces[k][:, 0:here]
        key_s[place, :] = pieces[k][:, here : 2 * here]
        value_s[place, :] = pieces[k][:, 2 * here :]
        grad_s[place, :] = grads[k][...]
        triple_s[place, 0:here] = mixes[k][...]
    scale = head_dim ** (-0.5)

    def prepare(i, _):
        place = pl.ds(pl.multiple_of(i * BLOCK, BLOCK), BLOCK)
        both = grad_s[place, :].astype(F32) * triple_s[place, 0:here].astype(F32)
        both = both.T
        for h in range(heads):
            centre_s[h, i] = jnp.sum(
                both[h * head_dim : (h + 1) * head_dim], axis=0, keepdims=True
            )
        query_t[i] = jnp.zeros((here, BLOCK), F32)
        return 0

    lax.fori_loop(0, blocks, prepare, 0)

    def one_key(j, _):
        key_place = pl.ds(pl.multiple_of(j * BLOCK, BLOCK), BLOCK)
        keys = key_s[key_place, :]
        values = value_s[key_place, :]
        keys_t = keys.astype(F32).T.astype(BF)
        doc_col = col_ref[key_place, :]

        def one_block(i, carry):
            grad_key, grad_value = carry
            place = pl.ds(pl.multiple_of(i * BLOCK, BLOCK), BLOCK)
            query = query_s[place, :]
            grad = grad_s[place, :]
            same = doc_col == row_ref[i]
            steps = []
            for h in range(heads):
                query_h = head_mask(query, h, heads, head_dim)
                grad_h = head_mask(grad, h, heads, head_dim)
                scores = jnp.where(same, dot_t(keys, query_h) * (scale * LOG2E), -jnp.inf)
                weight = jnp.exp2(scores - log_ref[h, i])
                grad_weight = dot_t(values, grad_h)
                grad_value = grad_value + dot(weight.astype(BF), grad_h)
                grad_score = (weight * (grad_weight - centre_s[h, i])).astype(BF)
                grad_key = grad_key + dot(grad_score, query_h)
                steps.append(dot(keys_t[h * head_dim : (h + 1) * head_dim], grad_score))
            step = jnp.concatenate(steps, axis=0) if heads > 1 else steps[0]
            query_t[i] = query_t[i] + step
            return grad_key, grad_value

        zero = jnp.zeros((BLOCK, here), F32)
        grad_key, grad_value = lax.fori_loop(low_ref[j], high_ref[j], one_block, (zero, zero))
        triple_s[key_place, here : 2 * here] = (grad_key * scale).astype(BF)
        triple_s[key_place, 2 * here :] = grad_value.astype(BF)
        return 0

    lax.fori_loop(0, blocks, one_key, 0)

    def finish(i, _):
        place = pl.ds(pl.multiple_of(i * BLOCK, BLOCK), BLOCK)
        triple_s[place, 0:here] = (query_t[i].T * scale).astype(BF)
        return 0

    lax.fori_loop(0, blocks, finish, 0)
    for k in range(parts):
        place = pl.ds(pl.multiple_of((me_ref[0] ^ k) * rows, rows), rows)
        outs[k][...] = triple_s[place, :]


def attend_back(pieces, mixes, grads, me, low, high, doc_col, doc_row, log_total, heads, head_dim):
    parts = len(pieces)
    rows, width = pieces[0].shape
    here = width // 3
    length = rows * parts
    blocks = length // BLOCK
    return pl.pallas_call(
        partial(attend_back_kernel, parts, heads, head_dim),
        name="attend_back",
        out_shape=[jax.ShapeDtypeStruct((rows, width), BF)] * parts,
        in_specs=[SM, SM, SM, VM, VM, VM] + [VM] * (3 * parts),
        out_specs=[VM] * parts,
        scratch_shapes=[pltpu.VMEM((length, here), BF)] * 4
        + [
            pltpu.VMEM((heads, blocks, 1, BLOCK), F32),
            pltpu.VMEM((blocks, here, BLOCK), F32),
            pltpu.VMEM((length, width), BF),
        ],
        compiler_params=params(),
        cost_estimate=cost(8e9, 4e6, 2e6),
    )(me, low, high, doc_col, doc_row, log_total, *pieces, *mixes, *grads)


CHUNK = 512


def feed_kernel(parts, has_old, me_ref, tokens_ref, embed_ref, cot_ref, vec_ref, bias_ref, *refs):
    mixes = refs[:parts]
    w_out, w_up, w_down = refs[parts : parts + 3]
    refs = refs[parts + 3 + has_old :]
    out_ref, act_ref, pre_ref, hidden_ref, branch_ref, middle_ref, sums_ref = refs[:7]
    grads = refs[7 : 7 + parts]
    total_s, back_s = refs[7 + parts :]
    me = me_ref[0]
    here = mixes[0].shape[1]
    middle = tokens_ref[0].astype(F32) + embed_ref[0].astype(F32)
    for k in range(parts):
        place = pl.ds(pl.multiple_of((me ^ k) * here, here), here)
        middle = middle + dot(mixes[k][...], w_out[place, :])
    scaled, inverse = norm_parts(middle)
    hidden_ref[...] = (scaled * vec_ref[2:3] + vec_ref[3:4]).astype(BF)
    middle_ref[...] = middle
    total_s[...] = jnp.zeros_like(total_s)
    back_s[...] = jnp.zeros_like(back_s)
    root = 0.7978845608028654

    def one_chunk(f, _):
        place = pl.ds(pl.multiple_of(f * CHUNK, CHUNK), CHUNK)
        value = dot(hidden_ref[...], w_up[:, place]) + bias_ref[f]
        square = value * value
        bend = jnp.tanh(root * (value + 0.044715 * (value * square)))
        half = 0.5 * (1.0 + bend)
        act = (value * half).astype(BF)
        slope = half + (0.5 * root) * value * (1.0 - bend * bend) * (1.0 + 0.134145 * square)
        act_ref[:, place] = act
        total_s[...] += dot(act, w_down[place, :])
        grad_pre = (dot_t(cot_ref[0], w_down[place, :]) * slope).astype(BF)
        pre_ref[:, place] = grad_pre
        back_s[...] += dot_t(grad_pre, w_up[:, place])
        return 0

    lax.fori_loop(0, w_up.shape[1] // CHUNK, one_chunk, 0)
    middle = middle_ref[...]
    out_ref[0] = (middle + total_s[...] + vec_ref[4:5]).astype(BF)
    scaled, inverse = norm_parts(middle)
    grad_hidden = back_s[...]
    sums_ref[0:1] = jnp.sum(grad_hidden * scaled, axis=0, keepdims=True)
    sums_ref[1:2] = jnp.sum(grad_hidden, axis=0, keepdims=True)
    cot = cot_ref[0].astype(F32)
    sums_ref[2:3] = jnp.sum(cot, axis=0, keepdims=True)
    sums_ref[3:8] = jnp.zeros((5, sums_ref.shape[1]), F32)
    grad_middle = cot + norm_back(grad_hidden, scaled, inverse, vec_ref[2:3])
    middle_ref[...] = grad_middle
    branch = grad_middle.astype(BF)
    branch_ref[...] = branch
    for k in range(parts):
        place = pl.ds(pl.multiple_of((me ^ k) * here, here), here)
        grads[k][...] = dot_t(branch, w_out[place, :]).astype(BF)


def feed(tokens, embed, cot, micro_index, mixes, vec, bias, w_out, w_up, w_down, old, me):
    micro, rows, model = tokens.shape
    parts = len(mixes)
    here = mixes[0].shape[1]
    hidden = w_up.shape[1]
    row_spec = pl.BlockSpec((1, rows, model), lambda i: (micro_index, 0, 0))
    whole = lambda shape: pl.BlockSpec(shape, lambda i: (0,) * len(shape))
    old_args = [] if old is None else [old]
    found = pl.pallas_call(
        partial(feed_kernel, parts, len(old_args)),
        name="feed",
        grid=(1,),
        out_shape=[
            jax.ShapeDtypeStruct((micro, rows, model), BF),
            jax.ShapeDtypeStruct((rows, hidden), BF),
            jax.ShapeDtypeStruct((rows, hidden), BF),
            jax.ShapeDtypeStruct((rows, model), BF),
            jax.ShapeDtypeStruct((rows, model), BF),
            jax.ShapeDtypeStruct((rows, model), F32),
            jax.ShapeDtypeStruct((8, model), F32),
        ]
        + [jax.ShapeDtypeStruct((rows, here), BF)] * parts,
        in_specs=[SM, row_spec, row_spec, row_spec, whole(vec.shape), whole(bias.shape)]
        + [whole((rows, here))] * parts
        + [whole(w_out.shape), whole(w_up.shape), whole(w_down.shape)]
        + [pl.BlockSpec(memory_space=pl.ANY)] * len(old_args),
        out_specs=[
            row_spec,
            whole((rows, hidden)),
            whole((rows, hidden)),
            whole((rows, model)),
            whole((rows, model)),
            whole((rows, model)),
            whole((8, model)),
        ]
        + [whole((rows, here))] * parts,
        scratch_shapes=[pltpu.VMEM((rows, model), F32)] * 2,
        input_output_aliases={9 + parts: 0} if old_args else {},
        compiler_params=params(),
        cost_estimate=cost(8 * rows * model * hidden + 4 * rows * model * model, 12e6, rows * hidden),
    )(me, tokens, embed, cot, vec, bias, *mixes, w_out, w_up, w_down, *old_args)
    return found[:7], found[7:]


def rest_grads_kernel(micro, parts, count, me_s, me_f, cot_ref, *refs):
    acts, pres, hiddens, branches = (refs[micro * t : micro * (t + 1)] for t in range(4))
    mixes = refs[4 * micro : 4 * micro + micro * parts]
    keep_ref, send_ref, bias_ref, hidden_t, cot_t, mixed_t = refs[4 * micro + micro * parts :]
    rows, model = hiddens[0].shape
    here = mixes[0].shape[1]
    ratio = acts[0].shape[1] // model
    part = model // count
    down = ratio * part
    for m in range(micro):
        hidden_t[m] = hiddens[m][...].astype(F32).T.astype(BF)
        cot_t[m] = cot_ref[m].astype(F32).T.astype(BF)
        for k in range(parts):
            place = pl.ds(pl.multiple_of((me_s[0] ^ k) * here, here), here)
            mixed_t[m, place, :] = mixes[m * parts + k][...].astype(F32).T.astype(BF)

    def one(j, target, slot):
        owner = me_f[0] ^ j
        place = pl.ds(pl.multiple_of(owner * part, part), part)
        for t in range(ratio + 1):
            lane = (t - 1) * model
            if t == 0:
                found = sum(dot(mixed_t[m, place, :], branches[m][...]) for m in range(micro))
            else:
                found = sum(
                    dot(hidden_t[m, place, :], pres[m][:, lane : lane + model])
                    for m in range(micro)
                )
            target[slot, t * part : (t + 1) * part, :] = found.astype(BF)
        if down % 128 == 0:
            wide = pl.ds(pl.multiple_of(owner * down, down), down)
            found = sum(dot(cot_t[m], acts[m][:, wide]) for m in range(micro))
            for t in range(model // down):
                target[slot, (ratio + 1) * part :, t * down : (t + 1) * down] = found[
                    t * down : (t + 1) * down
                ].astype(BF)
        else:
            base = pl.multiple_of((owner * down) // 128 * 128, 128)
            odd = (owner * down) % 128 // down
            wide = [acts[m][:, pl.ds(base, 128)] for m in range(micro)]
            found = sum(dot(cot_t[m], wide[m]) for m in range(micro))
            picked = found[:, 0:down]
            for s in range(1, 128 // down):
                picked = jnp.where(odd == s, found[:, s * down : (s + 1) * down], picked)
            for t in range(model // down):
                target[slot, (ratio + 1) * part :, t * down : (t + 1) * down] = picked[
                    t * down : (t + 1) * down
                ].astype(BF)

    def one_pair(s, _):
        one(2 * s, keep_ref, s)
        one(2 * s + 1, send_ref, s)
        return 0

    lax.fori_loop(0, count // 2, one_pair, 0)
    ones = jnp.ones((8, rows), BF)
    bias_ref[...] = sum(dot(ones, pres[m][...]) for m in range(micro))


def rest_grads(cot, acts, pres, hiddens, branches, mixes, me_s, me_f, count):
    micro, rows, model = cot.shape
    parts = len(mixes[0])
    hidden = acts[0].shape[1]
    height = (model + 2 * hidden) // count
    half = jax.ShapeDtypeStruct((count // 2, height, model), BF)
    flat = [item for group in mixes for item in group]
    return pl.pallas_call(
        partial(rest_grads_kernel, micro, parts, count),
        name="rest_grads",
        out_shape=(half, half, jax.ShapeDtypeStruct((8, hidden), F32)),
        in_specs=[SM, SM] + [VM] * (1 + 4 * micro + micro * parts),
        out_specs=(VM, VM, VM),
        scratch_shapes=[pltpu.VMEM((micro, model, rows), BF)] * 3,
        compiler_params=params(60 * 1024 * 1024),
        cost_estimate=cost(2 * micro * rows * model * (model + 2 * hidden), 24e6),
    )(me_s, me_f, cot, *acts, *pres, *hiddens, *branches, *flat)


def input_kernel(parts, has_old, me_ref, tokens_ref, embed_ref, middle_ref, wq_ref, vec_ref, *refs):
    pieces = refs[:parts]
    out_ref, sums_ref = refs[parts + has_old :]
    grad_hidden = dot_t(pieces[0][...], wq_ref[me_ref[0]])
    for k in range(1, parts):
        grad_hidden = grad_hidden + dot_t(pieces[k][...], wq_ref[me_ref[0] ^ k])
    rows = tokens_ref[0].astype(F32) + embed_ref[0].astype(F32)
    scaled, inverse = norm_parts(rows)
    sums_ref[0:1] = jnp.sum(grad_hidden * scaled, axis=0, keepdims=True)
    sums_ref[1:2] = jnp.sum(grad_hidden, axis=0, keepdims=True)
    sums_ref[2:8] = jnp.zeros((6, sums_ref.shape[1]), F32)
    out_ref[0] = middle_ref[...] + norm_back(grad_hidden, scaled, inverse, vec_ref[0:1])


def input_gradient(tokens, embed, micro_index, grad_middle, pieces, wq, vec, old, me):
    micro, rows, model = tokens.shape
    parts = len(pieces)
    width = pieces[0].shape[1]
    row_spec = pl.BlockSpec((1, rows, model), lambda i: (micro_index, 0, 0))
    whole = lambda shape: pl.BlockSpec(shape, lambda i: (0,) * len(shape))
    old_args = [] if old is None else [old]
    return pl.pallas_call(
        partial(input_kernel, parts, len(old_args)),
        name="input_gradient",
        grid=(1,),
        out_shape=(
            jax.ShapeDtypeStruct((micro, rows, model), F32),
            jax.ShapeDtypeStruct((8, model), F32),
        ),
        in_specs=[SM, row_spec, row_spec, whole((rows, model)), whole(wq.shape), whole(vec.shape)]
        + [whole((rows, width))] * parts
        + [pl.BlockSpec(memory_space=pl.ANY)] * len(old_args),
        out_specs=(row_spec, whole((8, model))),
        input_output_aliases={6 + parts: 0} if old_args else {},
        compiler_params=params(),
        cost_estimate=cost(2 * rows * model * width * parts, 6e6),
    )(me, tokens, embed, grad_middle, wq, vec, *pieces, *old_args)


def qkv_grads_kernel(micro, parts, count, me_s, me_f, *refs):
    hiddens = refs[:micro]
    pieces = refs[micro : micro + micro * parts]
    keep_ref, send_ref, hidden_t = refs[micro + micro * parts :]
    rows, model = hiddens[0].shape
    width = pieces[0].shape[1]
    part = model // count
    for m in range(micro):
        hidden_t[m] = hiddens[m][...].astype(F32).T.astype(BF)

    def one(j, target, slot):
        place = pl.ds(pl.multiple_of((me_f[0] ^ j) * part, part), part)
        for k in range(parts):
            found = sum(
                dot(hidden_t[m, place, :], pieces[m * parts + k][...]) for m in range(micro)
            )
            target[slot, me_s[0] ^ k] = found.astype(BF)

    def one_pair(s, _):
        one(2 * s, keep_ref, s)
        one(2 * s + 1, send_ref, s)
        return 0

    lax.fori_loop(0, count // 2, one_pair, 0)


def qkv_grads(hiddens, pieces, me_s, me_f, count):
    micro = len(hiddens)
    rows, model = hiddens[0].shape
    parts = len(pieces[0])
    width = pieces[0][0].shape[1]
    half = jax.ShapeDtypeStruct((count // 2, parts, model // count, width), BF)
    flat = [item for group in pieces for item in group]
    return pl.pallas_call(
        partial(qkv_grads_kernel, micro, parts, count),
        name="qkv_grads",
        out_shape=(half, half),
        in_specs=[SM, SM] + [VM] * (micro + micro * parts),
        out_specs=(VM, VM),
        scratch_shapes=[pltpu.VMEM((micro, model, rows), BF)],
        compiler_params=params(),
        cost_estimate=cost(2 * micro * rows * model * parts * width, 7e6),
    )(me_s, me_f, *hiddens, *flat)


def add_low(left, right):
    return (left.astype(F32) + right.astype(F32)).astype(BF)


def reduce_to_owner(keep, send, axis):
    size = lax.axis_size(axis)
    bit = 1
    while True:
        found = swap(send, axis, bit)
        bit *= 2
        if bit == size:
            return add_low(keep, found)[0]
        keep, send = (
            add_low(keep[0::2], found[0::2]),
            add_low(keep[1::2], found[1::2]),
        )


def sum_over(value, axis):
    size = lax.axis_size(axis)
    bit = 1
    while bit < size:
        value = (value.astype(F32) + swap(value, axis, bit).astype(F32)).astype(value.dtype)
        bit *= 2
    return value


def local(
    tokens,
    time_embed,
    doc_ids,
    out_grad,
    norm1_gain,
    norm1_shift,
    qkv_weight,
    out_weight,
    norm2_gain,
    norm2_shift,
    up_weight,
    up_bias,
    down_weight,
    down_bias,
):
    micro, _, rows, model = tokens.shape
    parts = lax.axis_size("seq")
    count = lax.axis_size("fsdp")
    hidden = up_weight.shape[1]
    ratio = hidden // model
    length = rows * parts
    head_dim = model // HEADS
    heads = HEADS // parts
    here = heads * head_dim
    blocks = length // BLOCK
    share = model // count
    seq_index = lax.axis_index("seq").astype(jnp.int32)
    fsdp_index = lax.axis_index("fsdp").astype(jnp.int32)
    me_s = seq_index.reshape(1)
    me_f = fsdp_index.reshape(1)
    tokens = tokens[:, 0]
    embed = time_embed[:, 0]
    cot = out_grad[:, 0]

    columns = jnp.stack(
        [norm1_gain, norm1_shift, norm2_gain, norm2_shift, down_bias]
        + [up_bias[t * share : (t + 1) * share] for t in range(ratio)]
        + [jnp.zeros_like(norm1_gain)] * (128 - 5 - ratio),
        axis=1,
    )
    first = jnp.concatenate([qkv_weight, columns], axis=1)
    rest = jnp.concatenate(
        [out_weight]
        + [up_weight[:, t * model : (t + 1) * model] for t in range(ratio)]
        + [down_weight],
        axis=0,
    )
    wq, vec = assemble_qkv(gather_pieces(first, "fsdp"), me_f, model, parts)
    w_out, w_up, w_down = assemble_rest(gather_pieces(rest, "fsdp"), me_f, model, hidden)
    bias = (
        vec[5 : 5 + ratio].reshape(ratio, count, share).transpose(1, 0, 2).reshape(-1, 1, CHUNK)
    )

    docs = jnp.zeros((micro, length), jnp.int32)
    for k, piece in enumerate(gather_pieces(doc_ids[:, 0], "seq")):
        docs = lax.dynamic_update_slice(docs, piece, (0, (seq_index ^ k) * rows))
    doc_row = docs.reshape(micro, blocks, 1, BLOCK)
    doc_col = docs.reshape(micro, length, 1)
    first_doc = doc_row[:, :, :, 0]
    last_doc = doc_row[:, :, :, BLOCK - 1]
    low = jnp.sum(docs[:, None, :] < first_doc, axis=2, dtype=jnp.int32) // BLOCK
    high = (jnp.sum(docs[:, None, :] <= last_doc, axis=2, dtype=jnp.int32) + BLOCK - 1) // BLOCK

    hiddens, triples, mixes, logs = [], [], [], []
    for m in range(micro):
        found = project(tokens, embed, m, wq, vec, me_s)
        hiddens.append(found[0])
        triples.append(exchange(found[1:], "seq"))
    sent = []
    for m in range(micro):
        outs, log_total = attend(
            triples[m], me_s, low[m], high[m], doc_col[m], doc_row[m], heads, head_dim
        )
        sent.append(outs)
        logs.append(log_total)
        mixes.append(exchange(outs, "seq"))
    layer_output = None
    acts, pres, seconds, branches, middles, sums, heads_grads = [], [], [], [], [], [], []
    for m in range(micro):
        found, grads = feed(
            tokens, embed, cot, m, mixes[m], vec, bias, w_out, w_up, w_down, layer_output, me_s
        )
        layer_output = found[0]
        acts.append(found[1])
        pres.append(found[2])
        seconds.append(found[3])
        branches.append(found[4])
        middles.append(found[5])
        sums.append(found[6])
        heads_grads.append(exchange(grads, "seq"))
    keep, send, bias_sum = rest_grads(
        cot, acts, pres, seconds, branches, mixes, me_s, me_f, count
    )
    rest_sum = sum_over(reduce_to_owner(keep, send, "fsdp"), "seq")
    input_grad = None
    backs, first_sums = [], []
    for m in range(micro):
        outs = attend_back(
            triples[m],
            sent[m],
            heads_grads[m],
            me_s,
            low[m],
            high[m],
            doc_col[m],
            doc_row[m],
            logs[m],
            heads,
            head_dim,
        )
        backs.append(exchange(outs, "seq"))
    for m in range(micro):
        input_grad, sum_one = input_gradient(
            tokens, embed, m, middles[m], backs[m], wq, vec, input_grad, me_s
        )
        first_sums.append(sum_one)
    keep, send = qkv_grads(hiddens, backs, me_s, me_f, count)
    qkv_sum = sum_over(reduce_to_owner(keep, send, "fsdp"), "seq")

    second = sum(sums)
    once = sum(first_sums)
    vectors = jnp.concatenate(
        [
            once[0:2],
            second[0:3],
            jnp.zeros((3, model), F32),
            bias_sum[0].reshape(ratio, model),
            jnp.zeros((4, model), F32),
        ],
        axis=0,
    )
    vectors = sum_over(sum_over(vectors, "fsdp"), "seq")
    pick = lambda row: lax.dynamic_slice(vectors[row], (fsdp_index * share,), (share,))
    grad_up_bias = lax.dynamic_slice(
        vectors[8 : 8 + ratio].reshape(hidden), (fsdp_index * (hidden // count),), (hidden // count,)
    )
    qkv_sum = qkv_sum.astype(F32)
    grad_qkv = (
        qkv_sum.reshape(parts, share, 3, here).transpose(1, 2, 0, 3).reshape(share, 3 * model)
    )
    rest_sum = rest_sum.astype(F32)
    grad_out = rest_sum[:share]
    grad_up = jnp.concatenate(
        [rest_sum[(1 + t) * share : (2 + t) * share] for t in range(ratio)], axis=1
    )
    down = ratio * share
    grad_down = (
        rest_sum[(1 + ratio) * share :]
        .reshape(down, model // down, down)
        .transpose(2, 1, 0)
        .reshape(down, model)
    )
    return (
        layer_output[:, None],
        input_grad[:, None],
        pick(0),
        pick(1),
        grad_qkv,
        grad_out,
        pick(2),
        pick(3),
        grad_up,
        grad_up_bias,
        grad_down,
        pick(4),
    )


def solution(mesh):
    rows = P(None, "fsdp", "seq", None)
    vector = P("fsdp")
    matrix = P("fsdp", None)
    return jax.shard_map(
        local,
        mesh=mesh,
        in_specs=(
            rows,
            rows,
            P(None, "fsdp", "seq"),
            rows,
            vector,
            vector,
            matrix,
            matrix,
            vector,
            vector,
            matrix,
            vector,
            matrix,
            vector,
        ),
        out_specs=(
            rows,
            rows,
            vector,
            vector,
            matrix,
            matrix,
            vector,
            vector,
            matrix,
            vector,
            matrix,
            vector,
        ),
        check_vma=False,
    )
```

```python
from functools import partial

import jax
import jax.numpy as jnp
from jax import lax
from jax.experimental import pallas as pl
from jax.experimental.pallas import tpu as pltpu
from jax.sharding import PartitionSpec as P

HEADS = 8
EPS = 1e-05
LOG2E = 1.4426950408889634
WIDE = 512
NARROW = 384
PACK = 256
VMEM_LIMIT = 24 * 1024 * 1024
BF = jnp.bfloat16
F32 = jnp.float32


def dot(a, b, dims=((1,), (0,))):
    return lax.dot_general(a, b, (dims, ((), ())), preferred_element_type=F32)


def dot_t(a, b):
    return dot(a, b, ((1,), (1,)))


def params(limit=VMEM_LIMIT):
    return pltpu.CompilerParams(vmem_limit_bytes=limit)


def cost(flops, read, transcendentals=0):
    return pl.CostEstimate(
        flops=int(flops), bytes_accessed=int(read), transcendentals=int(transcendentals)
    )


VM = pl.BlockSpec(memory_space=pltpu.VMEM)
SM = pl.BlockSpec(memory_space=pltpu.SMEM)


def swap(value, axis, bit):
    size = lax.axis_size(axis)
    return lax.ppermute(value, axis, [(i, i ^ bit) for i in range(size)])


def gather_pieces(value, axis):
    size = lax.axis_size(axis)
    held = {0: value}
    bit = size // 2
    while bit:
        held.update({j | bit: swap(item, axis, bit) for j, item in list(held.items())})
        bit //= 2
    return [held[j] for j in range(size)]


def exchange(pieces, axis):
    return [pieces[0]] + [swap(pieces[k], axis, k) for k in range(1, len(pieces))]


def assemble_qkv_kernel(count, seq_parts, part_width, me_ref, *refs):
    pieces, (wq_ref, vec_ref, col_ref) = refs[:count], refs[count:]
    rows, width = pieces[0].shape
    model = wq_ref.shape[1]
    for j in range(count):
        start = pl.multiple_of((me_ref[0] ^ j) * rows, rows)
        for d in range(seq_parts):
            for t in range(3):
                lane = t * model + d * part_width
                wq_ref[d, pl.ds(start, rows), t * part_width : (t + 1) * part_width] = pieces[j][
                    :, lane : lane + part_width
                ]
        col_ref[pl.ds(start, rows), :] = pieces[j][:, 3 * model :].astype(F32)
    vec_ref[...] = col_ref[...].T[: vec_ref.shape[0]]


def assemble_qkv(pieces, me, model, seq_parts):
    part_width = model // seq_parts
    count = len(pieces)
    return pl.pallas_call(
        partial(assemble_qkv_kernel, count, seq_parts, part_width),
        name="assemble_qkv",
        out_shape=(
            jax.ShapeDtypeStruct((seq_parts, model, 3 * part_width), BF),
            jax.ShapeDtypeStruct((16, model), F32),
        ),
        in_specs=[SM] + [VM] * count,
        out_specs=(VM, VM),
        scratch_shapes=[pltpu.VMEM((model, 128), F32)],
        compiler_params=params(),
        cost_estimate=cost(0, 4 * 3 * model * model),
    )(me, *pieces)


def assemble_rest_kernel(count, me_ref, *refs):
    pieces, (out_ref, up_ref, down_ref) = refs[:count], refs[count:]
    model = out_ref.shape[0]
    rows = model // count
    ratio = up_ref.shape[1] // model
    down_rows = ratio * rows
    for j in range(count):
        owner = me_ref[0] ^ j
        start = pl.multiple_of(owner * rows, rows)
        out_ref[pl.ds(start, rows), :] = pieces[j][:rows]
        for t in range(ratio):
            up_ref[pl.ds(start, rows), t * model : (t + 1) * model] = pieces[j][
                (1 + t) * rows : (2 + t) * rows
            ]
        down_ref[pl.ds(pl.multiple_of(owner * down_rows, down_rows), down_rows), :] = pieces[j][
            (1 + ratio) * rows :
        ]


def assemble_rest(pieces, me, model, hidden):
    count = len(pieces)
    return pl.pallas_call(
        partial(assemble_rest_kernel, count),
        name="assemble_rest",
        out_shape=(
            jax.ShapeDtypeStruct((model, model), BF),
            jax.ShapeDtypeStruct((model, hidden), BF),
            jax.ShapeDtypeStruct((hidden, model), BF),
        ),
        in_specs=[SM] + [VM] * count,
        out_specs=(VM, VM, VM),
        compiler_params=params(),
        cost_estimate=cost(0, 4 * (model * model + 2 * model * hidden)),
    )(me, *pieces)


def norm_parts(rows):
    mean_row = jnp.mean(rows, axis=-1, keepdims=True)
    centred = rows - mean_row
    inverse = lax.rsqrt(jnp.mean(centred * centred, axis=-1, keepdims=True) + EPS)
    return centred * inverse, inverse


def norm_back(grad_normed, scaled, inverse, gain):
    grad_scaled = grad_normed * gain
    centre = jnp.mean(grad_scaled, axis=-1, keepdims=True)
    along = jnp.mean(grad_scaled * scaled, axis=-1, keepdims=True)
    return inverse * (grad_scaled - centre - scaled * along)


def project_kernel(parts, me_ref, tokens_ref, embed_ref, wq_ref, vec_ref, hidden_ref, *outs):
    rows = tokens_ref[0].astype(F32) + embed_ref[0].astype(F32)
    scaled, _ = norm_parts(rows)
    hidden = (scaled * vec_ref[0:1] + vec_ref[1:2]).astype(BF)
    hidden_ref[...] = hidden
    for k in range(parts):
        outs[k][...] = dot(hidden, wq_ref[me_ref[0] ^ k]).astype(BF)


def project(tokens, embed, micro_index, wq, vec, me):
    _, rows, model = tokens.shape
    parts, _, width = wq.shape
    row_spec = pl.BlockSpec((1, rows, model), lambda i: (micro_index, 0, 0))
    whole = lambda shape: pl.BlockSpec(shape, lambda i: (0,) * len(shape))
    return pl.pallas_call(
        partial(project_kernel, parts),
        name="project",
        grid=(1,),
        out_shape=[jax.ShapeDtypeStruct((rows, model), BF)]
        + [jax.ShapeDtypeStruct((rows, width), BF)] * parts,
        in_specs=[SM, row_spec, row_spec, whole(wq.shape), whole(vec.shape)],
        out_specs=[whole((rows, model))] + [whole((rows, width))] * parts,
        compiler_params=params(),
        cost_estimate=cost(2 * rows * model * width * parts, 4e6),
    )(me, tokens, embed, wq, vec)


def head_mask(value, head, heads, head_dim):
    if heads == 1:
        return value
    lane = lax.broadcasted_iota(jnp.int32, value.shape, 1)
    keep = (lane >= head * head_dim) & (lane < (head + 1) * head_dim)
    return jnp.where(keep, value, jnp.zeros_like(value))


def spread_docs(doc_ref, doc_s):
    for start in range(0, doc_s.shape[0], 512):
        doc_s[start : start + 512, :] = jnp.broadcast_to(
            doc_ref[0:1, start : start + 512], (128, 512)
        ).T


def same_doc(doc_s, place, doc_row):
    column = doc_s[place, :]
    return jnp.concatenate([column] * (doc_row.shape[1] // 128), axis=1) == doc_row


def fold(value, combine):
    out = value[0:8]
    for start in range(8, value.shape[0], 8):
        out = combine(out, value[start : start + 8])
    return out


def attend_kernel(parts, heads, head_dim, me_ref, low_ref, high_ref, doc_ref, *refs):
    pieces = refs[:parts]
    outs = refs[parts : 2 * parts]
    log_ref = refs[2 * parts]
    query_s, key_s, value_t, doc_s, score_s, out_s = refs[2 * parts + 1 :]
    rows, width = pieces[0].shape
    here = width // 3
    length = rows * parts
    for k in range(parts):
        place = pl.ds(pl.multiple_of((me_ref[0] ^ k) * rows, rows), rows)
        query_s[place, :] = pieces[k][:, 0:here]
        key_s[place, :] = pieces[k][:, here : 2 * here]
        value_t[:, place] = pieces[k][:, 2 * here :].astype(F32).T.astype(BF)
    spread_docs(doc_ref, doc_s)
    scale = head_dim ** (-0.5) * LOG2E

    def one_block(i, _):
        place = pl.ds(pl.multiple_of(i * WIDE, WIDE), WIDE)
        query = query_s[place, :]
        queries = [head_mask(query, h, heads, head_dim) for h in range(heads)]
        doc_row = doc_ref[0:1, place]

        def score(j, tops):
            key_place = pl.ds(pl.multiple_of(j * NARROW, NARROW), NARROW)
            keys = key_s[key_place, :]
            same = same_doc(doc_s, key_place, doc_row)
            result = []
            for h in range(heads):
                scores = jnp.where(same, dot_t(keys, queries[h]) * scale, -jnp.inf)
                score_s[h, key_place, :] = scores
                result.append(jnp.maximum(tops[h], fold(scores, jnp.maximum)))
            return tuple(result)

        tops = lax.fori_loop(
            low_ref[i],
            high_ref[i],
            score,
            tuple(jnp.full((8, WIDE), -jnp.inf, F32) for _ in range(heads)),
        )
        tops = [jnp.max(top, axis=0, keepdims=True) for top in tops]

        def mix(j, carry):
            key_place = pl.ds(pl.multiple_of(j * NARROW, NARROW), NARROW)
            result = []
            for h in range(heads):
                total, acc = carry[h]
                weight = jnp.exp2(score_s[h, key_place, :] - tops[h])
                total = total + fold(weight, jnp.add)
                values = value_t[h * head_dim : (h + 1) * head_dim, key_place]
                result.append((total, acc + dot(values, weight.astype(BF))))
            return tuple(result)

        done = lax.fori_loop(
            low_ref[i],
            high_ref[i],
            mix,
            tuple(
                (jnp.zeros((8, WIDE), F32), jnp.zeros((head_dim, WIDE), F32))
                for _ in range(heads)
            ),
        )
        mixed = []
        for h in range(heads):
            total = jnp.sum(done[h][0], axis=0, keepdims=True)
            mixed.append(done[h][1] / total)
            log_ref[h, :, place] = jnp.broadcast_to(tops[h] + jnp.log2(total), (8, WIDE))
        mixed = jnp.concatenate(mixed, axis=0) if heads > 1 else mixed[0]
        out_s[place, :] = mixed.T.astype(BF)
        return 0

    lax.fori_loop(0, length // WIDE, one_block, 0)
    for k in range(parts):
        place = pl.ds(pl.multiple_of((me_ref[0] ^ k) * rows, rows), rows)
        outs[k][...] = out_s[place, :]


def attend(pieces, me, low, high, doc, heads, head_dim):
    parts = len(pieces)
    rows, width = pieces[0].shape
    here = width // 3
    length = rows * parts
    found = pl.pallas_call(
        partial(attend_kernel, parts, heads, head_dim),
        name="attend",
        out_shape=[jax.ShapeDtypeStruct((rows, here), BF)] * parts
        + [jax.ShapeDtypeStruct((heads, 8, length), F32)],
        in_specs=[SM, SM, SM, VM] + [VM] * parts,
        out_specs=[VM] * (parts + 1),
        scratch_shapes=[
            pltpu.VMEM((length, here), BF),
            pltpu.VMEM((length, here), BF),
            pltpu.VMEM((here, length), BF),
            pltpu.VMEM((length, 128), F32),
            pltpu.VMEM((heads, length, WIDE), F32),
            pltpu.VMEM((length, here), BF),
        ],
        compiler_params=params(),
        cost_estimate=cost(4e9, 3e6, 2e6),
    )(me, low, high, doc, *pieces)
    return found[:parts], found[parts]


def attend_back_kernel(parts, heads, head_dim, me_ref, low_ref, high_ref, doc_ref, log_ref, *refs):
    pieces = refs[:parts]
    mixes = refs[parts : 2 * parts]
    grads = refs[2 * parts : 3 * parts]
    outs = refs[3 * parts : 4 * parts]
    query_s, key_s, key_t, value_s, grad_s, centre_s, doc_s, query_t, pair_s = refs[4 * parts :]
    rows, width = pieces[0].shape
    here = width // 3
    length = rows * parts
    for k in range(parts):
        place = pl.ds(pl.multiple_of((me_ref[0] ^ k) * rows, rows), rows)
        query = pieces[k][:, 0:here]
        grad = grads[k][...]
        for h in range(heads):
            query_s[h, place, :] = head_mask(query, h, heads, head_dim)
            grad_s[h, place, :] = head_mask(grad, h, heads, head_dim)
        keys = pieces[k][:, here : 2 * here]
        key_s[place, :] = keys
        key_t[:, place] = keys.astype(F32).T.astype(BF)
        value_s[place, :] = pieces[k][:, 2 * here :]
        both = (grad.astype(F32) * mixes[k][...].astype(F32)).T
        for h in range(heads):
            centre = jnp.sum(both[h * head_dim : (h + 1) * head_dim], axis=0, keepdims=True)
            centre_s[h, :, place] = jnp.broadcast_to(centre, (8, rows))
    spread_docs(doc_ref, doc_s)
    query_t[...] = jnp.zeros_like(query_t)
    scale = head_dim ** (-0.5)

    def one_key(j, _):
        key_place = pl.ds(pl.multiple_of(j * WIDE, WIDE), WIDE)
        keys = key_s[key_place, :]
        values = value_s[key_place, :]
        keys_t = [key_t[h * head_dim : (h + 1) * head_dim, key_place] for h in range(heads)]

        def one_block(i, carry):
            grad_key, grad_value = carry
            place = pl.ds(pl.multiple_of(i * NARROW, NARROW), NARROW)
            same = same_doc(doc_s, key_place, doc_ref[0:1, place])
            for h in range(heads):
                query = query_s[h, place, :]
                grad = grad_s[h, place, :]
                scores = jnp.where(same, dot_t(keys, query) * (scale * LOG2E), -jnp.inf)
                weight = jnp.exp2(scores - log_ref[h, 0:1, place])
                grad_weight = dot_t(values, grad)
                grad_score = (weight * (grad_weight - centre_s[h, 0:1, place])).astype(BF)
                grad_value = grad_value + dot(weight.astype(BF), grad)
                grad_key = grad_key + dot(grad_score, query)
                query_t[h * head_dim : (h + 1) * head_dim, place] += dot(keys_t[h], grad_score)
            return grad_key, grad_value

        zero = jnp.zeros((WIDE, here), F32)
        grad_key, grad_value = lax.fori_loop(low_ref[j], high_ref[j], one_block, (zero, zero))
        pair_s[key_place, 0:here] = (grad_key * scale).astype(BF)
        pair_s[key_place, here:] = grad_value.astype(BF)
        return 0

    lax.fori_loop(0, length // WIDE, one_key, 0)
    for k in range(parts):
        place = pl.ds(pl.multiple_of((me_ref[0] ^ k) * rows, rows), rows)
        outs[k][:, 0:here] = (query_t[:, place].T * scale).astype(BF)
        outs[k][:, here:] = pair_s[place, :]


def attend_back(pieces, mixes, grads, me, low, high, doc, log_total, heads, head_dim):
    parts = len(pieces)
    rows, width = pieces[0].shape
    here = width // 3
    length = rows * parts
    return pl.pallas_call(
        partial(attend_back_kernel, parts, heads, head_dim),
        name="attend_back",
        out_shape=[jax.ShapeDtypeStruct((rows, width), BF)] * parts,
        in_specs=[SM, SM, SM, VM, VM] + [VM] * (3 * parts),
        out_specs=[VM] * parts,
        scratch_shapes=[
            pltpu.VMEM((heads, length, here), BF),
            pltpu.VMEM((length, here), BF),
            pltpu.VMEM((here, length), BF),
            pltpu.VMEM((length, here), BF),
            pltpu.VMEM((heads, length, here), BF),
            pltpu.VMEM((heads, 8, length), F32),
            pltpu.VMEM((length, 128), F32),
            pltpu.VMEM((here, length), F32),
            pltpu.VMEM((length, 2 * here), BF),
        ],
        compiler_params=params(),
        cost_estimate=cost(8e9, 4e6, 2e6),
    )(me, low, high, doc, log_total, *pieces, *mixes, *grads)


CHUNK = 512


def feed_kernel(parts, has_old, me_ref, tokens_ref, embed_ref, cot_ref, vec_ref, bias_ref, *refs):
    mixes = refs[:parts]
    w_out, w_up, w_down = refs[parts : parts + 3]
    refs = refs[parts + 3 + has_old :]
    out_ref, act_ref, pre_ref, hidden_ref, branch_ref, middle_ref, sums_ref = refs[:7]
    grads = refs[7 : 7 + parts]
    total_s, back_s = refs[7 + parts :]
    me = me_ref[0]
    here = mixes[0].shape[1]
    middle = tokens_ref[0].astype(F32) + embed_ref[0].astype(F32)
    for k in range(parts):
        place = pl.ds(pl.multiple_of((me ^ k) * here, here), here)
        middle = middle + dot(mixes[k][...], w_out[place, :])
    scaled, inverse = norm_parts(middle)
    hidden_ref[0] = (scaled * vec_ref[2:3] + vec_ref[3:4]).astype(BF)
    middle_ref[...] = middle
    total_s[...] = jnp.zeros_like(total_s)
    back_s[...] = jnp.zeros_like(back_s)
    root = 0.7978845608028654

    def one_chunk(f, _):
        place = pl.ds(pl.multiple_of(f * CHUNK, CHUNK), CHUNK)
        value = dot(hidden_ref[0], w_up[:, place]) + bias_ref[f]
        square = value * value
        bend = jnp.tanh(root * (value + 0.044715 * (value * square)))
        half = 0.5 * (1.0 + bend)
        act = (value * half).astype(BF)
        slope = half + (0.5 * root) * value * (1.0 - bend * bend) * (1.0 + 0.134145 * square)
        act_ref[0, :, place] = act
        total_s[...] += dot(act, w_down[place, :])
        grad_pre = (dot_t(cot_ref[0], w_down[place, :]) * slope).astype(BF)
        pre_ref[0, :, place] = grad_pre
        back_s[...] += dot_t(grad_pre, w_up[:, place])
        return 0

    lax.fori_loop(0, w_up.shape[1] // CHUNK, one_chunk, 0)
    middle = middle_ref[...]
    out_ref[0] = (middle + total_s[...] + vec_ref[4:5]).astype(BF)
    scaled, inverse = norm_parts(middle)
    grad_hidden = back_s[...]
    sums_ref[0:1] = jnp.sum(grad_hidden * scaled, axis=0, keepdims=True)
    sums_ref[1:2] = jnp.sum(grad_hidden, axis=0, keepdims=True)
    cot = cot_ref[0].astype(F32)
    sums_ref[2:3] = jnp.sum(cot, axis=0, keepdims=True)
    sums_ref[3:8] = jnp.zeros((5, sums_ref.shape[1]), F32)
    grad_middle = cot + norm_back(grad_hidden, scaled, inverse, vec_ref[2:3])
    middle_ref[...] = grad_middle
    branch = grad_middle.astype(BF)
    branch_ref[0] = branch
    for k in range(parts):
        place = pl.ds(pl.multiple_of((me ^ k) * here, here), here)
        grads[k][...] = dot_t(branch, w_out[place, :]).astype(BF)


def feed(tokens, embed, cot, micro_index, mixes, vec, bias, w_out, w_up, w_down, old, me):
    micro, rows, model = tokens.shape
    parts = len(mixes)
    here = mixes[0].shape[1]
    hidden = w_up.shape[1]
    row_spec = pl.BlockSpec((1, rows, model), lambda i: (micro_index, 0, 0))
    whole = lambda shape: pl.BlockSpec(shape, lambda i: (0,) * len(shape))
    wide_spec = pl.BlockSpec((1, rows, hidden), lambda i: (micro_index, 0, 0))
    old_args = [] if old is None else list(old)
    found = pl.pallas_call(
        partial(feed_kernel, parts, len(old_args)),
        name="feed",
        grid=(1,),
        out_shape=[
            jax.ShapeDtypeStruct((micro, rows, model), BF),
            jax.ShapeDtypeStruct((micro, rows, hidden), BF),
            jax.ShapeDtypeStruct((micro, rows, hidden), BF),
            jax.ShapeDtypeStruct((micro, rows, model), BF),
            jax.ShapeDtypeStruct((micro, rows, model), BF),
            jax.ShapeDtypeStruct((rows, model), F32),
            jax.ShapeDtypeStruct((8, model), F32),
        ]
        + [jax.ShapeDtypeStruct((rows, here), BF)] * parts,
        in_specs=[SM, row_spec, row_spec, row_spec, whole(vec.shape), whole(bias.shape)]
        + [whole((rows, here))] * parts
        + [whole(w_out.shape), whole(w_up.shape), whole(w_down.shape)]
        + [pl.BlockSpec(memory_space=pl.ANY)] * len(old_args),
        out_specs=[
            row_spec,
            wide_spec,
            wide_spec,
            row_spec,
            row_spec,
            whole((rows, model)),
            whole((8, model)),
        ]
        + [whole((rows, here))] * parts,
        scratch_shapes=[pltpu.VMEM((rows, model), F32)] * 2,
        input_output_aliases={9 + parts + t: t for t in range(len(old_args))},
        compiler_params=params(32 * 1024 * 1024),
        cost_estimate=cost(8 * rows * model * hidden + 4 * rows * model * model, 12e6, rows * hidden),
    )(me, tokens, embed, cot, vec, bias, *mixes, w_out, w_up, w_down, *old_args)
    return found[:7], found[7:]


def rest_grads_kernel(micro, parts, count, me_s, me_f, act_ref, pre_ref, hidden_ref, branch_ref,
                      cot_ref, *refs):
    mixes = refs[: micro * parts]
    keep_ref, send_ref, bias_ref = refs[micro * parts : micro * parts + 3]
    hidden_t, cot_t, mixed_t, up_s, down_s, out_s = refs[micro * parts + 3 :]
    targets = (keep_ref, send_ref)
    rows, model = hidden_ref.shape[1:]
    here = mixes[0].shape[1]
    share = model // count
    chunk = pl.program_id(0)
    owners, _, down_lanes = down_s.shape
    down_rows = model // parts
    up_rows, down_height, out_groups, _ = rest_layout(model, pl.num_programs(0) * model, parts, count)

    @pl.when(chunk == 0)
    def _():
        for m in range(micro):
            hidden_t[m] = hidden_ref[m].astype(F32).T.astype(BF)
            cot_t[m] = cot_ref[m].astype(F32).T.astype(BF)
            for k in range(parts):
                place = pl.ds(pl.multiple_of((me_s[0] ^ k) * here, here), here)
                mixed_t[m, place, :] = mixes[m * parts + k][...].astype(F32).T.astype(BF)
        found = sum(dot(mixed_t[m], branch_ref[m]) for m in range(micro)).astype(BF)
        for d in range(parts):
            out_s[d] = found[:, d * down_rows : (d + 1) * down_rows]
        tall = share // out_groups
        for j in range(count):
            base = (me_f[0] ^ j) * share
            for k in range(parts):
                for g in range(out_groups):
                    place = pl.ds(pl.multiple_of(base + g * tall, tall), tall)
                    top = up_rows + down_height
                    targets[j % 2][
                        k, j // 2, top : top + tall, g * down_rows : (g + 1) * down_rows
                    ] = out_s[me_s[0] ^ k, place, :]

    found = sum(dot(hidden_t[m], pre_ref[m]) for m in range(micro)).astype(BF)
    for q in range(model // PACK):
        up_s[q] = found[:, q * PACK : (q + 1) * PACK]
    for j in range(count):
        place = pl.ds(pl.multiple_of((me_f[0] ^ j) * share, share), share)
        for q in range(model // PACK):
            block = chunk * (model // PACK) + q
            groups = up_rows // share
            dest = me_s[0] ^ (block // groups)
            top = (q % groups) * share
            targets[j % 2][dest, j // 2, top : top + share, :] = up_s[q, place, :]

    found = sum(dot(cot_t[m], act_ref[m]) for m in range(micro)).astype(BF)
    for o in range(owners):
        down_s[o] = found[:, o * down_lanes : (o + 1) * down_lanes]
    groups = PACK // down_lanes
    tall = down_rows // groups
    for low in range(owners):
        owner = low ^ (me_f[0] % owners)
        slot = ((chunk ^ (me_f[0] // owners)) * owners + low) // 2
        for k in range(parts):
            for g in range(groups):
                place = pl.ds(pl.multiple_of((me_s[0] ^ k) * down_rows + g * tall, tall), tall)
                targets[low % 2][
                    k, slot, up_rows : up_rows + tall, g * down_lanes : (g + 1) * down_lanes
                ] = down_s[owner, place, :]

    ones = jnp.ones((8, rows), BF)
    bias_ref[...] = sum(dot(ones, pre_ref[m]) for m in range(micro))


def rest_layout(model, hidden, parts, count):
    share = model // count
    up_rows = share * (hidden // parts) // PACK
    down_rows = (model // parts) * (hidden // count) // PACK
    groups = PACK // (model // parts)
    if share % (16 * groups):
        groups = 1
    return up_rows, down_rows, groups, up_rows + down_rows + share // groups


def rest_grads(acts, pres, hiddens, branches, cot, mixes, me_s, me_f, count):
    micro, rows, model = cot.shape
    parts = len(mixes[0])
    hidden = acts.shape[2]
    height = rest_layout(model, hidden, parts, count)[3]
    half = (parts, count // 2, height, PACK)
    flat = [item for group in mixes for item in group]
    lanes = hidden // count
    whole = lambda shape: pl.BlockSpec(shape, lambda t: (0,) * len(shape))
    chunk = pl.BlockSpec((micro, rows, model), lambda t: (0, 0, t))
    return pl.pallas_call(
        partial(rest_grads_kernel, micro, parts, count),
        name="rest_grads",
        grid=(hidden // model,),
        out_shape=(
            jax.ShapeDtypeStruct(half, BF),
            jax.ShapeDtypeStruct(half, BF),
            jax.ShapeDtypeStruct((8, hidden), F32),
        ),
        in_specs=[SM, SM, chunk, chunk]
        + [whole(cot.shape)] * 3
        + [whole(flat[0].shape)] * len(flat),
        out_specs=(whole(half), whole(half), pl.BlockSpec((8, model), lambda t: (0, t))),
        scratch_shapes=[pltpu.VMEM((micro, model, rows), BF)] * 3
        + [
            pltpu.VMEM((model // PACK, model, PACK), BF),
            pltpu.VMEM((model // lanes, model, lanes), BF),
            pltpu.VMEM((parts, model, model // parts), BF),
        ],
        compiler_params=params(40 * 1024 * 1024),
        cost_estimate=cost(2 * micro * rows * model * (model + 2 * hidden), 24e6),
    )(me_s, me_f, acts, pres, hiddens, branches, cot, *flat)


def finish_rest_kernel(parts, me_ref, *refs):
    pieces = refs[:parts]
    out_ref, up_ref, down_ref, out_s, down_s = refs[parts:]
    share, hidden = up_ref.shape
    down_lanes, model = down_ref.shape
    up_rows, down_height, out_groups, _ = rest_layout(model, hidden, parts, model // share)
    down_rows = model // parts
    cols = hidden // parts
    for k in range(parts):
        dest = me_ref[0] ^ k
        for g in range(cols // PACK):
            place = pl.ds(pl.multiple_of(dest * cols + g * PACK, PACK), PACK)
            up_ref[:, place] = pieces[k][g * share : (g + 1) * share, :].astype(F32)
        groups = PACK // down_lanes
        tall = down_rows // groups
        for g in range(groups):
            place = pl.ds(pl.multiple_of(dest * down_rows + g * tall, tall), tall)
            down_s[place, :] = pieces[k][
                up_rows : up_rows + tall, g * down_lanes : (g + 1) * down_lanes
            ].astype(F32)
        tall = share // out_groups
        top = up_rows + down_height
        for g in range(out_groups):
            out_s[dest, g * tall : (g + 1) * tall, :] = pieces[k][
                top : top + tall, g * down_rows : (g + 1) * down_rows
            ].astype(F32)
    down_ref[...] = down_s[...].T
    for d in range(parts):
        out_ref[:, d * down_rows : (d + 1) * down_rows] = out_s[d]


def finish_rest(pieces, me, model, hidden, count):
    parts = len(pieces)
    share, lanes = model // count, hidden // count
    return pl.pallas_call(
        partial(finish_rest_kernel, parts),
        name="finish_rest",
        out_shape=(
            jax.ShapeDtypeStruct((share, model), F32),
            jax.ShapeDtypeStruct((share, hidden), F32),
            jax.ShapeDtypeStruct((lanes, model), F32),
        ),
        in_specs=[SM] + [VM] * parts,
        out_specs=(VM, VM, VM),
        scratch_shapes=[
            pltpu.VMEM((parts, share, model // parts), F32),
            pltpu.VMEM((model, lanes), F32),
        ],
        compiler_params=params(),
        cost_estimate=cost(0, 2e6),
    )(me, *pieces)


def finish_qkv_kernel(parts, me_ref, *refs):
    pieces = refs[:parts]
    out_ref, piece_s = refs[parts:]
    here = pieces[0].shape[1] // 3
    model = here * parts
    for k in range(parts):
        piece_s[me_ref[0] ^ k] = pieces[k][...].astype(F32)
    for d in range(parts):
        for t in range(3):
            lane = t * model + d * here
            out_ref[:, lane : lane + here] = piece_s[d, :, t * here : (t + 1) * here]


def finish_qkv(pieces, me):
    parts = len(pieces)
    share, width = pieces[0].shape
    return pl.pallas_call(
        partial(finish_qkv_kernel, parts),
        name="finish_qkv",
        out_shape=jax.ShapeDtypeStruct((share, parts * width), F32),
        in_specs=[SM] + [VM] * parts,
        out_specs=VM,
        scratch_shapes=[pltpu.VMEM((parts, share, width), F32)],
        compiler_params=params(),
        cost_estimate=cost(0, 1e6),
    )(me, *pieces)


def input_kernel(parts, has_old, me_ref, tokens_ref, embed_ref, middle_ref, wq_ref, vec_ref, *refs):
    pieces = refs[:parts]
    out_ref, sums_ref = refs[parts + has_old :]
    grad_hidden = dot_t(pieces[0][...], wq_ref[me_ref[0]])
    for k in range(1, parts):
        grad_hidden = grad_hidden + dot_t(pieces[k][...], wq_ref[me_ref[0] ^ k])
    rows = tokens_ref[0].astype(F32) + embed_ref[0].astype(F32)
    scaled, inverse = norm_parts(rows)
    sums_ref[0:1] = jnp.sum(grad_hidden * scaled, axis=0, keepdims=True)
    sums_ref[1:2] = jnp.sum(grad_hidden, axis=0, keepdims=True)
    sums_ref[2:8] = jnp.zeros((6, sums_ref.shape[1]), F32)
    out_ref[0] = middle_ref[...] + norm_back(grad_hidden, scaled, inverse, vec_ref[0:1])


def input_gradient(tokens, embed, micro_index, grad_middle, pieces, wq, vec, old, me):
    micro, rows, model = tokens.shape
    parts = len(pieces)
    width = pieces[0].shape[1]
    row_spec = pl.BlockSpec((1, rows, model), lambda i: (micro_index, 0, 0))
    whole = lambda shape: pl.BlockSpec(shape, lambda i: (0,) * len(shape))
    old_args = [] if old is None else [old]
    return pl.pallas_call(
        partial(input_kernel, parts, len(old_args)),
        name="input_gradient",
        grid=(1,),
        out_shape=(
            jax.ShapeDtypeStruct((micro, rows, model), F32),
            jax.ShapeDtypeStruct((8, model), F32),
        ),
        in_specs=[SM, row_spec, row_spec, whole((rows, model)), whole(wq.shape), whole(vec.shape)]
        + [whole((rows, width))] * parts
        + [pl.BlockSpec(memory_space=pl.ANY)] * len(old_args),
        out_specs=(row_spec, whole((8, model))),
        input_output_aliases={6 + parts: 0} if old_args else {},
        compiler_params=params(),
        cost_estimate=cost(2 * rows * model * width * parts, 6e6),
    )(me, tokens, embed, grad_middle, wq, vec, *pieces, *old_args)


def qkv_grads_kernel(micro, parts, count, me_s, me_f, *refs):
    hiddens = refs[:micro]
    pieces = refs[micro : micro + micro * parts]
    keep_ref, send_ref, hidden_t = refs[micro + micro * parts :]
    rows, model = hiddens[0].shape
    width = pieces[0].shape[1]
    part = model // count
    for m in range(micro):
        hidden_t[m] = hiddens[m][...].astype(F32).T.astype(BF)

    def one(j, target, slot):
        place = pl.ds(pl.multiple_of((me_f[0] ^ j) * part, part), part)
        for k in range(parts):
            found = sum(
                dot(hidden_t[m, place, :], pieces[m * parts + k][...]) for m in range(micro)
            )
            target[k, slot] = found.astype(BF)

    def one_pair(s, _):
        one(2 * s, keep_ref, s)
        one(2 * s + 1, send_ref, s)
        return 0

    lax.fori_loop(0, count // 2, one_pair, 0)


def qkv_grads(hiddens, pieces, me_s, me_f, count):
    micro = len(hiddens)
    rows, model = hiddens[0].shape
    parts = len(pieces[0])
    width = pieces[0][0].shape[1]
    half = jax.ShapeDtypeStruct((parts, count // 2, model // count, width), BF)
    flat = [item for group in pieces for item in group]
    return pl.pallas_call(
        partial(qkv_grads_kernel, micro, parts, count),
        name="qkv_grads",
        out_shape=(half, half),
        in_specs=[SM, SM] + [VM] * (micro + micro * parts),
        out_specs=(VM, VM),
        scratch_shapes=[pltpu.VMEM((micro, model, rows), BF)],
        compiler_params=params(),
        cost_estimate=cost(2 * micro * rows * model * parts * width, 7e6),
    )(me_s, me_f, *hiddens, *flat)


def add_low(left, right):
    return (left.astype(F32) + right.astype(F32)).astype(BF)


def reduce_to_owner(keep, send):
    parts = lax.axis_size("seq")
    size = lax.axis_size("fsdp")
    found = swap(send, "fsdp", 1)
    pieces = [add_low(keep[k], found[k]) for k in range(parts)]
    pieces = exchange(pieces, "seq")
    bit = 2
    keep = send = None
    if size == 2:
        final = sum(item.astype(F32) for item in pieces).astype(BF)[0]
    else:
        keep = sum(item[0::2].astype(F32) for item in pieces).astype(BF)
        send = sum(item[1::2].astype(F32) for item in pieces).astype(BF)
        while True:
            found = swap(send, "fsdp", bit)
            bit *= 2
            if bit == size:
                final = add_low(keep[0], found[0])
                break
            keep, send = (
                add_low(keep[0::2], found[0::2]),
                add_low(keep[1::2], found[1::2]),
            )
    return gather_pieces(final, "seq")


def sum_over(value, axis):
    size = lax.axis_size(axis)
    bit = 1
    while bit < size:
        value = (value.astype(F32) + swap(value, axis, bit).astype(F32)).astype(value.dtype)
        bit *= 2
    return value


def local(
    tokens,
    time_embed,
    doc_ids,
    out_grad,
    norm1_gain,
    norm1_shift,
    qkv_weight,
    out_weight,
    norm2_gain,
    norm2_shift,
    up_weight,
    up_bias,
    down_weight,
    down_bias,
):
    micro, _, rows, model = tokens.shape
    parts = lax.axis_size("seq")
    count = lax.axis_size("fsdp")
    hidden = up_weight.shape[1]
    ratio = hidden // model
    length = rows * parts
    head_dim = model // HEADS
    heads = HEADS // parts
    here = heads * head_dim
    share = model // count
    seq_index = lax.axis_index("seq").astype(jnp.int32)
    fsdp_index = lax.axis_index("fsdp").astype(jnp.int32)
    me_s = seq_index.reshape(1)
    me_f = fsdp_index.reshape(1)
    tokens = tokens[:, 0]
    embed = time_embed[:, 0]
    cot = out_grad[:, 0]

    columns = jnp.stack(
        [norm1_gain, norm1_shift, norm2_gain, norm2_shift, down_bias]
        + [up_bias[t * share : (t + 1) * share] for t in range(ratio)]
        + [jnp.zeros_like(norm1_gain)] * (128 - 5 - ratio),
        axis=1,
    )
    first = jnp.concatenate([qkv_weight, columns], axis=1)
    rest = jnp.concatenate(
        [out_weight]
        + [up_weight[:, t * model : (t + 1) * model] for t in range(ratio)]
        + [down_weight],
        axis=0,
    )
    wq, vec = assemble_qkv(gather_pieces(first, "fsdp"), me_f, model, parts)
    rest, _ = lax.optimization_barrier((rest, vec))
    w_out, w_up, w_down = assemble_rest(gather_pieces(rest, "fsdp"), me_f, model, hidden)
    bias = (
        vec[5 : 5 + ratio].reshape(ratio, count, share).transpose(1, 0, 2).reshape(-1, 1, CHUNK)
    )

    docs = jnp.zeros((micro, length), jnp.int32)
    for k, piece in enumerate(gather_pieces(doc_ids[:, 0], "seq")):
        docs = lax.dynamic_update_slice(docs, piece, (0, (seq_index ^ k) * rows))
    first_doc = docs[:, ::WIDE, None]
    last_doc = docs[:, WIDE - 1 :: WIDE, None]
    low = jnp.sum(docs[:, None, :] < first_doc, axis=2, dtype=jnp.int32) // NARROW
    high = jnp.sum(docs[:, None, :] <= last_doc, axis=2, dtype=jnp.int32)
    high = (high + NARROW - 1) // NARROW
    doc = docs.astype(F32).reshape(micro, 1, length)

    hiddens, triples, mixes, logs = [], [], [], []
    for m in range(micro):
        found = project(tokens, embed, m, wq, vec, me_s)
        hiddens.append(found[0])
        triples.append(exchange(found[1:], "seq"))
    sent = []
    for m in range(micro):
        outs, log_total = attend(
            triples[m], me_s, low[m], high[m], doc[m], heads, head_dim
        )
        sent.append(outs)
        logs.append(log_total)
        mixes.append(exchange(outs, "seq"))
    stacked = None
    middles, sums, heads_grads = [], [], []
    for m in range(micro):
        found, grads = feed(
            tokens, embed, cot, m, mixes[m], vec, bias, w_out, w_up, w_down, stacked, me_s
        )
        stacked = found[:5]
        middles.append(found[5])
        sums.append(found[6])
        heads_grads.append(exchange(grads, "seq"))
    layer_output, acts, pres, seconds, branches = stacked
    keep, send, bias_sum = rest_grads(
        acts, pres, seconds, branches, cot, mixes, me_s, me_f, count
    )
    grad_out, grad_up, grad_down = finish_rest(
        reduce_to_owner(keep, send), me_s, model, hidden, count
    )
    input_grad = None
    backs, first_sums = [], []
    for m in range(micro):
        outs = attend_back(
            triples[m],
            sent[m],
            heads_grads[m],
            me_s,
            low[m],
            high[m],
            doc[m],
            logs[m],
            heads,
            head_dim,
        )
        backs.append(exchange(outs, "seq"))
    keep, send = qkv_grads(hiddens, backs, me_s, me_f, count)
    for m in range(micro):
        pieces = backs[m]
        if m == micro - 1:
            pieces, _ = lax.optimization_barrier((pieces, send))
        input_grad, sum_one = input_gradient(
            tokens, embed, m, middles[m], pieces, wq, vec, input_grad, me_s
        )
        first_sums.append(sum_one)
    grad_qkv = finish_qkv(reduce_to_owner(keep, send), me_s)

    second = sum(sums)
    once = sum(first_sums)
    vectors = jnp.concatenate(
        [
            once[0:2],
            second[0:3],
            jnp.zeros((3, model), F32),
            bias_sum[0].reshape(ratio, model),
            jnp.zeros((4, model), F32),
        ],
        axis=0,
    )
    vectors = sum_over(sum_over(vectors, "fsdp"), "seq")
    pick = lambda row: lax.dynamic_slice(vectors[row], (fsdp_index * share,), (share,))
    grad_up_bias = lax.dynamic_slice(
        vectors[8 : 8 + ratio].reshape(hidden), (fsdp_index * (hidden // count),), (hidden // count,)
    )
    return (
        layer_output[:, None],
        input_grad[:, None],
        pick(0),
        pick(1),
        grad_qkv,
        grad_out,
        pick(2),
        pick(3),
        grad_up,
        grad_up_bias,
        grad_down,
        pick(4),
    )


def solution(mesh):
    rows = P(None, "fsdp", "seq", None)
    vector = P("fsdp")
    matrix = P("fsdp", None)
    return jax.shard_map(
        local,
        mesh=mesh,
        in_specs=(
            rows,
            rows,
            P(None, "fsdp", "seq"),
            rows,
            vector,
            vector,
            matrix,
            matrix,
            vector,
            vector,
            matrix,
            vector,
            matrix,
            vector,
        ),
        out_specs=(
            rows,
            rows,
            vector,
            vector,
            matrix,
            matrix,
            vector,
            vector,
            matrix,
            vector,
            matrix,
            vector,
        ),
        check_vma=False,
    )
```

```python
from functools import partial

import jax
import jax.numpy as jnp
from jax import lax
from jax.experimental import pallas as pl
from jax.experimental.pallas import tpu as pltpu
from jax.sharding import PartitionSpec as P

HEADS = 8
EPS = 1e-05
LOG2E = 1.4426950408889634
WIDE = 512
NARROW = 384
PACK = 256
VMEM_LIMIT = 24 * 1024 * 1024
BF = jnp.bfloat16
F32 = jnp.float32


def dot(a, b, dims=((1,), (0,))):
    return lax.dot_general(a, b, (dims, ((), ())), preferred_element_type=F32)


def dot_t(a, b):
    return dot(a, b, ((1,), (1,)))


def params(limit=VMEM_LIMIT):
    return pltpu.CompilerParams(vmem_limit_bytes=limit)


def cost(flops, read, transcendentals=0):
    return pl.CostEstimate(
        flops=int(flops), bytes_accessed=int(read), transcendentals=int(transcendentals)
    )


VM = pl.BlockSpec(memory_space=pltpu.VMEM)
HB = pl.BlockSpec(memory_space=pltpu.HBM)
SM = pl.BlockSpec(memory_space=pltpu.SMEM)


def fetch(pairs, sems):
    copies = [
        pltpu.make_async_copy(source, target, sems.at[i])
        for i, (source, target) in enumerate(pairs)
    ]
    for copy in copies:
        copy.start()
    for copy in copies:
        copy.wait()


def fetch_rows(pieces, me, rows_s, sems, first=0):
    rows = pieces[0].shape[0]
    return [
        (piece, rows_s.at[pl.ds(pl.multiple_of((me ^ k) * rows, rows), rows), :])
        for k, piece in enumerate(pieces)
    ]


def after(value, token):
    return lax.optimization_barrier((value, token))[0]


def swap(value, axis, bit):
    size = lax.axis_size(axis)
    return lax.ppermute(value, axis, [(i, i ^ bit) for i in range(size)])


def gather_pieces(value, axis):
    size = lax.axis_size(axis)
    held = {0: value}
    bit = size // 2
    while bit:
        held.update({j | bit: swap(item, axis, bit) for j, item in list(held.items())})
        bit //= 2
    return [held[j] for j in range(size)]


def exchange(pieces, axis):
    return [pieces[0]] + [swap(pieces[k], axis, k) for k in range(1, len(pieces))]


def assemble_qkv_kernel(count, seq_parts, part_width, me_ref, *refs):
    pieces, (wq_ref, piece_s, sems) = refs[:count], refs[count:]
    rows = pieces[0].shape[0]
    model = wq_ref.shape[1]
    fetch([(pieces[j], piece_s.at[j]) for j in range(count)], sems)
    for j in range(count):
        start = pl.multiple_of((me_ref[0] ^ j) * rows, rows)
        for d in range(seq_parts):
            for t in range(3):
                lane = t * model + d * part_width
                wq_ref[d, pl.ds(start, rows), t * part_width : (t + 1) * part_width] = piece_s[
                    j, :, lane : lane + part_width
                ]


def assemble_qkv(pieces, me, model, seq_parts):
    part_width = model // seq_parts
    count = len(pieces)
    return pl.pallas_call(
        partial(assemble_qkv_kernel, count, seq_parts, part_width),
        name="assemble_qkv",
        out_shape=jax.ShapeDtypeStruct((seq_parts, model, 3 * part_width), BF),
        in_specs=[SM] + [HB] * count,
        out_specs=VM,
        scratch_shapes=[
            pltpu.VMEM((count,) + pieces[0].shape, BF),
            pltpu.SemaphoreType.DMA((count,)),
        ],
        compiler_params=params(),
        cost_estimate=cost(0, 4 * 3 * model * model),
    )(me, *pieces)


def assemble_rest_kernel(count, me_ref, *refs):
    pieces, (out_ref, up_ref, down_ref, sems) = refs[:count], refs[count:]
    model = out_ref.shape[0]
    rows = model // count
    ratio = up_ref.shape[1] // model
    down_rows = ratio * rows
    pairs = []
    for j in range(count):
        owner = me_ref[0] ^ j
        place = pl.ds(pl.multiple_of(owner * rows, rows), rows)
        pairs.append((pieces[j].at[0:rows, :], out_ref.at[place, :]))
        for t in range(ratio):
            pairs.append(
                (
                    pieces[j].at[(1 + t) * rows : (2 + t) * rows, :],
                    up_ref.at[place, t * model : (t + 1) * model],
                )
            )
        place = pl.ds(pl.multiple_of(owner * down_rows, down_rows), down_rows)
        pairs.append((pieces[j].at[(1 + ratio) * rows :, :], down_ref.at[place, :]))
    fetch(pairs, sems)


def assemble_rest(pieces, me, model, hidden):
    count = len(pieces)
    return pl.pallas_call(
        partial(assemble_rest_kernel, count),
        name="assemble_rest",
        out_shape=(
            jax.ShapeDtypeStruct((model, model), BF),
            jax.ShapeDtypeStruct((model, hidden), BF),
            jax.ShapeDtypeStruct((hidden, model), BF),
        ),
        in_specs=[SM] + [HB] * count,
        out_specs=(VM, VM, VM),
        scratch_shapes=[pltpu.SemaphoreType.DMA((count * (2 + hidden // model),))],
        compiler_params=params(),
        cost_estimate=cost(0, 4 * (model * model + 2 * model * hidden)),
    )(me, *pieces)


def norm_parts(rows):
    mean_row = jnp.mean(rows, axis=-1, keepdims=True)
    centred = rows - mean_row
    inverse = lax.rsqrt(jnp.mean(centred * centred, axis=-1, keepdims=True) + EPS)
    return centred * inverse, inverse


def norm_back(grad_normed, scaled, inverse, gain):
    grad_scaled = grad_normed * gain
    centre = jnp.mean(grad_scaled, axis=-1, keepdims=True)
    along = jnp.mean(grad_scaled * scaled, axis=-1, keepdims=True)
    return inverse * (grad_scaled - centre - scaled * along)


def project_kernel(parts, me_ref, tokens_ref, embed_ref, wq_ref, vec_ref, hidden_ref, *outs):
    rows = tokens_ref[0].astype(F32) + embed_ref[0].astype(F32)
    scaled, _ = norm_parts(rows)
    hidden = (scaled * vec_ref[0:1] + vec_ref[1:2]).astype(BF)
    hidden_ref[...] = hidden
    for k in range(parts):
        outs[k][...] = dot(hidden, wq_ref[me_ref[0] ^ k]).astype(BF)


def project(tokens, embed, micro_index, wq, vec, me):
    _, rows, model = tokens.shape
    parts, _, width = wq.shape
    row_spec = pl.BlockSpec((1, rows, model), lambda i: (micro_index, 0, 0))
    whole = lambda shape: pl.BlockSpec(shape, lambda i: (0,) * len(shape))
    return pl.pallas_call(
        partial(project_kernel, parts),
        name="project",
        grid=(1,),
        out_shape=[jax.ShapeDtypeStruct((rows, model), BF)]
        + [jax.ShapeDtypeStruct((rows, width), BF)] * parts,
        in_specs=[SM, row_spec, row_spec, whole(wq.shape), whole(vec.shape)],
        out_specs=[whole((rows, model))] + [whole((rows, width))] * parts,
        compiler_params=params(),
        cost_estimate=cost(2 * rows * model * width * parts, 4e6),
    )(me, tokens, embed, wq, vec)


def head_mask(value, head, heads, head_dim):
    if heads == 1:
        return value
    lane = lax.broadcasted_iota(jnp.int32, value.shape, 1)
    keep = (lane >= head * head_dim) & (lane < (head + 1) * head_dim)
    return jnp.where(keep, value, jnp.zeros_like(value))


def spread_docs(doc_ref, doc_s):
    for start in range(0, doc_s.shape[0], 512):
        doc_s[start : start + 512, :] = jnp.broadcast_to(
            doc_ref[0:1, start : start + 512], (128, 512)
        ).T


def same_doc(doc_s, place, doc_row):
    column = doc_s[place, :]
    return jnp.concatenate([column] * (doc_row.shape[1] // 128), axis=1) == doc_row


def fold(value, combine):
    out = value[0:8]
    for start in range(8, value.shape[0], 8):
        out = combine(out, value[start : start + 8])
    return out


def attend_kernel(parts, heads, head_dim, me_ref, low_ref, high_ref, doc_ref, *refs):
    pieces = refs[:parts]
    outs = refs[parts : 2 * parts]
    log_ref = refs[2 * parts]
    triple_s, value_t, doc_s, score_s, out_s, sems = refs[2 * parts + 1 :]
    rows, width = pieces[0].shape
    here = width // 3
    length = rows * parts
    spread_docs(doc_ref, doc_s)
    fetch(fetch_rows(pieces, me_ref[0], triple_s, sems), sems)
    for start in range(0, length, WIDE):
        value_t[:, start : start + WIDE] = (
            triple_s[start : start + WIDE, 2 * here :].astype(F32).T.astype(BF)
        )
    scale = head_dim ** (-0.5) * LOG2E

    def one_block(i, _):
        place = pl.ds(pl.multiple_of(i * WIDE, WIDE), WIDE)
        query = triple_s[place, 0:here]
        queries = [head_mask(query, h, heads, head_dim) for h in range(heads)]
        doc_row = doc_ref[0:1, place]

        def score(j, tops):
            key_place = pl.ds(pl.multiple_of(j * NARROW, NARROW), NARROW)
            keys = triple_s[key_place, here : 2 * here]
            same = same_doc(doc_s, key_place, doc_row)
            result = []
            for h in range(heads):
                scores = jnp.where(same, dot_t(keys, queries[h]) * scale, -jnp.inf)
                score_s[h, key_place, :] = scores
                result.append(jnp.maximum(tops[h], fold(scores, jnp.maximum)))
            return tuple(result)

        tops = lax.fori_loop(
            low_ref[i],
            high_ref[i],
            score,
            tuple(jnp.full((8, WIDE), -jnp.inf, F32) for _ in range(heads)),
        )
        tops = [jnp.max(top, axis=0, keepdims=True) for top in tops]

        def mix(j, carry):
            key_place = pl.ds(pl.multiple_of(j * NARROW, NARROW), NARROW)
            result = []
            for h in range(heads):
                total, acc = carry[h]
                weight = jnp.exp2(score_s[h, key_place, :] - tops[h])
                total = total + fold(weight, jnp.add)
                values = value_t[h * head_dim : (h + 1) * head_dim, key_place]
                result.append((total, acc + dot(values, weight.astype(BF))))
            return tuple(result)

        done = lax.fori_loop(
            low_ref[i],
            high_ref[i],
            mix,
            tuple(
                (jnp.zeros((8, WIDE), F32), jnp.zeros((head_dim, WIDE), F32))
                for _ in range(heads)
            ),
        )
        mixed = []
        for h in range(heads):
            total = jnp.sum(done[h][0], axis=0, keepdims=True)
            mixed.append(done[h][1] / total)
            log_ref[h, :, place] = jnp.broadcast_to(tops[h] + jnp.log2(total), (8, WIDE))
        mixed = jnp.concatenate(mixed, axis=0) if heads > 1 else mixed[0]
        out_s[place, :] = mixed.T.astype(BF)
        return 0

    lax.fori_loop(0, length // WIDE, one_block, 0)
    for k in range(parts):
        place = pl.ds(pl.multiple_of((me_ref[0] ^ k) * rows, rows), rows)
        outs[k][...] = out_s[place, :]


def attend(pieces, me, low, high, doc, heads, head_dim):
    parts = len(pieces)
    rows, width = pieces[0].shape
    here = width // 3
    length = rows * parts
    found = pl.pallas_call(
        partial(attend_kernel, parts, heads, head_dim),
        name="attend",
        out_shape=[jax.ShapeDtypeStruct((rows, here), BF)] * parts
        + [jax.ShapeDtypeStruct((heads, 8, length), F32)],
        in_specs=[SM, SM, SM, VM] + [HB] * parts,
        out_specs=[VM] * (parts + 1),
        scratch_shapes=[
            pltpu.VMEM((length, width), BF),
            pltpu.VMEM((here, length), BF),
            pltpu.VMEM((length, 128), F32),
            pltpu.VMEM((heads, length, WIDE), F32),
            pltpu.VMEM((length, here), BF),
            pltpu.SemaphoreType.DMA((parts,)),
        ],
        compiler_params=params(),
        cost_estimate=cost(4e9, 3e6, 2e6),
    )(me, low, high, doc, *pieces)
    return found[:parts], found[parts]


def attend_back_kernel(parts, heads, head_dim, me_ref, low_ref, high_ref, doc_ref, log_ref, *refs):
    pieces = refs[:parts]
    mixes = refs[parts : 2 * parts]
    grads = refs[2 * parts : 3 * parts]
    outs = refs[3 * parts : 4 * parts]
    (
        triple_s,
        grad_all,
        mix_all,
        query_s,
        key_t,
        grad_s,
        centre_s,
        doc_s,
        query_t,
        pair_s,
        sems,
    ) = refs[4 * parts :]
    rows, width = pieces[0].shape
    here = width // 3
    length = rows * parts
    me = me_ref[0]
    spread_docs(doc_ref, doc_s)
    fetch(
        fetch_rows(pieces, me, triple_s, sems)
        + fetch_rows(grads, me, grad_all, sems)
        + fetch_rows(mixes, me, mix_all, sems),
        sems,
    )
    for start in range(0, length, WIDE):
        place = pl.ds(start, WIDE)
        query = triple_s[place, 0:here]
        grad = grad_all[place, :]
        for h in range(heads):
            query_s[h, place, :] = head_mask(query, h, heads, head_dim)
            grad_s[h, place, :] = head_mask(grad, h, heads, head_dim)
        key_t[:, place] = triple_s[place, here : 2 * here].astype(F32).T.astype(BF)
        both = (grad.astype(F32) * mix_all[place, :].astype(F32)).T
        for h in range(heads):
            centre = jnp.sum(both[h * head_dim : (h + 1) * head_dim], axis=0, keepdims=True)
            centre_s[h, :, place] = jnp.broadcast_to(centre, (8, WIDE))
    query_t[...] = jnp.zeros_like(query_t)
    scale = head_dim ** (-0.5)

    def one_key(j, _):
        key_place = pl.ds(pl.multiple_of(j * WIDE, WIDE), WIDE)
        keys = triple_s[key_place, here : 2 * here]
        values = triple_s[key_place, 2 * here :]
        keys_t = [key_t[h * head_dim : (h + 1) * head_dim, key_place] for h in range(heads)]

        def one_block(i, carry):
            grad_key, grad_value = carry
            place = pl.ds(pl.multiple_of(i * NARROW, NARROW), NARROW)
            same = same_doc(doc_s, key_place, doc_ref[0:1, place])
            for h in range(heads):
                query = query_s[h, place, :]
                grad = grad_s[h, place, :]
                scores = jnp.where(same, dot_t(keys, query) * (scale * LOG2E), -jnp.inf)
                weight = jnp.exp2(scores - log_ref[h, 0:1, place])
                grad_weight = dot_t(values, grad)
                grad_score = (weight * (grad_weight - centre_s[h, 0:1, place])).astype(BF)
                grad_value = grad_value + dot(weight.astype(BF), grad)
                grad_key = grad_key + dot(grad_score, query)
                query_t[h * head_dim : (h + 1) * head_dim, place] += dot(keys_t[h], grad_score)
            return grad_key, grad_value

        zero = jnp.zeros((WIDE, here), F32)
        grad_key, grad_value = lax.fori_loop(low_ref[j], high_ref[j], one_block, (zero, zero))
        pair_s[key_place, 0:here] = (grad_key * scale).astype(BF)
        pair_s[key_place, here:] = grad_value.astype(BF)
        return 0

    lax.fori_loop(0, length // WIDE, one_key, 0)
    for k in range(parts):
        place = pl.ds(pl.multiple_of((me_ref[0] ^ k) * rows, rows), rows)
        outs[k][:, 0:here] = (query_t[:, place].T * scale).astype(BF)
        outs[k][:, here:] = pair_s[place, :]


def attend_back(pieces, mixes, grads, me, low, high, doc, log_total, heads, head_dim):
    parts = len(pieces)
    rows, width = pieces[0].shape
    here = width // 3
    length = rows * parts
    return pl.pallas_call(
        partial(attend_back_kernel, parts, heads, head_dim),
        name="attend_back",
        out_shape=[jax.ShapeDtypeStruct((rows, width), BF)] * parts,
        in_specs=[SM, SM, SM, VM, VM] + [HB] * (3 * parts),
        out_specs=[VM] * parts,
        scratch_shapes=[
            pltpu.VMEM((length, width), BF),
            pltpu.VMEM((length, here), BF),
            pltpu.VMEM((length, here), BF),
            pltpu.VMEM((heads, length, here), BF),
            pltpu.VMEM((here, length), BF),
            pltpu.VMEM((heads, length, here), BF),
            pltpu.VMEM((heads, 8, length), F32),
            pltpu.VMEM((length, 128), F32),
            pltpu.VMEM((here, length), F32),
            pltpu.VMEM((length, 2 * here), BF),
            pltpu.SemaphoreType.DMA((3 * parts,)),
        ],
        compiler_params=params(),
        cost_estimate=cost(8e9, 4e6, 2e6),
    )(me, low, high, doc, log_total, *pieces, *mixes, *grads)


CHUNK = 512


def feed_kernel(parts, has_old, me_ref, tokens_ref, embed_ref, cot_ref, vec_ref, bias_ref, *refs):
    mixes = refs[:parts]
    w_out, w_up, w_down = refs[parts : parts + 3]
    refs = refs[parts + 3 + has_old :]
    out_ref, act_ref, pre_ref, hidden_ref, branch_ref, middle_ref, sums_ref = refs[:7]
    grads = refs[7 : 7 + parts]
    total_s, back_s, mix_s, sems = refs[7 + parts :]
    me = me_ref[0]
    here = mixes[0].shape[1]
    fetch([(mixes[k], mix_s.at[k]) for k in range(parts)], sems)
    middle = tokens_ref[0].astype(F32) + embed_ref[0].astype(F32)
    for k in range(parts):
        place = pl.ds(pl.multiple_of((me ^ k) * here, here), here)
        middle = middle + dot(mix_s[k], w_out[place, :])
    scaled, inverse = norm_parts(middle)
    hidden_ref[0] = (scaled * vec_ref[2:3] + vec_ref[3:4]).astype(BF)
    middle_ref[...] = middle
    total_s[...] = jnp.zeros_like(total_s)
    back_s[...] = jnp.zeros_like(back_s)
    root = 0.7978845608028654

    def one_chunk(f, _):
        place = pl.ds(pl.multiple_of(f * CHUNK, CHUNK), CHUNK)
        value = dot(hidden_ref[0], w_up[:, place]) + bias_ref[f]
        square = value * value
        bend = jnp.tanh(root * (value + 0.044715 * (value * square)))
        half = 0.5 * (1.0 + bend)
        act = (value * half).astype(BF)
        slope = half + (0.5 * root) * value * (1.0 - bend * bend) * (1.0 + 0.134145 * square)
        act_ref[0, :, place] = act
        total_s[...] += dot(act, w_down[place, :])
        grad_pre = (dot_t(cot_ref[0], w_down[place, :]) * slope).astype(BF)
        pre_ref[0, :, place] = grad_pre
        back_s[...] += dot_t(grad_pre, w_up[:, place])
        return 0

    lax.fori_loop(0, w_up.shape[1] // CHUNK, one_chunk, 0)
    middle = middle_ref[...]
    out_ref[0] = (middle + total_s[...] + vec_ref[4:5]).astype(BF)
    scaled, inverse = norm_parts(middle)
    grad_hidden = back_s[...]
    sums_ref[0:1] = jnp.sum(grad_hidden * scaled, axis=0, keepdims=True)
    sums_ref[1:2] = jnp.sum(grad_hidden, axis=0, keepdims=True)
    cot = cot_ref[0].astype(F32)
    sums_ref[2:3] = jnp.sum(cot, axis=0, keepdims=True)
    sums_ref[3:8] = jnp.zeros((5, sums_ref.shape[1]), F32)
    grad_middle = cot + norm_back(grad_hidden, scaled, inverse, vec_ref[2:3])
    middle_ref[...] = grad_middle
    branch = grad_middle.astype(BF)
    branch_ref[0] = branch
    for k in range(parts):
        place = pl.ds(pl.multiple_of((me ^ k) * here, here), here)
        grads[k][...] = dot_t(branch, w_out[place, :]).astype(BF)


def feed(tokens, embed, cot, micro_index, mixes, vec, bias, w_out, w_up, w_down, old, me):
    micro, rows, model = tokens.shape
    parts = len(mixes)
    here = mixes[0].shape[1]
    hidden = w_up.shape[1]
    row_spec = pl.BlockSpec((1, rows, model), lambda i: (micro_index, 0, 0))
    whole = lambda shape: pl.BlockSpec(shape, lambda i: (0,) * len(shape))
    wide_spec = pl.BlockSpec((1, rows, hidden), lambda i: (micro_index, 0, 0))
    old_args = [] if old is None else list(old)
    found = pl.pallas_call(
        partial(feed_kernel, parts, len(old_args)),
        name="feed",
        grid=(1,),
        out_shape=[
            jax.ShapeDtypeStruct((micro, rows, model), BF),
            jax.ShapeDtypeStruct((micro, rows, hidden), BF),
            jax.ShapeDtypeStruct((micro, rows, hidden), BF),
            jax.ShapeDtypeStruct((micro, rows, model), BF),
            jax.ShapeDtypeStruct((micro, rows, model), BF),
            jax.ShapeDtypeStruct((rows, model), F32),
            jax.ShapeDtypeStruct((8, model), F32),
        ]
        + [jax.ShapeDtypeStruct((rows, here), BF)] * parts,
        in_specs=[SM, row_spec, row_spec, row_spec, whole(vec.shape), whole(bias.shape)]
        + [HB] * parts
        + [whole(w_out.shape), whole(w_up.shape), whole(w_down.shape)]
        + [pl.BlockSpec(memory_space=pl.ANY)] * len(old_args),
        out_specs=[
            row_spec,
            wide_spec,
            wide_spec,
            row_spec,
            row_spec,
            whole((rows, model)),
            whole((8, model)),
        ]
        + [whole((rows, here))] * parts,
        scratch_shapes=[pltpu.VMEM((rows, model), F32)] * 2
        + [pltpu.VMEM((parts, rows, here), BF), pltpu.SemaphoreType.DMA((parts,))],
        input_output_aliases={9 + parts + t: t for t in range(len(old_args))},
        compiler_params=params(32 * 1024 * 1024),
        cost_estimate=cost(8 * rows * model * hidden + 4 * rows * model * model, 12e6, rows * hidden),
    )(me, tokens, embed, cot, vec, bias, *mixes, w_out, w_up, w_down, *old_args)
    return found[:7], found[7:]


def rest_grads_kernel(micro, parts, count, me_s, me_f, act_ref, pre_ref, hidden_ref, branch_ref,
                      cot_ref, *refs):
    mixes = refs[: micro * parts]
    keep_ref, send_ref, bias_ref = refs[micro * parts : micro * parts + 3]
    hidden_t, cot_t, mixed_t, up_s, down_s, out_s, mix_s, sems = refs[micro * parts + 3 :]
    targets = (keep_ref, send_ref)
    rows, model = hidden_ref.shape[1:]
    here = mixes[0].shape[1]
    share = model // count
    chunk = pl.program_id(0)
    owners, _, down_lanes = down_s.shape
    down_rows = model // parts
    up_rows, down_height, out_groups, _ = rest_layout(model, pl.num_programs(0) * model, parts, count)

    @pl.when(chunk == 0)
    def _():
        fetch([(mixes[i], mix_s.at[i]) for i in range(micro * parts)], sems)
        for m in range(micro):
            hidden_t[m] = hidden_ref[m].astype(F32).T.astype(BF)
            cot_t[m] = cot_ref[m].astype(F32).T.astype(BF)
            for k in range(parts):
                place = pl.ds(pl.multiple_of((me_s[0] ^ k) * here, here), here)
                mixed_t[m, place, :] = mix_s[m * parts + k].astype(F32).T.astype(BF)
        found = sum(dot(mixed_t[m], branch_ref[m]) for m in range(micro)).astype(BF)
        for d in range(parts):
            out_s[d] = found[:, d * down_rows : (d + 1) * down_rows]
        tall = share // out_groups
        for j in range(count):
            base = (me_f[0] ^ j) * share
            for k in range(parts):
                for g in range(out_groups):
                    place = pl.ds(pl.multiple_of(base + g * tall, tall), tall)
                    top = up_rows + down_height
                    targets[j % 2][
                        k, j // 2, top : top + tall, g * down_rows : (g + 1) * down_rows
                    ] = out_s[me_s[0] ^ k, place, :]

    found = sum(dot(hidden_t[m], pre_ref[m]) for m in range(micro)).astype(BF)
    for q in range(model // PACK):
        up_s[q] = found[:, q * PACK : (q + 1) * PACK]
    for j in range(count):
        place = pl.ds(pl.multiple_of((me_f[0] ^ j) * share, share), share)
        for q in range(model // PACK):
            block = chunk * (model // PACK) + q
            groups = up_rows // share
            dest = me_s[0] ^ (block // groups)
            top = (q % groups) * share
            targets[j % 2][dest, j // 2, top : top + share, :] = up_s[q, place, :]

    found = sum(dot(cot_t[m], act_ref[m]) for m in range(micro)).astype(BF)
    for o in range(owners):
        down_s[o] = found[:, o * down_lanes : (o + 1) * down_lanes]
    groups = PACK // down_lanes
    tall = down_rows // groups
    for low in range(owners):
        owner = low ^ (me_f[0] % owners)
        slot = ((chunk ^ (me_f[0] // owners)) * owners + low) // 2
        for k in range(parts):
            for g in range(groups):
                place = pl.ds(pl.multiple_of((me_s[0] ^ k) * down_rows + g * tall, tall), tall)
                targets[low % 2][
                    k, slot, up_rows : up_rows + tall, g * down_lanes : (g + 1) * down_lanes
                ] = down_s[owner, place, :]

    ones = jnp.ones((8, rows), BF)
    bias_ref[...] = sum(dot(ones, pre_ref[m]) for m in range(micro))


def rest_layout(model, hidden, parts, count):
    share = model // count
    up_rows = share * (hidden // parts) // PACK
    down_rows = (model // parts) * (hidden // count) // PACK
    groups = PACK // (model // parts)
    if share % (16 * groups):
        groups = 1
    return up_rows, down_rows, groups, up_rows + down_rows + share // groups


def rest_grads(acts, pres, hiddens, branches, cot, mixes, me_s, me_f, count):
    micro, rows, model = cot.shape
    parts = len(mixes[0])
    hidden = acts.shape[2]
    height = rest_layout(model, hidden, parts, count)[3]
    half = (parts, count // 2, height, PACK)
    flat = [item for group in mixes for item in group]
    lanes = hidden // count
    whole = lambda shape: pl.BlockSpec(shape, lambda t: (0,) * len(shape))
    chunk = pl.BlockSpec((micro, rows, model), lambda t: (0, 0, t))
    return pl.pallas_call(
        partial(rest_grads_kernel, micro, parts, count),
        name="rest_grads",
        grid=(hidden // model,),
        out_shape=(
            jax.ShapeDtypeStruct(half, BF),
            jax.ShapeDtypeStruct(half, BF),
            jax.ShapeDtypeStruct((8, hidden), F32),
        ),
        in_specs=[SM, SM, chunk, chunk]
        + [whole(cot.shape)] * 3
        + [HB] * len(flat),
        out_specs=(whole(half), whole(half), pl.BlockSpec((8, model), lambda t: (0, t))),
        scratch_shapes=[pltpu.VMEM((micro, model, rows), BF)] * 3
        + [
            pltpu.VMEM((model // PACK, model, PACK), BF),
            pltpu.VMEM((model // lanes, model, lanes), BF),
            pltpu.VMEM((parts, model, model // parts), BF),
            pltpu.VMEM((len(flat),) + flat[0].shape, BF),
            pltpu.SemaphoreType.DMA((len(flat),)),
        ],
        compiler_params=params(40 * 1024 * 1024),
        cost_estimate=cost(2 * micro * rows * model * (model + 2 * hidden), 24e6),
    )(me_s, me_f, acts, pres, hiddens, branches, cot, *flat)


def finish_rest_kernel(parts, me_ref, *refs):
    pieces = refs[:parts]
    out_ref, up_ref, down_ref, out_s, down_s = refs[parts:]
    share, hidden = up_ref.shape
    down_lanes, model = down_ref.shape
    up_rows, down_height, out_groups, _ = rest_layout(model, hidden, parts, model // share)
    down_rows = model // parts
    cols = hidden // parts
    for k in range(parts):
        dest = me_ref[0] ^ k
        for g in range(cols // PACK):
            place = pl.ds(pl.multiple_of(dest * cols + g * PACK, PACK), PACK)
            up_ref[:, place] = pieces[k][g * share : (g + 1) * share, :].astype(F32)
        groups = PACK // down_lanes
        tall = down_rows // groups
        for g in range(groups):
            place = pl.ds(pl.multiple_of(dest * down_rows + g * tall, tall), tall)
            down_s[place, :] = pieces[k][
                up_rows : up_rows + tall, g * down_lanes : (g + 1) * down_lanes
            ].astype(F32)
        tall = share // out_groups
        top = up_rows + down_height
        for g in range(out_groups):
            out_s[dest, g * tall : (g + 1) * tall, :] = pieces[k][
                top : top + tall, g * down_rows : (g + 1) * down_rows
            ].astype(F32)
    down_ref[...] = down_s[...].T
    for d in range(parts):
        out_ref[:, d * down_rows : (d + 1) * down_rows] = out_s[d]


def finish_rest(pieces, me, model, hidden, count):
    parts = len(pieces)
    share, lanes = model // count, hidden // count
    return pl.pallas_call(
        partial(finish_rest_kernel, parts),
        name="finish_rest",
        out_shape=(
            jax.ShapeDtypeStruct((share, model), F32),
            jax.ShapeDtypeStruct((share, hidden), F32),
            jax.ShapeDtypeStruct((lanes, model), F32),
        ),
        in_specs=[SM] + [VM] * parts,
        out_specs=(VM, VM, VM),
        scratch_shapes=[
            pltpu.VMEM((parts, share, model // parts), F32),
            pltpu.VMEM((model, lanes), F32),
        ],
        compiler_params=params(),
        cost_estimate=cost(0, 2e6),
    )(me, *pieces)


def finish_qkv_kernel(parts, me_ref, *refs):
    pieces = refs[:parts]
    out_ref, piece_s = refs[parts:]
    here = pieces[0].shape[1] // 3
    model = here * parts
    for k in range(parts):
        piece_s[me_ref[0] ^ k] = pieces[k][...].astype(F32)
    for d in range(parts):
        for t in range(3):
            lane = t * model + d * here
            out_ref[:, lane : lane + here] = piece_s[d, :, t * here : (t + 1) * here]


def finish_qkv(pieces, me):
    parts = len(pieces)
    share, width = pieces[0].shape
    return pl.pallas_call(
        partial(finish_qkv_kernel, parts),
        name="finish_qkv",
        out_shape=jax.ShapeDtypeStruct((share, parts * width), F32),
        in_specs=[SM] + [VM] * parts,
        out_specs=VM,
        scratch_shapes=[pltpu.VMEM((parts, share, width), F32)],
        compiler_params=params(),
        cost_estimate=cost(0, 1e6),
    )(me, *pieces)


def input_kernel(parts, has_old, me_ref, tokens_ref, embed_ref, middle_ref, wq_ref, vec_ref, *refs):
    pieces = refs[:parts]
    out_ref, sums_ref, piece_s, sems = refs[parts + has_old :]
    fetch([(pieces[k], piece_s.at[k]) for k in range(parts)], sems)
    grad_hidden = dot_t(piece_s[0], wq_ref[me_ref[0]])
    for k in range(1, parts):
        grad_hidden = grad_hidden + dot_t(piece_s[k], wq_ref[me_ref[0] ^ k])
    rows = tokens_ref[0].astype(F32) + embed_ref[0].astype(F32)
    scaled, inverse = norm_parts(rows)
    sums_ref[0:1] = jnp.sum(grad_hidden * scaled, axis=0, keepdims=True)
    sums_ref[1:2] = jnp.sum(grad_hidden, axis=0, keepdims=True)
    sums_ref[2:8] = jnp.zeros((6, sums_ref.shape[1]), F32)
    out_ref[0] = middle_ref[...] + norm_back(grad_hidden, scaled, inverse, vec_ref[0:1])


def input_gradient(tokens, embed, micro_index, grad_middle, pieces, wq, vec, old, me):
    micro, rows, model = tokens.shape
    parts = len(pieces)
    width = pieces[0].shape[1]
    row_spec = pl.BlockSpec((1, rows, model), lambda i: (micro_index, 0, 0))
    whole = lambda shape: pl.BlockSpec(shape, lambda i: (0,) * len(shape))
    old_args = [] if old is None else [old]
    return pl.pallas_call(
        partial(input_kernel, parts, len(old_args)),
        name="input_gradient",
        grid=(1,),
        out_shape=(
            jax.ShapeDtypeStruct((micro, rows, model), F32),
            jax.ShapeDtypeStruct((8, model), F32),
        ),
        in_specs=[SM, row_spec, row_spec, whole((rows, model)), whole(wq.shape), whole(vec.shape)]
        + [HB] * parts
        + [pl.BlockSpec(memory_space=pl.ANY)] * len(old_args),
        out_specs=(row_spec, whole((8, model))),
        scratch_shapes=[
            pltpu.VMEM((parts, rows, width), BF),
            pltpu.SemaphoreType.DMA((parts,)),
        ],
        input_output_aliases={6 + parts: 0} if old_args else {},
        compiler_params=params(),
        cost_estimate=cost(2 * rows * model * width * parts, 6e6),
    )(me, tokens, embed, grad_middle, wq, vec, *pieces, *old_args)


def qkv_grads_kernel(micro, parts, count, me_s, me_f, *refs):
    hiddens = refs[:micro]
    pieces = refs[micro : micro + micro * parts]
    keep_ref, send_ref, hidden_t, hidden_s, piece_s, sems = refs[micro + micro * parts :]
    model = hiddens[0].shape[1]
    part = model // count
    fetch(
        [(hiddens[m], hidden_s.at[m]) for m in range(micro)]
        + [(pieces[i], piece_s.at[i]) for i in range(micro * parts)],
        sems,
    )
    for m in range(micro):
        hidden_t[m] = hidden_s[m].astype(F32).T.astype(BF)

    def one(j, target, slot):
        place = pl.ds(pl.multiple_of((me_f[0] ^ j) * part, part), part)
        for k in range(parts):
            found = sum(
                dot(hidden_t[m, place, :], piece_s[m * parts + k]) for m in range(micro)
            )
            target[k, slot] = found.astype(BF)

    def one_pair(s, _):
        one(2 * s, keep_ref, s)
        one(2 * s + 1, send_ref, s)
        return 0

    lax.fori_loop(0, count // 2, one_pair, 0)


def qkv_grads(hiddens, pieces, me_s, me_f, count):
    micro = len(hiddens)
    rows, model = hiddens[0].shape
    parts = len(pieces[0])
    width = pieces[0][0].shape[1]
    half = jax.ShapeDtypeStruct((parts, count // 2, model // count, width), BF)
    flat = [item for group in pieces for item in group]
    return pl.pallas_call(
        partial(qkv_grads_kernel, micro, parts, count),
        name="qkv_grads",
        out_shape=(half, half),
        in_specs=[SM, SM] + [HB] * (micro + micro * parts),
        out_specs=(VM, VM),
        scratch_shapes=[
            pltpu.VMEM((micro, model, rows), BF),
            pltpu.VMEM((micro, rows, model), BF),
            pltpu.VMEM((micro * parts, rows, width), BF),
            pltpu.SemaphoreType.DMA((micro + micro * parts,)),
        ],
        compiler_params=params(),
        cost_estimate=cost(2 * micro * rows * model * parts * width, 7e6),
    )(me_s, me_f, *hiddens, *flat)


def add_low(left, right):
    return (left.astype(F32) + right.astype(F32)).astype(BF)


def reduce_to_owner(keep, send):
    parts = lax.axis_size("seq")
    size = lax.axis_size("fsdp")
    found = swap(send, "fsdp", 1)
    pieces = [add_low(keep[k], found[k]) for k in range(parts)]
    yield pieces
    pieces = exchange(pieces, "seq")
    bit = 2
    keep = send = None
    if size == 2:
        final = sum(item.astype(F32) for item in pieces).astype(BF)[0]
    else:
        keep = sum(item[0::2].astype(F32) for item in pieces).astype(BF)
        send = sum(item[1::2].astype(F32) for item in pieces).astype(BF)
        while True:
            yield keep, send
            found = swap(send, "fsdp", bit)
            bit *= 2
            if bit == size:
                final = add_low(keep[0], found[0])
                break
            keep, send = (
                add_low(keep[0::2], found[0::2]),
                add_low(keep[1::2], found[1::2]),
            )
    yield final
    yield gather_pieces(final, "seq")


def sum_over(value, axis):
    size = lax.axis_size(axis)
    bit = 1
    while bit < size:
        value = (value.astype(F32) + swap(value, axis, bit).astype(F32)).astype(value.dtype)
        bit *= 2
    return value


def local(
    tokens,
    time_embed,
    doc_ids,
    out_grad,
    norm1_gain,
    norm1_shift,
    qkv_weight,
    out_weight,
    norm2_gain,
    norm2_shift,
    up_weight,
    up_bias,
    down_weight,
    down_bias,
):
    micro, _, rows, model = tokens.shape
    parts = lax.axis_size("seq")
    count = lax.axis_size("fsdp")
    hidden = up_weight.shape[1]
    ratio = hidden // model
    length = rows * parts
    head_dim = model // HEADS
    heads = HEADS // parts
    here = heads * head_dim
    share = model // count
    seq_index = lax.axis_index("seq").astype(jnp.int32)
    fsdp_index = lax.axis_index("fsdp").astype(jnp.int32)
    me_s = seq_index.reshape(1)
    me_f = fsdp_index.reshape(1)
    tokens = tokens[:, 0]
    embed = time_embed[:, 0]
    cot = out_grad[:, 0]

    vectors = jnp.concatenate(
        [norm1_gain, norm1_shift, norm2_gain, norm2_shift, down_bias, norm1_gain, up_bias]
    )
    rest = jnp.concatenate(
        [out_weight]
        + [up_weight[:, t * model : (t + 1) * model] for t in range(ratio)]
        + [down_weight],
        axis=0,
    )
    pieces = gather_pieces(qkv_weight, "fsdp")
    wq = assemble_qkv(pieces, me_f, model, parts)
    vectors = jnp.stack(gather_pieces(vectors, "fsdp"))
    owners = jnp.arange(count, dtype=jnp.int32)
    place = (owners[:, None] == (owners[None, :] ^ fsdp_index)).astype(BF)
    vectors = jnp.dot(place, vectors, preferred_element_type=F32)
    vec = vectors[:, : 6 * share].reshape(count, 6, share).transpose(1, 0, 2).reshape(6, model)
    vec = jnp.concatenate([vec, jnp.zeros((2, model), F32)])
    bias = vectors[:, 6 * share :].reshape(-1, 1, CHUNK)
    w_out, w_up, w_down = assemble_rest(
        gather_pieces(after(rest, wq), "fsdp"), me_f, model, hidden
    )

    docs = jnp.zeros((micro, length), jnp.int32)
    for k, piece in enumerate(gather_pieces(after(doc_ids, pieces[count // 2])[:, 0], "seq")):
        docs = lax.dynamic_update_slice(docs, piece, (0, (seq_index ^ k) * rows))
    first_doc = docs[:, ::WIDE, None]
    last_doc = docs[:, WIDE - 1 :: WIDE, None]
    low = jnp.sum(docs[:, None, :] < first_doc, axis=2, dtype=jnp.int32) // NARROW
    high = jnp.sum(docs[:, None, :] <= last_doc, axis=2, dtype=jnp.int32)
    high = (high + NARROW - 1) // NARROW
    doc = docs.astype(F32).reshape(micro, 1, length)

    hiddens, triples, mixes, logs = [], [], [], []
    for m in range(micro):
        found = project(tokens, embed, m, wq, vec, me_s)
        hiddens.append(found[0])
        outs = after(found[1:], triples[-1]) if m else found[1:]
        triples.append(exchange(outs, "seq"))
    sent = []
    for m in range(micro):
        outs, log_total = attend(
            triples[m], me_s, low[m], high[m], doc[m], heads, head_dim
        )
        sent.append(outs)
        logs.append(log_total)
        mixes.append(exchange(outs, "seq"))
    stacked = None
    middles, sums, heads_grads = [], [], []
    for m in range(micro):
        found, grads = feed(
            tokens, embed, cot, m, mixes[m], vec, bias, w_out, w_up, w_down, stacked, me_s
        )
        stacked = found[:5]
        middles.append(found[5])
        sums.append(found[6])
        heads_grads.append(exchange(grads, "seq"))
    layer_output, acts, pres, seconds, branches = stacked
    keep, send, bias_sum = rest_grads(
        acts, pres, seconds, branches, cot, mixes, me_s, me_f, count
    )
    hops = reduce_to_owner(keep, send)
    backs = []
    for m in range(micro):
        grads = after(heads_grads[m], next(hops)) if m else heads_grads[m]
        outs = attend_back(
            triples[m],
            sent[m],
            grads,
            me_s,
            low[m],
            high[m],
            doc[m],
            logs[m],
            heads,
            head_dim,
        )
        backs.append(exchange(outs, "seq"))
    input_grad = None
    first_sums = []
    for m in range(micro - 1):
        input_grad, sum_one = input_gradient(
            tokens, embed, m, middles[m], backs[m], wq, vec, input_grad, me_s
        )
        first_sums.append(sum_one)
    last = after(backs[-1], (input_grad, next(hops)))
    keep, send = qkv_grads(hiddens, backs[:-1] + [last], me_s, me_f, count)
    last = after(last, send)
    input_grad, sum_one = input_gradient(
        tokens, embed, micro - 1, middles[-1], last, wq, vec, input_grad, me_s
    )
    first_sums.append(sum_one)
    *_, pieces = hops
    grad_out, grad_up, grad_down = finish_rest(pieces, me_s, model, hidden, count)
    *_, pieces = reduce_to_owner(keep, send)
    grad_qkv = finish_qkv(pieces, me_s)

    second = sum(sums)
    once = sum(first_sums)
    vectors = jnp.concatenate(
        [
            once[0:2],
            second[0:3],
            jnp.zeros((3, model), F32),
            bias_sum[0].reshape(ratio, model),
            jnp.zeros((4, model), F32),
        ],
        axis=0,
    )
    vectors = sum_over(sum_over(vectors, "fsdp"), "seq")
    pick = lambda row: lax.dynamic_slice(vectors[row], (fsdp_index * share,), (share,))
    grad_up_bias = lax.dynamic_slice(
        vectors[8 : 8 + ratio].reshape(hidden), (fsdp_index * (hidden // count),), (hidden // count,)
    )
    return (
        layer_output[:, None],
        input_grad[:, None],
        pick(0),
        pick(1),
        grad_qkv,
        grad_out,
        pick(2),
        pick(3),
        grad_up,
        grad_up_bias,
        grad_down,
        pick(4),
    )


def solution(mesh):
    rows = P(None, "fsdp", "seq", None)
    vector = P("fsdp")
    matrix = P("fsdp", None)
    return jax.shard_map(
        local,
        mesh=mesh,
        in_specs=(
            rows,
            rows,
            P(None, "fsdp", "seq"),
            rows,
            vector,
            vector,
            matrix,
            matrix,
            vector,
            vector,
            matrix,
            vector,
            matrix,
            vector,
        ),
        out_specs=(
            rows,
            rows,
            vector,
            vector,
            matrix,
            matrix,
            vector,
            vector,
            matrix,
            vector,
            matrix,
            vector,
        ),
        check_vma=False,
    )
```

```python
from functools import partial

import jax
import jax.numpy as jnp
from jax import lax
from jax.experimental import pallas as pl
from jax.experimental.pallas import tpu as pltpu
from jax.sharding import PartitionSpec as P

HEADS = 8
EPS = 1e-05
LOG2E = 1.4426950408889634
WIDE = 512
NARROW = 384
PACK = 256
VMEM_LIMIT = 65000 * 1024
BF = jnp.bfloat16
F32 = jnp.float32


def dot(a, b, dims=((1,), (0,))):
    return lax.dot_general(a, b, (dims, ((), ())), preferred_element_type=F32)


def dot_t(a, b):
    return dot(a, b, ((1,), (1,)))


def params(limit=VMEM_LIMIT):
    return pltpu.CompilerParams(vmem_limit_bytes=limit)


def cost(micros):
    return pl.CostEstimate(flops=int(micros * 1e8), bytes_accessed=1000, transcendentals=0)


VM = pl.BlockSpec(memory_space=pltpu.VMEM)
HB = pl.BlockSpec(memory_space=pltpu.HBM)
SM = pl.BlockSpec(memory_space=pltpu.SMEM)


def fetch(pairs, sems):
    copies = [
        pltpu.make_async_copy(source, target, sems.at[i])
        for i, (source, target) in enumerate(pairs)
    ]
    for copy in copies:
        copy.start()
    for copy in copies:
        copy.wait()


def fetch_rows(pieces, me, rows_s, sems, first=0):
    rows = pieces[0].shape[0]
    return [
        (piece, rows_s.at[pl.ds(pl.multiple_of((me ^ k) * rows, rows), rows), :])
        for k, piece in enumerate(pieces)
    ]


def after(value, token):
    return lax.optimization_barrier((value, token))[0]


def swap(value, axis, bit):
    size = lax.axis_size(axis)
    return lax.ppermute(value, axis, [(i, i ^ bit) for i in range(size)])


def gather_pieces(value, axis):
    return exchange([value] * lax.axis_size(axis), axis)


def gather_pairs(value, axis):
    far = [swap(value, axis, j) if j else value for j in range(0, lax.axis_size(axis), 2)]
    return [item for mine in far for item in (mine, swap(mine, axis, 1))]


def exchange(pieces, axis):
    return [pieces[0]] + [swap(pieces[k], axis, k) for k in range(1, len(pieces))]


def assemble_qkv_kernel(count, seq_parts, part_width, me_ref, *refs):
    pieces, small = refs[:count], refs[count : 2 * count]
    wq_ref, vec_ref, bias_ref, piece_s, small_s, sems = refs[2 * count :]
    rows = pieces[0].shape[0]
    model = wq_ref.shape[1]
    ratio = small[0].shape[0] - 5
    fetch([(pieces[j], piece_s.at[j]) for j in range(count)], sems)
    for j in range(count):
        owner = me_ref[0] ^ j
        start = pl.multiple_of(owner * rows, rows)
        for d in range(seq_parts):
            for t in range(3):
                lane = t * model + d * part_width
                wq_ref[d, pl.ds(start, rows), t * part_width : (t + 1) * part_width] = piece_s[
                    j, :, lane : lane + part_width
                ]
        small_s[owner] = small[j][...].astype(F32)
    vec_ref[5:8] = jnp.zeros((3, model), F32)
    for o in range(count):
        item = small_s[o]
        vec_ref[0:5, o * rows : (o + 1) * rows] = item[0:5]
        for t in range(ratio):
            lane = (o * ratio + t) * rows
            bias_ref[lane // CHUNK, :, lane % CHUNK : lane % CHUNK + rows] = item[5 + t : 6 + t]


def assemble_qkv(pieces, small, me, model, seq_parts, hidden):
    part_width = model // seq_parts
    count = len(pieces)
    return pl.pallas_call(
        partial(assemble_qkv_kernel, count, seq_parts, part_width),
        name="assemble_qkv",
        out_shape=(
            jax.ShapeDtypeStruct((seq_parts, model, 3 * part_width), BF),
            jax.ShapeDtypeStruct((8, model), F32),
            jax.ShapeDtypeStruct((hidden // CHUNK, 1, CHUNK), F32),
        ),
        in_specs=[SM] + [HB] * count + [VM] * count,
        out_specs=(VM, VM, VM),
        scratch_shapes=[
            pltpu.VMEM((count,) + pieces[0].shape, BF),
            pltpu.VMEM((count,) + small[0].shape, F32),
            pltpu.SemaphoreType.DMA((count,)),
        ],
        compiler_params=params(),
        cost_estimate=cost(2),
    )(me, *pieces, *small)


def assemble_rest_kernel(count, me_ref, *refs):
    pieces, (out_ref, up_ref, down_ref, sems) = refs[:count], refs[count:]
    model = out_ref.shape[0]
    rows = model // count
    ratio = up_ref.shape[1] // model
    down_rows = ratio * rows
    pairs = []
    for j in range(count):
        owner = me_ref[0] ^ j
        place = pl.ds(pl.multiple_of(owner * rows, rows), rows)
        pairs.append((pieces[j].at[0:rows, :], out_ref.at[place, :]))
        for t in range(ratio):
            pairs.append(
                (
                    pieces[j].at[(1 + t) * rows : (2 + t) * rows, :],
                    up_ref.at[place, t * model : (t + 1) * model],
                )
            )
        place = pl.ds(pl.multiple_of(owner * down_rows, down_rows), down_rows)
        pairs.append((pieces[j].at[(1 + ratio) * rows :, :], down_ref.at[place, :]))
    fetch(pairs, sems)


def assemble_rest(pieces, me, model, hidden):
    count = len(pieces)
    return pl.pallas_call(
        partial(assemble_rest_kernel, count),
        name="assemble_rest",
        out_shape=(
            jax.ShapeDtypeStruct((model, model), BF),
            jax.ShapeDtypeStruct((model, hidden), BF),
            jax.ShapeDtypeStruct((hidden, model), BF),
        ),
        in_specs=[SM] + [HB] * count,
        out_specs=(VM, VM, VM),
        scratch_shapes=[pltpu.SemaphoreType.DMA((count * (2 + hidden // model),))],
        compiler_params=params(),
        cost_estimate=cost(2),
    )(me, *pieces)


def norm_parts(rows):
    mean_row = jnp.mean(rows, axis=-1, keepdims=True)
    centred = rows - mean_row
    inverse = lax.rsqrt(jnp.mean(centred * centred, axis=-1, keepdims=True) + EPS)
    return centred * inverse, inverse


def norm_back(grad_normed, scaled, inverse, gain):
    grad_scaled = grad_normed * gain
    centre = jnp.mean(grad_scaled, axis=-1, keepdims=True)
    along = jnp.mean(grad_scaled * scaled, axis=-1, keepdims=True)
    return inverse * (grad_scaled - centre - scaled * along)


def project_kernel(parts, me_ref, tokens_ref, embed_ref, wq_ref, vec_ref, hidden_ref, *outs):
    rows = tokens_ref[0].astype(F32) + embed_ref[0].astype(F32)
    scaled, _ = norm_parts(rows)
    hidden = (scaled * vec_ref[0:1] + vec_ref[1:2]).astype(BF)
    hidden_ref[...] = hidden
    for k in range(parts):
        outs[k][...] = dot(hidden, wq_ref[me_ref[0] ^ k]).astype(BF)


def project(tokens, embed, micro_index, wq, vec, me):
    _, rows, model = tokens.shape
    parts, _, width = wq.shape
    row_spec = pl.BlockSpec((1, rows, model), lambda i: (micro_index, 0, 0))
    whole = lambda shape: pl.BlockSpec(shape, lambda i: (0,) * len(shape))
    return pl.pallas_call(
        partial(project_kernel, parts),
        name="project",
        grid=(1,),
        out_shape=[jax.ShapeDtypeStruct((rows, model), BF)]
        + [jax.ShapeDtypeStruct((rows, width), BF)] * parts,
        in_specs=[SM, row_spec, row_spec, whole(wq.shape), whole(vec.shape)],
        out_specs=[whole((rows, model))] + [whole((rows, width))] * parts,
        compiler_params=params(),
        cost_estimate=cost(2),
    )(me, tokens, embed, wq, vec)


def head_mask(value, head, heads, head_dim):
    if heads == 1:
        return value
    lane = lax.broadcasted_iota(jnp.int32, value.shape, 1)
    keep = (lane >= head * head_dim) & (lane < (head + 1) * head_dim)
    return jnp.where(keep, value, jnp.zeros_like(value))


def spread_docs(doc_ref, doc_s):
    for start in range(0, doc_s.shape[0], 512):
        doc_s[start : start + 512, :] = jnp.broadcast_to(
            doc_ref[0:1, start : start + 512], (128, 512)
        ).T


def same_doc(doc_s, place, doc_row):
    column = doc_s[place, :]
    return jnp.concatenate([column] * (doc_row.shape[1] // 128), axis=1) == doc_row


def fold(value, combine):
    out = value[0:8]
    for start in range(8, value.shape[0], 8):
        out = combine(out, value[start : start + 8])
    return out


def attend_kernel(parts, heads, head_dim, me_ref, low_ref, high_ref, doc_ref, *refs):
    pieces = refs[:parts]
    outs = refs[parts : 2 * parts]
    log_ref = refs[2 * parts]
    triple_s, value_t, doc_s, score_s, out_s, sems = refs[2 * parts + 1 :]
    rows, width = pieces[0].shape
    here = width // 3
    length = rows * parts
    spread_docs(doc_ref, doc_s)
    fetch(fetch_rows(pieces, me_ref[0], triple_s, sems), sems)
    for start in range(0, length, WIDE):
        value_t[:, start : start + WIDE] = (
            triple_s[start : start + WIDE, 2 * here :].astype(F32).T.astype(BF)
        )
    scale = head_dim ** (-0.5) * LOG2E

    def one_block(i, _):
        place = pl.ds(pl.multiple_of(i * WIDE, WIDE), WIDE)
        query = triple_s[place, 0:here]
        queries = [head_mask(query, h, heads, head_dim) for h in range(heads)]
        doc_row = doc_ref[0:1, place]

        def score(j, tops):
            key_place = pl.ds(pl.multiple_of(j * NARROW, NARROW), NARROW)
            keys = triple_s[key_place, here : 2 * here]
            same = same_doc(doc_s, key_place, doc_row)
            result = []
            for h in range(heads):
                scores = jnp.where(same, dot_t(keys, queries[h]) * scale, -jnp.inf)
                score_s[h, key_place, :] = scores
                result.append(jnp.maximum(tops[h], fold(scores, jnp.maximum)))
            return tuple(result)

        tops = lax.fori_loop(
            low_ref[i],
            high_ref[i],
            score,
            tuple(jnp.full((8, WIDE), -jnp.inf, F32) for _ in range(heads)),
        )
        tops = [jnp.max(top, axis=0, keepdims=True) for top in tops]

        def mix(j, carry):
            key_place = pl.ds(pl.multiple_of(j * NARROW, NARROW), NARROW)
            result = []
            for h in range(heads):
                total, acc = carry[h]
                weight = jnp.exp2(score_s[h, key_place, :] - tops[h])
                total = total + fold(weight, jnp.add)
                values = value_t[h * head_dim : (h + 1) * head_dim, key_place]
                result.append((total, acc + dot(values, weight.astype(BF))))
            return tuple(result)

        done = lax.fori_loop(
            low_ref[i],
            high_ref[i],
            mix,
            tuple(
                (jnp.zeros((8, WIDE), F32), jnp.zeros((head_dim, WIDE), F32))
                for _ in range(heads)
            ),
        )
        mixed = []
        for h in range(heads):
            total = jnp.sum(done[h][0], axis=0, keepdims=True)
            mixed.append(done[h][1] / total)
            log_ref[h, :, place] = jnp.broadcast_to(tops[h] + jnp.log2(total), (8, WIDE))
        mixed = jnp.concatenate(mixed, axis=0) if heads > 1 else mixed[0]
        out_s[place, :] = mixed.T.astype(BF)
        return 0

    lax.fori_loop(0, length // WIDE, one_block, 0)
    for k in range(parts):
        place = pl.ds(pl.multiple_of((me_ref[0] ^ k) * rows, rows), rows)
        outs[k][...] = out_s[place, :]


def attend(pieces, me, low, high, doc, heads, head_dim):
    parts = len(pieces)
    rows, width = pieces[0].shape
    here = width // 3
    length = rows * parts
    found = pl.pallas_call(
        partial(attend_kernel, parts, heads, head_dim),
        name="attend",
        out_shape=[jax.ShapeDtypeStruct((rows, here), BF)] * parts
        + [jax.ShapeDtypeStruct((heads, 8, length), F32)],
        in_specs=[SM, SM, SM, VM] + [HB] * parts,
        out_specs=[VM] * (parts + 1),
        scratch_shapes=[
            pltpu.VMEM((length, width), BF),
            pltpu.VMEM((here, length), BF),
            pltpu.VMEM((length, 128), F32),
            pltpu.VMEM((heads, length, WIDE), F32),
            pltpu.VMEM((length, here), BF),
            pltpu.SemaphoreType.DMA((parts,)),
        ],
        compiler_params=params(),
        cost_estimate=cost(8),
    )(me, low, high, doc, *pieces)
    return found[:parts], found[parts]


def attend_back_kernel(parts, heads, head_dim, me_ref, low_ref, high_ref, doc_ref, log_ref, *refs):
    pieces = refs[:parts]
    mixes = refs[parts : 2 * parts]
    grads = refs[2 * parts : 3 * parts]
    outs = refs[3 * parts : 4 * parts]
    (
        triple_s,
        grad_all,
        mix_all,
        query_s,
        key_t,
        grad_s,
        centre_s,
        doc_s,
        query_t,
        pair_s,
        sems,
    ) = refs[4 * parts :]
    rows, width = pieces[0].shape
    here = width // 3
    length = rows * parts
    me = me_ref[0]
    spread_docs(doc_ref, doc_s)
    fetch(
        fetch_rows(pieces, me, triple_s, sems)
        + fetch_rows(grads, me, grad_all, sems)
        + fetch_rows(mixes, me, mix_all, sems),
        sems,
    )
    for start in range(0, length, WIDE):
        place = pl.ds(start, WIDE)
        query = triple_s[place, 0:here]
        grad = grad_all[place, :]
        for h in range(heads):
            query_s[h, place, :] = head_mask(query, h, heads, head_dim)
            grad_s[h, place, :] = head_mask(grad, h, heads, head_dim)
        key_t[:, place] = triple_s[place, here : 2 * here].astype(F32).T.astype(BF)
        both = (grad.astype(F32) * mix_all[place, :].astype(F32)).T
        for h in range(heads):
            centre = jnp.sum(both[h * head_dim : (h + 1) * head_dim], axis=0, keepdims=True)
            centre_s[h, :, place] = jnp.broadcast_to(centre, (8, WIDE))
    query_t[...] = jnp.zeros_like(query_t)
    scale = head_dim ** (-0.5)

    def one_key(j, _):
        key_place = pl.ds(pl.multiple_of(j * WIDE, WIDE), WIDE)
        keys = triple_s[key_place, here : 2 * here]
        values = triple_s[key_place, 2 * here :]
        keys_t = [key_t[h * head_dim : (h + 1) * head_dim, key_place] for h in range(heads)]

        def one_block(i, carry):
            grad_key, grad_value = carry
            place = pl.ds(pl.multiple_of(i * NARROW, NARROW), NARROW)
            same = same_doc(doc_s, key_place, doc_ref[0:1, place])
            for h in range(heads):
                query = query_s[h, place, :]
                grad = grad_s[h, place, :]
                scores = jnp.where(same, dot_t(keys, query) * (scale * LOG2E), -jnp.inf)
                weight = jnp.exp2(scores - log_ref[h, 0:1, place])
                grad_weight = dot_t(values, grad)
                grad_score = (weight * (grad_weight - centre_s[h, 0:1, place])).astype(BF)
                grad_value = grad_value + dot(weight.astype(BF), grad)
                grad_key = grad_key + dot(grad_score, query)
                query_t[h * head_dim : (h + 1) * head_dim, place] += dot(keys_t[h], grad_score)
            return grad_key, grad_value

        zero = jnp.zeros((WIDE, here), F32)
        grad_key, grad_value = lax.fori_loop(low_ref[j], high_ref[j], one_block, (zero, zero))
        pair_s[key_place, 0:here] = (grad_key * scale).astype(BF)
        pair_s[key_place, here:] = grad_value.astype(BF)
        return 0

    lax.fori_loop(0, length // WIDE, one_key, 0)
    for k in range(parts):
        place = pl.ds(pl.multiple_of((me_ref[0] ^ k) * rows, rows), rows)
        outs[k][:, 0:here] = (query_t[:, place].T * scale).astype(BF)
        outs[k][:, here:] = pair_s[place, :]


def attend_back(pieces, mixes, grads, me, low, high, doc, log_total, heads, head_dim):
    parts = len(pieces)
    rows, width = pieces[0].shape
    here = width // 3
    length = rows * parts
    return pl.pallas_call(
        partial(attend_back_kernel, parts, heads, head_dim),
        name="attend_back",
        out_shape=[jax.ShapeDtypeStruct((rows, width), BF)] * parts,
        in_specs=[SM, SM, SM, VM, VM] + [HB] * (3 * parts),
        out_specs=[VM] * parts,
        scratch_shapes=[
            pltpu.VMEM((length, width), BF),
            pltpu.VMEM((length, here), BF),
            pltpu.VMEM((length, here), BF),
            pltpu.VMEM((heads, length, here), BF),
            pltpu.VMEM((here, length), BF),
            pltpu.VMEM((heads, length, here), BF),
            pltpu.VMEM((heads, 8, length), F32),
            pltpu.VMEM((length, 128), F32),
            pltpu.VMEM((here, length), F32),
            pltpu.VMEM((length, 2 * here), BF),
            pltpu.SemaphoreType.DMA((3 * parts,)),
        ],
        compiler_params=params(),
        cost_estimate=cost(12),
    )(me, low, high, doc, log_total, *pieces, *mixes, *grads)


CHUNK = 512


def feed_kernel(parts, has_old, me_ref, tokens_ref, embed_ref, cot_ref, vec_ref, bias_ref, *refs):
    mixes = refs[:parts]
    w_out, w_up, w_down = refs[parts : parts + 3]
    refs = refs[parts + 3 + has_old :]
    out_ref, act_ref, pre_ref, hidden_ref, branch_ref, middle_ref, sums_ref = refs[:7]
    grads = refs[7 : 7 + parts]
    total_s, back_s, mix_s, sems = refs[7 + parts :]
    me = me_ref[0]
    here = mixes[0].shape[1]
    chunk = pl.program_id(0)
    root = 0.7978845608028654

    @pl.when(chunk == 0)
    def _():
        fetch([(mixes[k], mix_s.at[k]) for k in range(parts)], sems)
        middle = tokens_ref[0].astype(F32) + embed_ref[0].astype(F32)
        for k in range(parts):
            place = pl.ds(pl.multiple_of((me ^ k) * here, here), here)
            middle = middle + dot(mix_s[k], w_out[place, :])
        scaled, _ = norm_parts(middle)
        hidden_ref[0] = (scaled * vec_ref[2:3] + vec_ref[3:4]).astype(BF)
        middle_ref[...] = middle
        total_s[...] = jnp.zeros_like(total_s)
        back_s[...] = jnp.zeros_like(back_s)

    value = dot(hidden_ref[0], w_up[...]) + bias_ref[chunk]
    square = value * value
    bend = jnp.tanh(root * (value + 0.044715 * (value * square)))
    half = 0.5 * (1.0 + bend)
    act = (value * half).astype(BF)
    slope = half + (0.5 * root) * value * (1.0 - bend * bend) * (1.0 + 0.134145 * square)
    act_ref[0] = act
    total_s[...] += dot(act, w_down[...])
    grad_pre = (dot_t(cot_ref[0], w_down[...]) * slope).astype(BF)
    pre_ref[0] = grad_pre
    back_s[...] += dot_t(grad_pre, w_up[...])

    @pl.when(chunk == pl.num_programs(0) - 1)
    def _():
        middle = middle_ref[...]
        out_ref[0] = (middle + total_s[...] + vec_ref[4:5]).astype(BF)
        scaled, inverse = norm_parts(middle)
        grad_hidden = back_s[...]
        sums_ref[0:1] = jnp.sum(grad_hidden * scaled, axis=0, keepdims=True)
        sums_ref[1:2] = jnp.sum(grad_hidden, axis=0, keepdims=True)
        cot = cot_ref[0].astype(F32)
        sums_ref[2:3] = jnp.sum(cot, axis=0, keepdims=True)
        sums_ref[3:8] = jnp.zeros((5, sums_ref.shape[1]), F32)
        grad_middle = cot + norm_back(grad_hidden, scaled, inverse, vec_ref[2:3])
        middle_ref[...] = grad_middle
        branch = grad_middle.astype(BF)
        branch_ref[0] = branch
        for k in range(parts):
            place = pl.ds(pl.multiple_of((me ^ k) * here, here), here)
            grads[k][...] = dot_t(branch, w_out[place, :]).astype(BF)


def feed(tokens, embed, cot, micro_index, mixes, vec, bias, w_out, w_up, w_down, old, me):
    micro, rows, model = tokens.shape
    parts = len(mixes)
    here = mixes[0].shape[1]
    hidden = w_up.shape[1]
    row_spec = pl.BlockSpec((1, rows, model), lambda i: (micro_index, 0, 0))
    whole = lambda shape: pl.BlockSpec(shape, lambda i: (0,) * len(shape))
    wide_spec = pl.BlockSpec((1, rows, CHUNK), lambda i: (micro_index, 0, i))
    old_args = [] if old is None else list(old)
    found = pl.pallas_call(
        partial(feed_kernel, parts, len(old_args)),
        name="feed",
        grid=(hidden // CHUNK,),
        out_shape=[
            jax.ShapeDtypeStruct((micro, rows, model), BF),
            jax.ShapeDtypeStruct((micro, rows, hidden), BF),
            jax.ShapeDtypeStruct((micro, rows, hidden), BF),
            jax.ShapeDtypeStruct((micro, rows, model), BF),
            jax.ShapeDtypeStruct((micro, rows, model), BF),
            jax.ShapeDtypeStruct((rows, model), F32),
            jax.ShapeDtypeStruct((8, model), F32),
        ]
        + [jax.ShapeDtypeStruct((rows, here), BF)] * parts,
        in_specs=[SM, row_spec, row_spec, row_spec, whole(vec.shape), whole(bias.shape)]
        + [HB] * parts
        + [
            whole(w_out.shape),
            pl.BlockSpec((model, CHUNK), lambda i: (0, i)),
            pl.BlockSpec((CHUNK, model), lambda i: (i, 0)),
        ]
        + [pl.BlockSpec(memory_space=pl.ANY)] * len(old_args),
        out_specs=[
            row_spec,
            wide_spec,
            wide_spec,
            row_spec,
            row_spec,
            whole((rows, model)),
            whole((8, model)),
        ]
        + [whole((rows, here))] * parts,
        scratch_shapes=[pltpu.VMEM((rows, model), F32)] * 2
        + [pltpu.VMEM((parts, rows, here), BF), pltpu.SemaphoreType.DMA((parts,))],
        input_output_aliases={9 + parts + t: t for t in range(len(old_args))},
        compiler_params=params(),
        cost_estimate=cost(8),
    )(me, tokens, embed, cot, vec, bias, *mixes, w_out, w_up, w_down, *old_args)
    return found[:7], found[7:]


def rest_grads_kernel(micro, parts, count, me_s, me_f, act_ref, pre_ref, hidden_ref, branch_ref,
                      cot_ref, *refs):
    mixes = refs[: micro * parts]
    keep_ref, send_ref, bias_ref = refs[micro * parts : micro * parts + 3]
    hidden_t, cot_t, mixed_t, up_s, down_s, out_s, mix_s, sems = refs[micro * parts + 3 :]
    targets = (keep_ref, send_ref)
    rows, model = hidden_ref.shape[1:]
    here = mixes[0].shape[1]
    share = model // count
    chunk = pl.program_id(0)
    owners, _, down_lanes = down_s.shape
    down_rows = model // parts
    up_rows, down_height, out_groups, _ = rest_layout(model, pl.num_programs(0) * model, parts, count)

    @pl.when(chunk == 0)
    def _():
        fetch([(mixes[i], mix_s.at[i]) for i in range(micro * parts)], sems)
        for m in range(micro):
            hidden_t[m] = hidden_ref[m].astype(F32).T.astype(BF)
            cot_t[m] = cot_ref[m].astype(F32).T.astype(BF)
            for k in range(parts):
                place = pl.ds(pl.multiple_of((me_s[0] ^ k) * here, here), here)
                mixed_t[m, place, :] = mix_s[m * parts + k].astype(F32).T.astype(BF)
        found = sum(dot(mixed_t[m], branch_ref[m]) for m in range(micro)).astype(BF)
        for d in range(parts):
            out_s[d] = found[:, d * down_rows : (d + 1) * down_rows]
        tall = share // out_groups
        for j in range(count):
            base = (me_f[0] ^ j) * share
            for k in range(parts):
                for g in range(out_groups):
                    place = pl.ds(pl.multiple_of(base + g * tall, tall), tall)
                    top = up_rows + down_height
                    targets[j % 2][
                        k, j // 2, top : top + tall, g * down_rows : (g + 1) * down_rows
                    ] = out_s[me_s[0] ^ k, place, :]

    found = sum(dot(hidden_t[m], pre_ref[m]) for m in range(micro)).astype(BF)
    for q in range(model // PACK):
        up_s[q] = found[:, q * PACK : (q + 1) * PACK]
    for j in range(count):
        place = pl.ds(pl.multiple_of((me_f[0] ^ j) * share, share), share)
        for q in range(model // PACK):
            block = chunk * (model // PACK) + q
            groups = up_rows // share
            dest = me_s[0] ^ (block // groups)
            top = (q % groups) * share
            targets[j % 2][dest, j // 2, top : top + share, :] = up_s[q, place, :]

    found = sum(dot(cot_t[m], act_ref[m]) for m in range(micro)).astype(BF)
    for o in range(owners):
        down_s[o] = found[:, o * down_lanes : (o + 1) * down_lanes]
    groups = PACK // down_lanes
    tall = down_rows // groups
    for low in range(owners):
        owner = low ^ (me_f[0] % owners)
        slot = ((chunk ^ (me_f[0] // owners)) * owners + low) // 2
        for k in range(parts):
            for g in range(groups):
                place = pl.ds(pl.multiple_of((me_s[0] ^ k) * down_rows + g * tall, tall), tall)
                targets[low % 2][
                    k, slot, up_rows : up_rows + tall, g * down_lanes : (g + 1) * down_lanes
                ] = down_s[owner, place, :]

    ones = jnp.ones((8, rows), BF)
    bias_ref[...] = sum(dot(ones, pre_ref[m]) for m in range(micro))


def rest_layout(model, hidden, parts, count):
    share = model // count
    up_rows = share * (hidden // parts) // PACK
    down_rows = (model // parts) * (hidden // count) // PACK
    groups = PACK // (model // parts)
    if share % (16 * groups):
        groups = 1
    return up_rows, down_rows, groups, up_rows + down_rows + share // groups


def rest_grads(acts, pres, hiddens, branches, cot, mixes, me_s, me_f, count):
    micro, rows, model = cot.shape
    parts = len(mixes[0])
    hidden = acts.shape[2]
    height = rest_layout(model, hidden, parts, count)[3]
    half = (parts, count // 2, height, PACK)
    flat = [item for group in mixes for item in group]
    lanes = hidden // count
    whole = lambda shape: pl.BlockSpec(shape, lambda t: (0,) * len(shape))
    chunk = pl.BlockSpec((micro, rows, model), lambda t: (0, 0, t))
    return pl.pallas_call(
        partial(rest_grads_kernel, micro, parts, count),
        name="rest_grads",
        grid=(hidden // model,),
        out_shape=(
            jax.ShapeDtypeStruct(half, BF),
            jax.ShapeDtypeStruct(half, BF),
            jax.ShapeDtypeStruct((8, hidden), F32),
        ),
        in_specs=[SM, SM, chunk, chunk]
        + [whole(cot.shape)] * 3
        + [HB] * len(flat),
        out_specs=(whole(half), whole(half), pl.BlockSpec((8, model), lambda t: (0, t))),
        scratch_shapes=[pltpu.VMEM((micro, model, rows), BF)] * 3
        + [
            pltpu.VMEM((model // PACK, model, PACK), BF),
            pltpu.VMEM((model // lanes, model, lanes), BF),
            pltpu.VMEM((parts, model, model // parts), BF),
            pltpu.VMEM((len(flat),) + flat[0].shape, BF),
            pltpu.SemaphoreType.DMA((len(flat),)),
        ],
        compiler_params=params(),
        cost_estimate=cost(12),
    )(me_s, me_f, acts, pres, hiddens, branches, cot, *flat)


def finish_rest_kernel(parts, me_ref, *refs):
    pieces = refs[:parts]
    out_ref, up_ref, down_ref, out_s, down_s = refs[parts:]
    share, hidden = up_ref.shape
    down_lanes, model = down_ref.shape
    up_rows, down_height, out_groups, _ = rest_layout(model, hidden, parts, model // share)
    down_rows = model // parts
    cols = hidden // parts
    for k in range(parts):
        dest = me_ref[0] ^ k
        for g in range(cols // PACK):
            place = pl.ds(pl.multiple_of(dest * cols + g * PACK, PACK), PACK)
            up_ref[:, place] = pieces[k][g * share : (g + 1) * share, :].astype(F32)
        groups = PACK // down_lanes
        tall = down_rows // groups
        for g in range(groups):
            place = pl.ds(pl.multiple_of(dest * down_rows + g * tall, tall), tall)
            down_s[place, :] = pieces[k][
                up_rows : up_rows + tall, g * down_lanes : (g + 1) * down_lanes
            ].astype(F32)
        tall = share // out_groups
        top = up_rows + down_height
        for g in range(out_groups):
            out_s[dest, g * tall : (g + 1) * tall, :] = pieces[k][
                top : top + tall, g * down_rows : (g + 1) * down_rows
            ].astype(F32)
    down_ref[...] = down_s[...].T
    for d in range(parts):
        out_ref[:, d * down_rows : (d + 1) * down_rows] = out_s[d]


def finish_rest(pieces, me, model, hidden, count):
    parts = len(pieces)
    share, lanes = model // count, hidden // count
    return pl.pallas_call(
        partial(finish_rest_kernel, parts),
        name="finish_rest",
        out_shape=(
            jax.ShapeDtypeStruct((share, model), F32),
            jax.ShapeDtypeStruct((share, hidden), F32),
            jax.ShapeDtypeStruct((lanes, model), F32),
        ),
        in_specs=[SM] + [VM] * parts,
        out_specs=(VM, VM, VM),
        scratch_shapes=[
            pltpu.VMEM((parts, share, model // parts), F32),
            pltpu.VMEM((model, lanes), F32),
        ],
        compiler_params=params(),
        cost_estimate=cost(1),
    )(me, *pieces)


def finish_qkv_kernel(parts, me_ref, *refs):
    pieces = refs[:parts]
    out_ref, piece_s = refs[parts:]
    here = pieces[0].shape[1] // 3
    model = here * parts
    for k in range(parts):
        piece_s[me_ref[0] ^ k] = pieces[k][...].astype(F32)
    for d in range(parts):
        for t in range(3):
            lane = t * model + d * here
            out_ref[:, lane : lane + here] = piece_s[d, :, t * here : (t + 1) * here]


def finish_qkv(pieces, me):
    parts = len(pieces)
    share, width = pieces[0].shape
    return pl.pallas_call(
        partial(finish_qkv_kernel, parts),
        name="finish_qkv",
        out_shape=jax.ShapeDtypeStruct((share, parts * width), F32),
        in_specs=[SM] + [VM] * parts,
        out_specs=VM,
        scratch_shapes=[pltpu.VMEM((parts, share, width), F32)],
        compiler_params=params(),
        cost_estimate=cost(1),
    )(me, *pieces)


def input_kernel(parts, has_old, me_ref, tokens_ref, embed_ref, middle_ref, wq_ref, vec_ref, *refs):
    pieces = refs[:parts]
    out_ref, sums_ref, piece_s, sems = refs[parts + has_old :]
    fetch([(pieces[k], piece_s.at[k]) for k in range(parts)], sems)
    grad_hidden = dot_t(piece_s[0], wq_ref[me_ref[0]])
    for k in range(1, parts):
        grad_hidden = grad_hidden + dot_t(piece_s[k], wq_ref[me_ref[0] ^ k])
    rows = tokens_ref[0].astype(F32) + embed_ref[0].astype(F32)
    scaled, inverse = norm_parts(rows)
    sums_ref[0:1] = jnp.sum(grad_hidden * scaled, axis=0, keepdims=True)
    sums_ref[1:2] = jnp.sum(grad_hidden, axis=0, keepdims=True)
    sums_ref[2:8] = jnp.zeros((6, sums_ref.shape[1]), F32)
    out_ref[0] = middle_ref[...] + norm_back(grad_hidden, scaled, inverse, vec_ref[0:1])


def input_gradient(tokens, embed, micro_index, grad_middle, pieces, wq, vec, old, me):
    micro, rows, model = tokens.shape
    parts = len(pieces)
    width = pieces[0].shape[1]
    row_spec = pl.BlockSpec((1, rows, model), lambda i: (micro_index, 0, 0))
    whole = lambda shape: pl.BlockSpec(shape, lambda i: (0,) * len(shape))
    old_args = [] if old is None else [old]
    return pl.pallas_call(
        partial(input_kernel, parts, len(old_args)),
        name="input_gradient",
        grid=(1,),
        out_shape=(
            jax.ShapeDtypeStruct((micro, rows, model), F32),
            jax.ShapeDtypeStruct((8, model), F32),
        ),
        in_specs=[SM, row_spec, row_spec, whole((rows, model)), whole(wq.shape), whole(vec.shape)]
        + [HB] * parts
        + [pl.BlockSpec(memory_space=pl.ANY)] * len(old_args),
        out_specs=(row_spec, whole((8, model))),
        scratch_shapes=[
            pltpu.VMEM((parts, rows, width), BF),
            pltpu.SemaphoreType.DMA((parts,)),
        ],
        input_output_aliases={6 + parts: 0} if old_args else {},
        compiler_params=params(),
        cost_estimate=cost(2.5),
    )(me, tokens, embed, grad_middle, wq, vec, *pieces, *old_args)


def qkv_grads_kernel(micro, parts, count, me_s, me_f, *refs):
    hiddens = refs[:micro]
    pieces = refs[micro : micro + micro * parts]
    keep_ref, send_ref, hidden_t, hidden_s, piece_s, sems = refs[micro + micro * parts :]
    model = hiddens[0].shape[1]
    part = model // count
    fetch(
        [(hiddens[m], hidden_s.at[m]) for m in range(micro)]
        + [(pieces[i], piece_s.at[i]) for i in range(micro * parts)],
        sems,
    )
    for m in range(micro):
        hidden_t[m] = hidden_s[m].astype(F32).T.astype(BF)

    def one(j, target, slot):
        place = pl.ds(pl.multiple_of((me_f[0] ^ j) * part, part), part)
        for k in range(parts):
            found = sum(
                dot(hidden_t[m, place, :], piece_s[m * parts + k]) for m in range(micro)
            )
            target[k, slot] = found.astype(BF)

    def one_pair(s, _):
        one(2 * s, keep_ref, s)
        one(2 * s + 1, send_ref, s)
        return 0

    lax.fori_loop(0, count // 2, one_pair, 0)


def qkv_grads(hiddens, pieces, me_s, me_f, count):
    micro = len(hiddens)
    rows, model = hiddens[0].shape
    parts = len(pieces[0])
    width = pieces[0][0].shape[1]
    half = jax.ShapeDtypeStruct((parts, count // 2, model // count, width), BF)
    flat = [item for group in pieces for item in group]
    return pl.pallas_call(
        partial(qkv_grads_kernel, micro, parts, count),
        name="qkv_grads",
        out_shape=(half, half),
        in_specs=[SM, SM] + [HB] * (micro + micro * parts),
        out_specs=(VM, VM),
        scratch_shapes=[
            pltpu.VMEM((micro, model, rows), BF),
            pltpu.VMEM((micro, rows, model), BF),
            pltpu.VMEM((micro * parts, rows, width), BF),
            pltpu.SemaphoreType.DMA((micro + micro * parts,)),
        ],
        compiler_params=params(),
        cost_estimate=cost(7),
    )(me_s, me_f, *hiddens, *flat)


def add_low(left, right):
    return (left.astype(F32) + right.astype(F32)).astype(BF)


def reduce_to_owner(keep, send):
    parts = lax.axis_size("seq")
    size = lax.axis_size("fsdp")
    found = swap(send, "fsdp", 1)
    pieces = [add_low(keep[k], found[k]) for k in range(parts)]
    yield pieces
    pieces = exchange(pieces, "seq")
    bit = 2
    keep = send = None
    if size == 2:
        final = sum(item.astype(F32) for item in pieces).astype(BF)[0]
    else:
        keep = sum(item[0::2].astype(F32) for item in pieces).astype(BF)
        send = sum(item[1::2].astype(F32) for item in pieces).astype(BF)
        while True:
            yield keep, send
            found = swap(send, "fsdp", bit)
            bit *= 2
            if bit == size:
                final = add_low(keep[0], found[0])
                break
            keep, send = (
                add_low(keep[0::2], found[0::2]),
                add_low(keep[1::2], found[1::2]),
            )
    yield final
    yield gather_pieces(final, "seq")


def sum_over(value, axis):
    size = lax.axis_size(axis)
    bit = 1
    while bit < size:
        value = (value.astype(F32) + swap(value, axis, bit).astype(F32)).astype(value.dtype)
        bit *= 2
    return value


def local(
    tokens,
    time_embed,
    doc_ids,
    out_grad,
    norm1_gain,
    norm1_shift,
    qkv_weight,
    out_weight,
    norm2_gain,
    norm2_shift,
    up_weight,
    up_bias,
    down_weight,
    down_bias,
):
    micro, _, rows, model = tokens.shape
    parts = lax.axis_size("seq")
    count = lax.axis_size("fsdp")
    hidden = up_weight.shape[1]
    ratio = hidden // model
    length = rows * parts
    head_dim = model // HEADS
    heads = HEADS // parts
    here = heads * head_dim
    share = model // count
    seq_index = lax.axis_index("seq").astype(jnp.int32)
    fsdp_index = lax.axis_index("fsdp").astype(jnp.int32)
    me_s = seq_index.reshape(1)
    me_f = fsdp_index.reshape(1)
    tokens = tokens[:, 0]
    embed = time_embed[:, 0]
    cot = out_grad[:, 0]

    pieces = gather_pairs(qkv_weight, "fsdp")
    near = pieces[2]
    small = [norm1_gain, norm1_shift, norm2_gain, norm2_shift, down_bias]
    small = [item.reshape(1, share) for item in small] + [up_bias.reshape(ratio, share)]
    small = gather_pairs(after(jnp.concatenate(small), near), "fsdp")
    wq, vec, bias = assemble_qkv(pieces, small, me_f, model, parts, hidden)
    rest = jnp.concatenate(
        [out_weight]
        + [up_weight[:, t * model : (t + 1) * model] for t in range(ratio)]
        + [down_weight],
        axis=0,
    )
    w_out, w_up, w_down = assemble_rest(
        gather_pairs(after(rest, pieces[1]), "fsdp"), me_f, model, hidden
    )

    docs = jnp.zeros((micro, length), jnp.int32)
    for k, piece in enumerate(gather_pieces(after(doc_ids, near)[:, 0], "seq")):
        docs = lax.dynamic_update_slice(docs, piece, (0, (seq_index ^ k) * rows))
    first_doc = docs[:, ::WIDE, None]
    last_doc = docs[:, WIDE - 1 :: WIDE, None]
    low = jnp.sum(docs[:, None, :] < first_doc, axis=2, dtype=jnp.int32) // NARROW
    high = jnp.sum(docs[:, None, :] <= last_doc, axis=2, dtype=jnp.int32)
    high = (high + NARROW - 1) // NARROW
    doc = docs.astype(F32).reshape(micro, 1, length)

    hiddens, triples, mixes, logs = [], [], [], []
    for m in range(micro):
        found = project(tokens, embed, m, wq, vec, me_s)
        hiddens.append(found[0])
        outs = after(found[1:], triples[-1]) if m else found[1:]
        triples.append(exchange(outs, "seq"))
    sent = []
    for m in range(micro):
        triple = after(triples[m], logs[-1]) if m else triples[m]
        outs, log_total = attend(
            triple, me_s, low[m], high[m], doc[m], heads, head_dim
        )
        sent.append(outs)
        logs.append(log_total)
        mixes.append(exchange(outs, "seq"))
    stacked = None
    middles, sums, heads_grads = [], [], []
    for m in range(micro):
        found, grads = feed(
            tokens,
            embed,
            cot,
            m,
            mixes[m] if m else after(mixes[m], logs[-1]),
            vec,
            bias,
            w_out,
            w_up,
            w_down,
            stacked,
            me_s,
        )
        stacked = found[:5]
        middles.append(found[5])
        sums.append(found[6])
        heads_grads.append(exchange(grads, "seq"))
    layer_output, acts, pres, seconds, branches = stacked
    keep, send, bias_sum = rest_grads(
        acts, pres, seconds, branches, cot, mixes, me_s, me_f, count
    )
    hops = reduce_to_owner(keep, send)
    backs = []
    for m in range(micro):
        grads = after(heads_grads[m], (next(hops), outs) if m else bias_sum)
        outs = attend_back(
            triples[m],
            sent[m],
            grads,
            me_s,
            low[m],
            high[m],
            doc[m],
            logs[m],
            heads,
            head_dim,
        )
        backs.append(exchange(outs, "seq"))
    input_grad = None
    first_sums = []
    for m in range(micro - 1):
        pieces = after(backs[m], outs) if m == 0 else backs[m]
        input_grad, sum_one = input_gradient(
            tokens, embed, m, middles[m], pieces, wq, vec, input_grad, me_s
        )
        first_sums.append(sum_one)
    last = after(backs[-1], (input_grad, next(hops)))
    keep, send = qkv_grads(hiddens, backs[:-1] + [last], me_s, me_f, count)
    last = after(last, send)
    input_grad, sum_one = input_gradient(
        tokens, embed, micro - 1, middles[-1], last, wq, vec, input_grad, me_s
    )
    first_sums.append(sum_one)
    *_, pieces = hops
    grad_out, grad_up, grad_down = finish_rest(pieces, me_s, model, hidden, count)
    *_, pieces = reduce_to_owner(keep, send)
    grad_qkv = finish_qkv(pieces, me_s)

    second = sum(sums)
    once = sum(first_sums)
    vectors = jnp.concatenate(
        [
            once[0:2],
            second[0:3],
            jnp.zeros((3, model), F32),
            bias_sum[0].reshape(ratio, model),
            jnp.zeros((4, model), F32),
        ],
        axis=0,
    )
    vectors = sum_over(sum_over(vectors, "fsdp"), "seq")
    pick = lambda row: lax.dynamic_slice(vectors[row], (fsdp_index * share,), (share,))
    grad_up_bias = lax.dynamic_slice(
        vectors[8 : 8 + ratio].reshape(hidden), (fsdp_index * (hidden // count),), (hidden // count,)
    )
    return (
        layer_output[:, None],
        input_grad[:, None],
        pick(0),
        pick(1),
        grad_qkv,
        grad_out,
        pick(2),
        pick(3),
        grad_up,
        grad_up_bias,
        grad_down,
        pick(4),
    )


def solution(mesh):
    rows = P(None, "fsdp", "seq", None)
    vector = P("fsdp")
    matrix = P("fsdp", None)
    return jax.shard_map(
        local,
        mesh=mesh,
        in_specs=(
            rows,
            rows,
            P(None, "fsdp", "seq"),
            rows,
            vector,
            vector,
            matrix,
            matrix,
            vector,
            vector,
            matrix,
            vector,
            matrix,
            vector,
        ),
        out_specs=(
            rows,
            rows,
            vector,
            vector,
            matrix,
            matrix,
            vector,
            vector,
            matrix,
            vector,
            matrix,
            vector,
        ),
        check_vma=False,
    )
```

```python
from functools import partial

import jax
import jax.numpy as jnp
from jax import lax
from jax.experimental import pallas as pl
from jax.experimental.pallas import tpu as pltpu
from jax.sharding import PartitionSpec as P


HEADS = 8
EPS = 1e-05
LOG2E = 1.4426950408889634
WIDE = 512
NARROW = 384
PACK = 256
VMEM_LIMIT = 18 * 1024 * 1024
BF = jnp.bfloat16
F32 = jnp.float32


def dot(a, b, dims=((1,), (0,))):
    return lax.dot_general(a, b, (dims, ((), ())), preferred_element_type=F32)


def dot_t(a, b):
    return dot(a, b, ((1,), (1,)))


def params(limit=VMEM_LIMIT):
    return pltpu.CompilerParams(vmem_limit_bytes=limit)


def cost(micros):
    return pl.CostEstimate(flops=int(micros * 1e8), bytes_accessed=1000, transcendentals=0)


VM = pl.BlockSpec(memory_space=pltpu.VMEM)
SM = pl.BlockSpec(memory_space=pltpu.SMEM)


def after(value, token):
    return lax.optimization_barrier((value, token))[0]


def swap(value, axis, bit):
    size = lax.axis_size(axis)
    return lax.ppermute(value, axis, [(i, i ^ bit) for i in range(size)])


def exchange(pieces, axis):
    return [pieces[0]] + [swap(pieces[k], axis, k) for k in range(1, len(pieces))]


def gather_pieces(value, axis):
    return exchange([value] * lax.axis_size(axis), axis)


def gather_pairs(value, axis):
    size = lax.axis_size(axis)
    far = [swap(value, axis, j) if j else value for j in range(0, size, 2)]
    result = []
    for mine in far:
        result += [mine, swap(mine, axis, 1)]
    return result


def assemble_qkv_kernel(count, seq_parts, part_width, me_ref, *refs):
    pieces, small = refs[:count], refs[count : 2 * count]
    wq_ref, vec_ref, bias_ref, small_s = refs[2 * count :]
    rows = pieces[0].shape[0]
    model = wq_ref.shape[1]
    ratio = small[0].shape[0] - 5
    for j in range(count):
        owner = me_ref[0] ^ j
        start = pl.multiple_of(owner * rows, rows)
        for d in range(seq_parts):
            for t in range(3):
                lane = t * model + d * part_width
                wq_ref[d, pl.ds(start, rows), t * part_width : (t + 1) * part_width] = pieces[j][
                    :, lane : lane + part_width
                ]
        small_s[owner] = small[j][...].astype(F32)
    vec_ref[5:8] = jnp.zeros((3, model), F32)
    for o in range(count):
        item = small_s[o]
        vec_ref[0:5, o * rows : (o + 1) * rows] = item[0:5]
        for t in range(ratio):
            lane = (o * ratio + t) * rows
            bias_ref[lane // CHUNK, :, lane % CHUNK : lane % CHUNK + rows] = item[5 + t : 6 + t]


def assemble_qkv(pieces, small, me, model, seq_parts, hidden):
    part_width = model // seq_parts
    count = len(pieces)
    return pl.pallas_call(
        partial(assemble_qkv_kernel, count, seq_parts, part_width),
        name="assemble_qkv",
        out_shape=(
            jax.ShapeDtypeStruct((seq_parts, model, 3 * part_width), BF),
            jax.ShapeDtypeStruct((8, model), F32),
            jax.ShapeDtypeStruct((hidden // CHUNK, 1, CHUNK), F32),
        ),
        in_specs=[SM] + [VM] * (2 * count),
        out_specs=(VM, VM, VM),
        scratch_shapes=[
            pltpu.VMEM((count,) + small[0].shape, F32),
        ],
        compiler_params=params(),
        cost_estimate=cost(2),
    )(me, *pieces, *small)


def assemble_rest_kernel(count, me_ref, *refs):
    pieces, (out_ref, up_ref, down_ref) = refs[:count], refs[count:]
    model = out_ref.shape[0]
    rows = model // count
    ratio = up_ref.shape[1] // model
    down_rows = ratio * rows
    for j in range(count):
        owner = me_ref[0] ^ j
        place = pl.ds(pl.multiple_of(owner * rows, rows), rows)
        out_ref[place, :] = pieces[j][0:rows, :]
        for t in range(ratio):
            up_ref[place, t * model : (t + 1) * model] = pieces[j][
                (1 + t) * rows : (2 + t) * rows, :
            ]
        place = pl.ds(pl.multiple_of(owner * down_rows, down_rows), down_rows)
        down_ref[place, :] = pieces[j][(1 + ratio) * rows :, :]


def assemble_rest(pieces, me, model, hidden):
    count = len(pieces)
    return pl.pallas_call(
        partial(assemble_rest_kernel, count),
        name="assemble_rest",
        out_shape=(
            jax.ShapeDtypeStruct((model, model), BF),
            jax.ShapeDtypeStruct((model, hidden), BF),
            jax.ShapeDtypeStruct((hidden, model), BF),
        ),
        in_specs=[SM] + [VM] * count,
        out_specs=(VM, VM, VM),
        compiler_params=params(),
        cost_estimate=cost(2),
    )(me, *pieces)


def norm_parts(rows):
    mean_row = jnp.mean(rows, axis=-1, keepdims=True)
    centred = rows - mean_row
    inverse = lax.rsqrt(jnp.mean(centred * centred, axis=-1, keepdims=True) + EPS)
    return centred * inverse, inverse


def norm_back(grad_normed, scaled, inverse, gain):
    grad_scaled = grad_normed * gain
    centre = jnp.mean(grad_scaled, axis=-1, keepdims=True)
    along = jnp.mean(grad_scaled * scaled, axis=-1, keepdims=True)
    return inverse * (grad_scaled - centre - scaled * along)


def project_kernel(parts, me_ref, tokens_ref, embed_ref, wq_ref, vec_ref, hidden_ref, *outs):
    rows = tokens_ref[0].astype(F32) + embed_ref[0].astype(F32)
    scaled, _ = norm_parts(rows)
    hidden = (scaled * vec_ref[0:1] + vec_ref[1:2]).astype(BF)
    hidden_ref[...] = hidden
    for k in range(parts):
        outs[k][...] = dot(hidden, wq_ref[me_ref[0] ^ k]).astype(BF)


def project(tokens, embed, micro_index, wq, vec, me):
    _, rows, model = tokens.shape
    parts, _, width = wq.shape
    row_spec = pl.BlockSpec((1, rows, model), lambda i: (micro_index, 0, 0))
    whole = lambda shape: pl.BlockSpec(shape, lambda i: (0,) * len(shape))
    return pl.pallas_call(
        partial(project_kernel, parts),
        name="project",
        grid=(1,),
        out_shape=[jax.ShapeDtypeStruct((rows, model), BF)]
        + [jax.ShapeDtypeStruct((rows, width), BF)] * parts,
        in_specs=[SM, row_spec, row_spec, whole(wq.shape), whole(vec.shape)],
        out_specs=[whole((rows, model))] + [whole((rows, width))] * parts,
        compiler_params=params(),
        cost_estimate=cost(2),
    )(me, tokens, embed, wq, vec)


def docs_kernel(parts, me_ref, *refs):
    pieces, (doc_ref, low_ref, high_ref) = refs[:parts], refs[parts:]
    micro, _, rows = pieces[0].shape
    for k in range(parts):
        place = pl.ds(pl.multiple_of((me_ref[0] ^ k) * rows, rows), rows)
        doc_ref[:, :, place] = pieces[k][...].astype(F32)
    for m in range(micro):
        doc = doc_ref[m]
        for i in range(doc.shape[1] // WIDE):
            first = doc[:, i * WIDE : i * WIDE + 1]
            last = doc[:, (i + 1) * WIDE - 1 : (i + 1) * WIDE]
            low = jnp.sum(jnp.where(doc < first, 1.0, 0.0)).astype(jnp.int32)
            high = jnp.sum(jnp.where(doc <= last, 1.0, 0.0)).astype(jnp.int32)
            low_ref[m, i] = low // NARROW
            high_ref[m, i] = (high + NARROW - 1) // NARROW


def assemble_docs(pieces, me):
    parts = len(pieces)
    micro, _, rows = pieces[0].shape
    length = rows * parts
    bounds = jax.ShapeDtypeStruct((micro, length // WIDE), jnp.int32)
    return pl.pallas_call(
        partial(docs_kernel, parts),
        name="assemble_docs",
        out_shape=(jax.ShapeDtypeStruct((micro, 1, length), F32), bounds, bounds),
        in_specs=[SM] + [VM] * parts,
        out_specs=(VM, SM, SM),
        compiler_params=params(),
        cost_estimate=cost(2),
    )(me, *pieces)


def head_mask(value, head, heads, head_dim):
    if heads == 1:
        return value
    lane = lax.broadcasted_iota(jnp.int32, value.shape, 1)
    keep = (lane >= head * head_dim) & (lane < (head + 1) * head_dim)
    return jnp.where(keep, value, jnp.zeros_like(value))


def spread_docs(doc_ref, doc_s):
    for start in range(0, doc_s.shape[0], 512):
        doc_s[start : start + 512, :] = jnp.broadcast_to(
            doc_ref[0:1, start : start + 512], (128, 512)
        ).T


def same_doc(doc_s, place, doc_row):
    column = doc_s[place, :]
    return jnp.concatenate([column] * (doc_row.shape[1] // 128), axis=1) == doc_row


def fold(value, combine):
    out = value[0:8]
    for start in range(8, value.shape[0], 8):
        out = combine(out, value[start : start + 8])
    return out


def place_rows(pieces, me, rows_s):
    rows = pieces[0].shape[0]
    for k, piece in enumerate(pieces):
        rows_s[pl.ds(pl.multiple_of((me ^ k) * rows, rows), rows), :] = piece[...]


def attend_kernel(parts, heads, head_dim, m, me_ref, low_ref, high_ref, docs_ref, *refs):
    doc_ref = docs_ref.at[m]
    pieces = refs[:parts]
    outs = refs[parts : 2 * parts]
    log_ref = refs[2 * parts]
    triple_s, value_t, doc_s, score_s, out_s = refs[2 * parts + 1 :]
    rows, width = pieces[0].shape
    here = width // 3
    length = rows * parts
    spread_docs(doc_ref, doc_s)
    place_rows(pieces, me_ref[0], triple_s)
    for start in range(0, length, WIDE):
        value_t[:, start : start + WIDE] = (
            triple_s[start : start + WIDE, 2 * here :].astype(F32).T.astype(BF)
        )
    scale = head_dim ** (-0.5) * LOG2E

    def one_block(i, _):
        place = pl.ds(pl.multiple_of(i * WIDE, WIDE), WIDE)
        query = triple_s[place, 0:here]
        queries = [head_mask(query, h, heads, head_dim) for h in range(heads)]
        doc_row = doc_ref[0:1, place]

        def score(j, tops):
            key_place = pl.ds(pl.multiple_of(j * NARROW, NARROW), NARROW)
            keys = triple_s[key_place, here : 2 * here]
            same = same_doc(doc_s, key_place, doc_row)
            result = []
            for h in range(heads):
                scores = jnp.where(same, dot_t(keys, queries[h]) * scale, -jnp.inf)
                score_s[h, key_place, :] = scores
                result.append(jnp.maximum(tops[h], fold(scores, jnp.maximum)))
            return tuple(result)

        tops = lax.fori_loop(
            low_ref[m, i],
            high_ref[m, i],
            score,
            tuple(jnp.full((8, WIDE), -jnp.inf, F32) for _ in range(heads)),
        )
        tops = [jnp.max(top, axis=0, keepdims=True) for top in tops]

        def mix(j, carry):
            key_place = pl.ds(pl.multiple_of(j * NARROW, NARROW), NARROW)
            result = []
            for h in range(heads):
                total, acc = carry[h]
                weight = jnp.exp2(score_s[h, key_place, :] - tops[h])
                total = total + fold(weight, jnp.add)
                values = value_t[h * head_dim : (h + 1) * head_dim, key_place]
                result.append((total, acc + dot(values, weight.astype(BF))))
            return tuple(result)

        done = lax.fori_loop(
            low_ref[m, i],
            high_ref[m, i],
            mix,
            tuple(
                (jnp.zeros((8, WIDE), F32), jnp.zeros((head_dim, WIDE), F32))
                for _ in range(heads)
            ),
        )
        mixed = []
        for h in range(heads):
            total = jnp.sum(done[h][0], axis=0, keepdims=True)
            mixed.append(done[h][1] / total)
            log_ref[h, :, place] = jnp.broadcast_to(tops[h] + jnp.log2(total), (8, WIDE))
        mixed = jnp.concatenate(mixed, axis=0) if heads > 1 else mixed[0]
        out_s[place, :] = mixed.T.astype(BF)
        return 0

    lax.fori_loop(0, length // WIDE, one_block, 0)
    for k in range(parts):
        place = pl.ds(pl.multiple_of((me_ref[0] ^ k) * rows, rows), rows)
        outs[k][...] = out_s[place, :]


def attend(pieces, me, low, high, doc, m, heads, head_dim):
    parts = len(pieces)
    rows, width = pieces[0].shape
    here = width // 3
    length = rows * parts
    found = pl.pallas_call(
        partial(attend_kernel, parts, heads, head_dim, m),
        name="attend",
        out_shape=[jax.ShapeDtypeStruct((rows, here), BF)] * parts
        + [jax.ShapeDtypeStruct((heads, 8, length), F32)],
        in_specs=[SM, SM, SM, VM] + [VM] * parts,
        out_specs=[VM] * (parts + 1),
        scratch_shapes=[
            pltpu.VMEM((length, width), BF),
            pltpu.VMEM((here, length), BF),
            pltpu.VMEM((length, 128), F32),
            pltpu.VMEM((heads, length, WIDE), F32),
            pltpu.VMEM((length, here), BF),
        ],
        compiler_params=params(),
        cost_estimate=cost(8),
    )(me, low, high, doc, *pieces)
    return found[:parts], found[parts]


def attend_back_kernel(
    parts, heads, head_dim, m, me_ref, low_ref, high_ref, docs_ref, log_ref, *refs
):
    doc_ref = docs_ref.at[m]
    pieces = refs[:parts]
    mixes = refs[parts : 2 * parts]
    grads = refs[2 * parts : 3 * parts]
    outs = refs[3 * parts : 4 * parts]
    (
        triple_s,
        grad_all,
        mix_all,
        query_s,
        key_t,
        grad_s,
        centre_s,
        doc_s,
        query_t,
        pair_s,
    ) = refs[4 * parts :]
    rows, width = pieces[0].shape
    here = width // 3
    length = rows * parts
    me = me_ref[0]
    spread_docs(doc_ref, doc_s)
    place_rows(pieces, me, triple_s)
    place_rows(grads, me, grad_all)
    place_rows(mixes, me, mix_all)
    for start in range(0, length, WIDE):
        place = pl.ds(start, WIDE)
        query = triple_s[place, 0:here]
        grad = grad_all[place, :]
        for h in range(heads):
            query_s[h, place, :] = head_mask(query, h, heads, head_dim)
            grad_s[h, place, :] = head_mask(grad, h, heads, head_dim)
        key_t[:, place] = triple_s[place, here : 2 * here].astype(F32).T.astype(BF)
        both = (grad.astype(F32) * mix_all[place, :].astype(F32)).T
        for h in range(heads):
            centre = jnp.sum(both[h * head_dim : (h + 1) * head_dim], axis=0, keepdims=True)
            centre_s[h, :, place] = jnp.broadcast_to(centre, (8, WIDE))
    query_t[...] = jnp.zeros_like(query_t)
    scale = head_dim ** (-0.5)

    def one_key(j, _):
        key_place = pl.ds(pl.multiple_of(j * WIDE, WIDE), WIDE)
        keys = triple_s[key_place, here : 2 * here]
        values = triple_s[key_place, 2 * here :]
        keys_t = [key_t[h * head_dim : (h + 1) * head_dim, key_place] for h in range(heads)]

        def one_block(i, carry):
            grad_key, grad_value = carry
            place = pl.ds(pl.multiple_of(i * NARROW, NARROW), NARROW)
            same = same_doc(doc_s, key_place, doc_ref[0:1, place])
            for h in range(heads):
                query = query_s[h, place, :]
                grad = grad_s[h, place, :]
                scores = jnp.where(same, dot_t(keys, query) * (scale * LOG2E), -jnp.inf)
                weight = jnp.exp2(scores - log_ref[h, 0:1, place])
                grad_weight = dot_t(values, grad)
                grad_score = (weight * (grad_weight - centre_s[h, 0:1, place])).astype(BF)
                grad_value = grad_value + dot(weight.astype(BF), grad)
                grad_key = grad_key + dot(grad_score, query)
                query_t[h * head_dim : (h + 1) * head_dim, place] += dot(keys_t[h], grad_score)
            return grad_key, grad_value

        zero = jnp.zeros((WIDE, here), F32)
        grad_key, grad_value = lax.fori_loop(
            low_ref[m, j], high_ref[m, j], one_block, (zero, zero)
        )
        pair_s[key_place, 0:here] = (grad_key * scale).astype(BF)
        pair_s[key_place, here:] = grad_value.astype(BF)
        return 0

    lax.fori_loop(0, length // WIDE, one_key, 0)
    for k in range(parts):
        place = pl.ds(pl.multiple_of((me_ref[0] ^ k) * rows, rows), rows)
        outs[k][:, 0:here] = (query_t[:, place].T * scale).astype(BF)
        outs[k][:, here:] = pair_s[place, :]


def attend_back(pieces, mixes, grads, me, low, high, doc, m, log_total, heads, head_dim):
    parts = len(pieces)
    rows, width = pieces[0].shape
    here = width // 3
    length = rows * parts
    return pl.pallas_call(
        partial(attend_back_kernel, parts, heads, head_dim, m),
        name="attend_back",
        out_shape=[jax.ShapeDtypeStruct((rows, width), BF)] * parts,
        in_specs=[SM, SM, SM, VM, VM] + [VM] * (3 * parts),
        out_specs=[VM] * parts,
        scratch_shapes=[
            pltpu.VMEM((length, width), BF),
            pltpu.VMEM((length, here), BF),
            pltpu.VMEM((length, here), BF),
            pltpu.VMEM((heads, length, here), BF),
            pltpu.VMEM((here, length), BF),
            pltpu.VMEM((heads, length, here), BF),
            pltpu.VMEM((heads, 8, length), F32),
            pltpu.VMEM((length, 128), F32),
            pltpu.VMEM((here, length), F32),
            pltpu.VMEM((length, 2 * here), BF),
        ],
        compiler_params=params(),
        cost_estimate=cost(12),
    )(me, low, high, doc, log_total, *pieces, *mixes, *grads)


CHUNK = 512


def feed_kernel(parts, has_old, me_ref, tokens_ref, embed_ref, cot_ref, vec_ref, bias_ref, *refs):
    mixes = refs[:parts]
    w_out, w_up, w_down = refs[parts : parts + 3]
    refs = refs[parts + 3 + has_old :]
    out_ref, act_ref, pre_ref, hidden_ref, branch_ref, middle_ref, sums_ref = refs[:7]
    grads = refs[7 : 7 + parts]
    total_s, back_s = refs[7 + parts :]
    me = me_ref[0]
    here = mixes[0].shape[1]
    middle = tokens_ref[0].astype(F32) + embed_ref[0].astype(F32)
    for k in range(parts):
        place = pl.ds(pl.multiple_of((me ^ k) * here, here), here)
        middle = middle + dot(mixes[k][...], w_out[place, :])
    scaled, inverse = norm_parts(middle)
    hidden_ref[0] = (scaled * vec_ref[2:3] + vec_ref[3:4]).astype(BF)
    middle_ref[...] = middle
    total_s[...] = jnp.zeros_like(total_s)
    back_s[...] = jnp.zeros_like(back_s)
    root = 0.7978845608028654

    def one_chunk(f, _):
        place = pl.ds(pl.multiple_of(f * CHUNK, CHUNK), CHUNK)
        value = dot(hidden_ref[0], w_up[:, place]) + bias_ref[f]
        square = value * value
        bend = jnp.tanh(root * (value + 0.044715 * (value * square)))
        half = 0.5 * (1.0 + bend)
        act = (value * half).astype(BF)
        slope = half + (0.5 * root) * value * (1.0 - bend * bend) * (1.0 + 0.134145 * square)
        act_ref[0, :, place] = act
        total_s[...] += dot(act, w_down[place, :])
        grad_pre = (dot_t(cot_ref[0], w_down[place, :]) * slope).astype(BF)
        pre_ref[0, :, place] = grad_pre
        back_s[...] += dot_t(grad_pre, w_up[:, place])
        return 0

    lax.fori_loop(0, w_up.shape[1] // CHUNK, one_chunk, 0)
    middle = middle_ref[...]
    out_ref[0] = (middle + total_s[...] + vec_ref[4:5]).astype(BF)
    scaled, inverse = norm_parts(middle)
    grad_hidden = back_s[...]
    sums_ref[0:1] = jnp.sum(grad_hidden * scaled, axis=0, keepdims=True)
    sums_ref[1:2] = jnp.sum(grad_hidden, axis=0, keepdims=True)
    cot = cot_ref[0].astype(F32)
    sums_ref[2:3] = jnp.sum(cot, axis=0, keepdims=True)
    sums_ref[3:8] = jnp.zeros((5, sums_ref.shape[1]), F32)
    grad_middle = cot + norm_back(grad_hidden, scaled, inverse, vec_ref[2:3])
    middle_ref[...] = grad_middle
    branch = grad_middle.astype(BF)
    branch_ref[0] = branch
    for k in range(parts):
        place = pl.ds(pl.multiple_of((me ^ k) * here, here), here)
        grads[k][...] = dot_t(branch, w_out[place, :]).astype(BF)


def feed(tokens, embed, cot, micro_index, mixes, vec, bias, w_out, w_up, w_down, old, me):
    micro, rows, model = tokens.shape
    parts = len(mixes)
    here = mixes[0].shape[1]
    hidden = w_up.shape[1]
    row_spec = pl.BlockSpec((1, rows, model), lambda i: (micro_index, 0, 0))
    whole = lambda shape: pl.BlockSpec(shape, lambda i: (0,) * len(shape))
    wide_spec = pl.BlockSpec((1, rows, hidden), lambda i: (micro_index, 0, 0))
    old_args = [] if old is None else list(old)
    found = pl.pallas_call(
        partial(feed_kernel, parts, len(old_args)),
        name="feed",
        grid=(1,),
        out_shape=[
            jax.ShapeDtypeStruct((micro, rows, model), BF),
            jax.ShapeDtypeStruct((micro, rows, hidden), BF),
            jax.ShapeDtypeStruct((micro, rows, hidden), BF),
            jax.ShapeDtypeStruct((micro, rows, model), BF),
            jax.ShapeDtypeStruct((micro, rows, model), BF),
            jax.ShapeDtypeStruct((rows, model), F32),
            jax.ShapeDtypeStruct((8, model), F32),
        ]
        + [jax.ShapeDtypeStruct((rows, here), BF)] * parts,
        in_specs=[SM, row_spec, row_spec, row_spec, whole(vec.shape), whole(bias.shape)]
        + [whole((rows, here))] * parts
        + [whole(w_out.shape), whole(w_up.shape), whole(w_down.shape)]
        + [pl.BlockSpec(memory_space=pl.ANY)] * len(old_args),
        out_specs=[
            row_spec,
            wide_spec,
            wide_spec,
            row_spec,
            row_spec,
            whole((rows, model)),
            whole((8, model)),
        ]
        + [whole((rows, here))] * parts,
        scratch_shapes=[pltpu.VMEM((rows, model), F32)] * 2,
        input_output_aliases={9 + parts + t: t for t in range(len(old_args))},
        compiler_params=params(28 * 1024 * 1024),
        cost_estimate=cost(8),
    )(me, tokens, embed, cot, vec, bias, *mixes, w_out, w_up, w_down, *old_args)
    return found[:7], found[7:]


def rest_grads_kernel(micro, parts, count, me_s, me_f, act_ref, pre_ref, hidden_ref, branch_ref,
                      cot_ref, *refs):
    mixes = refs[: micro * parts]
    keep_ref, send_ref, bias_ref = refs[micro * parts : micro * parts + 3]
    hidden_t, cot_t, mixed_t, up_s, down_s, out_s = refs[micro * parts + 3 :]
    targets = (keep_ref, send_ref)
    rows, model = hidden_ref.shape[1:]
    here = mixes[0].shape[1]
    share = model // count
    chunk = pl.program_id(0)
    owners, _, down_lanes = down_s.shape
    down_rows = model // parts
    up_rows, down_height, out_groups, _ = rest_layout(model, pl.num_programs(0) * model, parts, count)

    @pl.when(chunk == 0)
    def _():
        for m in range(micro):
            hidden_t[m] = hidden_ref[m].astype(F32).T.astype(BF)
            cot_t[m] = cot_ref[m].astype(F32).T.astype(BF)
            for k in range(parts):
                place = pl.ds(pl.multiple_of((me_s[0] ^ k) * here, here), here)
                mixed_t[m, place, :] = mixes[m * parts + k][...].astype(F32).T.astype(BF)
        found = sum(dot(mixed_t[m], branch_ref[m]) for m in range(micro)).astype(BF)
        for d in range(parts):
            out_s[d] = found[:, d * down_rows : (d + 1) * down_rows]
        tall = share // out_groups
        for j in range(count):
            base = (me_f[0] ^ j) * share
            for k in range(parts):
                for g in range(out_groups):
                    place = pl.ds(pl.multiple_of(base + g * tall, tall), tall)
                    top = up_rows + down_height
                    targets[j % 2][
                        k, j // 2, top : top + tall, g * down_rows : (g + 1) * down_rows
                    ] = out_s[me_s[0] ^ k, place, :]

    found = sum(dot(hidden_t[m], pre_ref[m]) for m in range(micro)).astype(BF)
    for q in range(model // PACK):
        up_s[q] = found[:, q * PACK : (q + 1) * PACK]
    for j in range(count):
        place = pl.ds(pl.multiple_of((me_f[0] ^ j) * share, share), share)
        for q in range(model // PACK):
            block = chunk * (model // PACK) + q
            groups = up_rows // share
            dest = me_s[0] ^ (block // groups)
            top = (q % groups) * share
            targets[j % 2][dest, j // 2, top : top + share, :] = up_s[q, place, :]

    found = sum(dot(cot_t[m], act_ref[m]) for m in range(micro)).astype(BF)
    for o in range(owners):
        down_s[o] = found[:, o * down_lanes : (o + 1) * down_lanes]
    groups = PACK // down_lanes
    tall = down_rows // groups
    for low in range(owners):
        owner = low ^ (me_f[0] % owners)
        slot = ((chunk ^ (me_f[0] // owners)) * owners + low) // 2
        for k in range(parts):
            for g in range(groups):
                place = pl.ds(pl.multiple_of((me_s[0] ^ k) * down_rows + g * tall, tall), tall)
                targets[low % 2][
                    k, slot, up_rows : up_rows + tall, g * down_lanes : (g + 1) * down_lanes
                ] = down_s[owner, place, :]

    ones = jnp.ones((8, rows), BF)
    bias_ref[...] = sum(dot(ones, pre_ref[m]) for m in range(micro))


def rest_layout(model, hidden, parts, count):
    share = model // count
    up_rows = share * (hidden // parts) // PACK
    down_rows = (model // parts) * (hidden // count) // PACK
    groups = PACK // (model // parts)
    if share % (16 * groups):
        groups = 1
    return up_rows, down_rows, groups, up_rows + down_rows + share // groups


def rest_grads(acts, pres, hiddens, branches, cot, mixes, me_s, me_f, count):
    micro, rows, model = cot.shape
    parts = len(mixes[0])
    hidden = acts.shape[2]
    height = rest_layout(model, hidden, parts, count)[3]
    half = (parts, count // 2, height, PACK)
    flat = [item for group in mixes for item in group]
    lanes = hidden // count
    whole = lambda shape: pl.BlockSpec(shape, lambda t: (0,) * len(shape))
    chunk = pl.BlockSpec((micro, rows, model), lambda t: (0, 0, t))
    return pl.pallas_call(
        partial(rest_grads_kernel, micro, parts, count),
        name="rest_grads",
        grid=(hidden // model,),
        out_shape=(
            jax.ShapeDtypeStruct(half, BF),
            jax.ShapeDtypeStruct(half, BF),
            jax.ShapeDtypeStruct((8, hidden), F32),
        ),
        in_specs=[SM, SM, chunk, chunk]
        + [whole(cot.shape)] * 3
        + [whole(flat[0].shape)] * len(flat),
        out_specs=(whole(half), whole(half), pl.BlockSpec((8, model), lambda t: (0, t))),
        scratch_shapes=[pltpu.VMEM((micro, model, rows), BF)] * 3
        + [
            pltpu.VMEM((model // PACK, model, PACK), BF),
            pltpu.VMEM((model // lanes, model, lanes), BF),
            pltpu.VMEM((parts, model, model // parts), BF),
        ],
        compiler_params=params(36 * 1024 * 1024),
        cost_estimate=cost(12),
    )(me_s, me_f, acts, pres, hiddens, branches, cot, *flat)


def finish_rest_kernel(parts, me_ref, *refs):
    pieces = refs[:parts]
    out_ref, up_ref, down_ref, out_s, down_s = refs[parts:]
    share, hidden = up_ref.shape
    down_lanes, model = down_ref.shape
    up_rows, down_height, out_groups, _ = rest_layout(model, hidden, parts, model // share)
    down_rows = model // parts
    cols = hidden // parts
    for k in range(parts):
        dest = me_ref[0] ^ k
        for g in range(cols // PACK):
            place = pl.ds(pl.multiple_of(dest * cols + g * PACK, PACK), PACK)
            up_ref[:, place] = pieces[k][g * share : (g + 1) * share, :].astype(F32)
        groups = PACK // down_lanes
        tall = down_rows // groups
        for g in range(groups):
            place = pl.ds(pl.multiple_of(dest * down_rows + g * tall, tall), tall)
            down_s[place, :] = pieces[k][
                up_rows : up_rows + tall, g * down_lanes : (g + 1) * down_lanes
            ].astype(F32)
        tall = share // out_groups
        top = up_rows + down_height
        for g in range(out_groups):
            out_s[dest, g * tall : (g + 1) * tall, :] = pieces[k][
                top : top + tall, g * down_rows : (g + 1) * down_rows
            ].astype(F32)
    down_ref[...] = down_s[...].T
    for d in range(parts):
        out_ref[:, d * down_rows : (d + 1) * down_rows] = out_s[d]


def finish_rest(pieces, me, model, hidden, count):
    parts = len(pieces)
    share, lanes = model // count, hidden // count
    return pl.pallas_call(
        partial(finish_rest_kernel, parts),
        name="finish_rest",
        out_shape=(
            jax.ShapeDtypeStruct((share, model), F32),
            jax.ShapeDtypeStruct((share, hidden), F32),
            jax.ShapeDtypeStruct((lanes, model), F32),
        ),
        in_specs=[SM] + [VM] * parts,
        out_specs=(VM, VM, VM),
        scratch_shapes=[
            pltpu.VMEM((parts, share, model // parts), F32),
            pltpu.VMEM((model, lanes), F32),
        ],
        compiler_params=params(),
        cost_estimate=cost(1),
    )(me, *pieces)


def finish_qkv_kernel(parts, me_ref, *refs):
    pieces = refs[:parts]
    out_ref, piece_s = refs[parts:]
    here = pieces[0].shape[1] // 3
    model = here * parts
    for k in range(parts):
        piece_s[me_ref[0] ^ k] = pieces[k][...].astype(F32)
    for d in range(parts):
        for t in range(3):
            lane = t * model + d * here
            out_ref[:, lane : lane + here] = piece_s[d, :, t * here : (t + 1) * here]


def finish_qkv(pieces, me):
    parts = len(pieces)
    share, width = pieces[0].shape
    return pl.pallas_call(
        partial(finish_qkv_kernel, parts),
        name="finish_qkv",
        out_shape=jax.ShapeDtypeStruct((share, parts * width), F32),
        in_specs=[SM] + [VM] * parts,
        out_specs=VM,
        scratch_shapes=[pltpu.VMEM((parts, share, width), F32)],
        compiler_params=params(),
        cost_estimate=cost(1),
    )(me, *pieces)


def input_kernel(parts, has_old, me_ref, tokens_ref, embed_ref, middle_ref, wq_ref, vec_ref, *refs):
    pieces = refs[:parts]
    out_ref, sums_ref = refs[parts + has_old :]
    grad_hidden = dot_t(pieces[0][...], wq_ref[me_ref[0]])
    for k in range(1, parts):
        grad_hidden = grad_hidden + dot_t(pieces[k][...], wq_ref[me_ref[0] ^ k])
    rows = tokens_ref[0].astype(F32) + embed_ref[0].astype(F32)
    scaled, inverse = norm_parts(rows)
    sums_ref[0:1] = jnp.sum(grad_hidden * scaled, axis=0, keepdims=True)
    sums_ref[1:2] = jnp.sum(grad_hidden, axis=0, keepdims=True)
    sums_ref[2:8] = jnp.zeros((6, sums_ref.shape[1]), F32)
    out_ref[0] = middle_ref[...] + norm_back(grad_hidden, scaled, inverse, vec_ref[0:1])


def input_gradient(tokens, embed, micro_index, grad_middle, pieces, wq, vec, old, me):
    micro, rows, model = tokens.shape
    parts = len(pieces)
    width = pieces[0].shape[1]
    row_spec = pl.BlockSpec((1, rows, model), lambda i: (micro_index, 0, 0))
    whole = lambda shape: pl.BlockSpec(shape, lambda i: (0,) * len(shape))
    old_args = [] if old is None else [old]
    return pl.pallas_call(
        partial(input_kernel, parts, len(old_args)),
        name="input_gradient",
        grid=(1,),
        out_shape=(
            jax.ShapeDtypeStruct((micro, rows, model), F32),
            jax.ShapeDtypeStruct((8, model), F32),
        ),
        in_specs=[SM, row_spec, row_spec, whole((rows, model)), whole(wq.shape), whole(vec.shape)]
        + [whole((rows, width))] * parts
        + [pl.BlockSpec(memory_space=pl.ANY)] * len(old_args),
        out_specs=(row_spec, whole((8, model))),
        input_output_aliases={6 + parts: 0} if old_args else {},
        compiler_params=params(),
        cost_estimate=cost(2.5),
    )(me, tokens, embed, grad_middle, wq, vec, *pieces, *old_args)


def qkv_grads_kernel(micro, parts, count, me_s, me_f, *refs):
    hiddens = refs[:micro]
    pieces = refs[micro : micro + micro * parts]
    keep_ref, send_ref, hidden_t = refs[micro + micro * parts :]
    model = hiddens[0].shape[1]
    part = model // count
    for m in range(micro):
        hidden_t[m] = hiddens[m][...].astype(F32).T.astype(BF)

    def one(j, target, slot):
        place = pl.ds(pl.multiple_of((me_f[0] ^ j) * part, part), part)
        for k in range(parts):
            found = sum(
                dot(hidden_t[m, place, :], pieces[m * parts + k][...]) for m in range(micro)
            )
            target[k, slot] = found.astype(BF)

    def one_pair(s, _):
        one(2 * s, keep_ref, s)
        one(2 * s + 1, send_ref, s)
        return 0

    lax.fori_loop(0, count // 2, one_pair, 0)


def qkv_grads(hiddens, pieces, me_s, me_f, count):
    micro = len(hiddens)
    rows, model = hiddens[0].shape
    parts = len(pieces[0])
    width = pieces[0][0].shape[1]
    half = jax.ShapeDtypeStruct((parts, count // 2, model // count, width), BF)
    flat = [item for group in pieces for item in group]
    return pl.pallas_call(
        partial(qkv_grads_kernel, micro, parts, count),
        name="qkv_grads",
        out_shape=(half, half),
        in_specs=[SM, SM] + [VM] * (micro + micro * parts),
        out_specs=(VM, VM),
        scratch_shapes=[pltpu.VMEM((micro, model, rows), BF)],
        compiler_params=params(),
        cost_estimate=cost(7),
    )(me_s, me_f, *hiddens, *flat)


def total(items, dtype):
    found = items[0].astype(F32)
    for item in items[1:]:
        found = found + item.astype(F32)
    return found.astype(dtype)


def small_call(kernel, outs, *args):
    return pl.pallas_call(
        kernel,
        out_shape=outs,
        in_specs=[VM] * len(args),
        out_specs=jax.tree.map(lambda _: VM, outs),
        compiler_params=params(),
        cost_estimate=cost(0.5),
    )(*args)


def add_parts(keep, found):
    def kernel(keep_ref, found_ref, *outs):
        for k, out in enumerate(outs):
            out[...] = total([keep_ref[k], found_ref[k]], out.dtype)

    out = jax.ShapeDtypeStruct(keep.shape[1:], keep.dtype)
    return small_call(kernel, [out] * keep.shape[0], keep, found)


def add_halves(*items):
    def kernel(*refs):
        keep_ref, send_ref = refs[-2:]
        for s in range(keep_ref.shape[0]):
            keep_ref[s] = total([item[2 * s] for item in refs[:-2]], keep_ref.dtype)
            send_ref[s] = total([item[2 * s + 1] for item in refs[:-2]], keep_ref.dtype)

    half = (items[0].shape[0] // 2,) + items[0].shape[1:]
    out = jax.ShapeDtypeStruct(half, items[0].dtype)
    return small_call(kernel, [out, out], *items)


def add_all(*items):
    def kernel(*refs):
        refs[-1][...] = total([item[...] for item in refs[:-1]], refs[-1].dtype)

    return small_call(kernel, jax.ShapeDtypeStruct(items[0].shape, items[0].dtype), *items)


def reduce_to_owner(keep, send):
    size = lax.axis_size("fsdp")
    pieces = add_parts(keep, swap(send, "fsdp", 1))
    yield pieces
    pieces = exchange(pieces, "seq")
    if size == 2:
        final = add_all(*pieces)
    else:
        keep, send = add_halves(*pieces)
        bit = 2
        while True:
            yield keep, send
            found = swap(send, "fsdp", bit)
            bit *= 2
            if bit == size:
                final = add_all(keep, found)
                break
            keep, send = add_halves(keep, found)
    final = final.reshape(final.shape[1:])
    yield final
    yield gather_pieces(final, "seq")


def gather_sums(first, second, bias):
    def kernel(*refs):
        bias_ref, out_ref = refs[-2:]
        model = out_ref.shape[1]
        once, twice = refs[: len(first)], refs[len(first) : -2]
        out_ref[0:2] = total([item[0:2] for item in once], F32)
        out_ref[2:5] = total([item[0:3] for item in twice], F32)
        out_ref[5:8] = jnp.zeros((3, model), F32)
        for t in range(8):
            lanes = bias_ref.shape[1] // 8
            row = 8 + (t * lanes) // model
            lane = (t * lanes) % model
            out_ref[row : row + 1, lane : lane + lanes] = bias_ref[0:1, t * lanes : (t + 1) * lanes]

    model = first[0].shape[1]
    rows = 8 + bias.shape[1] // model
    out = jax.ShapeDtypeStruct((rows, model), F32)
    return small_call(kernel, out, *first, *second, bias)


def sum_over(value, axis):
    bit = 1
    while bit < lax.axis_size(axis):
        value = add_all(value, swap(value, axis, bit))
        bit *= 2
    return value


def layer(
    tokens,
    time_embed,
    doc_ids,
    out_grad,
    norm1_gain,
    norm1_shift,
    qkv_weight,
    out_weight,
    norm2_gain,
    norm2_shift,
    up_weight,
    up_bias,
    down_weight,
    down_bias,
):
    micro, _, _, model = tokens.shape
    parts = lax.axis_size("seq")
    count = lax.axis_size("fsdp")
    hidden = up_weight.shape[1]
    ratio = hidden // model
    head_dim = model // HEADS
    heads = HEADS // parts
    share = model // count
    seq_index = lax.axis_index("seq").astype(jnp.int32)
    fsdp_index = lax.axis_index("fsdp").astype(jnp.int32)
    me_s = seq_index.reshape(1)
    me_f = fsdp_index.reshape(1)
    tokens = tokens[:, 0]
    embed = time_embed[:, 0]
    cot = out_grad[:, 0]

    pieces = gather_pairs(qkv_weight, "fsdp")
    near = pieces[2]
    small = [norm1_gain, norm1_shift, norm2_gain, norm2_shift, down_bias]
    small = [item.reshape(1, share) for item in small] + [up_bias.reshape(ratio, share)]
    small = gather_pairs(after(jnp.concatenate(small), near), "fsdp")
    wq, vec, bias = assemble_qkv(pieces, small, me_f, model, parts, hidden)
    rest = jnp.concatenate(
        [out_weight]
        + [up_weight[:, t * model : (t + 1) * model] for t in range(ratio)]
        + [down_weight],
        axis=0,
    )
    rest = gather_pairs(after(rest, (pieces[2], pieces[4], pieces[6])), "fsdp")

    docs = gather_pieces(after(doc_ids, near), "seq")
    doc, low, high = assemble_docs(docs, me_s)

    hiddens, triples, mixes, logs = [], [], [], []
    for m in range(micro):
        found = project(tokens, embed, m, wq, vec, me_s)
        hiddens.append(found[0])
        outs = after(found[1:], triples[-1]) if m else found[1:]
        triples.append(exchange(outs, "seq"))
    sent = []
    for m in range(micro):
        triple = after(triples[m], logs[-1]) if m else triples[m]
        outs, log_total = attend(triple, me_s, low, high, doc, m, heads, head_dim)
        sent.append(outs)
        logs.append(log_total)
        mixes.append(exchange(outs, "seq"))
    w_out, w_up, w_down = assemble_rest(rest, me_f, model, hidden)
    stacked = None
    middles, sums, heads_grads = [], [], []
    for m in range(micro):
        mixed = mixes[m] if m else after(mixes[m], logs[-1])
        found, grads = feed(
            tokens, embed, cot, m, mixed, vec, bias, w_out, w_up, w_down, stacked, me_s
        )
        stacked = found[:5]
        middles.append(found[5])
        sums.append(found[6])
        heads_grads.append(exchange(grads, "seq"))
    layer_output, acts, pres, seconds, branches = stacked
    keep, send, bias_sum = rest_grads(acts, pres, seconds, branches, cot, mixes, me_s, me_f, count)
    hops = reduce_to_owner(keep, send)
    backs = []
    for m in range(micro):
        grads = after(heads_grads[m], (next(hops), outs) if m else bias_sum)
        outs = attend_back(
            triples[m],
            sent[m],
            grads,
            me_s,
            low,
            high,
            doc,
            m,
            logs[m],
            heads,
            head_dim,
        )
        backs.append(exchange(outs, "seq"))
    input_grad = None
    first_sums = []
    for m in range(micro - 1):
        pieces = after(backs[m], outs) if m == 0 else backs[m]
        input_grad, sum_one = input_gradient(
            tokens, embed, m, middles[m], pieces, wq, vec, input_grad, me_s
        )
        first_sums.append(sum_one)
    last = after(backs[-1], (input_grad, next(hops)))
    keep, send = qkv_grads(hiddens, backs[:-1] + [last], me_s, me_f, count)
    last = after(last, send)
    input_grad, sum_one = input_gradient(
        tokens, embed, micro - 1, middles[-1], last, wq, vec, input_grad, me_s
    )
    first_sums.append(sum_one)
    *_, pieces = hops
    grad_out, grad_up, grad_down = finish_rest(pieces, me_s, model, hidden, count)
    *_, pieces = reduce_to_owner(keep, send)
    grad_qkv = finish_qkv(pieces, me_s)

    vectors = gather_sums(first_sums, sums, bias_sum)
    vectors = sum_over(sum_over(vectors, "fsdp"), "seq")
    pick = lambda row: lax.dynamic_slice(vectors[row], (fsdp_index * share,), (share,))
    grad_up_bias = lax.dynamic_slice(
        vectors[8 : 8 + ratio].reshape(hidden), (fsdp_index * (hidden // count),), (hidden // count,)
    )
    return (
        layer_output[:, None],
        input_grad[:, None],
        pick(0),
        pick(1),
        grad_qkv,
        grad_out,
        pick(2),
        pick(3),
        grad_up,
        grad_up_bias,
        grad_down,
        pick(4),
    )


def solution(mesh):
    rows = P(None, "fsdp", "seq", None)
    vector = P("fsdp")
    matrix = P("fsdp", None)
    return jax.shard_map(
        layer,
        mesh=mesh,
        in_specs=(
            rows,
            rows,
            P(None, "fsdp", "seq"),
            rows,
            vector,
            vector,
            matrix,
            matrix,
            vector,
            vector,
            matrix,
            vector,
            matrix,
            vector,
        ),
        out_specs=(
            rows,
            rows,
            vector,
            vector,
            matrix,
            matrix,
            vector,
            vector,
            matrix,
            vector,
            matrix,
            vector,
        ),
        check_vma=False,
    )
```

```python
from functools import partial

import jax
import jax.numpy as jnp
from jax import lax
from jax.experimental import pallas as pl
from jax.experimental.pallas import tpu as pltpu
from jax.sharding import PartitionSpec as P


HEADS = 8
EPS = 1e-05
LOG2E = 1.4426950408889634
WIDE = 512
NARROW = 384
PACK = 256
VMEM_LIMIT = 18 * 1024 * 1024
BF = jnp.bfloat16
F32 = jnp.float32


def dot(a, b, dims=((1,), (0,))):
    return lax.dot_general(a, b, (dims, ((), ())), preferred_element_type=F32)


def dot_t(a, b):
    return dot(a, b, ((1,), (1,)))


def params(limit=VMEM_LIMIT):
    return pltpu.CompilerParams(vmem_limit_bytes=limit)


def cost(micros):
    return pl.CostEstimate(flops=int(micros * 1e8), bytes_accessed=1000, transcendentals=0)


VM = pl.BlockSpec(memory_space=pltpu.VMEM)
SM = pl.BlockSpec(memory_space=pltpu.SMEM)


def after(value, token):
    return lax.optimization_barrier((value, token))[0]


def swap(value, axis, bit):
    size = lax.axis_size(axis)
    return lax.ppermute(value, axis, [(i, i ^ bit) for i in range(size)])


def exchange(pieces, axis):
    return [pieces[0]] + [swap(pieces[k], axis, k) for k in range(1, len(pieces))]


def gather_pieces(value, axis):
    return exchange([value] * lax.axis_size(axis), axis)


def gather_pairs(value, axis):
    size = lax.axis_size(axis)
    far = [swap(value, axis, j) if j else value for j in range(0, size, 2)]
    result = []
    for mine in far:
        result += [mine, swap(mine, axis, 1)]
    return result


def assemble_qkv_kernel(count, seq_parts, part_width, me_ref, *refs):
    pieces, small = refs[:count], refs[count : 2 * count]
    wq_ref, vec_ref, bias_ref, small_s = refs[2 * count :]
    rows = pieces[0].shape[0]
    model = wq_ref.shape[1]
    ratio = small[0].shape[0] - 5
    for j in range(count):
        owner = me_ref[0] ^ j
        start = pl.multiple_of(owner * rows, rows)
        for d in range(seq_parts):
            for t in range(3):
                lane = t * model + d * part_width
                wq_ref[d, pl.ds(start, rows), t * part_width : (t + 1) * part_width] = pieces[j][
                    :, lane : lane + part_width
                ]
        small_s[owner] = small[j][...].astype(F32)
    vec_ref[5:8] = jnp.zeros((3, model), F32)
    for o in range(count):
        item = small_s[o]
        vec_ref[0:5, o * rows : (o + 1) * rows] = item[0:5]
        for t in range(ratio):
            lane = (o * ratio + t) * rows
            bias_ref[lane // CHUNK, :, lane % CHUNK : lane % CHUNK + rows] = item[5 + t : 6 + t]


def assemble_qkv(pieces, small, me, model, seq_parts, hidden):
    part_width = model // seq_parts
    count = len(pieces)
    return pl.pallas_call(
        partial(assemble_qkv_kernel, count, seq_parts, part_width),
        name="assemble_qkv",
        out_shape=(
            jax.ShapeDtypeStruct((seq_parts, model, 3 * part_width), BF),
            jax.ShapeDtypeStruct((8, model), F32),
            jax.ShapeDtypeStruct((hidden // CHUNK, 1, CHUNK), F32),
        ),
        in_specs=[SM] + [VM] * (2 * count),
        out_specs=(VM, VM, VM),
        scratch_shapes=[
            pltpu.VMEM((count,) + small[0].shape, F32),
        ],
        compiler_params=params(),
        cost_estimate=cost(2),
    )(me, *pieces, *small)


def assemble_rest_kernel(count, me_ref, *refs):
    pieces, (out_ref, up_ref, down_ref) = refs[:count], refs[count:]
    model = out_ref.shape[0]
    rows = model // count
    ratio = up_ref.shape[1] // model
    down_rows = ratio * rows
    for j in range(count):
        owner = me_ref[0] ^ j
        place = pl.ds(pl.multiple_of(owner * rows, rows), rows)
        out_ref[place, :] = pieces[j][0:rows, :]
        for t in range(ratio):
            up_ref[place, t * model : (t + 1) * model] = pieces[j][
                (1 + t) * rows : (2 + t) * rows, :
            ]
        place = pl.ds(pl.multiple_of(owner * down_rows, down_rows), down_rows)
        down_ref[place, :] = pieces[j][(1 + ratio) * rows :, :]


def assemble_rest(pieces, me, model, hidden):
    count = len(pieces)
    return pl.pallas_call(
        partial(assemble_rest_kernel, count),
        name="assemble_rest",
        out_shape=(
            jax.ShapeDtypeStruct((model, model), BF),
            jax.ShapeDtypeStruct((model, hidden), BF),
            jax.ShapeDtypeStruct((hidden, model), BF),
        ),
        in_specs=[SM] + [VM] * count,
        out_specs=(VM, VM, VM),
        compiler_params=params(),
        cost_estimate=cost(2),
    )(me, *pieces)


def norm_parts(rows):
    mean_row = jnp.mean(rows, axis=-1, keepdims=True)
    centred = rows - mean_row
    inverse = lax.rsqrt(jnp.mean(centred * centred, axis=-1, keepdims=True) + EPS)
    return centred * inverse, inverse


def norm_back(grad_normed, scaled, inverse, gain):
    grad_scaled = grad_normed * gain
    centre = jnp.mean(grad_scaled, axis=-1, keepdims=True)
    along = jnp.mean(grad_scaled * scaled, axis=-1, keepdims=True)
    return inverse * (grad_scaled - centre - scaled * along)


def project_kernel(parts, me_ref, tokens_ref, embed_ref, wq_ref, vec_ref, hidden_ref, *outs):
    rows = tokens_ref[0].astype(F32) + embed_ref[0].astype(F32)
    scaled, _ = norm_parts(rows)
    hidden = (scaled * vec_ref[0:1] + vec_ref[1:2]).astype(BF)
    hidden_ref[...] = hidden
    for k in range(parts):
        outs[k][...] = dot(hidden, wq_ref[me_ref[0] ^ k]).astype(BF)


def project(tokens, embed, micro_index, wq, vec, me):
    _, rows, model = tokens.shape
    parts, _, width = wq.shape
    row_spec = pl.BlockSpec((1, rows, model), lambda i: (micro_index, 0, 0))
    whole = lambda shape: pl.BlockSpec(shape, lambda i: (0,) * len(shape))
    return pl.pallas_call(
        partial(project_kernel, parts),
        name="project",
        grid=(1,),
        out_shape=[jax.ShapeDtypeStruct((rows, model), BF)]
        + [jax.ShapeDtypeStruct((rows, width), BF)] * parts,
        in_specs=[SM, row_spec, row_spec, whole(wq.shape), whole(vec.shape)],
        out_specs=[whole((rows, model))] + [whole((rows, width))] * parts,
        compiler_params=params(),
        cost_estimate=cost(2),
    )(me, tokens, embed, wq, vec)


def docs_kernel(parts, me_ref, *refs):
    pieces, (doc_ref, low_ref, high_ref) = refs[:parts], refs[parts:]
    micro, _, rows = pieces[0].shape
    for k in range(parts):
        place = pl.ds(pl.multiple_of((me_ref[0] ^ k) * rows, rows), rows)
        doc_ref[:, :, place] = pieces[k][...].astype(F32)
    for m in range(micro):
        doc = doc_ref[m]
        for i in range(doc.shape[1] // WIDE):
            first = doc[:, i * WIDE : i * WIDE + 1]
            last = doc[:, (i + 1) * WIDE - 1 : (i + 1) * WIDE]
            low = jnp.sum(jnp.where(doc < first, 1.0, 0.0)).astype(jnp.int32)
            high = jnp.sum(jnp.where(doc <= last, 1.0, 0.0)).astype(jnp.int32)
            low_ref[m, i] = low // NARROW
            high_ref[m, i] = (high + NARROW - 1) // NARROW


def assemble_docs(pieces, me):
    parts = len(pieces)
    micro, _, rows = pieces[0].shape
    length = rows * parts
    bounds = jax.ShapeDtypeStruct((micro, length // WIDE), jnp.int32)
    return pl.pallas_call(
        partial(docs_kernel, parts),
        name="assemble_docs",
        out_shape=(jax.ShapeDtypeStruct((micro, 1, length), F32), bounds, bounds),
        in_specs=[SM] + [VM] * parts,
        out_specs=(VM, SM, SM),
        compiler_params=params(),
        cost_estimate=cost(2),
    )(me, *pieces)


def head_mask(value, head, heads, head_dim):
    if heads == 1:
        return value
    lane = lax.broadcasted_iota(jnp.int32, value.shape, 1)
    keep = (lane >= head * head_dim) & (lane < (head + 1) * head_dim)
    return jnp.where(keep, value, jnp.zeros_like(value))


def spread_docs(doc_ref, doc_s):
    for start in range(0, doc_s.shape[0], 512):
        doc_s[start : start + 512, :] = jnp.broadcast_to(
            doc_ref[0:1, start : start + 512], (128, 512)
        ).T


def same_doc(doc_s, place, doc_row):
    column = doc_s[place, :]
    return jnp.concatenate([column] * (doc_row.shape[1] // 128), axis=1) == doc_row


def fold(value, combine):
    out = value[0:8]
    for start in range(8, value.shape[0], 8):
        out = combine(out, value[start : start + 8])
    return out


def place_rows(pieces, me, rows_s):
    rows = pieces[0].shape[0]
    for k, piece in enumerate(pieces):
        rows_s[pl.ds(pl.multiple_of((me ^ k) * rows, rows), rows), :] = piece[...]


def attend_kernel(parts, heads, head_dim, m, me_ref, low_ref, high_ref, docs_ref, *refs):
    doc_ref = docs_ref.at[m]
    pieces = refs[:parts]
    outs = refs[parts : 2 * parts]
    log_ref = refs[2 * parts]
    triple_s, value_t, doc_s, score_s, out_s = refs[2 * parts + 1 :]
    rows, width = pieces[0].shape
    here = width // 3
    length = rows * parts
    spread_docs(doc_ref, doc_s)
    place_rows(pieces, me_ref[0], triple_s)
    for start in range(0, length, WIDE):
        value_t[:, start : start + WIDE] = (
            triple_s[start : start + WIDE, 2 * here :].astype(F32).T.astype(BF)
        )
    scale = head_dim ** (-0.5) * LOG2E

    def one_block(i, _):
        place = pl.ds(pl.multiple_of(i * WIDE, WIDE), WIDE)
        query = triple_s[place, 0:here]
        queries = [head_mask(query, h, heads, head_dim) for h in range(heads)]
        doc_row = doc_ref[0:1, place]

        def score(j, tops):
            key_place = pl.ds(pl.multiple_of(j * NARROW, NARROW), NARROW)
            keys = triple_s[key_place, here : 2 * here]
            same = same_doc(doc_s, key_place, doc_row)
            result = []
            for h in range(heads):
                scores = jnp.where(same, dot_t(keys, queries[h]) * scale, -jnp.inf)
                score_s[h, key_place, :] = scores
                result.append(jnp.maximum(tops[h], fold(scores, jnp.maximum)))
            return tuple(result)

        tops = lax.fori_loop(
            low_ref[m, i],
            high_ref[m, i],
            score,
            tuple(jnp.full((8, WIDE), -jnp.inf, F32) for _ in range(heads)),
        )
        tops = [jnp.max(top, axis=0, keepdims=True) for top in tops]

        def mix(j, carry):
            key_place = pl.ds(pl.multiple_of(j * NARROW, NARROW), NARROW)
            result = []
            for h in range(heads):
                total, acc = carry[h]
                weight = jnp.exp2(score_s[h, key_place, :] - tops[h])
                total = total + fold(weight, jnp.add)
                values = value_t[h * head_dim : (h + 1) * head_dim, key_place]
                result.append((total, acc + dot(values, weight.astype(BF))))
            return tuple(result)

        done = lax.fori_loop(
            low_ref[m, i],
            high_ref[m, i],
            mix,
            tuple(
                (jnp.zeros((8, WIDE), F32), jnp.zeros((head_dim, WIDE), F32))
                for _ in range(heads)
            ),
        )
        mixed = []
        for h in range(heads):
            total = jnp.sum(done[h][0], axis=0, keepdims=True)
            mixed.append(done[h][1] / total)
            log_ref[h, :, place] = jnp.broadcast_to(tops[h] + jnp.log2(total), (8, WIDE))
        mixed = jnp.concatenate(mixed, axis=0) if heads > 1 else mixed[0]
        out_s[place, :] = mixed.T.astype(BF)
        return 0

    lax.fori_loop(0, length // WIDE, one_block, 0)
    for k in range(parts):
        place = pl.ds(pl.multiple_of((me_ref[0] ^ k) * rows, rows), rows)
        outs[k][...] = out_s[place, :]


def attend(pieces, me, low, high, doc, m, heads, head_dim):
    parts = len(pieces)
    rows, width = pieces[0].shape
    here = width // 3
    length = rows * parts
    found = pl.pallas_call(
        partial(attend_kernel, parts, heads, head_dim, m),
        name="attend",
        out_shape=[jax.ShapeDtypeStruct((rows, here), BF)] * parts
        + [jax.ShapeDtypeStruct((heads, 8, length), F32)],
        in_specs=[SM, SM, SM, VM] + [VM] * parts,
        out_specs=[VM] * (parts + 1),
        scratch_shapes=[
            pltpu.VMEM((length, width), BF),
            pltpu.VMEM((here, length), BF),
            pltpu.VMEM((length, 128), F32),
            pltpu.VMEM((heads, length, WIDE), F32),
            pltpu.VMEM((length, here), BF),
        ],
        compiler_params=params(),
        cost_estimate=cost(8),
    )(me, low, high, doc, *pieces)
    return found[:parts], found[parts]


def attend_back_kernel(
    parts, heads, head_dim, m, me_ref, low_ref, high_ref, docs_ref, log_ref, *refs
):
    doc_ref = docs_ref.at[m]
    pieces = refs[:parts]
    mixes = refs[parts : 2 * parts]
    grads = refs[2 * parts : 3 * parts]
    outs = refs[3 * parts : 4 * parts]
    (
        triple_s,
        grad_all,
        mix_all,
        query_s,
        key_t,
        grad_s,
        centre_s,
        doc_s,
        query_t,
        pair_s,
    ) = refs[4 * parts :]
    rows, width = pieces[0].shape
    here = width // 3
    length = rows * parts
    me = me_ref[0]
    spread_docs(doc_ref, doc_s)
    place_rows(pieces, me, triple_s)
    place_rows(grads, me, grad_all)
    place_rows(mixes, me, mix_all)
    for start in range(0, length, WIDE):
        place = pl.ds(start, WIDE)
        query = triple_s[place, 0:here]
        grad = grad_all[place, :]
        for h in range(heads):
            query_s[h, place, :] = head_mask(query, h, heads, head_dim)
            grad_s[h, place, :] = head_mask(grad, h, heads, head_dim)
        key_t[:, place] = triple_s[place, here : 2 * here].astype(F32).T.astype(BF)
        both = (grad.astype(F32) * mix_all[place, :].astype(F32)).T
        for h in range(heads):
            centre = jnp.sum(both[h * head_dim : (h + 1) * head_dim], axis=0, keepdims=True)
            centre_s[h, :, place] = jnp.broadcast_to(centre, (8, WIDE))
    query_t[...] = jnp.zeros_like(query_t)
    scale = head_dim ** (-0.5)

    def one_key(j, _):
        key_place = pl.ds(pl.multiple_of(j * WIDE, WIDE), WIDE)
        keys = triple_s[key_place, here : 2 * here]
        values = triple_s[key_place, 2 * here :]
        keys_t = [key_t[h * head_dim : (h + 1) * head_dim, key_place] for h in range(heads)]

        def one_block(i, carry):
            grad_key, grad_value = carry
            place = pl.ds(pl.multiple_of(i * NARROW, NARROW), NARROW)
            same = same_doc(doc_s, key_place, doc_ref[0:1, place])
            for h in range(heads):
                query = query_s[h, place, :]
                grad = grad_s[h, place, :]
                scores = jnp.where(same, dot_t(keys, query) * (scale * LOG2E), -jnp.inf)
                weight = jnp.exp2(scores - log_ref[h, 0:1, place])
                grad_weight = dot_t(values, grad)
                grad_score = (weight * (grad_weight - centre_s[h, 0:1, place])).astype(BF)
                grad_value = grad_value + dot(weight.astype(BF), grad)
                grad_key = grad_key + dot(grad_score, query)
                query_t[h * head_dim : (h + 1) * head_dim, place] += dot(keys_t[h], grad_score)
            return grad_key, grad_value

        zero = jnp.zeros((WIDE, here), F32)
        grad_key, grad_value = lax.fori_loop(
            low_ref[m, j], high_ref[m, j], one_block, (zero, zero)
        )
        pair_s[key_place, 0:here] = (grad_key * scale).astype(BF)
        pair_s[key_place, here:] = grad_value.astype(BF)
        return 0

    lax.fori_loop(0, length // WIDE, one_key, 0)
    for k in range(parts):
        place = pl.ds(pl.multiple_of((me_ref[0] ^ k) * rows, rows), rows)
        outs[k][:, 0:here] = (query_t[:, place].T * scale).astype(BF)
        outs[k][:, here:] = pair_s[place, :]


def attend_back(pieces, mixes, grads, me, low, high, doc, m, log_total, heads, head_dim):
    parts = len(pieces)
    rows, width = pieces[0].shape
    here = width // 3
    length = rows * parts
    return pl.pallas_call(
        partial(attend_back_kernel, parts, heads, head_dim, m),
        name="attend_back",
        out_shape=[jax.ShapeDtypeStruct((rows, width), BF)] * parts,
        in_specs=[SM, SM, SM, VM, VM] + [VM] * (3 * parts),
        out_specs=[VM] * parts,
        scratch_shapes=[
            pltpu.VMEM((length, width), BF),
            pltpu.VMEM((length, here), BF),
            pltpu.VMEM((length, here), BF),
            pltpu.VMEM((heads, length, here), BF),
            pltpu.VMEM((here, length), BF),
            pltpu.VMEM((heads, length, here), BF),
            pltpu.VMEM((heads, 8, length), F32),
            pltpu.VMEM((length, 128), F32),
            pltpu.VMEM((here, length), F32),
            pltpu.VMEM((length, 2 * here), BF),
        ],
        compiler_params=params(),
        cost_estimate=cost(12),
    )(me, low, high, doc, log_total, *pieces, *mixes, *grads)


CHUNK = 512


def feed_kernel(parts, has_old, me_ref, tokens_ref, embed_ref, cot_ref, vec_ref, bias_ref, *refs):
    mixes = refs[:parts]
    w_out, w_up, w_down = refs[parts : parts + 3]
    refs = refs[parts + 3 + has_old :]
    out_ref, act_ref, pre_ref, hidden_ref, branch_ref, middle_ref, sums_ref = refs[:7]
    grads = refs[7 : 7 + parts]
    total_s, back_s = refs[7 + parts :]
    me = me_ref[0]
    here = mixes[0].shape[1]
    middle = tokens_ref[0].astype(F32) + embed_ref[0].astype(F32)
    for k in range(parts):
        place = pl.ds(pl.multiple_of((me ^ k) * here, here), here)
        middle = middle + dot(mixes[k][...], w_out[place, :])
    scaled, inverse = norm_parts(middle)
    hidden_ref[0] = (scaled * vec_ref[2:3] + vec_ref[3:4]).astype(BF)
    middle_ref[...] = middle
    total_s[...] = jnp.zeros_like(total_s)
    back_s[...] = jnp.zeros_like(back_s)
    root = 0.7978845608028654

    def one_chunk(f, _):
        place = pl.ds(pl.multiple_of(f * CHUNK, CHUNK), CHUNK)
        value = dot(hidden_ref[0], w_up[:, place]) + bias_ref[f]
        square = value * value
        bend = jnp.tanh(root * (value + 0.044715 * (value * square)))
        half = 0.5 * (1.0 + bend)
        act = (value * half).astype(BF)
        slope = half + (0.5 * root) * value * (1.0 - bend * bend) * (1.0 + 0.134145 * square)
        act_ref[0, :, place] = act
        total_s[...] += dot(act, w_down[place, :])
        grad_pre = (dot_t(cot_ref[0], w_down[place, :]) * slope).astype(BF)
        pre_ref[0, :, place] = grad_pre
        back_s[...] += dot_t(grad_pre, w_up[:, place])
        return 0

    lax.fori_loop(0, w_up.shape[1] // CHUNK, one_chunk, 0)
    middle = middle_ref[...]
    out_ref[0] = (middle + total_s[...] + vec_ref[4:5]).astype(BF)
    scaled, inverse = norm_parts(middle)
    grad_hidden = back_s[...]
    sums_ref[0:1] = jnp.sum(grad_hidden * scaled, axis=0, keepdims=True)
    sums_ref[1:2] = jnp.sum(grad_hidden, axis=0, keepdims=True)
    cot = cot_ref[0].astype(F32)
    sums_ref[2:3] = jnp.sum(cot, axis=0, keepdims=True)
    sums_ref[3:8] = jnp.zeros((5, sums_ref.shape[1]), F32)
    grad_middle = cot + norm_back(grad_hidden, scaled, inverse, vec_ref[2:3])
    middle_ref[...] = grad_middle
    branch = grad_middle.astype(BF)
    branch_ref[0] = branch
    for k in range(parts):
        place = pl.ds(pl.multiple_of((me ^ k) * here, here), here)
        grads[k][...] = dot_t(branch, w_out[place, :]).astype(BF)


def feed(tokens, embed, cot, micro_index, mixes, vec, bias, w_out, w_up, w_down, old, me):
    micro, rows, model = tokens.shape
    parts = len(mixes)
    here = mixes[0].shape[1]
    hidden = w_up.shape[1]
    row_spec = pl.BlockSpec((1, rows, model), lambda i: (micro_index, 0, 0))
    whole = lambda shape: pl.BlockSpec(shape, lambda i: (0,) * len(shape))
    wide_spec = pl.BlockSpec((1, rows, hidden), lambda i: (micro_index, 0, 0))
    old_args = [] if old is None else list(old)
    found = pl.pallas_call(
        partial(feed_kernel, parts, len(old_args)),
        name="feed",
        grid=(1,),
        out_shape=[
            jax.ShapeDtypeStruct((micro, rows, model), BF),
            jax.ShapeDtypeStruct((micro, rows, hidden), BF),
            jax.ShapeDtypeStruct((micro, rows, hidden), BF),
            jax.ShapeDtypeStruct((micro, rows, model), BF),
            jax.ShapeDtypeStruct((micro, rows, model), BF),
            jax.ShapeDtypeStruct((rows, model), F32),
            jax.ShapeDtypeStruct((8, model), F32),
        ]
        + [jax.ShapeDtypeStruct((rows, here), BF)] * parts,
        in_specs=[SM, row_spec, row_spec, row_spec, whole(vec.shape), whole(bias.shape)]
        + [whole((rows, here))] * parts
        + [whole(w_out.shape), whole(w_up.shape), whole(w_down.shape)]
        + [pl.BlockSpec(memory_space=pl.ANY)] * len(old_args),
        out_specs=[
            row_spec,
            wide_spec,
            wide_spec,
            row_spec,
            row_spec,
            whole((rows, model)),
            whole((8, model)),
        ]
        + [whole((rows, here))] * parts,
        scratch_shapes=[pltpu.VMEM((rows, model), F32)] * 2,
        input_output_aliases={9 + parts + t: t for t in range(len(old_args))},
        compiler_params=params(28 * 1024 * 1024),
        cost_estimate=cost(8),
    )(me, tokens, embed, cot, vec, bias, *mixes, w_out, w_up, w_down, *old_args)
    return found[:7], found[7:]


def rest_grads_kernel(micro, parts, count, me_s, me_f, act_ref, pre_ref, hidden_ref, branch_ref,
                      cot_ref, *refs):
    mixes = refs[: micro * parts]
    keep_ref, send_ref, bias_ref = refs[micro * parts : micro * parts + 3]
    hidden_t, cot_t, mixed_t, up_s, down_s, out_s = refs[micro * parts + 3 :]
    targets = (keep_ref, send_ref)
    rows, model = hidden_ref.shape[1:]
    here = mixes[0].shape[1]
    share = model // count
    chunk = pl.program_id(0)
    owners, _, down_lanes = down_s.shape
    down_rows = model // parts
    up_rows, down_height, out_groups, _ = rest_layout(model, pl.num_programs(0) * model, parts, count)

    @pl.when(chunk == 0)
    def _():
        for m in range(micro):
            hidden_t[m] = hidden_ref[m].astype(F32).T.astype(BF)
            cot_t[m] = cot_ref[m].astype(F32).T.astype(BF)
            for k in range(parts):
                place = pl.ds(pl.multiple_of((me_s[0] ^ k) * here, here), here)
                mixed_t[m, place, :] = mixes[m * parts + k][...].astype(F32).T.astype(BF)
        found = sum(dot(mixed_t[m], branch_ref[m]) for m in range(micro)).astype(BF)
        for d in range(parts):
            out_s[d] = found[:, d * down_rows : (d + 1) * down_rows]
        tall = share // out_groups
        for j in range(count):
            base = (me_f[0] ^ j) * share
            for k in range(parts):
                for g in range(out_groups):
                    place = pl.ds(pl.multiple_of(base + g * tall, tall), tall)
                    top = up_rows + down_height
                    targets[j % 2][
                        k, j // 2, top : top + tall, g * down_rows : (g + 1) * down_rows
                    ] = out_s[me_s[0] ^ k, place, :]

    found = sum(dot(hidden_t[m], pre_ref[m]) for m in range(micro)).astype(BF)
    for q in range(model // PACK):
        up_s[q] = found[:, q * PACK : (q + 1) * PACK]
    for j in range(count):
        place = pl.ds(pl.multiple_of((me_f[0] ^ j) * share, share), share)
        for q in range(model // PACK):
            block = chunk * (model // PACK) + q
            groups = up_rows // share
            dest = me_s[0] ^ (block // groups)
            top = (q % groups) * share
            targets[j % 2][dest, j // 2, top : top + share, :] = up_s[q, place, :]

    found = sum(dot(cot_t[m], act_ref[m]) for m in range(micro)).astype(BF)
    for o in range(owners):
        down_s[o] = found[:, o * down_lanes : (o + 1) * down_lanes]
    groups = PACK // down_lanes
    tall = down_rows // groups
    for low in range(owners):
        owner = low ^ (me_f[0] % owners)
        slot = ((chunk ^ (me_f[0] // owners)) * owners + low) // 2
        for k in range(parts):
            for g in range(groups):
                place = pl.ds(pl.multiple_of((me_s[0] ^ k) * down_rows + g * tall, tall), tall)
                targets[low % 2][
                    k, slot, up_rows : up_rows + tall, g * down_lanes : (g + 1) * down_lanes
                ] = down_s[owner, place, :]

    ones = jnp.ones((8, rows), BF)
    bias_ref[...] = sum(dot(ones, pre_ref[m]) for m in range(micro))


def rest_layout(model, hidden, parts, count):
    share = model // count
    up_rows = share * (hidden // parts) // PACK
    down_rows = (model // parts) * (hidden // count) // PACK
    groups = PACK // (model // parts)
    if share % (16 * groups):
        groups = 1
    return up_rows, down_rows, groups, up_rows + down_rows + share // groups


def rest_grads(acts, pres, hiddens, branches, cot, mixes, me_s, me_f, count):
    micro, rows, model = cot.shape
    parts = len(mixes[0])
    hidden = acts.shape[2]
    height = rest_layout(model, hidden, parts, count)[3]
    half = (parts, count // 2, height, PACK)
    flat = [item for group in mixes for item in group]
    lanes = hidden // count
    whole = lambda shape: pl.BlockSpec(shape, lambda t: (0,) * len(shape))
    chunk = pl.BlockSpec((micro, rows, model), lambda t: (0, 0, t))
    return pl.pallas_call(
        partial(rest_grads_kernel, micro, parts, count),
        name="rest_grads",
        grid=(hidden // model,),
        out_shape=(
            jax.ShapeDtypeStruct(half, BF),
            jax.ShapeDtypeStruct(half, BF),
            jax.ShapeDtypeStruct((8, hidden), F32),
        ),
        in_specs=[SM, SM, chunk, chunk]
        + [whole(cot.shape)] * 3
        + [whole(flat[0].shape)] * len(flat),
        out_specs=(whole(half), whole(half), pl.BlockSpec((8, model), lambda t: (0, t))),
        scratch_shapes=[pltpu.VMEM((micro, model, rows), BF)] * 3
        + [
            pltpu.VMEM((model // PACK, model, PACK), BF),
            pltpu.VMEM((model // lanes, model, lanes), BF),
            pltpu.VMEM((parts, model, model // parts), BF),
        ],
        compiler_params=params(36 * 1024 * 1024),
        cost_estimate=cost(12),
    )(me_s, me_f, acts, pres, hiddens, branches, cot, *flat)


def finish_rest_kernel(parts, me_ref, *refs):
    pieces = refs[:parts]
    out_ref, up_ref, down_ref, out_s, down_s = refs[parts:]
    share, hidden = up_ref.shape
    down_lanes, model = down_ref.shape
    up_rows, down_height, out_groups, _ = rest_layout(model, hidden, parts, model // share)
    down_rows = model // parts
    cols = hidden // parts
    for k in range(parts):
        dest = me_ref[0] ^ k
        for g in range(cols // PACK):
            place = pl.ds(pl.multiple_of(dest * cols + g * PACK, PACK), PACK)
            up_ref[:, place] = pieces[k][g * share : (g + 1) * share, :].astype(F32)
        groups = PACK // down_lanes
        tall = down_rows // groups
        for g in range(groups):
            place = pl.ds(pl.multiple_of(dest * down_rows + g * tall, tall), tall)
            down_s[place, :] = pieces[k][
                up_rows : up_rows + tall, g * down_lanes : (g + 1) * down_lanes
            ].astype(F32)
        tall = share // out_groups
        top = up_rows + down_height
        for g in range(out_groups):
            out_s[dest, g * tall : (g + 1) * tall, :] = pieces[k][
                top : top + tall, g * down_rows : (g + 1) * down_rows
            ].astype(F32)
    down_ref[...] = down_s[...].T
    for d in range(parts):
        out_ref[:, d * down_rows : (d + 1) * down_rows] = out_s[d]


def finish_rest(pieces, me, model, hidden, count):
    parts = len(pieces)
    share, lanes = model // count, hidden // count
    return pl.pallas_call(
        partial(finish_rest_kernel, parts),
        name="finish_rest",
        out_shape=(
            jax.ShapeDtypeStruct((share, model), F32),
            jax.ShapeDtypeStruct((share, hidden), F32),
            jax.ShapeDtypeStruct((lanes, model), F32),
        ),
        in_specs=[SM] + [VM] * parts,
        out_specs=(VM, VM, VM),
        scratch_shapes=[
            pltpu.VMEM((parts, share, model // parts), F32),
            pltpu.VMEM((model, lanes), F32),
        ],
        compiler_params=params(),
        cost_estimate=cost(1),
    )(me, *pieces)


def finish_qkv_kernel(parts, me_ref, *refs):
    pieces = refs[:parts]
    out_ref, piece_s = refs[parts:]
    here = pieces[0].shape[1] // 3
    model = here * parts
    for k in range(parts):
        piece_s[me_ref[0] ^ k] = pieces[k][...].astype(F32)
    for d in range(parts):
        for t in range(3):
            lane = t * model + d * here
            out_ref[:, lane : lane + here] = piece_s[d, :, t * here : (t + 1) * here]


def finish_qkv(pieces, me):
    parts = len(pieces)
    share, width = pieces[0].shape
    return pl.pallas_call(
        partial(finish_qkv_kernel, parts),
        name="finish_qkv",
        out_shape=jax.ShapeDtypeStruct((share, parts * width), F32),
        in_specs=[SM] + [VM] * parts,
        out_specs=VM,
        scratch_shapes=[pltpu.VMEM((parts, share, width), F32)],
        compiler_params=params(),
        cost_estimate=cost(1),
    )(me, *pieces)


def input_kernel(parts, has_old, me_ref, tokens_ref, embed_ref, middle_ref, wq_ref, vec_ref, *refs):
    pieces = refs[:parts]
    out_ref, sums_ref = refs[parts + has_old :]
    grad_hidden = dot_t(pieces[0][...], wq_ref[me_ref[0]])
    for k in range(1, parts):
        grad_hidden = grad_hidden + dot_t(pieces[k][...], wq_ref[me_ref[0] ^ k])
    rows = tokens_ref[0].astype(F32) + embed_ref[0].astype(F32)
    scaled, inverse = norm_parts(rows)
    sums_ref[0:1] = jnp.sum(grad_hidden * scaled, axis=0, keepdims=True)
    sums_ref[1:2] = jnp.sum(grad_hidden, axis=0, keepdims=True)
    sums_ref[2:8] = jnp.zeros((6, sums_ref.shape[1]), F32)
    out_ref[0] = middle_ref[...] + norm_back(grad_hidden, scaled, inverse, vec_ref[0:1])


def input_gradient(tokens, embed, micro_index, grad_middle, pieces, wq, vec, old, me):
    micro, rows, model = tokens.shape
    parts = len(pieces)
    width = pieces[0].shape[1]
    row_spec = pl.BlockSpec((1, rows, model), lambda i: (micro_index, 0, 0))
    whole = lambda shape: pl.BlockSpec(shape, lambda i: (0,) * len(shape))
    old_args = [] if old is None else [old]
    return pl.pallas_call(
        partial(input_kernel, parts, len(old_args)),
        name="input_gradient",
        grid=(1,),
        out_shape=(
            jax.ShapeDtypeStruct((micro, rows, model), F32),
            jax.ShapeDtypeStruct((8, model), F32),
        ),
        in_specs=[SM, row_spec, row_spec, whole((rows, model)), whole(wq.shape), whole(vec.shape)]
        + [whole((rows, width))] * parts
        + [pl.BlockSpec(memory_space=pl.ANY)] * len(old_args),
        out_specs=(row_spec, whole((8, model))),
        input_output_aliases={6 + parts: 0} if old_args else {},
        compiler_params=params(),
        cost_estimate=cost(2.5),
    )(me, tokens, embed, grad_middle, wq, vec, *pieces, *old_args)


def qkv_first_kernel(micro, parts, count, me_f, *refs):
    hiddens = refs[:micro]
    pieces = refs[micro : micro + micro * parts]
    out_ref, hidden_t = refs[micro + micro * parts :]
    share = hiddens[0].shape[1] // count
    for m in range(micro):
        hidden_t[m] = hiddens[m][...].astype(F32).T.astype(BF)

    def one(j, _):
        place = pl.ds(pl.multiple_of((me_f[0] ^ j) * share, share), share)
        for k in range(parts):
            out_ref[k, j] = sum(
                dot(hidden_t[m, place, :], pieces[m * parts + k][...]) for m in range(micro)
            )
        return 0

    lax.fori_loop(0, count, one, 0)


def qkv_last_kernel(parts, count, me_f, first_ref, hidden_ref, *refs):
    pieces, (keep_ref, send_ref, hidden_t) = refs[:parts], refs[parts:]
    share = hidden_ref.shape[1] // count
    hidden_t[...] = hidden_ref[...].astype(F32).T.astype(BF)

    def one_pair(s, _):
        for j, target in ((2 * s, keep_ref), (2 * s + 1, send_ref)):
            place = pl.ds(pl.multiple_of((me_f[0] ^ j) * share, share), share)
            for k in range(parts):
                found = first_ref[k, j] + dot(hidden_t[place, :], pieces[k][...])
                target[k, s] = found.astype(BF)
        return 0

    lax.fori_loop(0, count // 2, one_pair, 0)


def qkv_first(hiddens, pieces, me_f, count):
    micro = len(hiddens)
    rows, model = hiddens[0].shape
    parts = len(pieces[0])
    width = pieces[0][0].shape[1]
    flat = [item for group in pieces for item in group]
    return pl.pallas_call(
        partial(qkv_first_kernel, micro, parts, count),
        name="qkv_first",
        out_shape=jax.ShapeDtypeStruct((parts, count, model // count, width), F32),
        in_specs=[SM] + [VM] * (micro + micro * parts),
        out_specs=VM,
        scratch_shapes=[pltpu.VMEM((micro, model, rows), BF)],
        compiler_params=params(),
        cost_estimate=cost(5),
    )(me_f, *hiddens, *flat)


def qkv_last(first, hidden, pieces, me_f, count):
    rows, model = hidden.shape
    parts = len(pieces)
    width = pieces[0].shape[1]
    half = jax.ShapeDtypeStruct((parts, count // 2, model // count, width), BF)
    return pl.pallas_call(
        partial(qkv_last_kernel, parts, count),
        name="qkv_last",
        out_shape=(half, half),
        in_specs=[SM] + [VM] * (2 + parts),
        out_specs=(VM, VM),
        scratch_shapes=[pltpu.VMEM((model, rows), BF)],
        compiler_params=params(),
        cost_estimate=cost(4),
    )(me_f, first, hidden, *pieces)


def total(items, dtype):
    found = items[0].astype(F32)
    for item in items[1:]:
        found = found + item.astype(F32)
    return found.astype(dtype)


def small_call(kernel, outs, *args):
    return pl.pallas_call(
        kernel,
        out_shape=outs,
        in_specs=[VM] * len(args),
        out_specs=jax.tree.map(lambda _: VM, outs),
        compiler_params=params(),
        cost_estimate=cost(0.5),
    )(*args)


def add_parts(keep, found):
    def kernel(keep_ref, found_ref, *outs):
        for k, out in enumerate(outs):
            out[...] = total([keep_ref[k], found_ref[k]], out.dtype)

    out = jax.ShapeDtypeStruct(keep.shape[1:], keep.dtype)
    return small_call(kernel, [out] * keep.shape[0], keep, found)


def add_halves(*items):
    def kernel(*refs):
        keep_ref, send_ref = refs[-2:]
        for s in range(keep_ref.shape[0]):
            keep_ref[s] = total([item[2 * s] for item in refs[:-2]], keep_ref.dtype)
            send_ref[s] = total([item[2 * s + 1] for item in refs[:-2]], keep_ref.dtype)

    half = (items[0].shape[0] // 2,) + items[0].shape[1:]
    out = jax.ShapeDtypeStruct(half, items[0].dtype)
    return small_call(kernel, [out, out], *items)


def add_all(*items):
    def kernel(*refs):
        refs[-1][...] = total([item[...] for item in refs[:-1]], refs[-1].dtype)

    return small_call(kernel, jax.ShapeDtypeStruct(items[0].shape, items[0].dtype), *items)


def add_split(keep, found):
    def kernel(keep_ref, found_ref, *outs):
        for k in range(keep_ref.shape[0]):
            for s in range(keep_ref.shape[1]):
                out = outs[s % 2]
                out[k, s // 2] = total([keep_ref[k, s], found_ref[k, s]], out.dtype)

    parts, slots = keep.shape[:2]
    out = jax.ShapeDtypeStruct((parts, slots // 2) + keep.shape[2:], keep.dtype)
    return small_call(kernel, [out, out], keep, found)


def reduce_early(keep, send):
    size = lax.axis_size("fsdp")
    found = swap(send, "fsdp", 1)
    bit = 2
    while bit < size:
        keep, send = add_split(keep, found)
        yield keep, send
        found = swap(send, "fsdp", bit)
        bit *= 2
    shape = keep.shape[:1] + keep.shape[2:]
    pieces = add_parts(keep.reshape(shape), found.reshape(shape))
    yield pieces
    final = add_all(*exchange(pieces, "seq"))
    yield final
    yield gather_pieces(final, "seq")


def reduce_last(keep, found, vectors):
    size = lax.axis_size("fsdp")
    pieces = add_parts(keep, found)
    other = swap(vectors, "fsdp", 1)
    pieces, other = lax.optimization_barrier((exchange(pieces, "seq"), other))
    keep, send = add_halves(*pieces)
    vectors = add_all(vectors, other)
    others = exchange([vectors] * lax.axis_size("seq"), "seq")
    bit = 2
    while bit < size:
        found, others = lax.optimization_barrier((swap(send, "fsdp", bit), others))
        vectors = add_all(*others)
        if bit * 2 < size:
            keep, send = add_halves(keep, found)
        else:
            final = add_all(keep, found)
        others = [vectors, swap(vectors, "fsdp", bit)]
        bit *= 2
    final = gather_pieces(final.reshape(final.shape[1:]), "seq")
    final, others = lax.optimization_barrier((final, others))
    return final, add_all(*others)


def gather_sums(first, second, bias):
    def kernel(*refs):
        bias_ref, out_ref = refs[-2:]
        model = out_ref.shape[1]
        once, twice = refs[: len(first)], refs[len(first) : -2]
        out_ref[0:2] = total([item[0:2] for item in once], F32)
        out_ref[2:5] = total([item[0:3] for item in twice], F32)
        out_ref[5:8] = jnp.zeros((3, model), F32)
        for t in range(8):
            lanes = bias_ref.shape[1] // 8
            row = 8 + (t * lanes) // model
            lane = (t * lanes) % model
            out_ref[row : row + 1, lane : lane + lanes] = bias_ref[0:1, t * lanes : (t + 1) * lanes]

    model = first[0].shape[1]
    rows = 8 + bias.shape[1] // model
    out = jax.ShapeDtypeStruct((rows, model), F32)
    return small_call(kernel, out, *first, *second, bias)


def layer(
    tokens,
    time_embed,
    doc_ids,
    out_grad,
    norm1_gain,
    norm1_shift,
    qkv_weight,
    out_weight,
    norm2_gain,
    norm2_shift,
    up_weight,
    up_bias,
    down_weight,
    down_bias,
):
    micro, _, _, model = tokens.shape
    parts = lax.axis_size("seq")
    count = lax.axis_size("fsdp")
    hidden = up_weight.shape[1]
    ratio = hidden // model
    head_dim = model // HEADS
    heads = HEADS // parts
    share = model // count
    seq_index = lax.axis_index("seq").astype(jnp.int32)
    fsdp_index = lax.axis_index("fsdp").astype(jnp.int32)
    me_s = seq_index.reshape(1)
    me_f = fsdp_index.reshape(1)
    tokens = tokens[:, 0]
    embed = time_embed[:, 0]
    cot = out_grad[:, 0]

    pieces = gather_pairs(qkv_weight, "fsdp")
    near = pieces[2]
    small = [norm1_gain, norm1_shift, norm2_gain, norm2_shift, down_bias]
    small = [item.reshape(1, share) for item in small] + [up_bias.reshape(ratio, share)]
    small = gather_pairs(after(jnp.concatenate(small), near), "fsdp")
    docs = gather_pieces(after(doc_ids, near), "seq")
    doc, low, high = assemble_docs(docs, me_s)
    small = after(small, doc)
    wq, vec, bias = assemble_qkv(pieces, small, me_f, model, parts, hidden)
    rest = jnp.concatenate(
        [out_weight]
        + [up_weight[:, t * model : (t + 1) * model] for t in range(ratio)]
        + [down_weight],
        axis=0,
    )
    rest = gather_pairs(after(rest, (pieces[2], pieces[4], pieces[6])), "fsdp")

    hiddens, triples, mixes, logs = [], [], [], []
    for m in range(micro):
        found = project(tokens, embed, m, wq, vec, me_s)
        hiddens.append(found[0])
        outs = after(found[1:], triples[-1]) if m else found[1:]
        triples.append(exchange(outs, "seq"))
    sent = []
    for m in range(micro):
        triple = after(triples[m], logs[-1]) if m else triples[m]
        outs, log_total = attend(triple, me_s, low, high, doc, m, heads, head_dim)
        sent.append(outs)
        logs.append(log_total)
        mixes.append(exchange(outs, "seq"))
    w_out, w_up, w_down = assemble_rest(rest, me_f, model, hidden)
    stacked = None
    middles, sums, heads_grads = [], [], []
    for m in range(micro):
        mixed = mixes[m] if m else after(mixes[m], logs[-1])
        found, grads = feed(
            tokens, embed, cot, m, mixed, vec, bias, w_out, w_up, w_down, stacked, me_s
        )
        stacked = found[:5]
        middles.append(found[5])
        sums.append(found[6])
        heads_grads.append(exchange(grads, "seq"))
    layer_output, acts, pres, seconds, branches = stacked
    keep, send, bias_sum = rest_grads(acts, pres, seconds, branches, cot, mixes, me_s, me_f, count)
    hops = reduce_early(keep, send)
    backs = []
    for m in range(micro):
        grads = after(heads_grads[m], (next(hops), outs) if m else bias_sum)
        outs = attend_back(
            triples[m],
            sent[m],
            grads,
            me_s,
            low,
            high,
            doc,
            m,
            logs[m],
            heads,
            head_dim,
        )
        backs.append(exchange(outs, "seq"))
    input_grad = None
    first_sums = []
    for m in range(micro - 1):
        pieces = after(backs[m], outs) if m == 0 else backs[m]
        input_grad, sum_one = input_gradient(
            tokens, embed, m, middles[m], pieces, wq, vec, input_grad, me_s
        )
        first_sums.append(sum_one)
    first = qkv_first(hiddens[:-1], after(backs[:-1], input_grad), me_f, count)
    last = after(backs[-1], (first, next(hops)))
    keep, send = qkv_last(first, hiddens[-1], last, me_f, count)
    found = swap(send, "fsdp", 1)
    last = after(last, send)
    input_grad, sum_one = input_gradient(
        tokens, embed, micro - 1, middles[-1], last, wq, vec, input_grad, me_s
    )
    first_sums.append(sum_one)
    *_, pieces = hops
    grad_out, grad_up, grad_down = finish_rest(pieces, me_s, model, hidden, count)
    vectors = gather_sums(first_sums, sums, bias_sum)
    pieces, vectors = reduce_last(keep, found, vectors)
    grad_qkv = finish_qkv(pieces, me_s)

    pick = lambda row: lax.dynamic_slice(vectors[row], (fsdp_index * share,), (share,))
    grad_up_bias = lax.dynamic_slice(
        vectors[8 : 8 + ratio].reshape(hidden), (fsdp_index * (hidden // count),), (hidden // count,)
    )
    return (
        layer_output[:, None],
        input_grad[:, None],
        pick(0),
        pick(1),
        grad_qkv,
        grad_out,
        pick(2),
        pick(3),
        grad_up,
        grad_up_bias,
        grad_down,
        pick(4),
    )


def solution(mesh):
    rows = P(None, "fsdp", "seq", None)
    vector = P("fsdp")
    matrix = P("fsdp", None)
    return jax.shard_map(
        layer,
        mesh=mesh,
        in_specs=(
            rows,
            rows,
            P(None, "fsdp", "seq"),
            rows,
            vector,
            vector,
            matrix,
            matrix,
            vector,
            vector,
            matrix,
            vector,
            matrix,
            vector,
        ),
        out_specs=(
            rows,
            rows,
            vector,
            vector,
            matrix,
            matrix,
            vector,
            vector,
            matrix,
            vector,
            matrix,
            vector,
        ),
        check_vma=False,
    )
```

```python
from functools import partial

import jax
import jax.numpy as jnp
from jax import lax
from jax.experimental import pallas as pl
from jax.experimental.pallas import tpu as pltpu
from jax.sharding import PartitionSpec as P


HEADS = 8
EPS = 1e-05
LOG2E = 1.4426950408889634
WIDE = 512
NARROW = 384
PACK = 256
VMEM_LIMIT = 16 * 1024 * 1024
BF = jnp.bfloat16
F32 = jnp.float32


def dot(a, b, dims=((1,), (0,))):
    return lax.dot_general(a, b, (dims, ((), ())), preferred_element_type=F32)


def dot_t(a, b):
    return dot(a, b, ((1,), (1,)))


def params(limit=VMEM_LIMIT):
    return pltpu.CompilerParams(vmem_limit_bytes=limit)


def cost(micros):
    return pl.CostEstimate(flops=int(micros * 1e8), bytes_accessed=1000, transcendentals=0)


VM = pl.BlockSpec(memory_space=pltpu.VMEM)
SM = pl.BlockSpec(memory_space=pltpu.SMEM)


def after(value, token):
    return lax.optimization_barrier((value, token))[0]


def swap(value, axis, bit):
    size = lax.axis_size(axis)
    return lax.ppermute(value, axis, [(i, i ^ bit) for i in range(size)])


def exchange(pieces, axis):
    return [pieces[0]] + [swap(pieces[k], axis, k) for k in range(1, len(pieces))]


def gather_pieces(value, axis):
    return exchange([value] * lax.axis_size(axis), axis)


def gather_pairs(value, axis):
    size = lax.axis_size(axis)
    far = [swap(value, axis, j) if j else value for j in range(0, size, 2)]
    result = []
    for mine in far:
        result += [mine, swap(mine, axis, 1)]
    return result


def assemble_qkv_kernel(count, seq_parts, part_width, me_ref, *refs):
    pieces, small = refs[:count], refs[count : 2 * count]
    wq_ref, vec_ref, bias_ref, small_s = refs[2 * count :]
    rows = pieces[0].shape[0]
    model = wq_ref.shape[1]
    ratio = small[0].shape[0] - 5
    for j in range(count):
        owner = me_ref[0] ^ j
        start = pl.multiple_of(owner * rows, rows)
        for d in range(seq_parts):
            for t in range(3):
                lane = t * model + d * part_width
                wq_ref[d, pl.ds(start, rows), t * part_width : (t + 1) * part_width] = pieces[j][
                    :, lane : lane + part_width
                ]
        small_s[owner] = small[j][...].astype(F32)
    vec_ref[5:8] = jnp.zeros((3, model), F32)
    for o in range(count):
        item = small_s[o]
        vec_ref[0:5, o * rows : (o + 1) * rows] = item[0:5]
        for t in range(ratio):
            lane = (o * ratio + t) * rows
            bias_ref[lane // CHUNK, :, lane % CHUNK : lane % CHUNK + rows] = item[5 + t : 6 + t]


def assemble_qkv(pieces, small, me, model, seq_parts, hidden):
    part_width = model // seq_parts
    count = len(pieces)
    return pl.pallas_call(
        partial(assemble_qkv_kernel, count, seq_parts, part_width),
        name="assemble_qkv",
        out_shape=(
            jax.ShapeDtypeStruct((seq_parts, model, 3 * part_width), BF),
            jax.ShapeDtypeStruct((8, model), F32),
            jax.ShapeDtypeStruct((hidden // CHUNK, 1, CHUNK), F32),
        ),
        in_specs=[SM] + [VM] * (2 * count),
        out_specs=(VM, VM, VM),
        scratch_shapes=[
            pltpu.VMEM((count,) + small[0].shape, F32),
        ],
        compiler_params=params(),
        cost_estimate=cost(2),
    )(me, *pieces, *small)


def pack_rest_kernel(out_ref, up_ref, down_ref, all_ref):
    rows, model = out_ref.shape
    ratio = up_ref.shape[1] // model
    all_ref[0:rows] = out_ref[...]
    for t in range(ratio):
        all_ref[(1 + t) * rows : (2 + t) * rows] = up_ref[:, t * model : (t + 1) * model]
    all_ref[(1 + ratio) * rows :] = down_ref[...]


def pack_rest(out_weight, up_weight, down_weight):
    rows, model = out_weight.shape
    height = rows + 2 * down_weight.shape[0]
    return pl.pallas_call(
        pack_rest_kernel,
        name="pack_rest",
        out_shape=jax.ShapeDtypeStruct((height, model), BF),
        in_specs=[VM] * 3,
        out_specs=VM,
        compiler_params=params(),
        cost_estimate=cost(1),
    )(out_weight, up_weight, down_weight)


def assemble_rest_kernel(count, me_ref, *refs):
    pieces, (out_ref, up_ref, down_ref) = refs[:count], refs[count:]
    model = out_ref.shape[0]
    rows = model // count
    ratio = up_ref.shape[1] // model
    down_rows = ratio * rows
    for j in range(count):
        owner = me_ref[0] ^ j
        place = pl.ds(pl.multiple_of(owner * rows, rows), rows)
        out_ref[place, :] = pieces[j][0:rows, :]
        for t in range(ratio):
            up_ref[place, t * model : (t + 1) * model] = pieces[j][
                (1 + t) * rows : (2 + t) * rows, :
            ]
        place = pl.ds(pl.multiple_of(owner * down_rows, down_rows), down_rows)
        down_ref[place, :] = pieces[j][(1 + ratio) * rows :, :]


def assemble_rest(pieces, me, model, hidden):
    count = len(pieces)
    return pl.pallas_call(
        partial(assemble_rest_kernel, count),
        name="assemble_rest",
        out_shape=(
            jax.ShapeDtypeStruct((model, model), BF),
            jax.ShapeDtypeStruct((model, hidden), BF),
            jax.ShapeDtypeStruct((hidden, model), BF),
        ),
        in_specs=[SM] + [VM] * count,
        out_specs=(VM, VM, VM),
        compiler_params=params(),
        cost_estimate=cost(2),
    )(me, *pieces)


def norm_parts(rows):
    mean_row = jnp.mean(rows, axis=-1, keepdims=True)
    centred = rows - mean_row
    inverse = lax.rsqrt(jnp.mean(centred * centred, axis=-1, keepdims=True) + EPS)
    return centred * inverse, inverse


def norm_back(grad_normed, scaled, inverse, gain):
    grad_scaled = grad_normed * gain
    centre = jnp.mean(grad_scaled, axis=-1, keepdims=True)
    along = jnp.mean(grad_scaled * scaled, axis=-1, keepdims=True)
    return inverse * (grad_scaled - centre - scaled * along)


def project_kernel(parts, me_ref, tokens_ref, embed_ref, wq_ref, vec_ref, hidden_ref, *outs):
    rows = tokens_ref[0].astype(F32) + embed_ref[0].astype(F32)
    scaled, _ = norm_parts(rows)
    hidden = (scaled * vec_ref[0:1] + vec_ref[1:2]).astype(BF)
    hidden_ref[...] = hidden
    for k in range(parts):
        outs[k][...] = dot(hidden, wq_ref[me_ref[0] ^ k]).astype(BF)


def project(tokens, embed, micro_index, wq, vec, me):
    _, rows, model = tokens.shape
    parts, _, width = wq.shape
    row_spec = pl.BlockSpec((1, rows, model), lambda i: (micro_index, 0, 0))
    whole = lambda shape: pl.BlockSpec(shape, lambda i: (0,) * len(shape))
    return pl.pallas_call(
        partial(project_kernel, parts),
        name="project",
        grid=(1,),
        out_shape=[jax.ShapeDtypeStruct((rows, model), BF)]
        + [jax.ShapeDtypeStruct((rows, width), BF)] * parts,
        in_specs=[SM, row_spec, row_spec, whole(wq.shape), whole(vec.shape)],
        out_specs=[whole((rows, model))] + [whole((rows, width))] * parts,
        compiler_params=params(),
        cost_estimate=cost(2),
    )(me, tokens, embed, wq, vec)


def docs_kernel(parts, me_ref, *refs):
    pieces, (doc_ref, low_ref, high_ref) = refs[:parts], refs[parts:]
    micro, _, rows = pieces[0].shape
    for k in range(parts):
        place = pl.ds(pl.multiple_of((me_ref[0] ^ k) * rows, rows), rows)
        doc_ref[:, :, place] = pieces[k][...].astype(F32)
    for m in range(micro):
        doc = doc_ref[m]
        for i in range(doc.shape[1] // WIDE):
            first = doc[:, i * WIDE : i * WIDE + 1]
            last = doc[:, (i + 1) * WIDE - 1 : (i + 1) * WIDE]
            low = jnp.sum(jnp.where(doc < first, 1.0, 0.0)).astype(jnp.int32)
            high = jnp.sum(jnp.where(doc <= last, 1.0, 0.0)).astype(jnp.int32)
            low_ref[m, i] = low // NARROW
            high_ref[m, i] = (high + NARROW - 1) // NARROW


def assemble_docs(pieces, me):
    parts = len(pieces)
    micro, _, rows = pieces[0].shape
    length = rows * parts
    bounds = jax.ShapeDtypeStruct((micro, length // WIDE), jnp.int32)
    return pl.pallas_call(
        partial(docs_kernel, parts),
        name="assemble_docs",
        out_shape=(jax.ShapeDtypeStruct((micro, 1, length), F32), bounds, bounds),
        in_specs=[SM] + [VM] * parts,
        out_specs=(VM, SM, SM),
        compiler_params=params(),
        cost_estimate=cost(2),
    )(me, *pieces)


def head_mask(value, head, heads, head_dim):
    if heads == 1:
        return value
    lane = lax.broadcasted_iota(jnp.int32, value.shape, 1)
    keep = (lane >= head * head_dim) & (lane < (head + 1) * head_dim)
    return jnp.where(keep, value, jnp.zeros_like(value))


def spread_docs(doc_ref, doc_s):
    for start in range(0, doc_s.shape[0], 512):
        doc_s[start : start + 512, :] = jnp.broadcast_to(
            doc_ref[0:1, start : start + 512], (128, 512)
        ).T


def same_doc(doc_s, place, doc_row):
    column = doc_s[place, :]
    return jnp.concatenate([column] * (doc_row.shape[1] // 128), axis=1) == doc_row


def fold(value, combine):
    out = value[0:8]
    for start in range(8, value.shape[0], 8):
        out = combine(out, value[start : start + 8])
    return out


def place_rows(pieces, me, rows_s):
    rows = pieces[0].shape[0]
    for k, piece in enumerate(pieces):
        rows_s[pl.ds(pl.multiple_of((me ^ k) * rows, rows), rows), :] = piece[...]


def attend_kernel(parts, heads, head_dim, m, me_ref, low_ref, high_ref, docs_ref, *refs):
    doc_ref = docs_ref.at[m]
    pieces = refs[:parts]
    outs = refs[parts : 2 * parts]
    log_ref = refs[2 * parts]
    triple_s, value_t, doc_s, score_s, out_s = refs[2 * parts + 1 :]
    rows, width = pieces[0].shape
    here = width // 3
    length = rows * parts
    spread_docs(doc_ref, doc_s)
    place_rows(pieces, me_ref[0], triple_s)
    for start in range(0, length, WIDE):
        value_t[:, start : start + WIDE] = (
            triple_s[start : start + WIDE, 2 * here :].astype(F32).T.astype(BF)
        )
    scale = head_dim ** (-0.5) * LOG2E

    def one_block(i, _):
        place = pl.ds(pl.multiple_of(i * WIDE, WIDE), WIDE)
        query = triple_s[place, 0:here]
        queries = [head_mask(query, h, heads, head_dim) for h in range(heads)]
        doc_row = doc_ref[0:1, place]

        def score(j, tops):
            key_place = pl.ds(pl.multiple_of(j * NARROW, NARROW), NARROW)
            keys = triple_s[key_place, here : 2 * here]
            same = same_doc(doc_s, key_place, doc_row)
            result = []
            for h in range(heads):
                scores = jnp.where(same, dot_t(keys, queries[h]) * scale, -jnp.inf)
                score_s[h, key_place, :] = scores
                result.append(jnp.maximum(tops[h], fold(scores, jnp.maximum)))
            return tuple(result)

        tops = lax.fori_loop(
            low_ref[m, i],
            high_ref[m, i],
            score,
            tuple(jnp.full((8, WIDE), -jnp.inf, F32) for _ in range(heads)),
        )
        tops = [jnp.max(top, axis=0, keepdims=True) for top in tops]

        def mix(j, carry):
            key_place = pl.ds(pl.multiple_of(j * NARROW, NARROW), NARROW)
            result = []
            for h in range(heads):
                total, acc = carry[h]
                weight = jnp.exp2(score_s[h, key_place, :] - tops[h])
                total = total + fold(weight, jnp.add)
                values = value_t[h * head_dim : (h + 1) * head_dim, key_place]
                result.append((total, acc + dot(values, weight.astype(BF))))
            return tuple(result)

        done = lax.fori_loop(
            low_ref[m, i],
            high_ref[m, i],
            mix,
            tuple(
                (jnp.zeros((8, WIDE), F32), jnp.zeros((head_dim, WIDE), F32))
                for _ in range(heads)
            ),
        )
        mixed = []
        for h in range(heads):
            total = jnp.sum(done[h][0], axis=0, keepdims=True)
            mixed.append(done[h][1] / total)
            log_ref[h, :, place] = jnp.broadcast_to(tops[h] + jnp.log2(total), (8, WIDE))
        mixed = jnp.concatenate(mixed, axis=0) if heads > 1 else mixed[0]
        out_s[place, :] = mixed.T.astype(BF)
        return 0

    lax.fori_loop(0, length // WIDE, one_block, 0)
    for k in range(parts):
        place = pl.ds(pl.multiple_of((me_ref[0] ^ k) * rows, rows), rows)
        outs[k][...] = out_s[place, :]


def attend(pieces, me, low, high, doc, m, heads, head_dim):
    parts = len(pieces)
    rows, width = pieces[0].shape
    here = width // 3
    length = rows * parts
    found = pl.pallas_call(
        partial(attend_kernel, parts, heads, head_dim, m),
        name="attend",
        out_shape=[jax.ShapeDtypeStruct((rows, here), BF)] * parts
        + [jax.ShapeDtypeStruct((heads, 8, length), F32)],
        in_specs=[SM, SM, SM, VM] + [VM] * parts,
        out_specs=[VM] * (parts + 1),
        scratch_shapes=[
            pltpu.VMEM((length, width), BF),
            pltpu.VMEM((here, length), BF),
            pltpu.VMEM((length, 128), F32),
            pltpu.VMEM((heads, length, WIDE), F32),
            pltpu.VMEM((length, here), BF),
        ],
        compiler_params=params(),
        cost_estimate=cost(8),
    )(me, low, high, doc, *pieces)
    return found[:parts], found[parts]


def attend_back_kernel(
    parts, heads, head_dim, m, me_ref, low_ref, high_ref, docs_ref, log_ref, *refs
):
    doc_ref = docs_ref.at[m]
    pieces = refs[:parts]
    mixes = refs[parts : 2 * parts]
    grads = refs[2 * parts : 3 * parts]
    outs = refs[3 * parts : 4 * parts]
    (
        triple_s,
        grad_all,
        mix_all,
        query_s,
        key_t,
        grad_s,
        centre_s,
        doc_s,
        query_t,
        pair_s,
    ) = refs[4 * parts :]
    rows, width = pieces[0].shape
    here = width // 3
    length = rows * parts
    me = me_ref[0]
    spread_docs(doc_ref, doc_s)
    place_rows(pieces, me, triple_s)
    place_rows(grads, me, grad_all)
    place_rows(mixes, me, mix_all)
    for start in range(0, length, WIDE):
        place = pl.ds(start, WIDE)
        query = triple_s[place, 0:here]
        grad = grad_all[place, :]
        for h in range(heads):
            query_s[h, place, :] = head_mask(query, h, heads, head_dim)
            grad_s[h, place, :] = head_mask(grad, h, heads, head_dim)
        key_t[:, place] = triple_s[place, here : 2 * here].astype(F32).T.astype(BF)
        both = (grad.astype(F32) * mix_all[place, :].astype(F32)).T
        for h in range(heads):
            centre = jnp.sum(both[h * head_dim : (h + 1) * head_dim], axis=0, keepdims=True)
            centre_s[h, :, place] = jnp.broadcast_to(centre, (8, WIDE))
    query_t[...] = jnp.zeros_like(query_t)
    scale = head_dim ** (-0.5)

    def one_key(j, _):
        key_place = pl.ds(pl.multiple_of(j * WIDE, WIDE), WIDE)
        keys = triple_s[key_place, here : 2 * here]
        values = triple_s[key_place, 2 * here :]
        keys_t = [key_t[h * head_dim : (h + 1) * head_dim, key_place] for h in range(heads)]

        def one_block(i, carry):
            grad_key, grad_value = carry
            place = pl.ds(pl.multiple_of(i * NARROW, NARROW), NARROW)
            same = same_doc(doc_s, key_place, doc_ref[0:1, place])
            for h in range(heads):
                query = query_s[h, place, :]
                grad = grad_s[h, place, :]
                scores = jnp.where(same, dot_t(keys, query) * (scale * LOG2E), -jnp.inf)
                weight = jnp.exp2(scores - log_ref[h, 0:1, place])
                grad_weight = dot_t(values, grad)
                grad_score = (weight * (grad_weight - centre_s[h, 0:1, place])).astype(BF)
                grad_value = grad_value + dot(weight.astype(BF), grad)
                grad_key = grad_key + dot(grad_score, query)
                query_t[h * head_dim : (h + 1) * head_dim, place] += dot(keys_t[h], grad_score)
            return grad_key, grad_value

        zero = jnp.zeros((WIDE, here), F32)
        grad_key, grad_value = lax.fori_loop(
            low_ref[m, j], high_ref[m, j], one_block, (zero, zero)
        )
        pair_s[key_place, 0:here] = (grad_key * scale).astype(BF)
        pair_s[key_place, here:] = grad_value.astype(BF)
        return 0

    lax.fori_loop(0, length // WIDE, one_key, 0)
    for k in range(parts):
        place = pl.ds(pl.multiple_of((me_ref[0] ^ k) * rows, rows), rows)
        outs[k][:, 0:here] = (query_t[:, place].T * scale).astype(BF)
        outs[k][:, here:] = pair_s[place, :]


def attend_back(pieces, mixes, grads, me, low, high, doc, m, log_total, heads, head_dim):
    parts = len(pieces)
    rows, width = pieces[0].shape
    here = width // 3
    length = rows * parts
    return pl.pallas_call(
        partial(attend_back_kernel, parts, heads, head_dim, m),
        name="attend_back",
        out_shape=[jax.ShapeDtypeStruct((rows, width), BF)] * parts,
        in_specs=[SM, SM, SM, VM, VM] + [VM] * (3 * parts),
        out_specs=[VM] * parts,
        scratch_shapes=[
            pltpu.VMEM((length, width), BF),
            pltpu.VMEM((length, here), BF),
            pltpu.VMEM((length, here), BF),
            pltpu.VMEM((heads, length, here), BF),
            pltpu.VMEM((here, length), BF),
            pltpu.VMEM((heads, length, here), BF),
            pltpu.VMEM((heads, 8, length), F32),
            pltpu.VMEM((length, 128), F32),
            pltpu.VMEM((here, length), F32),
            pltpu.VMEM((length, 2 * here), BF),
        ],
        compiler_params=params(),
        cost_estimate=cost(12),
    )(me, low, high, doc, log_total, *pieces, *mixes, *grads)


CHUNK = 512


def feed_kernel(parts, has_old, me_ref, tokens_ref, embed_ref, cot_ref, vec_ref, bias_ref, *refs):
    mixes = refs[:parts]
    w_out, w_up, w_down = refs[parts : parts + 3]
    refs = refs[parts + 3 + has_old :]
    out_ref, act_ref, pre_ref, hidden_ref, branch_ref, middle_ref, sums_ref = refs[:7]
    grads = refs[7 : 7 + parts]
    total_s, back_s = refs[7 + parts :]
    me = me_ref[0]
    here = mixes[0].shape[1]
    middle = tokens_ref[0].astype(F32) + embed_ref[0].astype(F32)
    for k in range(parts):
        place = pl.ds(pl.multiple_of((me ^ k) * here, here), here)
        middle = middle + dot(mixes[k][...], w_out[place, :])
    scaled, inverse = norm_parts(middle)
    hidden_ref[0] = (scaled * vec_ref[2:3] + vec_ref[3:4]).astype(BF)
    middle_ref[...] = middle
    total_s[...] = jnp.zeros_like(total_s)
    back_s[...] = jnp.zeros_like(back_s)
    root = 0.7978845608028654

    def one_chunk(f, _):
        place = pl.ds(pl.multiple_of(f * CHUNK, CHUNK), CHUNK)
        value = dot(hidden_ref[0], w_up[:, place]) + bias_ref[f]
        square = value * value
        bend = jnp.tanh(root * (value + 0.044715 * (value * square)))
        half = 0.5 * (1.0 + bend)
        act = (value * half).astype(BF)
        slope = half + (0.5 * root) * value * (1.0 - bend * bend) * (1.0 + 0.134145 * square)
        act_ref[0, :, place] = act
        total_s[...] += dot(act, w_down[place, :])
        grad_pre = (dot_t(cot_ref[0], w_down[place, :]) * slope).astype(BF)
        pre_ref[0, :, place] = grad_pre
        back_s[...] += dot_t(grad_pre, w_up[:, place])
        return 0

    lax.fori_loop(0, w_up.shape[1] // CHUNK, one_chunk, 0)
    middle = middle_ref[...]
    out_ref[0] = (middle + total_s[...] + vec_ref[4:5]).astype(BF)
    scaled, inverse = norm_parts(middle)
    grad_hidden = back_s[...]
    sums_ref[0:1] = jnp.sum(grad_hidden * scaled, axis=0, keepdims=True)
    sums_ref[1:2] = jnp.sum(grad_hidden, axis=0, keepdims=True)
    cot = cot_ref[0].astype(F32)
    sums_ref[2:3] = jnp.sum(cot, axis=0, keepdims=True)
    sums_ref[3:8] = jnp.zeros((5, sums_ref.shape[1]), F32)
    grad_middle = cot + norm_back(grad_hidden, scaled, inverse, vec_ref[2:3])
    middle_ref[...] = grad_middle
    branch = grad_middle.astype(BF)
    branch_ref[0] = branch
    for k in range(parts):
        place = pl.ds(pl.multiple_of((me ^ k) * here, here), here)
        grads[k][...] = dot_t(branch, w_out[place, :]).astype(BF)


def feed(tokens, embed, cot, micro_index, mixes, vec, bias, w_out, w_up, w_down, old, me):
    micro, rows, model = tokens.shape
    parts = len(mixes)
    here = mixes[0].shape[1]
    hidden = w_up.shape[1]
    row_spec = pl.BlockSpec((1, rows, model), lambda i: (micro_index, 0, 0))
    whole = lambda shape: pl.BlockSpec(shape, lambda i: (0,) * len(shape))
    wide_spec = pl.BlockSpec((1, rows, hidden), lambda i: (micro_index, 0, 0))
    old_args = [] if old is None else list(old)
    found = pl.pallas_call(
        partial(feed_kernel, parts, len(old_args)),
        name="feed",
        grid=(1,),
        out_shape=[
            jax.ShapeDtypeStruct((micro, rows, model), BF),
            jax.ShapeDtypeStruct((micro, rows, hidden), BF),
            jax.ShapeDtypeStruct((micro, rows, hidden), BF),
            jax.ShapeDtypeStruct((micro, rows, model), BF),
            jax.ShapeDtypeStruct((micro, rows, model), BF),
            jax.ShapeDtypeStruct((rows, model), F32),
            jax.ShapeDtypeStruct((8, model), F32),
        ]
        + [jax.ShapeDtypeStruct((rows, here), BF)] * parts,
        in_specs=[SM, row_spec, row_spec, row_spec, whole(vec.shape), whole(bias.shape)]
        + [whole((rows, here))] * parts
        + [whole(w_out.shape), whole(w_up.shape), whole(w_down.shape)]
        + [pl.BlockSpec(memory_space=pl.ANY)] * len(old_args),
        out_specs=[
            row_spec,
            wide_spec,
            wide_spec,
            row_spec,
            row_spec,
            whole((rows, model)),
            whole((8, model)),
        ]
        + [whole((rows, here))] * parts,
        scratch_shapes=[pltpu.VMEM((rows, model), F32)] * 2,
        input_output_aliases={9 + parts + t: t for t in range(len(old_args))},
        compiler_params=params(20 * 1024 * 1024),
        cost_estimate=cost(8),
    )(me, tokens, embed, cot, vec, bias, *mixes, w_out, w_up, w_down, *old_args)
    return found[:7], found[7:]


def rest_grads_kernel(micro, parts, count, me_s, me_f, act_ref, pre_ref, hidden_ref, branch_ref,
                      cot_ref, *refs):
    mixes = refs[: micro * parts]
    keep_ref, send_ref, bias_ref = refs[micro * parts : micro * parts + 3]
    hidden_t, cot_t, mixed_t, up_s, down_s, out_s = refs[micro * parts + 3 :]
    targets = (keep_ref, send_ref)
    rows, model = hidden_ref.shape[1:]
    here = mixes[0].shape[1]
    share = model // count
    chunk = pl.program_id(0)
    owners, _, down_lanes = down_s.shape
    down_rows = model // parts
    up_rows, down_height, out_groups, _ = rest_layout(model, pl.num_programs(0) * model, parts, count)

    @pl.when(chunk == 0)
    def _():
        for m in range(micro):
            hidden_t[m] = hidden_ref[m].astype(F32).T.astype(BF)
            cot_t[m] = cot_ref[m].astype(F32).T.astype(BF)
            for k in range(parts):
                place = pl.ds(pl.multiple_of((me_s[0] ^ k) * here, here), here)
                mixed_t[m, place, :] = mixes[m * parts + k][...].astype(F32).T.astype(BF)
        found = sum(dot(mixed_t[m], branch_ref[m]) for m in range(micro)).astype(BF)
        for d in range(parts):
            out_s[d] = found[:, d * down_rows : (d + 1) * down_rows]
        tall = share // out_groups
        for j in range(count):
            base = (me_f[0] ^ j) * share
            for k in range(parts):
                for g in range(out_groups):
                    place = pl.ds(pl.multiple_of(base + g * tall, tall), tall)
                    top = up_rows + down_height
                    targets[j % 2][
                        k, j // 2, top : top + tall, g * down_rows : (g + 1) * down_rows
                    ] = out_s[me_s[0] ^ k, place, :]

    found = sum(dot(hidden_t[m], pre_ref[m]) for m in range(micro)).astype(BF)
    for q in range(model // PACK):
        up_s[q] = found[:, q * PACK : (q + 1) * PACK]
    for j in range(count):
        place = pl.ds(pl.multiple_of((me_f[0] ^ j) * share, share), share)
        for q in range(model // PACK):
            block = chunk * (model // PACK) + q
            groups = up_rows // share
            dest = me_s[0] ^ (block // groups)
            top = (q % groups) * share
            targets[j % 2][dest, j // 2, top : top + share, :] = up_s[q, place, :]

    found = sum(dot(cot_t[m], act_ref[m]) for m in range(micro)).astype(BF)
    for o in range(owners):
        down_s[o] = found[:, o * down_lanes : (o + 1) * down_lanes]
    groups = PACK // down_lanes
    tall = down_rows // groups
    for low in range(owners):
        owner = low ^ (me_f[0] % owners)
        slot = ((chunk ^ (me_f[0] // owners)) * owners + low) // 2
        for k in range(parts):
            for g in range(groups):
                place = pl.ds(pl.multiple_of((me_s[0] ^ k) * down_rows + g * tall, tall), tall)
                targets[low % 2][
                    k, slot, up_rows : up_rows + tall, g * down_lanes : (g + 1) * down_lanes
                ] = down_s[owner, place, :]

    ones = jnp.ones((8, rows), BF)
    bias_ref[...] = sum(dot(ones, pre_ref[m]) for m in range(micro))


def rest_layout(model, hidden, parts, count):
    share = model // count
    up_rows = share * (hidden // parts) // PACK
    down_rows = (model // parts) * (hidden // count) // PACK
    groups = PACK // (model // parts)
    if share % (16 * groups):
        groups = 1
    return up_rows, down_rows, groups, up_rows + down_rows + share // groups


def rest_grads(acts, pres, hiddens, branches, cot, mixes, me_s, me_f, count):
    micro, rows, model = cot.shape
    parts = len(mixes[0])
    hidden = acts.shape[2]
    height = rest_layout(model, hidden, parts, count)[3]
    half = (parts, count // 2, height, PACK)
    flat = [item for group in mixes for item in group]
    lanes = hidden // count
    whole = lambda shape: pl.BlockSpec(shape, lambda t: (0,) * len(shape))
    chunk = pl.BlockSpec((micro, rows, model), lambda t: (0, 0, t))
    return pl.pallas_call(
        partial(rest_grads_kernel, micro, parts, count),
        name="rest_grads",
        grid=(hidden // model,),
        out_shape=(
            jax.ShapeDtypeStruct(half, BF),
            jax.ShapeDtypeStruct(half, BF),
            jax.ShapeDtypeStruct((8, hidden), F32),
        ),
        in_specs=[SM, SM, chunk, chunk]
        + [whole(cot.shape)] * 3
        + [whole(flat[0].shape)] * len(flat),
        out_specs=(whole(half), whole(half), pl.BlockSpec((8, model), lambda t: (0, t))),
        scratch_shapes=[pltpu.VMEM((micro, model, rows), BF)] * 3
        + [
            pltpu.VMEM((model // PACK, model, PACK), BF),
            pltpu.VMEM((model // lanes, model, lanes), BF),
            pltpu.VMEM((parts, model, model // parts), BF),
        ],
        compiler_params=params(26 * 1024 * 1024),
        cost_estimate=cost(12),
    )(me_s, me_f, acts, pres, hiddens, branches, cot, *flat)


def finish_rest_kernel(parts, me_ref, *refs):
    pieces = refs[:parts]
    out_ref, up_ref, down_ref, out_s, down_s = refs[parts:]
    share, hidden = up_ref.shape
    down_lanes, model = down_ref.shape
    up_rows, down_height, out_groups, _ = rest_layout(model, hidden, parts, model // share)
    down_rows = model // parts
    cols = hidden // parts
    for k in range(parts):
        dest = me_ref[0] ^ k
        for g in range(cols // PACK):
            place = pl.ds(pl.multiple_of(dest * cols + g * PACK, PACK), PACK)
            up_ref[:, place] = pieces[k][g * share : (g + 1) * share, :].astype(F32)
        groups = PACK // down_lanes
        tall = down_rows // groups
        for g in range(groups):
            place = pl.ds(pl.multiple_of(dest * down_rows + g * tall, tall), tall)
            down_s[place, :] = pieces[k][
                up_rows : up_rows + tall, g * down_lanes : (g + 1) * down_lanes
            ].astype(F32)
        tall = share // out_groups
        top = up_rows + down_height
        for g in range(out_groups):
            out_s[dest, g * tall : (g + 1) * tall, :] = pieces[k][
                top : top + tall, g * down_rows : (g + 1) * down_rows
            ].astype(F32)
    down_ref[...] = down_s[...].T
    for d in range(parts):
        out_ref[:, d * down_rows : (d + 1) * down_rows] = out_s[d]


def finish_rest(pieces, me, model, hidden, count):
    parts = len(pieces)
    share, lanes = model // count, hidden // count
    return pl.pallas_call(
        partial(finish_rest_kernel, parts),
        name="finish_rest",
        out_shape=(
            jax.ShapeDtypeStruct((share, model), F32),
            jax.ShapeDtypeStruct((share, hidden), F32),
            jax.ShapeDtypeStruct((lanes, model), F32),
        ),
        in_specs=[SM] + [VM] * parts,
        out_specs=(VM, VM, VM),
        scratch_shapes=[
            pltpu.VMEM((parts, share, model // parts), F32),
            pltpu.VMEM((model, lanes), F32),
        ],
        compiler_params=params(),
        cost_estimate=cost(1),
    )(me, *pieces)


def finish_qkv_kernel(parts, me_ref, *refs):
    pieces = refs[:parts]
    out_ref, piece_s = refs[parts:]
    here = pieces[0].shape[1] // 3
    model = here * parts
    for k in range(parts):
        piece_s[me_ref[0] ^ k] = pieces[k][...].astype(F32)
    for d in range(parts):
        for t in range(3):
            lane = t * model + d * here
            out_ref[:, lane : lane + here] = piece_s[d, :, t * here : (t + 1) * here]


def finish_qkv(pieces, me):
    parts = len(pieces)
    share, width = pieces[0].shape
    return pl.pallas_call(
        partial(finish_qkv_kernel, parts),
        name="finish_qkv",
        out_shape=jax.ShapeDtypeStruct((share, parts * width), F32),
        in_specs=[SM] + [VM] * parts,
        out_specs=VM,
        scratch_shapes=[pltpu.VMEM((parts, share, width), F32)],
        compiler_params=params(),
        cost_estimate=cost(1),
    )(me, *pieces)


def input_kernel(parts, has_old, me_ref, tokens_ref, embed_ref, middle_ref, wq_ref, vec_ref, *refs):
    pieces = refs[:parts]
    out_ref, sums_ref = refs[parts + has_old :]
    grad_hidden = dot_t(pieces[0][...], wq_ref[me_ref[0]])
    for k in range(1, parts):
        grad_hidden = grad_hidden + dot_t(pieces[k][...], wq_ref[me_ref[0] ^ k])
    rows = tokens_ref[0].astype(F32) + embed_ref[0].astype(F32)
    scaled, inverse = norm_parts(rows)
    sums_ref[0:1] = jnp.sum(grad_hidden * scaled, axis=0, keepdims=True)
    sums_ref[1:2] = jnp.sum(grad_hidden, axis=0, keepdims=True)
    sums_ref[2:8] = jnp.zeros((6, sums_ref.shape[1]), F32)
    out_ref[0] = middle_ref[...] + norm_back(grad_hidden, scaled, inverse, vec_ref[0:1])


def input_gradient(tokens, embed, micro_index, grad_middle, pieces, wq, vec, old, me):
    micro, rows, model = tokens.shape
    parts = len(pieces)
    width = pieces[0].shape[1]
    row_spec = pl.BlockSpec((1, rows, model), lambda i: (micro_index, 0, 0))
    whole = lambda shape: pl.BlockSpec(shape, lambda i: (0,) * len(shape))
    old_args = [] if old is None else [old]
    return pl.pallas_call(
        partial(input_kernel, parts, len(old_args)),
        name="input_gradient",
        grid=(1,),
        out_shape=(
            jax.ShapeDtypeStruct((micro, rows, model), F32),
            jax.ShapeDtypeStruct((8, model), F32),
        ),
        in_specs=[SM, row_spec, row_spec, whole((rows, model)), whole(wq.shape), whole(vec.shape)]
        + [whole((rows, width))] * parts
        + [pl.BlockSpec(memory_space=pl.ANY)] * len(old_args),
        out_specs=(row_spec, whole((8, model))),
        input_output_aliases={6 + parts: 0} if old_args else {},
        compiler_params=params(),
        cost_estimate=cost(2.5),
    )(me, tokens, embed, grad_middle, wq, vec, *pieces, *old_args)


def qkv_first_kernel(micro, parts, count, me_f, *refs):
    hiddens = refs[:micro]
    pieces = refs[micro : micro + micro * parts]
    out_ref, hidden_t = refs[micro + micro * parts :]
    share = hiddens[0].shape[1] // count
    for m in range(micro):
        hidden_t[m] = hiddens[m][...].astype(F32).T.astype(BF)

    def one(j, _):
        place = pl.ds(pl.multiple_of((me_f[0] ^ j) * share, share), share)
        for k in range(parts):
            out_ref[k, j] = sum(
                dot(hidden_t[m, place, :], pieces[m * parts + k][...]) for m in range(micro)
            )
        return 0

    lax.fori_loop(0, count, one, 0)


def qkv_last_kernel(parts, count, me_f, first_ref, hidden_ref, *refs):
    pieces, (keep_ref, send_ref, hidden_t) = refs[:parts], refs[parts:]
    share = hidden_ref.shape[1] // count
    hidden_t[...] = hidden_ref[...].astype(F32).T.astype(BF)

    def one_pair(s, _):
        for j, target in ((2 * s, keep_ref), (2 * s + 1, send_ref)):
            place = pl.ds(pl.multiple_of((me_f[0] ^ j) * share, share), share)
            for k in range(parts):
                found = first_ref[k, j] + dot(hidden_t[place, :], pieces[k][...])
                target[k, s] = found.astype(BF)
        return 0

    lax.fori_loop(0, count // 2, one_pair, 0)


def qkv_first(hiddens, pieces, me_f, count):
    micro = len(hiddens)
    rows, model = hiddens[0].shape
    parts = len(pieces[0])
    width = pieces[0][0].shape[1]
    flat = [item for group in pieces for item in group]
    return pl.pallas_call(
        partial(qkv_first_kernel, micro, parts, count),
        name="qkv_first",
        out_shape=jax.ShapeDtypeStruct((parts, count, model // count, width), F32),
        in_specs=[SM] + [VM] * (micro + micro * parts),
        out_specs=VM,
        scratch_shapes=[pltpu.VMEM((micro, model, rows), BF)],
        compiler_params=params(),
        cost_estimate=cost(5),
    )(me_f, *hiddens, *flat)


def qkv_last(first, hidden, pieces, me_f, count):
    rows, model = hidden.shape
    parts = len(pieces)
    width = pieces[0].shape[1]
    half = jax.ShapeDtypeStruct((parts, count // 2, model // count, width), BF)
    return pl.pallas_call(
        partial(qkv_last_kernel, parts, count),
        name="qkv_last",
        out_shape=(half, half),
        in_specs=[SM] + [VM] * (2 + parts),
        out_specs=(VM, VM),
        scratch_shapes=[pltpu.VMEM((model, rows), BF)],
        compiler_params=params(),
        cost_estimate=cost(4),
    )(me_f, first, hidden, *pieces)


def total(items, dtype):
    found = items[0].astype(F32)
    for item in items[1:]:
        found = found + item.astype(F32)
    return found.astype(dtype)


def small_call(kernel, outs, *args):
    return pl.pallas_call(
        kernel,
        out_shape=outs,
        in_specs=[VM] * len(args),
        out_specs=jax.tree.map(lambda _: VM, outs),
        compiler_params=params(),
        cost_estimate=cost(0.5),
    )(*args)


def add_parts(keep, found):
    def kernel(keep_ref, found_ref, *outs):
        for k, out in enumerate(outs):
            out[...] = total([keep_ref[k], found_ref[k]], out.dtype)

    out = jax.ShapeDtypeStruct(keep.shape[1:], keep.dtype)
    return small_call(kernel, [out] * keep.shape[0], keep, found)


def add_all(*items):
    def kernel(*refs):
        refs[-1][...] = total([item[...] for item in refs[:-1]], refs[-1].dtype)

    return small_call(kernel, jax.ShapeDtypeStruct(items[0].shape, items[0].dtype), *items)


def reduce_early(keep, send):
    parts, slots = keep.shape[:2]
    found = swap(send, "fsdp", 1)

    def by_slot(keep_ref, found_ref, *outs):
        for k in range(parts):
            for s in range(slots):
                outs[s][k] = total([keep_ref[k, s], found_ref[k, s]], BF)

    out = jax.ShapeDtypeStruct(keep.shape[:1] + keep.shape[2:], BF)
    shares = small_call(by_slot, [out] * slots, keep, found)
    yield shares
    shares = far_exchange(shares)

    def by_part(*refs):
        for k in range(parts):
            refs[slots + k][...] = total([item[k] for item in refs[:slots]], BF)

    out = jax.ShapeDtypeStruct(keep.shape[2:], BF)
    pieces = small_call(by_part, [out] * parts, *shares)
    yield pieces
    final = add_all(*exchange(pieces, "seq"))
    yield final
    yield gather_pieces(final, "seq")


def far_exchange(shares):
    return [shares[0]] + [swap(shares[s], "fsdp", 2 * s) for s in range(1, len(shares))]


def reduce_last(keep, found, vectors):
    slots = keep.shape[1]
    both = lax.optimization_barrier
    pieces = add_parts(keep, found)
    other = swap(vectors, "fsdp", 1)
    pieces, other = both((exchange(pieces, "seq"), other))

    def by_slot(*refs):
        for s in range(slots):
            refs[s - slots][...] = total([item[s] for item in refs[:-slots]], BF)

    out = jax.ShapeDtypeStruct(keep.shape[2:], BF)
    shares = small_call(by_slot, [out] * slots, *pieces)
    vectors = add_all(vectors, other)
    others = exchange([vectors] * lax.axis_size("seq"), "seq")
    shares, others = both((far_exchange(shares), others))
    final = add_all(*shares)
    vectors = add_all(*others)
    others = far_exchange([vectors] * slots)
    pieces, others = both((gather_pieces(final, "seq"), others))
    return pieces, add_all(*others)


def gather_sums(first, second, bias):
    def kernel(*refs):
        bias_ref, out_ref = refs[-2:]
        model = out_ref.shape[1]
        once, twice = refs[: len(first)], refs[len(first) : -2]
        out_ref[0:2] = total([item[0:2] for item in once], F32)
        out_ref[2:5] = total([item[0:3] for item in twice], F32)
        out_ref[5:8] = jnp.zeros((3, model), F32)
        for t in range(8):
            lanes = bias_ref.shape[1] // 8
            row = 8 + (t * lanes) // model
            lane = (t * lanes) % model
            out_ref[row : row + 1, lane : lane + lanes] = bias_ref[0:1, t * lanes : (t + 1) * lanes]

    model = first[0].shape[1]
    rows = 8 + bias.shape[1] // model
    out = jax.ShapeDtypeStruct((rows, model), F32)
    return small_call(kernel, out, *first, *second, bias)


def layer(
    tokens,
    time_embed,
    doc_ids,
    out_grad,
    norm1_gain,
    norm1_shift,
    qkv_weight,
    out_weight,
    norm2_gain,
    norm2_shift,
    up_weight,
    up_bias,
    down_weight,
    down_bias,
):
    micro, _, _, model = tokens.shape
    parts = lax.axis_size("seq")
    count = lax.axis_size("fsdp")
    hidden = up_weight.shape[1]
    ratio = hidden // model
    head_dim = model // HEADS
    heads = HEADS // parts
    share = model // count
    seq_index = lax.axis_index("seq").astype(jnp.int32)
    fsdp_index = lax.axis_index("fsdp").astype(jnp.int32)
    me_s = seq_index.reshape(1)
    me_f = fsdp_index.reshape(1)
    tokens = tokens[:, 0]
    embed = time_embed[:, 0]
    cot = out_grad[:, 0]

    pieces = gather_pairs(qkv_weight, "fsdp")
    small = [norm1_gain, norm1_shift, norm2_gain, norm2_shift, down_bias]
    small = [item.reshape(1, share) for item in small] + [up_bias.reshape(ratio, share)]
    small = gather_pairs(jnp.concatenate(small), "fsdp")
    docs = gather_pieces(doc_ids, "seq")
    doc, low, high = assemble_docs(docs, me_s)
    small = after(small, doc)
    wq, vec, bias = assemble_qkv(pieces, small, me_f, model, parts, hidden)
    rest = pack_rest(out_weight, up_weight, down_weight)
    rest = gather_pairs(rest, "fsdp")

    hiddens, triples, mixes, logs = [], [], [], []
    for m in range(micro):
        found = project(tokens, embed, m, wq, vec, me_s)
        hiddens.append(found[0])
        outs = after(found[1:], triples[-1]) if m else found[1:]
        triples.append(exchange(outs, "seq"))
    sent = []
    for m in range(micro):
        triple = after(triples[m], logs[-1]) if m else triples[m]
        outs, log_total = attend(triple, me_s, low, high, doc, m, heads, head_dim)
        sent.append(outs)
        logs.append(log_total)
        mixes.append(exchange(outs, "seq"))
    w_out, w_up, w_down = assemble_rest(rest, me_f, model, hidden)
    stacked = None
    middles, sums, heads_grads = [], [], []
    for m in range(micro):
        mixed = mixes[m] if m else after(mixes[m], logs[-1])
        found, grads = feed(
            tokens, embed, cot, m, mixed, vec, bias, w_out, w_up, w_down, stacked, me_s
        )
        stacked = found[:5]
        middles.append(found[5])
        sums.append(found[6])
        heads_grads.append(exchange(grads, "seq"))
    layer_output, acts, pres, seconds, branches = stacked
    keep, send, bias_sum = rest_grads(acts, pres, seconds, branches, cot, mixes, me_s, me_f, count)
    hops = reduce_early(keep, send)
    backs = []
    for m in range(micro):
        token = bias_sum if m == 0 else (outs, next(hops)) if m == 1 else outs
        grads = after(heads_grads[m], token)
        outs = attend_back(
            triples[m],
            sent[m],
            grads,
            me_s,
            low,
            high,
            doc,
            m,
            logs[m],
            heads,
            head_dim,
        )
        backs.append(exchange(outs, "seq"))
    input_grad = None
    first_sums = []
    for m in range(micro - 1):
        pieces = after(backs[m], outs) if m == 0 else backs[m]
        input_grad, sum_one = input_gradient(
            tokens, embed, m, middles[m], pieces, wq, vec, input_grad, me_s
        )
        first_sums.append(sum_one)
    first = qkv_first(hiddens[:-1], after(backs[:-1], input_grad), me_f, count)
    last = after(backs[-1], (first, next(hops)))
    keep, send = qkv_last(first, hiddens[-1], last, me_f, count)
    found = swap(send, "fsdp", 1)
    last = after(last, send)
    input_grad, sum_one = input_gradient(
        tokens, embed, micro - 1, middles[-1], last, wq, vec, input_grad, me_s
    )
    first_sums.append(sum_one)
    *_, pieces = hops
    grad_out, grad_up, grad_down = finish_rest(pieces, me_s, model, hidden, count)
    vectors = gather_sums(first_sums, sums, bias_sum)
    pieces, vectors = reduce_last(keep, found, vectors)
    grad_qkv = finish_qkv(pieces, me_s)

    pick = lambda row: lax.dynamic_slice(vectors[row], (fsdp_index * share,), (share,))
    grad_up_bias = lax.dynamic_slice(
        vectors[8 : 8 + ratio].reshape(hidden), (fsdp_index * (hidden // count),), (hidden // count,)
    )
    return (
        layer_output[:, None],
        input_grad[:, None],
        pick(0),
        pick(1),
        grad_qkv,
        grad_out,
        pick(2),
        pick(3),
        grad_up,
        grad_up_bias,
        grad_down,
        pick(4),
    )


def solution(mesh):
    rows = P(None, "fsdp", "seq", None)
    vector = P("fsdp")
    matrix = P("fsdp", None)
    return jax.shard_map(
        layer,
        mesh=mesh,
        in_specs=(
            rows,
            rows,
            P(None, "fsdp", "seq"),
            rows,
            vector,
            vector,
            matrix,
            matrix,
            vector,
            vector,
            matrix,
            vector,
            matrix,
            vector,
        ),
        out_specs=(
            rows,
            rows,
            vector,
            vector,
            matrix,
            matrix,
            vector,
            vector,
            matrix,
            vector,
            matrix,
            vector,
        ),
        check_vma=False,
    )
```

```python
from functools import partial

import jax
import jax.numpy as jnp
from jax import lax
from jax.experimental import pallas as pl
from jax.experimental.pallas import tpu as pltpu
from jax.sharding import PartitionSpec as P


HEADS = 8
EPS = 1e-05
LOG2E = 1.4426950408889634
WIDE = 512
NARROW = 384
PACK = 256
VMEM_LIMIT = 16 * 1024 * 1024
BF = jnp.bfloat16
F32 = jnp.float32


def dot(a, b, dims=((1,), (0,))):
    return lax.dot_general(a, b, (dims, ((), ())), preferred_element_type=F32)


def dot_t(a, b):
    return dot(a, b, ((1,), (1,)))


def params(limit=VMEM_LIMIT):
    return pltpu.CompilerParams(vmem_limit_bytes=limit)


def cost(micros):
    return pl.CostEstimate(flops=int(micros * 1e8), bytes_accessed=1000, transcendentals=0)


VM = pl.BlockSpec(memory_space=pltpu.VMEM)
SM = pl.BlockSpec(memory_space=pltpu.SMEM)


def after(value, token):
    return lax.optimization_barrier((value, token))[0]


def swap(value, axis, bit):
    size = lax.axis_size(axis)
    return lax.ppermute(value, axis, [(i, i ^ bit) for i in range(size)])


def exchange(pieces, axis):
    return [pieces[0]] + [swap(pieces[k], axis, k) for k in range(1, len(pieces))]


def gather_pieces(value, axis):
    return exchange([value] * lax.axis_size(axis), axis)


def gather_pairs(value, axis):
    size = lax.axis_size(axis)
    far = [swap(value, axis, j) if j else value for j in range(0, size, 2)]
    result = []
    for mine in far:
        result += [mine, swap(mine, axis, 1)]
    return result


def assemble_qkv_kernel(count, seq_parts, part_width, me_ref, *refs):
    pieces, small = refs[:count], refs[count : 2 * count]
    wq_ref, vec_ref, bias_ref, small_s = refs[2 * count :]
    rows = pieces[0].shape[0]
    model = wq_ref.shape[1]
    ratio = small[0].shape[0] - 5
    for j in range(count):
        owner = me_ref[0] ^ j
        start = pl.multiple_of(owner * rows, rows)
        for d in range(seq_parts):
            for t in range(3):
                lane = t * model + d * part_width
                wq_ref[d, pl.ds(start, rows), t * part_width : (t + 1) * part_width] = pieces[j][
                    :, lane : lane + part_width
                ]
        small_s[owner] = small[j][...].astype(F32)
    vec_ref[5:8] = jnp.zeros((3, model), F32)
    for o in range(count):
        item = small_s[o]
        vec_ref[0:5, o * rows : (o + 1) * rows] = item[0:5]
        for t in range(ratio):
            lane = (o * ratio + t) * rows
            bias_ref[lane // CHUNK, :, lane % CHUNK : lane % CHUNK + rows] = item[5 + t : 6 + t]


def assemble_qkv(pieces, small, me, model, seq_parts, hidden):
    part_width = model // seq_parts
    count = len(pieces)
    return pl.pallas_call(
        partial(assemble_qkv_kernel, count, seq_parts, part_width),
        name="assemble_qkv",
        out_shape=(
            jax.ShapeDtypeStruct((seq_parts, model, 3 * part_width), BF),
            jax.ShapeDtypeStruct((8, model), F32),
            jax.ShapeDtypeStruct((hidden // CHUNK, 1, CHUNK), F32),
        ),
        in_specs=[SM] + [VM] * (2 * count),
        out_specs=(VM, VM, VM),
        scratch_shapes=[
            pltpu.VMEM((count,) + small[0].shape, F32),
        ],
        compiler_params=params(),
        cost_estimate=cost(2),
    )(me, *pieces, *small)


def pack_rest_kernel(out_ref, up_ref, down_ref, all_ref):
    rows, model = out_ref.shape
    ratio = up_ref.shape[1] // model
    all_ref[0:rows] = out_ref[...]
    for t in range(ratio):
        all_ref[(1 + t) * rows : (2 + t) * rows] = up_ref[:, t * model : (t + 1) * model]
    all_ref[(1 + ratio) * rows :] = down_ref[...]


def pack_rest(out_weight, up_weight, down_weight):
    rows, model = out_weight.shape
    height = rows + 2 * down_weight.shape[0]
    return pl.pallas_call(
        pack_rest_kernel,
        name="pack_rest",
        out_shape=jax.ShapeDtypeStruct((height, model), BF),
        in_specs=[VM] * 3,
        out_specs=VM,
        compiler_params=params(),
        cost_estimate=cost(1),
    )(out_weight, up_weight, down_weight)


def assemble_rest_kernel(count, me_ref, *refs):
    pieces, (out_ref, up_ref, down_ref) = refs[:count], refs[count:]
    model = out_ref.shape[0]
    rows = model // count
    ratio = up_ref.shape[1] // model
    down_rows = ratio * rows
    for j in range(count):
        owner = me_ref[0] ^ j
        place = pl.ds(pl.multiple_of(owner * rows, rows), rows)
        out_ref[place, :] = pieces[j][0:rows, :]
        for t in range(ratio):
            up_ref[place, t * model : (t + 1) * model] = pieces[j][
                (1 + t) * rows : (2 + t) * rows, :
            ]
        place = pl.ds(pl.multiple_of(owner * down_rows, down_rows), down_rows)
        down_ref[place, :] = pieces[j][(1 + ratio) * rows :, :]


def assemble_rest(pieces, me, model, hidden):
    count = len(pieces)
    return pl.pallas_call(
        partial(assemble_rest_kernel, count),
        name="assemble_rest",
        out_shape=(
            jax.ShapeDtypeStruct((model, model), BF),
            jax.ShapeDtypeStruct((model, hidden), BF),
            jax.ShapeDtypeStruct((hidden, model), BF),
        ),
        in_specs=[SM] + [VM] * count,
        out_specs=(VM, VM, VM),
        compiler_params=params(),
        cost_estimate=cost(2),
    )(me, *pieces)


def norm_parts(rows):
    mean_row = jnp.mean(rows, axis=-1, keepdims=True)
    centred = rows - mean_row
    inverse = lax.rsqrt(jnp.mean(centred * centred, axis=-1, keepdims=True) + EPS)
    return centred * inverse, inverse


def norm_back(grad_normed, scaled, inverse, gain):
    grad_scaled = grad_normed * gain
    centre = jnp.mean(grad_scaled, axis=-1, keepdims=True)
    along = jnp.mean(grad_scaled * scaled, axis=-1, keepdims=True)
    return inverse * (grad_scaled - centre - scaled * along)


def project_kernel(parts, me_ref, tokens_ref, embed_ref, wq_ref, vec_ref, hidden_ref, *outs):
    rows = tokens_ref[0].astype(F32) + embed_ref[0].astype(F32)
    scaled, _ = norm_parts(rows)
    hidden = (scaled * vec_ref[0:1] + vec_ref[1:2]).astype(BF)
    hidden_ref[...] = hidden
    for k in range(parts):
        outs[k][...] = dot(hidden, wq_ref[me_ref[0] ^ k]).astype(BF)


def project(tokens, embed, micro_index, wq, vec, me):
    _, rows, model = tokens.shape
    parts, _, width = wq.shape
    row_spec = pl.BlockSpec((1, rows, model), lambda i: (micro_index, 0, 0))
    whole = lambda shape: pl.BlockSpec(shape, lambda i: (0,) * len(shape))
    return pl.pallas_call(
        partial(project_kernel, parts),
        name="project",
        grid=(1,),
        out_shape=[jax.ShapeDtypeStruct((rows, model), BF)]
        + [jax.ShapeDtypeStruct((rows, width), BF)] * parts,
        in_specs=[SM, row_spec, row_spec, whole(wq.shape), whole(vec.shape)],
        out_specs=[whole((rows, model))] + [whole((rows, width))] * parts,
        compiler_params=params(),
        cost_estimate=cost(2),
    )(me, tokens, embed, wq, vec)


def docs_kernel(parts, me_ref, *refs):
    pieces, (doc_ref, low_ref, high_ref) = refs[:parts], refs[parts:]
    micro, _, rows = pieces[0].shape
    for k in range(parts):
        place = pl.ds(pl.multiple_of((me_ref[0] ^ k) * rows, rows), rows)
        doc_ref[:, :, place] = pieces[k][...].astype(F32)
    for m in range(micro):
        doc = doc_ref[m]
        for i in range(doc.shape[1] // WIDE):
            first = doc[:, i * WIDE : i * WIDE + 1]
            last = doc[:, (i + 1) * WIDE - 1 : (i + 1) * WIDE]
            low = jnp.sum(jnp.where(doc < first, 1.0, 0.0)).astype(jnp.int32)
            high = jnp.sum(jnp.where(doc <= last, 1.0, 0.0)).astype(jnp.int32)
            low_ref[m, i] = low // NARROW
            high_ref[m, i] = (high + NARROW - 1) // NARROW


def assemble_docs(pieces, me):
    parts = len(pieces)
    micro, _, rows = pieces[0].shape
    length = rows * parts
    bounds = jax.ShapeDtypeStruct((micro, length // WIDE), jnp.int32)
    return pl.pallas_call(
        partial(docs_kernel, parts),
        name="assemble_docs",
        out_shape=(jax.ShapeDtypeStruct((micro, 1, length), F32), bounds, bounds),
        in_specs=[SM] + [VM] * parts,
        out_specs=(VM, SM, SM),
        compiler_params=params(),
        cost_estimate=cost(2),
    )(me, *pieces)


def head_mask(value, head, heads, head_dim):
    if heads == 1:
        return value
    lane = lax.broadcasted_iota(jnp.int32, value.shape, 1)
    keep = (lane >= head * head_dim) & (lane < (head + 1) * head_dim)
    return jnp.where(keep, value, jnp.zeros_like(value))


def spread_docs(doc_ref, doc_s):
    for start in range(0, doc_s.shape[0], 512):
        doc_s[start : start + 512, :] = jnp.broadcast_to(
            doc_ref[0:1, start : start + 512], (128, 512)
        ).T


def same_doc(doc_s, place, doc_row):
    column = doc_s[place, :]
    return jnp.concatenate([column] * (doc_row.shape[1] // 128), axis=1) == doc_row


def fold(value, combine):
    out = value[0:8]
    for start in range(8, value.shape[0], 8):
        out = combine(out, value[start : start + 8])
    return out


def place_rows(pieces, me, rows_s):
    rows = pieces[0].shape[0]
    for k, piece in enumerate(pieces):
        rows_s[pl.ds(pl.multiple_of((me ^ k) * rows, rows), rows), :] = piece[...]


def attend_kernel(parts, heads, head_dim, m, me_ref, low_ref, high_ref, docs_ref, *refs):
    doc_ref = docs_ref.at[m]
    pieces = refs[:parts]
    outs = refs[parts : 2 * parts]
    log_ref = refs[2 * parts]
    triple_s, value_t, doc_s, score_s, out_s = refs[2 * parts + 1 :]
    rows, width = pieces[0].shape
    here = width // 3
    length = rows * parts
    spread_docs(doc_ref, doc_s)
    place_rows(pieces, me_ref[0], triple_s)
    for start in range(0, length, WIDE):
        value_t[:, start : start + WIDE] = (
            triple_s[start : start + WIDE, 2 * here :].astype(F32).T.astype(BF)
        )
    scale = head_dim ** (-0.5) * LOG2E

    def one_block(i, _):
        place = pl.ds(pl.multiple_of(i * WIDE, WIDE), WIDE)
        query = triple_s[place, 0:here]
        queries = [head_mask(query, h, heads, head_dim) for h in range(heads)]
        doc_row = doc_ref[0:1, place]

        def score(j, tops):
            key_place = pl.ds(pl.multiple_of(j * NARROW, NARROW), NARROW)
            keys = triple_s[key_place, here : 2 * here]
            same = same_doc(doc_s, key_place, doc_row)
            result = []
            for h in range(heads):
                scores = jnp.where(same, dot_t(keys, queries[h]) * scale, -jnp.inf)
                score_s[h, key_place, :] = scores
                result.append(jnp.maximum(tops[h], fold(scores, jnp.maximum)))
            return tuple(result)

        tops = lax.fori_loop(
            low_ref[m, i],
            high_ref[m, i],
            score,
            tuple(jnp.full((8, WIDE), -jnp.inf, F32) for _ in range(heads)),
        )
        tops = [jnp.max(top, axis=0, keepdims=True) for top in tops]

        def mix(j, carry):
            key_place = pl.ds(pl.multiple_of(j * NARROW, NARROW), NARROW)
            result = []
            for h in range(heads):
                total, acc = carry[h]
                weight = jnp.exp2(score_s[h, key_place, :] - tops[h])
                total = total + fold(weight, jnp.add)
                values = value_t[h * head_dim : (h + 1) * head_dim, key_place]
                result.append((total, acc + dot(values, weight.astype(BF))))
            return tuple(result)

        done = lax.fori_loop(
            low_ref[m, i],
            high_ref[m, i],
            mix,
            tuple(
                (jnp.zeros((8, WIDE), F32), jnp.zeros((head_dim, WIDE), F32))
                for _ in range(heads)
            ),
        )
        mixed = []
        for h in range(heads):
            total = jnp.sum(done[h][0], axis=0, keepdims=True)
            mixed.append(done[h][1] / total)
            log_ref[h, :, place] = jnp.broadcast_to(tops[h] + jnp.log2(total), (8, WIDE))
        mixed = jnp.concatenate(mixed, axis=0) if heads > 1 else mixed[0]
        out_s[place, :] = mixed.T.astype(BF)
        return 0

    lax.fori_loop(0, length // WIDE, one_block, 0)
    for k in range(parts):
        place = pl.ds(pl.multiple_of((me_ref[0] ^ k) * rows, rows), rows)
        outs[k][...] = out_s[place, :]


def attend(pieces, me, low, high, doc, m, heads, head_dim):
    parts = len(pieces)
    rows, width = pieces[0].shape
    here = width // 3
    length = rows * parts
    found = pl.pallas_call(
        partial(attend_kernel, parts, heads, head_dim, m),
        name="attend",
        out_shape=[jax.ShapeDtypeStruct((rows, here), BF)] * parts
        + [jax.ShapeDtypeStruct((heads, 8, length), F32)],
        in_specs=[SM, SM, SM, VM] + [VM] * parts,
        out_specs=[VM] * (parts + 1),
        scratch_shapes=[
            pltpu.VMEM((length, width), BF),
            pltpu.VMEM((here, length), BF),
            pltpu.VMEM((length, 128), F32),
            pltpu.VMEM((heads, length, WIDE), F32),
            pltpu.VMEM((length, here), BF),
        ],
        compiler_params=params(),
        cost_estimate=cost(8),
    )(me, low, high, doc, *pieces)
    return found[:parts], found[parts]


def attend_back_kernel(
    parts, heads, head_dim, m, me_ref, low_ref, high_ref, docs_ref, log_ref, *refs
):
    doc_ref = docs_ref.at[m]
    pieces = refs[:parts]
    mixes = refs[parts : 2 * parts]
    grads = refs[2 * parts : 3 * parts]
    outs = refs[3 * parts : 4 * parts]
    (
        triple_s,
        grad_all,
        mix_all,
        query_s,
        key_t,
        grad_s,
        centre_s,
        doc_s,
        query_t,
        pair_s,
    ) = refs[4 * parts :]
    rows, width = pieces[0].shape
    here = width // 3
    length = rows * parts
    me = me_ref[0]
    spread_docs(doc_ref, doc_s)
    place_rows(pieces, me, triple_s)
    place_rows(grads, me, grad_all)
    place_rows(mixes, me, mix_all)
    for start in range(0, length, WIDE):
        place = pl.ds(start, WIDE)
        query = triple_s[place, 0:here]
        grad = grad_all[place, :]
        for h in range(heads):
            query_s[h, place, :] = head_mask(query, h, heads, head_dim)
            grad_s[h, place, :] = head_mask(grad, h, heads, head_dim)
        key_t[:, place] = triple_s[place, here : 2 * here].astype(F32).T.astype(BF)
        both = (grad.astype(F32) * mix_all[place, :].astype(F32)).T
        for h in range(heads):
            centre = jnp.sum(both[h * head_dim : (h + 1) * head_dim], axis=0, keepdims=True)
            centre_s[h, :, place] = jnp.broadcast_to(centre, (8, WIDE))
    query_t[...] = jnp.zeros_like(query_t)
    scale = head_dim ** (-0.5)

    def one_key(j, _):
        key_place = pl.ds(pl.multiple_of(j * WIDE, WIDE), WIDE)
        keys = triple_s[key_place, here : 2 * here]
        values = triple_s[key_place, 2 * here :]
        keys_t = [key_t[h * head_dim : (h + 1) * head_dim, key_place] for h in range(heads)]

        def one_block(i, carry):
            grad_key, grad_value = carry
            place = pl.ds(pl.multiple_of(i * NARROW, NARROW), NARROW)
            same = same_doc(doc_s, key_place, doc_ref[0:1, place])
            for h in range(heads):
                query = query_s[h, place, :]
                grad = grad_s[h, place, :]
                scores = jnp.where(same, dot_t(keys, query) * (scale * LOG2E), -jnp.inf)
                weight = jnp.exp2(scores - log_ref[h, 0:1, place])
                grad_weight = dot_t(values, grad)
                grad_score = (weight * (grad_weight - centre_s[h, 0:1, place])).astype(BF)
                grad_value = grad_value + dot(weight.astype(BF), grad)
                grad_key = grad_key + dot(grad_score, query)
                query_t[h * head_dim : (h + 1) * head_dim, place] += dot(keys_t[h], grad_score)
            return grad_key, grad_value

        zero = jnp.zeros((WIDE, here), F32)
        grad_key, grad_value = lax.fori_loop(
            low_ref[m, j], high_ref[m, j], one_block, (zero, zero)
        )
        pair_s[key_place, 0:here] = (grad_key * scale).astype(BF)
        pair_s[key_place, here:] = grad_value.astype(BF)
        return 0

    lax.fori_loop(0, length // WIDE, one_key, 0)
    for k in range(parts):
        place = pl.ds(pl.multiple_of((me_ref[0] ^ k) * rows, rows), rows)
        outs[k][:, 0:here] = (query_t[:, place].T * scale).astype(BF)
        outs[k][:, here:] = pair_s[place, :]


def attend_back(pieces, mixes, grads, me, low, high, doc, m, log_total, heads, head_dim):
    parts = len(pieces)
    rows, width = pieces[0].shape
    here = width // 3
    length = rows * parts
    return pl.pallas_call(
        partial(attend_back_kernel, parts, heads, head_dim, m),
        name="attend_back",
        out_shape=[jax.ShapeDtypeStruct((rows, width), BF)] * parts,
        in_specs=[SM, SM, SM, VM, VM] + [VM] * (3 * parts),
        out_specs=[VM] * parts,
        scratch_shapes=[
            pltpu.VMEM((length, width), BF),
            pltpu.VMEM((length, here), BF),
            pltpu.VMEM((length, here), BF),
            pltpu.VMEM((heads, length, here), BF),
            pltpu.VMEM((here, length), BF),
            pltpu.VMEM((heads, length, here), BF),
            pltpu.VMEM((heads, 8, length), F32),
            pltpu.VMEM((length, 128), F32),
            pltpu.VMEM((here, length), F32),
            pltpu.VMEM((length, 2 * here), BF),
        ],
        compiler_params=params(),
        cost_estimate=cost(12),
    )(me, low, high, doc, log_total, *pieces, *mixes, *grads)


CHUNK = 512


def feed_kernel(parts, has_old, me_ref, tokens_ref, embed_ref, cot_ref, vec_ref, bias_ref, *refs):
    mixes = refs[:parts]
    w_out, w_up, w_down = refs[parts : parts + 3]
    refs = refs[parts + 3 + has_old :]
    out_ref, act_ref, pre_ref, hidden_ref, branch_ref, middle_ref, sums_ref = refs[:7]
    grads = refs[7 : 7 + parts]
    total_s, back_s = refs[7 + parts :]
    me = me_ref[0]
    here = mixes[0].shape[1]
    middle = tokens_ref[0].astype(F32) + embed_ref[0].astype(F32)
    for k in range(parts):
        place = pl.ds(pl.multiple_of((me ^ k) * here, here), here)
        middle = middle + dot(mixes[k][...], w_out[place, :])
    scaled, inverse = norm_parts(middle)
    hidden_ref[0] = (scaled * vec_ref[2:3] + vec_ref[3:4]).astype(BF)
    middle_ref[...] = middle
    total_s[...] = jnp.zeros_like(total_s)
    back_s[...] = jnp.zeros_like(back_s)
    root = 0.7978845608028654

    def one_chunk(f, _):
        place = pl.ds(pl.multiple_of(f * CHUNK, CHUNK), CHUNK)
        value = dot(hidden_ref[0], w_up[:, place]) + bias_ref[f]
        square = value * value
        bend = jnp.tanh(root * (value + 0.044715 * (value * square)))
        half = 0.5 * (1.0 + bend)
        act = (value * half).astype(BF)
        slope = half + (0.5 * root) * value * (1.0 - bend * bend) * (1.0 + 0.134145 * square)
        act_ref[0, :, place] = act
        total_s[...] += dot(act, w_down[place, :])
        grad_pre = (dot_t(cot_ref[0], w_down[place, :]) * slope).astype(BF)
        pre_ref[0, :, place] = grad_pre
        back_s[...] += dot_t(grad_pre, w_up[:, place])
        return 0

    lax.fori_loop(0, w_up.shape[1] // CHUNK, one_chunk, 0)
    middle = middle_ref[...]
    out_ref[0] = (middle + total_s[...] + vec_ref[4:5]).astype(BF)
    scaled, inverse = norm_parts(middle)
    grad_hidden = back_s[...]
    sums_ref[0:1] = jnp.sum(grad_hidden * scaled, axis=0, keepdims=True)
    sums_ref[1:2] = jnp.sum(grad_hidden, axis=0, keepdims=True)
    cot = cot_ref[0].astype(F32)
    sums_ref[2:3] = jnp.sum(cot, axis=0, keepdims=True)
    sums_ref[3:8] = jnp.zeros((5, sums_ref.shape[1]), F32)
    grad_middle = cot + norm_back(grad_hidden, scaled, inverse, vec_ref[2:3])
    middle_ref[...] = grad_middle
    branch = grad_middle.astype(BF)
    branch_ref[0] = branch
    for k in range(parts):
        place = pl.ds(pl.multiple_of((me ^ k) * here, here), here)
        grads[k][...] = dot_t(branch, w_out[place, :]).astype(BF)


def feed(tokens, embed, cot, micro_index, mixes, vec, bias, w_out, w_up, w_down, old, me):
    micro, rows, model = tokens.shape
    parts = len(mixes)
    here = mixes[0].shape[1]
    hidden = w_up.shape[1]
    row_spec = pl.BlockSpec((1, rows, model), lambda i: (micro_index, 0, 0))
    whole = lambda shape: pl.BlockSpec(shape, lambda i: (0,) * len(shape))
    wide_spec = pl.BlockSpec((1, rows, hidden), lambda i: (micro_index, 0, 0))
    old_args = [] if old is None else list(old)
    found = pl.pallas_call(
        partial(feed_kernel, parts, len(old_args)),
        name="feed",
        grid=(1,),
        out_shape=[
            jax.ShapeDtypeStruct((micro, rows, model), BF),
            jax.ShapeDtypeStruct((micro, rows, hidden), BF),
            jax.ShapeDtypeStruct((micro, rows, hidden), BF),
            jax.ShapeDtypeStruct((micro, rows, model), BF),
            jax.ShapeDtypeStruct((micro, rows, model), BF),
            jax.ShapeDtypeStruct((rows, model), F32),
            jax.ShapeDtypeStruct((8, model), F32),
        ]
        + [jax.ShapeDtypeStruct((rows, here), BF)] * parts,
        in_specs=[SM, row_spec, row_spec, row_spec, whole(vec.shape), whole(bias.shape)]
        + [whole((rows, here))] * parts
        + [whole(w_out.shape), whole(w_up.shape), whole(w_down.shape)]
        + [pl.BlockSpec(memory_space=pl.ANY)] * len(old_args),
        out_specs=[
            row_spec,
            wide_spec,
            wide_spec,
            row_spec,
            row_spec,
            whole((rows, model)),
            whole((8, model)),
        ]
        + [whole((rows, here))] * parts,
        scratch_shapes=[pltpu.VMEM((rows, model), F32)] * 2,
        input_output_aliases={9 + parts + t: t for t in range(len(old_args))},
        compiler_params=params(20 * 1024 * 1024),
        cost_estimate=cost(8),
    )(me, tokens, embed, cot, vec, bias, *mixes, w_out, w_up, w_down, *old_args)
    return found[:7], found[7:]


def rest_grads_kernel(micro, parts, count, me_s, me_f, act_ref, pre_ref, hidden_ref, branch_ref,
                      cot_ref, *refs):
    mixes = refs[: micro * parts]
    keep_ref, send_ref, bias_ref = refs[micro * parts : micro * parts + 3]
    hidden_t, cot_t, mixed_t, up_s, down_s, out_s = refs[micro * parts + 3 :]
    targets = (keep_ref, send_ref)
    rows, model = hidden_ref.shape[1:]
    here = mixes[0].shape[1]
    share = model // count
    chunk = pl.program_id(0)
    owners, _, down_lanes = down_s.shape
    down_rows = model // parts
    up_rows, down_height, out_groups, _ = rest_layout(model, pl.num_programs(0) * model, parts, count)

    @pl.when(chunk == 0)
    def _():
        for m in range(micro):
            hidden_t[m] = hidden_ref[m].astype(F32).T.astype(BF)
            cot_t[m] = cot_ref[m].astype(F32).T.astype(BF)
            for k in range(parts):
                place = pl.ds(pl.multiple_of((me_s[0] ^ k) * here, here), here)
                mixed_t[m, place, :] = mixes[m * parts + k][...].astype(F32).T.astype(BF)
        found = sum(dot(mixed_t[m], branch_ref[m]) for m in range(micro)).astype(BF)
        for d in range(parts):
            out_s[d] = found[:, d * down_rows : (d + 1) * down_rows]
        tall = share // out_groups
        for j in range(count):
            base = (me_f[0] ^ j) * share
            for k in range(parts):
                for g in range(out_groups):
                    place = pl.ds(pl.multiple_of(base + g * tall, tall), tall)
                    top = up_rows + down_height
                    targets[j % 2][
                        k, j // 2, top : top + tall, g * down_rows : (g + 1) * down_rows
                    ] = out_s[me_s[0] ^ k, place, :]

    found = sum(dot(hidden_t[m], pre_ref[m]) for m in range(micro)).astype(BF)
    for q in range(model // PACK):
        up_s[q] = found[:, q * PACK : (q + 1) * PACK]
    for j in range(count):
        place = pl.ds(pl.multiple_of((me_f[0] ^ j) * share, share), share)
        for q in range(model // PACK):
            block = chunk * (model // PACK) + q
            groups = up_rows // share
            dest = me_s[0] ^ (block // groups)
            top = (q % groups) * share
            targets[j % 2][dest, j // 2, top : top + share, :] = up_s[q, place, :]

    found = sum(dot(cot_t[m], act_ref[m]) for m in range(micro)).astype(BF)
    for o in range(owners):
        down_s[o] = found[:, o * down_lanes : (o + 1) * down_lanes]
    groups = PACK // down_lanes
    tall = down_rows // groups
    for low in range(owners):
        owner = low ^ (me_f[0] % owners)
        slot = ((chunk ^ (me_f[0] // owners)) * owners + low) // 2
        for k in range(parts):
            for g in range(groups):
                place = pl.ds(pl.multiple_of((me_s[0] ^ k) * down_rows + g * tall, tall), tall)
                targets[low % 2][
                    k, slot, up_rows : up_rows + tall, g * down_lanes : (g + 1) * down_lanes
                ] = down_s[owner, place, :]

    ones = jnp.ones((8, rows), BF)
    bias_ref[...] = sum(dot(ones, pre_ref[m]) for m in range(micro))


def rest_layout(model, hidden, parts, count):
    share = model // count
    up_rows = share * (hidden // parts) // PACK
    down_rows = (model // parts) * (hidden // count) // PACK
    groups = PACK // (model // parts)
    if share % (16 * groups):
        groups = 1
    return up_rows, down_rows, groups, up_rows + down_rows + share // groups


def rest_grads(acts, pres, hiddens, branches, cot, mixes, me_s, me_f, count):
    micro, rows, model = cot.shape
    parts = len(mixes[0])
    hidden = acts.shape[2]
    height = rest_layout(model, hidden, parts, count)[3]
    half = (parts, count // 2, height, PACK)
    flat = [item for group in mixes for item in group]
    lanes = hidden // count
    whole = lambda shape: pl.BlockSpec(shape, lambda t: (0,) * len(shape))
    chunk = pl.BlockSpec((micro, rows, model), lambda t: (0, 0, t))
    return pl.pallas_call(
        partial(rest_grads_kernel, micro, parts, count),
        name="rest_grads",
        grid=(hidden // model,),
        out_shape=(
            jax.ShapeDtypeStruct(half, BF),
            jax.ShapeDtypeStruct(half, BF),
            jax.ShapeDtypeStruct((8, hidden), F32),
        ),
        in_specs=[SM, SM, chunk, chunk]
        + [whole(cot.shape)] * 3
        + [whole(flat[0].shape)] * len(flat),
        out_specs=(whole(half), whole(half), pl.BlockSpec((8, model), lambda t: (0, t))),
        scratch_shapes=[pltpu.VMEM((micro, model, rows), BF)] * 3
        + [
            pltpu.VMEM((model // PACK, model, PACK), BF),
            pltpu.VMEM((model // lanes, model, lanes), BF),
            pltpu.VMEM((parts, model, model // parts), BF),
        ],
        compiler_params=params(26 * 1024 * 1024),
        cost_estimate=cost(12),
    )(me_s, me_f, acts, pres, hiddens, branches, cot, *flat)


def finish_rest_kernel(parts, me_ref, *refs):
    pieces = refs[:parts]
    out_ref, up_ref, down_ref, out_s, down_s = refs[parts:]
    share, hidden = up_ref.shape
    down_lanes, model = down_ref.shape
    up_rows, down_height, out_groups, _ = rest_layout(model, hidden, parts, model // share)
    down_rows = model // parts
    cols = hidden // parts
    for k in range(parts):
        dest = me_ref[0] ^ k
        for g in range(cols // PACK):
            place = pl.ds(pl.multiple_of(dest * cols + g * PACK, PACK), PACK)
            up_ref[:, place] = pieces[k][g * share : (g + 1) * share, :].astype(F32)
        groups = PACK // down_lanes
        tall = down_rows // groups
        for g in range(groups):
            place = pl.ds(pl.multiple_of(dest * down_rows + g * tall, tall), tall)
            down_s[place, :] = pieces[k][
                up_rows : up_rows + tall, g * down_lanes : (g + 1) * down_lanes
            ].astype(F32)
        tall = share // out_groups
        top = up_rows + down_height
        for g in range(out_groups):
            out_s[dest, g * tall : (g + 1) * tall, :] = pieces[k][
                top : top + tall, g * down_rows : (g + 1) * down_rows
            ].astype(F32)
    down_ref[...] = down_s[...].T
    for d in range(parts):
        out_ref[:, d * down_rows : (d + 1) * down_rows] = out_s[d]


def finish_rest(pieces, me, model, hidden, count):
    parts = len(pieces)
    share, lanes = model // count, hidden // count
    return pl.pallas_call(
        partial(finish_rest_kernel, parts),
        name="finish_rest",
        out_shape=(
            jax.ShapeDtypeStruct((share, model), F32),
            jax.ShapeDtypeStruct((share, hidden), F32),
            jax.ShapeDtypeStruct((lanes, model), F32),
        ),
        in_specs=[SM] + [VM] * parts,
        out_specs=(VM, VM, VM),
        scratch_shapes=[
            pltpu.VMEM((parts, share, model // parts), F32),
            pltpu.VMEM((model, lanes), F32),
        ],
        compiler_params=params(),
        cost_estimate=cost(1),
    )(me, *pieces)


def finish_qkv_kernel(parts, ratio, me_ref, *refs):
    pieces = refs[:parts]
    out_ref, vector_ref, piece_s = refs[parts:]
    share = out_ref.shape[0]
    here = pieces[0].shape[1] // 3
    model = here * parts
    each = vector_rows(parts, ratio)
    for k in range(parts):
        piece_s[me_ref[0] ^ k] = pieces[k][...].astype(F32)
    for d in range(parts):
        for t in range(3):
            lane = t * model + d * here
            out_ref[:, lane : lane + here] = piece_s[d, 0:share, t * here : (t + 1) * here]
    for r in range(5 + ratio):
        row = share + r % each
        vector_ref[r : r + 1, :] = piece_s[r // each, row : row + 1, 0:share]


def finish_qkv(pieces, ratio, me):
    parts = len(pieces)
    height, width = pieces[0].shape
    share = height - EXTRA
    return pl.pallas_call(
        partial(finish_qkv_kernel, parts, ratio),
        name="finish_qkv",
        out_shape=(
            jax.ShapeDtypeStruct((share, parts * width), F32),
            jax.ShapeDtypeStruct((5 + ratio, share), F32),
        ),
        in_specs=[SM] + [VM] * parts,
        out_specs=(VM, VM),
        scratch_shapes=[pltpu.VMEM((parts, height, width), F32)],
        compiler_params=params(),
        cost_estimate=cost(1),
    )(me, *pieces)


def input_kernel(parts, has_old, me_ref, tokens_ref, embed_ref, middle_ref, wq_ref, vec_ref, *refs):
    pieces = refs[:parts]
    out_ref, sums_ref = refs[parts + has_old :]
    grad_hidden = dot_t(pieces[0][...], wq_ref[me_ref[0]])
    for k in range(1, parts):
        grad_hidden = grad_hidden + dot_t(pieces[k][...], wq_ref[me_ref[0] ^ k])
    rows = tokens_ref[0].astype(F32) + embed_ref[0].astype(F32)
    scaled, inverse = norm_parts(rows)
    sums_ref[0:1] = jnp.sum(grad_hidden * scaled, axis=0, keepdims=True)
    sums_ref[1:2] = jnp.sum(grad_hidden, axis=0, keepdims=True)
    sums_ref[2:8] = jnp.zeros((6, sums_ref.shape[1]), F32)
    out_ref[0] = middle_ref[...] + norm_back(grad_hidden, scaled, inverse, vec_ref[0:1])


def input_gradient(tokens, embed, micro_index, grad_middle, pieces, wq, vec, old, me):
    micro, rows, model = tokens.shape
    parts = len(pieces)
    width = pieces[0].shape[1]
    row_spec = pl.BlockSpec((1, rows, model), lambda i: (micro_index, 0, 0))
    whole = lambda shape: pl.BlockSpec(shape, lambda i: (0,) * len(shape))
    old_args = [] if old is None else [old]
    return pl.pallas_call(
        partial(input_kernel, parts, len(old_args)),
        name="input_gradient",
        grid=(1,),
        out_shape=(
            jax.ShapeDtypeStruct((micro, rows, model), F32),
            jax.ShapeDtypeStruct((8, model), F32),
        ),
        in_specs=[SM, row_spec, row_spec, whole((rows, model)), whole(wq.shape), whole(vec.shape)]
        + [whole((rows, width))] * parts
        + [pl.BlockSpec(memory_space=pl.ANY)] * len(old_args),
        out_specs=(row_spec, whole((8, model))),
        input_output_aliases={6 + parts: 0} if old_args else {},
        compiler_params=params(),
        cost_estimate=cost(2.5),
    )(me, tokens, embed, grad_middle, wq, vec, *pieces, *old_args)


def qkv_first_kernel(micro, parts, count, me_f, *refs):
    hiddens = refs[:micro]
    pieces = refs[micro : micro + micro * parts]
    out_ref, hidden_t = refs[micro + micro * parts :]
    share = hiddens[0].shape[1] // count
    for m in range(micro):
        hidden_t[m] = hiddens[m][...].astype(F32).T.astype(BF)

    def one(j, _):
        place = pl.ds(pl.multiple_of((me_f[0] ^ j) * share, share), share)
        for k in range(parts):
            out_ref[k, j] = sum(
                dot(hidden_t[m, place, :], pieces[m * parts + k][...]) for m in range(micro)
            )
        return 0

    lax.fori_loop(0, count, one, 0)


EXTRA = 8


def vector_rows(parts, ratio):
    return -(-(5 + ratio) // parts)


def qkv_last_kernel(parts, count, micro, me_s, me_f, first_ref, hidden_ref, *refs):
    pieces, refs = refs[:parts], refs[parts:]
    once, twice, bias_ref = refs[:micro], refs[micro : 2 * micro], refs[2 * micro]
    keep_ref, send_ref, hidden_t, vector_s = refs[2 * micro + 1 :]
    model = hidden_ref.shape[1]
    share = model // count
    ratio = bias_ref.shape[1] // model
    each = vector_rows(parts, ratio)
    hidden_t[...] = hidden_ref[...].astype(F32).T.astype(BF)
    ones = total([item[0:2] for item in once], F32)
    twos = total([item[0:3] for item in twice], F32)
    vector_s[...] = jnp.zeros_like(vector_s)
    for o in range(count):
        for r in range(5 + ratio):
            if r < 2:
                value = ones[r : r + 1, o * share : (o + 1) * share]
            elif r < 5:
                value = twos[r - 2 : r - 1, o * share : (o + 1) * share]
            else:
                lane = (o * ratio + r - 5) * share
                value = bias_ref[0:1, lane : lane + share]
            vector_s[o, r // each, r % each : r % each + 1, 0:share] = value

    def one_pair(s, _):
        for j, target in ((2 * s, keep_ref), (2 * s + 1, send_ref)):
            owner = me_f[0] ^ j
            place = pl.ds(pl.multiple_of(owner * share, share), share)
            for k in range(parts):
                found = first_ref[k, j] + dot(hidden_t[place, :], pieces[k][...])
                target[k, s, 0:share, :] = found.astype(BF)
                target[k, s, share:, :] = vector_s[owner, me_s[0] ^ k].astype(BF)
        return 0

    lax.fori_loop(0, count // 2, one_pair, 0)


def qkv_first(hiddens, pieces, me_f, count):
    micro = len(hiddens)
    rows, model = hiddens[0].shape
    parts = len(pieces[0])
    width = pieces[0][0].shape[1]
    flat = [item for group in pieces for item in group]
    return pl.pallas_call(
        partial(qkv_first_kernel, micro, parts, count),
        name="qkv_first",
        out_shape=jax.ShapeDtypeStruct((parts, count, model // count, width), F32),
        in_specs=[SM] + [VM] * (micro + micro * parts),
        out_specs=VM,
        scratch_shapes=[pltpu.VMEM((micro, model, rows), BF)],
        compiler_params=params(),
        cost_estimate=cost(5),
    )(me_f, *hiddens, *flat)


def qkv_last(first, hidden, pieces, once, twice, bias, me_s, me_f, count):
    rows, model = hidden.shape
    parts = len(pieces)
    width = pieces[0].shape[1]
    half = jax.ShapeDtypeStruct((parts, count // 2, model // count + EXTRA, width), BF)
    return pl.pallas_call(
        partial(qkv_last_kernel, parts, count, len(once)),
        name="qkv_last",
        out_shape=(half, half),
        in_specs=[SM, SM] + [VM] * (3 + parts + 2 * len(once)),
        out_specs=(VM, VM),
        scratch_shapes=[
            pltpu.VMEM((model, rows), BF),
            pltpu.VMEM((count, parts, EXTRA, width), F32),
        ],
        compiler_params=params(),
        cost_estimate=cost(4),
    )(me_s, me_f, first, hidden, *pieces, *once, *twice, bias)


def total(items, dtype):
    found = items[0].astype(F32)
    for item in items[1:]:
        found = found + item.astype(F32)
    return found.astype(dtype)


def small_call(kernel, outs, *args):
    return pl.pallas_call(
        kernel,
        out_shape=outs,
        in_specs=[VM] * len(args),
        out_specs=jax.tree.map(lambda _: VM, outs),
        compiler_params=params(),
        cost_estimate=cost(0.5),
    )(*args)


def add_parts(keep, found):
    def kernel(keep_ref, found_ref, *outs):
        for k, out in enumerate(outs):
            out[...] = total([keep_ref[k], found_ref[k]], out.dtype)

    out = jax.ShapeDtypeStruct(keep.shape[1:], keep.dtype)
    return small_call(kernel, [out] * keep.shape[0], keep, found)


def add_all(*items):
    def kernel(*refs):
        refs[-1][...] = total([item[...] for item in refs[:-1]], refs[-1].dtype)

    return small_call(kernel, jax.ShapeDtypeStruct(items[0].shape, items[0].dtype), *items)


def reduce_early(keep, send):
    parts, slots = keep.shape[:2]
    found = swap(send, "fsdp", 1)

    def by_slot(keep_ref, found_ref, *outs):
        for k in range(parts):
            for s in range(slots):
                outs[s][k] = total([keep_ref[k, s], found_ref[k, s]], BF)

    out = jax.ShapeDtypeStruct(keep.shape[:1] + keep.shape[2:], BF)
    shares = small_call(by_slot, [out] * slots, keep, found)
    yield shares
    shares = far_exchange(shares)

    def by_part(*refs):
        for k in range(parts):
            refs[slots + k][...] = total([item[k] for item in refs[:slots]], BF)

    out = jax.ShapeDtypeStruct(keep.shape[2:], BF)
    pieces = small_call(by_part, [out] * parts, *shares)
    yield pieces
    final = add_all(*exchange(pieces, "seq"))
    yield final
    yield gather_pieces(final, "seq")


def far_exchange(shares):
    return [shares[0]] + [swap(shares[s], "fsdp", 2 * s) for s in range(1, len(shares))]


def reduce_last(keep, send):
    slots = keep.shape[1]
    pieces = add_parts(keep, swap(send, "fsdp", 1))
    pieces = exchange(pieces, "seq")

    def by_slot(*refs):
        for s in range(slots):
            refs[s - slots][...] = total([item[s] for item in refs[:-slots]], BF)

    out = jax.ShapeDtypeStruct(keep.shape[2:], BF)
    shares = small_call(by_slot, [out] * slots, *pieces)
    final = add_all(*far_exchange(shares))
    return gather_pieces(final, "seq")


def layer(
    tokens,
    time_embed,
    doc_ids,
    out_grad,
    norm1_gain,
    norm1_shift,
    qkv_weight,
    out_weight,
    norm2_gain,
    norm2_shift,
    up_weight,
    up_bias,
    down_weight,
    down_bias,
):
    micro, _, _, model = tokens.shape
    parts = lax.axis_size("seq")
    count = lax.axis_size("fsdp")
    hidden = up_weight.shape[1]
    ratio = hidden // model
    head_dim = model // HEADS
    heads = HEADS // parts
    share = model // count
    seq_index = lax.axis_index("seq").astype(jnp.int32)
    fsdp_index = lax.axis_index("fsdp").astype(jnp.int32)
    me_s = seq_index.reshape(1)
    me_f = fsdp_index.reshape(1)
    tokens = tokens[:, 0]
    embed = time_embed[:, 0]
    cot = out_grad[:, 0]

    pieces = gather_pairs(qkv_weight, "fsdp")
    small = [norm1_gain, norm1_shift, norm2_gain, norm2_shift, down_bias]
    small = [item.reshape(1, share) for item in small] + [up_bias.reshape(ratio, share)]
    small = gather_pairs(jnp.concatenate(small), "fsdp")
    docs = gather_pieces(doc_ids, "seq")
    doc, low, high = assemble_docs(docs, me_s)
    small = after(small, doc)
    wq, vec, bias = assemble_qkv(pieces, small, me_f, model, parts, hidden)
    rest = pack_rest(out_weight, up_weight, down_weight)
    rest = gather_pairs(rest, "fsdp")

    hiddens, triples, mixes, logs = [], [], [], []
    for m in range(micro):
        found = project(tokens, embed, m, wq, vec, me_s)
        hiddens.append(found[0])
        outs = after(found[1:], triples[-1]) if m else found[1:]
        triples.append(exchange(outs, "seq"))
    sent = []
    for m in range(micro):
        triple = after(triples[m], logs[-1]) if m else triples[m]
        outs, log_total = attend(triple, me_s, low, high, doc, m, heads, head_dim)
        sent.append(outs)
        logs.append(log_total)
        mixes.append(exchange(outs, "seq"))
    w_out, w_up, w_down = assemble_rest(rest, me_f, model, hidden)
    stacked = None
    middles, sums, heads_grads = [], [], []
    for m in range(micro):
        mixed = mixes[m] if m else after(mixes[m], logs[-1])
        found, grads = feed(
            tokens, embed, cot, m, mixed, vec, bias, w_out, w_up, w_down, stacked, me_s
        )
        stacked = found[:5]
        middles.append(found[5])
        sums.append(found[6])
        heads_grads.append(exchange(grads, "seq"))
    layer_output, acts, pres, seconds, branches = stacked
    keep, send, bias_sum = rest_grads(acts, pres, seconds, branches, cot, mixes, me_s, me_f, count)
    hops = reduce_early(keep, send)
    backs = []
    for m in range(micro):
        token = bias_sum if m == 0 else (outs, next(hops)) if m == 1 else outs
        grads = after(heads_grads[m], token)
        outs = attend_back(
            triples[m],
            sent[m],
            grads,
            me_s,
            low,
            high,
            doc,
            m,
            logs[m],
            heads,
            head_dim,
        )
        backs.append(exchange(outs, "seq"))
    input_grad = None
    first_sums = []
    for m in range(micro - 1):
        pieces = after(backs[m], outs) if m == 0 else backs[m]
        input_grad, sum_one = input_gradient(
            tokens, embed, m, middles[m], pieces, wq, vec, input_grad, me_s
        )
        first_sums.append(sum_one)
    first = qkv_first(hiddens[:-1], after(backs[:-1], input_grad), me_f, count)
    last = after(backs[-1], first)
    input_grad, sum_one = input_gradient(
        tokens, embed, micro - 1, middles[-1], last, wq, vec, input_grad, me_s
    )
    first_sums.append(sum_one)
    last = after(last, next(hops))
    keep, send = qkv_last(first, hiddens[-1], last, first_sums, sums, bias_sum, me_s, me_f, count)
    pieces = reduce_last(keep, send)
    grad_qkv, vectors = finish_qkv(pieces, ratio, me_s)
    *_, pieces = hops
    grad_out, grad_up, grad_down = finish_rest(pieces, me_s, model, hidden, count)
    return (
        layer_output[:, None],
        input_grad[:, None],
        vectors[0],
        vectors[1],
        grad_qkv,
        grad_out,
        vectors[2],
        vectors[3],
        grad_up,
        vectors[5:].reshape(hidden // count),
        grad_down,
        vectors[4],
    )


def solution(mesh):
    rows = P(None, "fsdp", "seq", None)
    vector = P("fsdp")
    matrix = P("fsdp", None)
    return jax.shard_map(
        layer,
        mesh=mesh,
        in_specs=(
            rows,
            rows,
            P(None, "fsdp", "seq"),
            rows,
            vector,
            vector,
            matrix,
            matrix,
            vector,
            vector,
            matrix,
            vector,
            matrix,
            vector,
        ),
        out_specs=(
            rows,
            rows,
            vector,
            vector,
            matrix,
            matrix,
            vector,
            vector,
            matrix,
            vector,
            matrix,
            vector,
        ),
        check_vma=False,
    )
```

```python
from functools import partial

import jax
import jax.numpy as jnp
from jax import lax
from jax.experimental import pallas as pl
from jax.experimental.pallas import tpu as pltpu
from jax.sharding import PartitionSpec as P


HEADS = 8
EPS = 1e-05
LOG2E = 1.4426950408889634
WIDE = 512
NARROW = 384
PACK = 256
VMEM_LIMIT = 16 * 1024 * 1024
BF = jnp.bfloat16
F32 = jnp.float32


def dot(a, b, dims=((1,), (0,))):
    return lax.dot_general(a, b, (dims, ((), ())), preferred_element_type=F32)


def dot_t(a, b):
    return dot(a, b, ((1,), (1,)))


def params(limit=VMEM_LIMIT):
    return pltpu.CompilerParams(vmem_limit_bytes=limit)


def cost(micros):
    return pl.CostEstimate(flops=int(micros * 1e8), bytes_accessed=1000, transcendentals=0)


VM = pl.BlockSpec(memory_space=pltpu.VMEM)
SM = pl.BlockSpec(memory_space=pltpu.SMEM)


def after(value, token):
    return lax.optimization_barrier((value, token))[0]


def swap(value, axis, bit):
    size = lax.axis_size(axis)
    return lax.ppermute(value, axis, [(i, i ^ bit) for i in range(size)])


def exchange(pieces, axis):
    return [pieces[0]] + [swap(pieces[k], axis, k) for k in range(1, len(pieces))]


def gather_pieces(value, axis):
    return exchange([value] * lax.axis_size(axis), axis)


def gather_pairs(value, axis):
    size = lax.axis_size(axis)
    far = [swap(value, axis, j) if j else value for j in range(0, size, 2)]
    result = []
    for mine in far:
        result += [mine, swap(mine, axis, 1)]
    return result


def assemble_qkv_kernel(count, seq_parts, part_width, me_ref, *refs):
    pieces, small = refs[:count], refs[count : 2 * count]
    wq_ref, vec_ref, bias_ref, small_s = refs[2 * count :]
    rows = pieces[0].shape[0]
    model = wq_ref.shape[1]
    ratio = small[0].shape[0] - 5
    for j in range(count):
        owner = me_ref[0] ^ j
        start = pl.multiple_of(owner * rows, rows)
        for d in range(seq_parts):
            for t in range(3):
                lane = t * model + d * part_width
                wq_ref[d, pl.ds(start, rows), t * part_width : (t + 1) * part_width] = pieces[j][
                    :, lane : lane + part_width
                ]
        small_s[owner] = small[j][...].astype(F32)
    vec_ref[5:8] = jnp.zeros((3, model), F32)
    for o in range(count):
        item = small_s[o]
        vec_ref[0:5, o * rows : (o + 1) * rows] = item[0:5]
        for t in range(ratio):
            lane = (o * ratio + t) * rows
            bias_ref[lane // CHUNK, :, lane % CHUNK : lane % CHUNK + rows] = item[5 + t : 6 + t]


def assemble_qkv(pieces, small, me, model, seq_parts, hidden):
    part_width = model // seq_parts
    count = len(pieces)
    return pl.pallas_call(
        partial(assemble_qkv_kernel, count, seq_parts, part_width),
        name="assemble_qkv",
        out_shape=(
            jax.ShapeDtypeStruct((seq_parts, model, 3 * part_width), BF),
            jax.ShapeDtypeStruct((8, model), F32),
            jax.ShapeDtypeStruct((hidden // CHUNK, 1, CHUNK), F32),
        ),
        in_specs=[SM] + [VM] * (2 * count),
        out_specs=(VM, VM, VM),
        scratch_shapes=[
            pltpu.VMEM((count,) + small[0].shape, F32),
        ],
        compiler_params=params(),
        cost_estimate=cost(2),
    )(me, *pieces, *small)


def pack_rest_kernel(out_ref, up_ref, down_ref, all_ref):
    rows, model = out_ref.shape
    ratio = up_ref.shape[1] // model
    all_ref[0:rows] = out_ref[...]
    for t in range(ratio):
        all_ref[(1 + t) * rows : (2 + t) * rows] = up_ref[:, t * model : (t + 1) * model]
    all_ref[(1 + ratio) * rows :] = down_ref[...]


def pack_rest(out_weight, up_weight, down_weight):
    rows, model = out_weight.shape
    height = rows + 2 * down_weight.shape[0]
    return pl.pallas_call(
        pack_rest_kernel,
        name="pack_rest",
        out_shape=jax.ShapeDtypeStruct((height, model), BF),
        in_specs=[VM] * 3,
        out_specs=VM,
        compiler_params=params(),
        cost_estimate=cost(1),
    )(out_weight, up_weight, down_weight)


def assemble_rest_kernel(count, me_ref, *refs):
    pieces, (out_ref, up_ref, down_ref) = refs[:count], refs[count:]
    model = out_ref.shape[0]
    rows = model // count
    ratio = up_ref.shape[1] // model
    down_rows = ratio * rows
    for j in range(count):
        owner = me_ref[0] ^ j
        place = pl.ds(pl.multiple_of(owner * rows, rows), rows)
        out_ref[place, :] = pieces[j][0:rows, :]
        for t in range(ratio):
            up_ref[place, t * model : (t + 1) * model] = pieces[j][
                (1 + t) * rows : (2 + t) * rows, :
            ]
        place = pl.ds(pl.multiple_of(owner * down_rows, down_rows), down_rows)
        down_ref[place, :] = pieces[j][(1 + ratio) * rows :, :]


def assemble_rest(pieces, me, model, hidden):
    count = len(pieces)
    return pl.pallas_call(
        partial(assemble_rest_kernel, count),
        name="assemble_rest",
        out_shape=(
            jax.ShapeDtypeStruct((model, model), BF),
            jax.ShapeDtypeStruct((model, hidden), BF),
            jax.ShapeDtypeStruct((hidden, model), BF),
        ),
        in_specs=[SM] + [VM] * count,
        out_specs=(VM, VM, VM),
        compiler_params=params(),
        cost_estimate=cost(2),
    )(me, *pieces)


def norm_parts(rows):
    mean_row = jnp.mean(rows, axis=-1, keepdims=True)
    centred = rows - mean_row
    inverse = lax.rsqrt(jnp.mean(centred * centred, axis=-1, keepdims=True) + EPS)
    return centred * inverse, inverse


def norm_back(grad_normed, scaled, inverse, gain):
    grad_scaled = grad_normed * gain
    centre = jnp.mean(grad_scaled, axis=-1, keepdims=True)
    along = jnp.mean(grad_scaled * scaled, axis=-1, keepdims=True)
    return inverse * (grad_scaled - centre - scaled * along)


def project_kernel(parts, me_ref, tokens_ref, embed_ref, wq_ref, vec_ref, hidden_ref, *outs):
    rows = tokens_ref[0].astype(F32) + embed_ref[0].astype(F32)
    scaled, _ = norm_parts(rows)
    hidden = (scaled * vec_ref[0:1] + vec_ref[1:2]).astype(BF)
    hidden_ref[...] = hidden
    for k in range(parts):
        outs[k][...] = dot(hidden, wq_ref[me_ref[0] ^ k]).astype(BF)


def project(tokens, embed, micro_index, wq, vec, me):
    _, rows, model = tokens.shape
    parts, _, width = wq.shape
    row_spec = pl.BlockSpec((1, rows, model), lambda i: (micro_index, 0, 0))
    whole = lambda shape: pl.BlockSpec(shape, lambda i: (0,) * len(shape))
    return pl.pallas_call(
        partial(project_kernel, parts),
        name="project",
        grid=(1,),
        out_shape=[jax.ShapeDtypeStruct((rows, model), BF)]
        + [jax.ShapeDtypeStruct((rows, width), BF)] * parts,
        in_specs=[SM, row_spec, row_spec, whole(wq.shape), whole(vec.shape)],
        out_specs=[whole((rows, model))] + [whole((rows, width))] * parts,
        compiler_params=params(),
        cost_estimate=cost(2),
    )(me, tokens, embed, wq, vec)


def docs_kernel(parts, me_ref, *refs):
    pieces, (doc_ref, low_ref, high_ref) = refs[:parts], refs[parts:]
    micro, _, rows = pieces[0].shape
    for k in range(parts):
        place = pl.ds(pl.multiple_of((me_ref[0] ^ k) * rows, rows), rows)
        doc_ref[:, :, place] = pieces[k][...].astype(F32)
    for m in range(micro):
        doc = doc_ref[m]
        for i in range(doc.shape[1] // WIDE):
            first = doc[:, i * WIDE : i * WIDE + 1]
            last = doc[:, (i + 1) * WIDE - 1 : (i + 1) * WIDE]
            low = jnp.sum(jnp.where(doc < first, 1.0, 0.0)).astype(jnp.int32)
            high = jnp.sum(jnp.where(doc <= last, 1.0, 0.0)).astype(jnp.int32)
            low_ref[m, i] = low // NARROW
            high_ref[m, i] = (high + NARROW - 1) // NARROW


def assemble_docs(pieces, me):
    parts = len(pieces)
    micro, _, rows = pieces[0].shape
    length = rows * parts
    bounds = jax.ShapeDtypeStruct((micro, length // WIDE), jnp.int32)
    return pl.pallas_call(
        partial(docs_kernel, parts),
        name="assemble_docs",
        out_shape=(jax.ShapeDtypeStruct((micro, 1, length), F32), bounds, bounds),
        in_specs=[SM] + [VM] * parts,
        out_specs=(VM, SM, SM),
        compiler_params=params(),
        cost_estimate=cost(2),
    )(me, *pieces)


def head_mask(value, head, heads, head_dim):
    if heads == 1:
        return value
    lane = lax.broadcasted_iota(jnp.int32, value.shape, 1)
    keep = (lane >= head * head_dim) & (lane < (head + 1) * head_dim)
    return jnp.where(keep, value, jnp.zeros_like(value))


def spread_docs(doc_ref, doc_s):
    for start in range(0, doc_s.shape[0], 512):
        doc_s[start : start + 512, :] = jnp.broadcast_to(
            doc_ref[0:1, start : start + 512], (128, 512)
        ).T


def same_doc(doc_s, place, doc_row):
    column = doc_s[place, :]
    return jnp.concatenate([column] * (doc_row.shape[1] // 128), axis=1) == doc_row


def fold(value, combine):
    out = value[0:8]
    for start in range(8, value.shape[0], 8):
        out = combine(out, value[start : start + 8])
    return out


def place_rows(pieces, me, rows_s):
    rows = pieces[0].shape[0]
    for k, piece in enumerate(pieces):
        rows_s[pl.ds(pl.multiple_of((me ^ k) * rows, rows), rows), :] = piece[...]


def attend_kernel(parts, heads, head_dim, m, me_ref, low_ref, high_ref, docs_ref, *refs):
    doc_ref = docs_ref.at[m]
    pieces = refs[:parts]
    outs = refs[parts : 2 * parts]
    log_ref = refs[2 * parts]
    triple_s, value_t, doc_s, score_s, out_s = refs[2 * parts + 1 :]
    rows, width = pieces[0].shape
    here = width // 3
    length = rows * parts
    spread_docs(doc_ref, doc_s)
    place_rows(pieces, me_ref[0], triple_s)
    for start in range(0, length, WIDE):
        value_t[:, start : start + WIDE] = (
            triple_s[start : start + WIDE, 2 * here :].astype(F32).T.astype(BF)
        )
    scale = head_dim ** (-0.5) * LOG2E

    def one_block(i, _):
        place = pl.ds(pl.multiple_of(i * WIDE, WIDE), WIDE)
        query = triple_s[place, 0:here]
        queries = [head_mask(query, h, heads, head_dim) for h in range(heads)]
        doc_row = doc_ref[0:1, place]

        def score(j, tops):
            key_place = pl.ds(pl.multiple_of(j * NARROW, NARROW), NARROW)
            keys = triple_s[key_place, here : 2 * here]
            same = same_doc(doc_s, key_place, doc_row)
            result = []
            for h in range(heads):
                scores = jnp.where(same, dot_t(keys, queries[h]) * scale, -jnp.inf)
                score_s[h, key_place, :] = scores
                result.append(jnp.maximum(tops[h], fold(scores, jnp.maximum)))
            return tuple(result)

        tops = lax.fori_loop(
            low_ref[m, i],
            high_ref[m, i],
            score,
            tuple(jnp.full((8, WIDE), -jnp.inf, F32) for _ in range(heads)),
        )
        tops = [jnp.max(top, axis=0, keepdims=True) for top in tops]

        def mix(j, carry):
            key_place = pl.ds(pl.multiple_of(j * NARROW, NARROW), NARROW)
            result = []
            for h in range(heads):
                total, acc = carry[h]
                weight = jnp.exp2(score_s[h, key_place, :] - tops[h])
                total = total + fold(weight, jnp.add)
                values = value_t[h * head_dim : (h + 1) * head_dim, key_place]
                result.append((total, acc + dot(values, weight.astype(BF))))
            return tuple(result)

        done = lax.fori_loop(
            low_ref[m, i],
            high_ref[m, i],
            mix,
            tuple(
                (jnp.zeros((8, WIDE), F32), jnp.zeros((head_dim, WIDE), F32))
                for _ in range(heads)
            ),
        )
        mixed = []
        for h in range(heads):
            total = jnp.sum(done[h][0], axis=0, keepdims=True)
            mixed.append(done[h][1] / total)
            log_ref[h, :, place] = jnp.broadcast_to(tops[h] + jnp.log2(total), (8, WIDE))
        mixed = jnp.concatenate(mixed, axis=0) if heads > 1 else mixed[0]
        out_s[place, :] = mixed.T.astype(BF)
        return 0

    lax.fori_loop(0, length // WIDE, one_block, 0)
    for k in range(parts):
        place = pl.ds(pl.multiple_of((me_ref[0] ^ k) * rows, rows), rows)
        outs[k][...] = out_s[place, :]


def attend(pieces, me, low, high, doc, m, heads, head_dim):
    parts = len(pieces)
    rows, width = pieces[0].shape
    here = width // 3
    length = rows * parts
    found = pl.pallas_call(
        partial(attend_kernel, parts, heads, head_dim, m),
        name="attend",
        out_shape=[jax.ShapeDtypeStruct((rows, here), BF)] * parts
        + [jax.ShapeDtypeStruct((heads, 8, length), F32)],
        in_specs=[SM, SM, SM, VM] + [VM] * parts,
        out_specs=[VM] * (parts + 1),
        scratch_shapes=[
            pltpu.VMEM((length, width), BF),
            pltpu.VMEM((here, length), BF),
            pltpu.VMEM((length, 128), F32),
            pltpu.VMEM((heads, length, WIDE), F32),
            pltpu.VMEM((length, here), BF),
        ],
        compiler_params=params(),
        cost_estimate=cost(8),
    )(me, low, high, doc, *pieces)
    return found[:parts], found[parts]


def attend_back_kernel(
    parts, heads, head_dim, m, me_ref, low_ref, high_ref, docs_ref, log_ref, *refs
):
    doc_ref = docs_ref.at[m]
    pieces = refs[:parts]
    mixes = refs[parts : 2 * parts]
    grads = refs[2 * parts : 3 * parts]
    outs = refs[3 * parts : 4 * parts]
    (
        triple_s,
        grad_all,
        mix_all,
        query_s,
        key_t,
        grad_s,
        centre_s,
        doc_s,
        query_t,
        pair_s,
    ) = refs[4 * parts :]
    rows, width = pieces[0].shape
    here = width // 3
    length = rows * parts
    me = me_ref[0]
    spread_docs(doc_ref, doc_s)
    place_rows(pieces, me, triple_s)
    place_rows(grads, me, grad_all)
    place_rows(mixes, me, mix_all)
    for start in range(0, length, WIDE):
        place = pl.ds(start, WIDE)
        query = triple_s[place, 0:here]
        grad = grad_all[place, :]
        for h in range(heads):
            query_s[h, place, :] = head_mask(query, h, heads, head_dim)
            grad_s[h, place, :] = head_mask(grad, h, heads, head_dim)
        key_t[:, place] = triple_s[place, here : 2 * here].astype(F32).T.astype(BF)
        both = (grad.astype(F32) * mix_all[place, :].astype(F32)).T
        for h in range(heads):
            centre = jnp.sum(both[h * head_dim : (h + 1) * head_dim], axis=0, keepdims=True)
            centre_s[h, :, place] = jnp.broadcast_to(centre, (8, WIDE))
    query_t[...] = jnp.zeros_like(query_t)
    scale = head_dim ** (-0.5)

    def one_key(j, _):
        key_place = pl.ds(pl.multiple_of(j * WIDE, WIDE), WIDE)
        keys = triple_s[key_place, here : 2 * here]
        values = triple_s[key_place, 2 * here :]
        keys_t = [key_t[h * head_dim : (h + 1) * head_dim, key_place] for h in range(heads)]

        def one_block(i, carry):
            grad_key, grad_value = carry
            place = pl.ds(pl.multiple_of(i * NARROW, NARROW), NARROW)
            same = same_doc(doc_s, key_place, doc_ref[0:1, place])
            for h in range(heads):
                query = query_s[h, place, :]
                grad = grad_s[h, place, :]
                scores = jnp.where(same, dot_t(keys, query) * (scale * LOG2E), -jnp.inf)
                weight = jnp.exp2(scores - log_ref[h, 0:1, place])
                grad_weight = dot_t(values, grad)
                grad_score = (weight * (grad_weight - centre_s[h, 0:1, place])).astype(BF)
                grad_value = grad_value + dot(weight.astype(BF), grad)
                grad_key = grad_key + dot(grad_score, query)
                query_t[h * head_dim : (h + 1) * head_dim, place] += dot(keys_t[h], grad_score)
            return grad_key, grad_value

        zero = jnp.zeros((WIDE, here), F32)
        grad_key, grad_value = lax.fori_loop(
            low_ref[m, j], high_ref[m, j], one_block, (zero, zero)
        )
        pair_s[key_place, 0:here] = (grad_key * scale).astype(BF)
        pair_s[key_place, here:] = grad_value.astype(BF)
        return 0

    lax.fori_loop(0, length // WIDE, one_key, 0)
    for k in range(parts):
        place = pl.ds(pl.multiple_of((me_ref[0] ^ k) * rows, rows), rows)
        outs[k][:, 0:here] = (query_t[:, place].T * scale).astype(BF)
        outs[k][:, here:] = pair_s[place, :]


def attend_back(pieces, mixes, grads, me, low, high, doc, m, log_total, heads, head_dim):
    parts = len(pieces)
    rows, width = pieces[0].shape
    here = width // 3
    length = rows * parts
    return pl.pallas_call(
        partial(attend_back_kernel, parts, heads, head_dim, m),
        name="attend_back",
        out_shape=[jax.ShapeDtypeStruct((rows, width), BF)] * parts,
        in_specs=[SM, SM, SM, VM, VM] + [VM] * (3 * parts),
        out_specs=[VM] * parts,
        scratch_shapes=[
            pltpu.VMEM((length, width), BF),
            pltpu.VMEM((length, here), BF),
            pltpu.VMEM((length, here), BF),
            pltpu.VMEM((heads, length, here), BF),
            pltpu.VMEM((here, length), BF),
            pltpu.VMEM((heads, length, here), BF),
            pltpu.VMEM((heads, 8, length), F32),
            pltpu.VMEM((length, 128), F32),
            pltpu.VMEM((here, length), F32),
            pltpu.VMEM((length, 2 * here), BF),
        ],
        compiler_params=params(),
        cost_estimate=cost(12),
    )(me, low, high, doc, log_total, *pieces, *mixes, *grads)


CHUNK = 512


def feed_kernel(parts, has_old, me_ref, tokens_ref, embed_ref, cot_ref, vec_ref, bias_ref, *refs):
    mixes = refs[:parts]
    w_out, w_up, w_down = refs[parts : parts + 3]
    refs = refs[parts + 3 + has_old :]
    out_ref, act_ref, pre_ref, hidden_ref, branch_ref, middle_ref, sums_ref = refs[:7]
    grads = refs[7 : 7 + parts]
    total_s, back_s = refs[7 + parts :]
    me = me_ref[0]
    here = mixes[0].shape[1]
    middle = tokens_ref[0].astype(F32) + embed_ref[0].astype(F32)
    for k in range(parts):
        place = pl.ds(pl.multiple_of((me ^ k) * here, here), here)
        middle = middle + dot(mixes[k][...], w_out[place, :])
    scaled, inverse = norm_parts(middle)
    hidden_ref[0] = (scaled * vec_ref[2:3] + vec_ref[3:4]).astype(BF)
    middle_ref[...] = middle
    total_s[...] = jnp.zeros_like(total_s)
    back_s[...] = jnp.zeros_like(back_s)
    root = 0.7978845608028654

    def one_chunk(f, _):
        place = pl.ds(pl.multiple_of(f * CHUNK, CHUNK), CHUNK)
        value = dot(hidden_ref[0], w_up[:, place]) + bias_ref[f]
        square = value * value
        bend = jnp.tanh(root * (value + 0.044715 * (value * square)))
        half = 0.5 * (1.0 + bend)
        act = (value * half).astype(BF)
        slope = half + (0.5 * root) * value * (1.0 - bend * bend) * (1.0 + 0.134145 * square)
        act_ref[0, :, place] = act
        total_s[...] += dot(act, w_down[place, :])
        grad_pre = (dot_t(cot_ref[0], w_down[place, :]) * slope).astype(BF)
        pre_ref[0, :, place] = grad_pre
        back_s[...] += dot_t(grad_pre, w_up[:, place])
        return 0

    lax.fori_loop(0, w_up.shape[1] // CHUNK, one_chunk, 0)
    middle = middle_ref[...]
    out_ref[0] = (middle + total_s[...] + vec_ref[4:5]).astype(BF)
    scaled, inverse = norm_parts(middle)
    grad_hidden = back_s[...]
    sums_ref[0:1] = jnp.sum(grad_hidden * scaled, axis=0, keepdims=True)
    sums_ref[1:2] = jnp.sum(grad_hidden, axis=0, keepdims=True)
    cot = cot_ref[0].astype(F32)
    sums_ref[2:3] = jnp.sum(cot, axis=0, keepdims=True)
    sums_ref[3:8] = jnp.zeros((5, sums_ref.shape[1]), F32)
    grad_middle = cot + norm_back(grad_hidden, scaled, inverse, vec_ref[2:3])
    middle_ref[...] = grad_middle
    branch = grad_middle.astype(BF)
    branch_ref[0] = branch
    for k in range(parts):
        place = pl.ds(pl.multiple_of((me ^ k) * here, here), here)
        grads[k][...] = dot_t(branch, w_out[place, :]).astype(BF)


def feed(tokens, embed, cot, micro_index, mixes, vec, bias, w_out, w_up, w_down, old, me):
    micro, rows, model = tokens.shape
    parts = len(mixes)
    here = mixes[0].shape[1]
    hidden = w_up.shape[1]
    row_spec = pl.BlockSpec((1, rows, model), lambda i: (micro_index, 0, 0))
    whole = lambda shape: pl.BlockSpec(shape, lambda i: (0,) * len(shape))
    wide_spec = pl.BlockSpec((1, rows, hidden), lambda i: (micro_index, 0, 0))
    old_args = [] if old is None else list(old)
    found = pl.pallas_call(
        partial(feed_kernel, parts, len(old_args)),
        name="feed",
        grid=(1,),
        out_shape=[
            jax.ShapeDtypeStruct((micro, rows, model), BF),
            jax.ShapeDtypeStruct((micro, rows, hidden), BF),
            jax.ShapeDtypeStruct((micro, rows, hidden), BF),
            jax.ShapeDtypeStruct((micro, rows, model), BF),
            jax.ShapeDtypeStruct((micro, rows, model), BF),
            jax.ShapeDtypeStruct((rows, model), F32),
            jax.ShapeDtypeStruct((8, model), F32),
        ]
        + [jax.ShapeDtypeStruct((rows, here), BF)] * parts,
        in_specs=[SM, row_spec, row_spec, row_spec, whole(vec.shape), whole(bias.shape)]
        + [whole((rows, here))] * parts
        + [whole(w_out.shape), whole(w_up.shape), whole(w_down.shape)]
        + [pl.BlockSpec(memory_space=pl.ANY)] * len(old_args),
        out_specs=[
            row_spec,
            wide_spec,
            wide_spec,
            row_spec,
            row_spec,
            whole((rows, model)),
            whole((8, model)),
        ]
        + [whole((rows, here))] * parts,
        scratch_shapes=[pltpu.VMEM((rows, model), F32)] * 2,
        input_output_aliases={9 + parts + t: t for t in range(len(old_args))},
        compiler_params=params(20 * 1024 * 1024),
        cost_estimate=cost(8),
    )(me, tokens, embed, cot, vec, bias, *mixes, w_out, w_up, w_down, *old_args)
    return found[:7], found[7:]


def rest_grads_kernel(micro, parts, count, me_s, me_f, act_ref, pre_ref, hidden_ref, branch_ref,
                      cot_ref, *refs):
    mixes = refs[: micro * parts]
    keep_ref, send_ref, bias_ref = refs[micro * parts : micro * parts + 3]
    hidden_t, cot_t, mixed_t, up_s, down_s, out_s = refs[micro * parts + 3 :]
    targets = (keep_ref, send_ref)
    rows, model = hidden_ref.shape[1:]
    here = mixes[0].shape[1]
    share = model // count
    chunk = pl.program_id(0)
    owners, _, down_lanes = down_s.shape
    down_rows = model // parts
    up_rows, down_height, out_groups, _ = rest_layout(model, pl.num_programs(0) * model, parts, count)

    @pl.when(chunk == 0)
    def _():
        for m in range(micro):
            hidden_t[m] = hidden_ref[m].astype(F32).T.astype(BF)
            cot_t[m] = cot_ref[m].astype(F32).T.astype(BF)
            for k in range(parts):
                place = pl.ds(pl.multiple_of((me_s[0] ^ k) * here, here), here)
                mixed_t[m, place, :] = mixes[m * parts + k][...].astype(F32).T.astype(BF)
        found = sum(dot(mixed_t[m], branch_ref[m]) for m in range(micro)).astype(BF)
        for d in range(parts):
            out_s[d] = found[:, d * down_rows : (d + 1) * down_rows]
        tall = share // out_groups
        for j in range(count):
            base = (me_f[0] ^ j) * share
            for k in range(parts):
                for g in range(out_groups):
                    place = pl.ds(pl.multiple_of(base + g * tall, tall), tall)
                    top = up_rows + down_height
                    targets[j % 2][
                        k, j // 2, top : top + tall, g * down_rows : (g + 1) * down_rows
                    ] = out_s[me_s[0] ^ k, place, :]

    found = sum(dot(hidden_t[m], pre_ref[m]) for m in range(micro)).astype(BF)
    for q in range(model // PACK):
        up_s[q] = found[:, q * PACK : (q + 1) * PACK]
    for j in range(count):
        place = pl.ds(pl.multiple_of((me_f[0] ^ j) * share, share), share)
        for q in range(model // PACK):
            block = chunk * (model // PACK) + q
            groups = up_rows // share
            dest = me_s[0] ^ (block // groups)
            top = (q % groups) * share
            targets[j % 2][dest, j // 2, top : top + share, :] = up_s[q, place, :]

    found = sum(dot(cot_t[m], act_ref[m]) for m in range(micro)).astype(BF)
    for o in range(owners):
        down_s[o] = found[:, o * down_lanes : (o + 1) * down_lanes]
    groups = PACK // down_lanes
    tall = down_rows // groups
    for low in range(owners):
        owner = low ^ (me_f[0] % owners)
        slot = ((chunk ^ (me_f[0] // owners)) * owners + low) // 2
        for k in range(parts):
            for g in range(groups):
                place = pl.ds(pl.multiple_of((me_s[0] ^ k) * down_rows + g * tall, tall), tall)
                targets[low % 2][
                    k, slot, up_rows : up_rows + tall, g * down_lanes : (g + 1) * down_lanes
                ] = down_s[owner, place, :]

    ones = jnp.ones((8, rows), BF)
    bias_ref[...] = sum(dot(ones, pre_ref[m]) for m in range(micro))


def rest_layout(model, hidden, parts, count):
    share = model // count
    up_rows = share * (hidden // parts) // PACK
    down_rows = (model // parts) * (hidden // count) // PACK
    groups = PACK // (model // parts)
    if share % (16 * groups):
        groups = 1
    return up_rows, down_rows, groups, up_rows + down_rows + share // groups


def rest_grads(acts, pres, hiddens, branches, cot, mixes, me_s, me_f, count):
    micro, rows, model = cot.shape
    parts = len(mixes[0])
    hidden = acts.shape[2]
    height = rest_layout(model, hidden, parts, count)[3]
    half = (parts, count // 2, height, PACK)
    flat = [item for group in mixes for item in group]
    lanes = hidden // count
    whole = lambda shape: pl.BlockSpec(shape, lambda t: (0,) * len(shape))
    chunk = pl.BlockSpec((micro, rows, model), lambda t: (0, 0, t))
    return pl.pallas_call(
        partial(rest_grads_kernel, micro, parts, count),
        name="rest_grads",
        grid=(hidden // model,),
        out_shape=(
            jax.ShapeDtypeStruct(half, BF),
            jax.ShapeDtypeStruct(half, BF),
            jax.ShapeDtypeStruct((8, hidden), F32),
        ),
        in_specs=[SM, SM, chunk, chunk]
        + [whole(cot.shape)] * 3
        + [whole(flat[0].shape)] * len(flat),
        out_specs=(whole(half), whole(half), pl.BlockSpec((8, model), lambda t: (0, t))),
        scratch_shapes=[pltpu.VMEM((micro, model, rows), BF)] * 3
        + [
            pltpu.VMEM((model // PACK, model, PACK), BF),
            pltpu.VMEM((model // lanes, model, lanes), BF),
            pltpu.VMEM((parts, model, model // parts), BF),
        ],
        compiler_params=params(26 * 1024 * 1024),
        cost_estimate=cost(12),
    )(me_s, me_f, acts, pres, hiddens, branches, cot, *flat)


def finish_rest_kernel(parts, me_ref, *refs):
    pieces = refs[:parts]
    out_ref, up_ref, down_ref, out_s, down_s = refs[parts:]
    share, hidden = up_ref.shape
    down_lanes, model = down_ref.shape
    up_rows, down_height, out_groups, _ = rest_layout(model, hidden, parts, model // share)
    down_rows = model // parts
    cols = hidden // parts
    for k in range(parts):
        dest = me_ref[0] ^ k
        for g in range(cols // PACK):
            place = pl.ds(pl.multiple_of(dest * cols + g * PACK, PACK), PACK)
            up_ref[:, place] = pieces[k][g * share : (g + 1) * share, :].astype(F32)
        groups = PACK // down_lanes
        tall = down_rows // groups
        for g in range(groups):
            place = pl.ds(pl.multiple_of(dest * down_rows + g * tall, tall), tall)
            down_s[place, :] = pieces[k][
                up_rows : up_rows + tall, g * down_lanes : (g + 1) * down_lanes
            ].astype(F32)
        tall = share // out_groups
        top = up_rows + down_height
        for g in range(out_groups):
            out_s[dest, g * tall : (g + 1) * tall, :] = pieces[k][
                top : top + tall, g * down_rows : (g + 1) * down_rows
            ].astype(F32)
    down_ref[...] = down_s[...].T
    for d in range(parts):
        out_ref[:, d * down_rows : (d + 1) * down_rows] = out_s[d]


def finish_rest(pieces, me, model, hidden, count):
    parts = len(pieces)
    share, lanes = model // count, hidden // count
    return pl.pallas_call(
        partial(finish_rest_kernel, parts),
        name="finish_rest",
        out_shape=(
            jax.ShapeDtypeStruct((share, model), F32),
            jax.ShapeDtypeStruct((share, hidden), F32),
            jax.ShapeDtypeStruct((lanes, model), F32),
        ),
        in_specs=[SM] + [VM] * parts,
        out_specs=(VM, VM, VM),
        scratch_shapes=[
            pltpu.VMEM((parts, share, model // parts), F32),
            pltpu.VMEM((model, lanes), F32),
        ],
        compiler_params=params(),
        cost_estimate=cost(1),
    )(me, *pieces)


def finish_qkv_kernel(parts, ratio, me_ref, *refs):
    pieces = refs[:parts]
    out_ref, vector_ref, piece_s = refs[parts:]
    share = out_ref.shape[0]
    here = pieces[0].shape[1] // 3
    model = here * parts
    each = vector_rows(parts, ratio)
    for k in range(parts):
        piece_s[me_ref[0] ^ k] = pieces[k][...].astype(F32)
    for d in range(parts):
        for t in range(3):
            lane = t * model + d * here
            out_ref[:, lane : lane + here] = piece_s[d, 0:share, t * here : (t + 1) * here]
    for r in range(5 + ratio):
        row = share + r % each
        vector_ref[r : r + 1, :] = piece_s[r // each, row : row + 1, 0:share]


def finish_qkv(pieces, ratio, me):
    parts = len(pieces)
    height, width = pieces[0].shape
    share = height - EXTRA
    return pl.pallas_call(
        partial(finish_qkv_kernel, parts, ratio),
        name="finish_qkv",
        out_shape=(
            jax.ShapeDtypeStruct((share, parts * width), F32),
            jax.ShapeDtypeStruct((5 + ratio, share), F32),
        ),
        in_specs=[SM] + [VM] * parts,
        out_specs=(VM, VM),
        scratch_shapes=[pltpu.VMEM((parts, height, width), F32)],
        compiler_params=params(),
        cost_estimate=cost(1),
    )(me, *pieces)


def input_kernel(parts, has_old, me_ref, tokens_ref, embed_ref, middle_ref, wq_ref, vec_ref, *refs):
    pieces = refs[:parts]
    out_ref, sums_ref = refs[parts + has_old :]
    grad_hidden = dot_t(pieces[0][...], wq_ref[me_ref[0]])
    for k in range(1, parts):
        grad_hidden = grad_hidden + dot_t(pieces[k][...], wq_ref[me_ref[0] ^ k])
    rows = tokens_ref[0].astype(F32) + embed_ref[0].astype(F32)
    scaled, inverse = norm_parts(rows)
    sums_ref[0:1] = jnp.sum(grad_hidden * scaled, axis=0, keepdims=True)
    sums_ref[1:2] = jnp.sum(grad_hidden, axis=0, keepdims=True)
    sums_ref[2:8] = jnp.zeros((6, sums_ref.shape[1]), F32)
    out_ref[0] = middle_ref[...] + norm_back(grad_hidden, scaled, inverse, vec_ref[0:1])


def input_gradient(tokens, embed, micro_index, grad_middle, pieces, wq, vec, old, me):
    micro, rows, model = tokens.shape
    parts = len(pieces)
    width = pieces[0].shape[1]
    row_spec = pl.BlockSpec((1, rows, model), lambda i: (micro_index, 0, 0))
    whole = lambda shape: pl.BlockSpec(shape, lambda i: (0,) * len(shape))
    old_args = [] if old is None else [old]
    return pl.pallas_call(
        partial(input_kernel, parts, len(old_args)),
        name="input_gradient",
        grid=(1,),
        out_shape=(
            jax.ShapeDtypeStruct((micro, rows, model), F32),
            jax.ShapeDtypeStruct((8, model), F32),
        ),
        in_specs=[SM, row_spec, row_spec, whole((rows, model)), whole(wq.shape), whole(vec.shape)]
        + [whole((rows, width))] * parts
        + [pl.BlockSpec(memory_space=pl.ANY)] * len(old_args),
        out_specs=(row_spec, whole((8, model))),
        input_output_aliases={6 + parts: 0} if old_args else {},
        compiler_params=params(),
        cost_estimate=cost(2.5),
    )(me, tokens, embed, grad_middle, wq, vec, *pieces, *old_args)


def qkv_first_kernel(micro, parts, count, me_f, *refs):
    hiddens = refs[:micro]
    pieces = refs[micro : micro + micro * parts]
    out_ref, hidden_t = refs[micro + micro * parts :]
    share = hiddens[0].shape[1] // count
    for m in range(micro):
        hidden_t[m] = hiddens[m][...].astype(F32).T.astype(BF)

    def one(j, _):
        place = pl.ds(pl.multiple_of((me_f[0] ^ j) * share, share), share)
        for k in range(parts):
            out_ref[k, j] = sum(
                dot(hidden_t[m, place, :], pieces[m * parts + k][...]) for m in range(micro)
            )
        return 0

    lax.fori_loop(0, count, one, 0)


EXTRA = 8


def vector_rows(parts, ratio):
    return -(-(5 + ratio) // parts)


def qkv_last_kernel(parts, count, micro, me_s, me_f, first_ref, hidden_ref, *refs):
    pieces, refs = refs[:parts], refs[parts:]
    once, twice, bias_ref = refs[:micro], refs[micro : 2 * micro], refs[2 * micro]
    keep_ref, send_ref, hidden_t, vector_s = refs[2 * micro + 1 :]
    model = hidden_ref.shape[1]
    share = model // count
    ratio = bias_ref.shape[1] // model
    each = vector_rows(parts, ratio)
    hidden_t[...] = hidden_ref[...].astype(F32).T.astype(BF)
    ones = total([item[0:2] for item in once], F32)
    twos = total([item[0:3] for item in twice], F32)
    vector_s[...] = jnp.zeros_like(vector_s)
    for o in range(count):
        for r in range(5 + ratio):
            if r < 2:
                value = ones[r : r + 1, o * share : (o + 1) * share]
            elif r < 5:
                value = twos[r - 2 : r - 1, o * share : (o + 1) * share]
            else:
                lane = (o * ratio + r - 5) * share
                value = bias_ref[0:1, lane : lane + share]
            vector_s[o, r // each, r % each : r % each + 1, 0:share] = value

    def one_pair(s, _):
        for j, target in ((2 * s, keep_ref), (2 * s + 1, send_ref)):
            owner = me_f[0] ^ j
            place = pl.ds(pl.multiple_of(owner * share, share), share)
            for k in range(parts):
                found = first_ref[k, j] + dot(hidden_t[place, :], pieces[k][...])
                target[k, s, 0:share, :] = found.astype(BF)
                target[k, s, share:, :] = vector_s[owner, me_s[0] ^ k].astype(BF)
        return 0

    lax.fori_loop(0, count // 2, one_pair, 0)


def qkv_first(hiddens, pieces, me_f, count):
    micro = len(hiddens)
    rows, model = hiddens[0].shape
    parts = len(pieces[0])
    width = pieces[0][0].shape[1]
    flat = [item for group in pieces for item in group]
    return pl.pallas_call(
        partial(qkv_first_kernel, micro, parts, count),
        name="qkv_first",
        out_shape=jax.ShapeDtypeStruct((parts, count, model // count, width), F32),
        in_specs=[SM] + [VM] * (micro + micro * parts),
        out_specs=VM,
        scratch_shapes=[pltpu.VMEM((micro, model, rows), BF)],
        compiler_params=params(),
        cost_estimate=cost(5),
    )(me_f, *hiddens, *flat)


def qkv_last(first, hidden, pieces, once, twice, bias, me_s, me_f, count):
    rows, model = hidden.shape
    parts = len(pieces)
    width = pieces[0].shape[1]
    half = jax.ShapeDtypeStruct((parts, count // 2, model // count + EXTRA, width), BF)
    return pl.pallas_call(
        partial(qkv_last_kernel, parts, count, len(once)),
        name="qkv_last",
        out_shape=(half, half),
        in_specs=[SM, SM] + [VM] * (3 + parts + 2 * len(once)),
        out_specs=(VM, VM),
        scratch_shapes=[
            pltpu.VMEM((model, rows), BF),
            pltpu.VMEM((count, parts, EXTRA, width), F32),
        ],
        compiler_params=params(),
        cost_estimate=cost(4),
    )(me_s, me_f, first, hidden, *pieces, *once, *twice, bias)


def total(items, dtype):
    found = items[0].astype(F32)
    for item in items[1:]:
        found = found + item.astype(F32)
    return found.astype(dtype)


def small_call(kernel, outs, *args):
    return pl.pallas_call(
        kernel,
        out_shape=outs,
        in_specs=[VM] * len(args),
        out_specs=jax.tree.map(lambda _: VM, outs),
        compiler_params=params(),
        cost_estimate=cost(0.5),
    )(*args)


def add_parts(keep, found):
    def kernel(keep_ref, found_ref, *outs):
        for k, out in enumerate(outs):
            out[...] = total([keep_ref[k], found_ref[k]], out.dtype)

    out = jax.ShapeDtypeStruct(keep.shape[1:], keep.dtype)
    return small_call(kernel, [out] * keep.shape[0], keep, found)


def add_all(*items):
    def kernel(*refs):
        refs[-1][...] = total([item[...] for item in refs[:-1]], refs[-1].dtype)

    return small_call(kernel, jax.ShapeDtypeStruct(items[0].shape, items[0].dtype), *items)


def reduce_early(keep, send):
    parts, slots = keep.shape[:2]
    found = swap(send, "fsdp", 1)

    def by_slot(keep_ref, found_ref, *outs):
        for k in range(parts):
            for s in range(slots):
                outs[s][k] = total([keep_ref[k, s], found_ref[k, s]], BF)

    out = jax.ShapeDtypeStruct(keep.shape[:1] + keep.shape[2:], BF)
    shares = small_call(by_slot, [out] * slots, keep, found)
    yield shares
    shares = far_exchange(shares)

    def by_part(*refs):
        for k in range(parts):
            refs[slots + k][...] = total([item[k] for item in refs[:slots]], BF)

    out = jax.ShapeDtypeStruct(keep.shape[2:], BF)
    pieces = small_call(by_part, [out] * parts, *shares)
    yield pieces
    pieces = exchange(pieces, "seq")
    final = add_all(*pieces)
    yield final
    yield gather_pieces(final, "seq")


def far_exchange(shares):
    return [shares[0]] + [swap(shares[s], "fsdp", 2 * s) for s in range(1, len(shares))]


def reduce_last(keep, send):
    slots = keep.shape[1]
    found = swap(send, "fsdp", 1)
    pieces = add_parts(keep, found)
    pieces = exchange(pieces, "seq")

    def by_slot(*refs):
        for s in range(slots):
            refs[s - slots][...] = total([item[s] for item in refs[:-slots]], BF)

    out = jax.ShapeDtypeStruct(keep.shape[2:], BF)
    shares = small_call(by_slot, [out] * slots, *pieces)
    shares = far_exchange(shares)
    final = add_all(*shares)
    return gather_pieces(final, "seq")


def layer(
    tokens,
    time_embed,
    doc_ids,
    out_grad,
    norm1_gain,
    norm1_shift,
    qkv_weight,
    out_weight,
    norm2_gain,
    norm2_shift,
    up_weight,
    up_bias,
    down_weight,
    down_bias,
):
    micro, _, _, model = tokens.shape
    parts = lax.axis_size("seq")
    count = lax.axis_size("fsdp")
    hidden = up_weight.shape[1]
    ratio = hidden // model
    head_dim = model // HEADS
    heads = HEADS // parts
    share = model // count
    seq_index = lax.axis_index("seq").astype(jnp.int32)
    fsdp_index = lax.axis_index("fsdp").astype(jnp.int32)
    me_s = seq_index.reshape(1)
    me_f = fsdp_index.reshape(1)
    tokens = tokens[:, 0]
    embed = time_embed[:, 0]
    cot = out_grad[:, 0]

    pieces = gather_pairs(qkv_weight, "fsdp")
    small = [norm1_gain, norm1_shift, norm2_gain, norm2_shift, down_bias]
    small = [item.reshape(1, share) for item in small] + [up_bias.reshape(ratio, share)]
    small = gather_pairs(jnp.concatenate(small), "fsdp")
    docs = gather_pieces(doc_ids, "seq")
    doc, low, high = assemble_docs(docs, me_s)
    small = after(small, doc)
    wq, vec, bias = assemble_qkv(pieces, small, me_f, model, parts, hidden)
    rest = pack_rest(out_weight, up_weight, down_weight)
    rest = gather_pairs(rest, "fsdp")

    hiddens, triples, mixes, logs = [], [], [], []
    for m in range(micro):
        found = project(tokens, embed, m, wq, vec, me_s)
        hiddens.append(found[0])
        outs = after(found[1:], triples[-1]) if m else found[1:]
        triples.append(exchange(outs, "seq"))
    sent = []
    for m in range(micro):
        triple = after(triples[m], logs[-1]) if m else triples[m]
        outs, log_total = attend(triple, me_s, low, high, doc, m, heads, head_dim)
        sent.append(outs)
        logs.append(log_total)
        mixes.append(exchange(outs, "seq"))
    w_out, w_up, w_down = assemble_rest(rest, me_f, model, hidden)
    stacked = None
    middles, sums, heads_grads = [], [], []
    for m in range(micro):
        mixed = mixes[m] if m else after(mixes[m], logs[-1])
        found, grads = feed(
            tokens, embed, cot, m, mixed, vec, bias, w_out, w_up, w_down, stacked, me_s
        )
        stacked = found[:5]
        middles.append(found[5])
        sums.append(found[6])
        heads_grads.append(exchange(grads, "seq"))
    layer_output, acts, pres, seconds, branches = stacked
    keep, send, bias_sum = rest_grads(acts, pres, seconds, branches, cot, mixes, me_s, me_f, count)
    hops = reduce_early(keep, send)
    backs = []
    for m in range(micro):
        token = bias_sum if m == 0 else (outs, next(hops)) if m == 1 else outs
        grads = after(heads_grads[m], token)
        outs = attend_back(
            triples[m],
            sent[m],
            grads,
            me_s,
            low,
            high,
            doc,
            m,
            logs[m],
            heads,
            head_dim,
        )
        backs.append(exchange(outs, "seq"))
    input_grad = None
    first_sums = []
    for m in range(micro - 1):
        pieces = after(backs[m], outs) if m == 0 else backs[m]
        input_grad, sum_one = input_gradient(
            tokens, embed, m, middles[m], pieces, wq, vec, input_grad, me_s
        )
        first_sums.append(sum_one)
    first = qkv_first(hiddens[:-1], after(backs[:-1], input_grad), me_f, count)
    last = after(backs[-1], first)
    input_grad, sum_one = input_gradient(
        tokens, embed, micro - 1, middles[-1], last, wq, vec, input_grad, me_s
    )
    first_sums.append(sum_one)
    keep, send = qkv_last(first, hiddens[-1], last, first_sums, sums, bias_sum, me_s, me_f, count)
    pieces = reduce_last(keep, send)
    grad_qkv, vectors = finish_qkv(pieces, ratio, me_s)
    *_, pieces = hops
    grad_out, grad_up, grad_down = finish_rest(pieces, me_s, model, hidden, count)
    return (
        layer_output[:, None],
        input_grad[:, None],
        vectors[0],
        vectors[1],
        grad_qkv,
        grad_out,
        vectors[2],
        vectors[3],
        grad_up,
        vectors[5:].reshape(hidden // count),
        grad_down,
        vectors[4],
    )


def solution(mesh):
    rows = P(None, "fsdp", "seq", None)
    vector = P("fsdp")
    matrix = P("fsdp", None)
    return jax.shard_map(
        layer,
        mesh=mesh,
        in_specs=(
            rows,
            rows,
            P(None, "fsdp", "seq"),
            rows,
            vector,
            vector,
            matrix,
            matrix,
            vector,
            vector,
            matrix,
            vector,
            matrix,
            vector,
        ),
        out_specs=(
            rows,
            rows,
            vector,
            vector,
            matrix,
            matrix,
            vector,
            vector,
            matrix,
            vector,
            matrix,
            vector,
        ),
        check_vma=False,
    )
```

```python
from functools import partial

import jax
import jax.numpy as jnp
from jax import lax
from jax.experimental import pallas as pl
from jax.experimental.pallas import tpu as pltpu
from jax.sharding import PartitionSpec as P


HEADS = 8
EPS = 1e-05
LOG2E = 1.4426950408889634
WIDE = 512
NARROW = 384
PACK = 256
VMEM_LIMIT = 16 * 1024 * 1024
BF = jnp.bfloat16
F32 = jnp.float32


def dot(a, b, dims=((1,), (0,))):
    return lax.dot_general(a, b, (dims, ((), ())), preferred_element_type=F32)


def dot_t(a, b):
    return dot(a, b, ((1,), (1,)))


def params(limit=VMEM_LIMIT):
    return pltpu.CompilerParams(vmem_limit_bytes=limit)


def cost(micros):
    return pl.CostEstimate(flops=int(micros * 1e8), bytes_accessed=1000, transcendentals=0)


VM = pl.BlockSpec(memory_space=pltpu.VMEM)
SM = pl.BlockSpec(memory_space=pltpu.SMEM)


def after(value, token):
    return lax.optimization_barrier((value, token))[0]


def swap(value, axis, bit):
    size = lax.axis_size(axis)
    return lax.ppermute(value, axis, [(i, i ^ bit) for i in range(size)])


def exchange(pieces, axis):
    return [pieces[0]] + [swap(pieces[k], axis, k) for k in range(1, len(pieces))]


def gather_pieces(value, axis):
    return exchange([value] * lax.axis_size(axis), axis)


def gather_pairs(value, axis):
    size = lax.axis_size(axis)
    far = [swap(value, axis, j) if j else value for j in range(0, size, 2)]
    result = []
    for mine in far:
        result += [mine, swap(mine, axis, 1)]
    return result


def assemble_qkv_kernel(count, seq_parts, part_width, me_ref, *refs):
    pieces, small = refs[:count], refs[count : 2 * count]
    wq_ref, vec_ref, bias_ref, small_s = refs[2 * count :]
    rows = pieces[0].shape[0]
    model = wq_ref.shape[1]
    ratio = small[0].shape[0] - 5
    for j in range(count):
        owner = me_ref[0] ^ j
        start = pl.multiple_of(owner * rows, rows)
        for d in range(seq_parts):
            for t in range(3):
                lane = t * model + d * part_width
                wq_ref[d, pl.ds(start, rows), t * part_width : (t + 1) * part_width] = pieces[j][
                    :, lane : lane + part_width
                ]
        small_s[owner] = small[j][...].astype(F32)
    vec_ref[5:8] = jnp.zeros((3, model), F32)
    for o in range(count):
        item = small_s[o]
        vec_ref[0:5, o * rows : (o + 1) * rows] = item[0:5]
        for t in range(ratio):
            lane = (o * ratio + t) * rows
            bias_ref[lane // CHUNK, :, lane % CHUNK : lane % CHUNK + rows] = item[5 + t : 6 + t]


def assemble_qkv(pieces, small, me, model, seq_parts, hidden):
    part_width = model // seq_parts
    count = len(pieces)
    return pl.pallas_call(
        partial(assemble_qkv_kernel, count, seq_parts, part_width),
        name="assemble_qkv",
        out_shape=(
            jax.ShapeDtypeStruct((seq_parts, model, 3 * part_width), BF),
            jax.ShapeDtypeStruct((8, model), F32),
            jax.ShapeDtypeStruct((hidden // CHUNK, 1, CHUNK), F32),
        ),
        in_specs=[SM] + [VM] * (2 * count),
        out_specs=(VM, VM, VM),
        scratch_shapes=[
            pltpu.VMEM((count,) + small[0].shape, F32),
        ],
        compiler_params=params(),
        cost_estimate=cost(2),
    )(me, *pieces, *small)


def pack_rest_kernel(out_ref, up_ref, down_ref, all_ref):
    rows, model = out_ref.shape
    ratio = up_ref.shape[1] // model
    all_ref[0:rows] = out_ref[...]
    for t in range(ratio):
        all_ref[(1 + t) * rows : (2 + t) * rows] = up_ref[:, t * model : (t + 1) * model]
    all_ref[(1 + ratio) * rows :] = down_ref[...]


def pack_rest(out_weight, up_weight, down_weight):
    rows, model = out_weight.shape
    height = rows + 2 * down_weight.shape[0]
    return pl.pallas_call(
        pack_rest_kernel,
        name="pack_rest",
        out_shape=jax.ShapeDtypeStruct((height, model), BF),
        in_specs=[VM] * 3,
        out_specs=VM,
        compiler_params=params(),
        cost_estimate=cost(1),
    )(out_weight, up_weight, down_weight)


def assemble_rest_kernel(count, me_ref, *refs):
    pieces, (out_ref, up_ref, down_ref) = refs[:count], refs[count:]
    model = out_ref.shape[0]
    rows = model // count
    ratio = up_ref.shape[1] // model
    down_rows = ratio * rows
    for j in range(count):
        owner = me_ref[0] ^ j
        place = pl.ds(pl.multiple_of(owner * rows, rows), rows)
        out_ref[place, :] = pieces[j][0:rows, :]
        for t in range(ratio):
            up_ref[place, t * model : (t + 1) * model] = pieces[j][
                (1 + t) * rows : (2 + t) * rows, :
            ]
        place = pl.ds(pl.multiple_of(owner * down_rows, down_rows), down_rows)
        down_ref[place, :] = pieces[j][(1 + ratio) * rows :, :]


def assemble_rest(pieces, me, model, hidden):
    count = len(pieces)
    return pl.pallas_call(
        partial(assemble_rest_kernel, count),
        name="assemble_rest",
        out_shape=(
            jax.ShapeDtypeStruct((model, model), BF),
            jax.ShapeDtypeStruct((model, hidden), BF),
            jax.ShapeDtypeStruct((hidden, model), BF),
        ),
        in_specs=[SM] + [VM] * count,
        out_specs=(VM, VM, VM),
        compiler_params=params(),
        cost_estimate=cost(2),
    )(me, *pieces)


def norm_parts(rows):
    mean_row = jnp.mean(rows, axis=-1, keepdims=True)
    centred = rows - mean_row
    inverse = lax.rsqrt(jnp.mean(centred * centred, axis=-1, keepdims=True) + EPS)
    return centred * inverse, inverse


def norm_back(grad_normed, scaled, inverse, gain):
    grad_scaled = grad_normed * gain
    centre = jnp.mean(grad_scaled, axis=-1, keepdims=True)
    along = jnp.mean(grad_scaled * scaled, axis=-1, keepdims=True)
    return inverse * (grad_scaled - centre - scaled * along)


def project_kernel(parts, me_ref, tokens_ref, embed_ref, wq_ref, vec_ref, hidden_ref, *outs):
    half = hidden_ref.shape[0] // 2

    def one(i, _):
        place = pl.ds(pl.multiple_of(i * half, half), half)
        rows = tokens_ref[0, place, :].astype(F32) + embed_ref[0, place, :].astype(F32)
        scaled, _ = norm_parts(rows)
        hidden = (scaled * vec_ref[0:1] + vec_ref[1:2]).astype(BF)
        hidden_ref[place, :] = hidden
        for k in range(parts):
            outs[k][place, :] = dot(hidden, wq_ref[me_ref[0] ^ k]).astype(BF)
        return 0

    lax.fori_loop(0, 2, one, 0)


def project(tokens, embed, micro_index, wq, vec, me):
    _, rows, model = tokens.shape
    parts, _, width = wq.shape
    row_spec = pl.BlockSpec((1, rows, model), lambda i: (micro_index, 0, 0))
    whole = lambda shape: pl.BlockSpec(shape, lambda i: (0,) * len(shape))
    return pl.pallas_call(
        partial(project_kernel, parts),
        name="project",
        grid=(1,),
        out_shape=[jax.ShapeDtypeStruct((rows, model), BF)]
        + [jax.ShapeDtypeStruct((rows, width), BF)] * parts,
        in_specs=[SM, row_spec, row_spec, whole(wq.shape), whole(vec.shape)],
        out_specs=[whole((rows, model))] + [whole((rows, width))] * parts,
        compiler_params=params(),
        cost_estimate=cost(2),
    )(me, tokens, embed, wq, vec)


def docs_kernel(parts, me_ref, *refs):
    pieces, (doc_ref, low_ref, high_ref) = refs[:parts], refs[parts:]
    micro, _, rows = pieces[0].shape
    for k in range(parts):
        place = pl.ds(pl.multiple_of((me_ref[0] ^ k) * rows, rows), rows)
        doc_ref[:, :, place] = pieces[k][...].astype(F32)
    for m in range(micro):
        doc = doc_ref[m]
        for i in range(doc.shape[1] // WIDE):
            first = doc[:, i * WIDE : i * WIDE + 1]
            last = doc[:, (i + 1) * WIDE - 1 : (i + 1) * WIDE]
            low = jnp.sum(jnp.where(doc < first, 1.0, 0.0)).astype(jnp.int32)
            high = jnp.sum(jnp.where(doc <= last, 1.0, 0.0)).astype(jnp.int32)
            low_ref[m, i] = low // NARROW
            high_ref[m, i] = (high + NARROW - 1) // NARROW


def assemble_docs(pieces, me):
    parts = len(pieces)
    micro, _, rows = pieces[0].shape
    length = rows * parts
    bounds = jax.ShapeDtypeStruct((micro, length // WIDE), jnp.int32)
    return pl.pallas_call(
        partial(docs_kernel, parts),
        name="assemble_docs",
        out_shape=(jax.ShapeDtypeStruct((micro, 1, length), F32), bounds, bounds),
        in_specs=[SM] + [VM] * parts,
        out_specs=(VM, SM, SM),
        compiler_params=params(),
        cost_estimate=cost(2),
    )(me, *pieces)


def head_mask(value, head, heads, head_dim):
    if heads == 1:
        return value
    lane = lax.broadcasted_iota(jnp.int32, value.shape, 1)
    keep = (lane >= head * head_dim) & (lane < (head + 1) * head_dim)
    return jnp.where(keep, value, jnp.zeros_like(value))


def spread_docs(doc_ref, doc_s):
    def one(i, _):
        place = pl.ds(pl.multiple_of(i * WIDE, WIDE), WIDE)
        doc_s[place, :] = jnp.broadcast_to(doc_ref[0:1, place], (128, WIDE)).T
        return 0

    lax.fori_loop(0, doc_s.shape[0] // WIDE, one, 0)


def same_doc(doc_s, place, doc_row):
    column = doc_s[place, :]
    return jnp.concatenate([column] * (doc_row.shape[1] // 128), axis=1) == doc_row


def fold(value, combine):
    out = value[0:8]
    for start in range(8, value.shape[0], 8):
        out = combine(out, value[start : start + 8])
    return out


def place_rows(pieces, me, rows_s):
    rows = pieces[0].shape[0]
    for k, piece in enumerate(pieces):
        rows_s[pl.ds(pl.multiple_of((me ^ k) * rows, rows), rows), :] = piece[...]


def attend_kernel(parts, heads, head_dim, m, me_ref, low_ref, high_ref, docs_ref, *refs):
    doc_ref = docs_ref.at[m]
    pieces = refs[:parts]
    outs = refs[parts : 2 * parts]
    log_ref = refs[2 * parts]
    triple_s, value_t, doc_s, score_s, out_s = refs[2 * parts + 1 :]
    rows, width = pieces[0].shape
    here = width // 3
    length = rows * parts
    spread_docs(doc_ref, doc_s)
    place_rows(pieces, me_ref[0], triple_s)

    def turn(i, _):
        place = pl.ds(pl.multiple_of(i * WIDE, WIDE), WIDE)
        value_t[:, place] = triple_s[place, 2 * here :].astype(F32).T.astype(BF)
        return 0

    lax.fori_loop(0, length // WIDE, turn, 0)
    scale = head_dim ** (-0.5) * LOG2E

    def one_block(i, _):
        place = pl.ds(pl.multiple_of(i * WIDE, WIDE), WIDE)
        query = triple_s[place, 0:here]
        queries = [head_mask(query, h, heads, head_dim) for h in range(heads)]
        doc_row = doc_ref[0:1, place]

        def score(j, tops):
            key_place = pl.ds(pl.multiple_of(j * NARROW, NARROW), NARROW)
            keys = triple_s[key_place, here : 2 * here]
            same = same_doc(doc_s, key_place, doc_row)
            result = []
            for h in range(heads):
                scores = jnp.where(same, dot_t(keys, queries[h]) * scale, -jnp.inf)
                score_s[h, key_place, :] = scores
                result.append(jnp.maximum(tops[h], fold(scores, jnp.maximum)))
            return tuple(result)

        tops = lax.fori_loop(
            low_ref[m, i],
            high_ref[m, i],
            score,
            tuple(jnp.full((8, WIDE), -jnp.inf, F32) for _ in range(heads)),
        )
        tops = [jnp.max(top, axis=0, keepdims=True) for top in tops]

        def mix(j, carry):
            key_place = pl.ds(pl.multiple_of(j * NARROW, NARROW), NARROW)
            result = []
            for h in range(heads):
                total, acc = carry[h]
                weight = jnp.exp2(score_s[h, key_place, :] - tops[h])
                total = total + fold(weight, jnp.add)
                values = value_t[h * head_dim : (h + 1) * head_dim, key_place]
                result.append((total, acc + dot(values, weight.astype(BF))))
            return tuple(result)

        done = lax.fori_loop(
            low_ref[m, i],
            high_ref[m, i],
            mix,
            tuple(
                (jnp.zeros((8, WIDE), F32), jnp.zeros((head_dim, WIDE), F32))
                for _ in range(heads)
            ),
        )
        mixed = []
        for h in range(heads):
            total = jnp.sum(done[h][0], axis=0, keepdims=True)
            mixed.append(done[h][1] / total)
            log_ref[h, :, place] = jnp.broadcast_to(tops[h] + jnp.log2(total), (8, WIDE))
        mixed = jnp.concatenate(mixed, axis=0) if heads > 1 else mixed[0]
        out_s[place, :] = mixed.T.astype(BF)
        return 0

    lax.fori_loop(0, length // WIDE, one_block, 0)
    for k in range(parts):
        place = pl.ds(pl.multiple_of((me_ref[0] ^ k) * rows, rows), rows)
        outs[k][...] = out_s[place, :]


def attend(pieces, me, low, high, doc, m, heads, head_dim):
    parts = len(pieces)
    rows, width = pieces[0].shape
    here = width // 3
    length = rows * parts
    found = pl.pallas_call(
        partial(attend_kernel, parts, heads, head_dim, m),
        name="attend",
        out_shape=[jax.ShapeDtypeStruct((rows, here), BF)] * parts
        + [jax.ShapeDtypeStruct((heads, 8, length), F32)],
        in_specs=[SM, SM, SM, VM] + [VM] * parts,
        out_specs=[VM] * (parts + 1),
        scratch_shapes=[
            pltpu.VMEM((length, width), BF),
            pltpu.VMEM((here, length), BF),
            pltpu.VMEM((length, 128), F32),
            pltpu.VMEM((heads, length, WIDE), F32),
            pltpu.VMEM((length, here), BF),
        ],
        compiler_params=params(),
        cost_estimate=cost(8),
    )(me, low, high, doc, *pieces)
    return found[:parts], found[parts]


def attend_back_kernel(
    parts, heads, head_dim, m, me_ref, low_ref, high_ref, docs_ref, log_ref, *refs
):
    doc_ref = docs_ref.at[m]
    pieces = refs[:parts]
    mixes = refs[parts : 2 * parts]
    grads = refs[2 * parts : 3 * parts]
    outs = refs[3 * parts : 4 * parts]
    (
        triple_s,
        grad_all,
        mix_all,
        query_s,
        key_t,
        grad_s,
        centre_s,
        doc_s,
        query_t,
    ) = refs[4 * parts :]
    rows, width = pieces[0].shape
    here = width // 3
    length = rows * parts
    me = me_ref[0]
    spread_docs(doc_ref, doc_s)
    place_rows(pieces, me, triple_s)
    place_rows(grads, me, grad_all)
    place_rows(mixes, me, mix_all)

    def prepare(i, _):
        place = pl.ds(pl.multiple_of(i * WIDE, WIDE), WIDE)
        query = triple_s[place, 0:here]
        grad = grad_all[place, :]
        for h in range(heads):
            query_s[h, place, :] = head_mask(query, h, heads, head_dim)
            grad_s[h, place, :] = head_mask(grad, h, heads, head_dim)
        key_t[:, place] = triple_s[place, here : 2 * here].astype(F32).T.astype(BF)
        both = (grad.astype(F32) * mix_all[place, :].astype(F32)).T
        for h in range(heads):
            centre = jnp.sum(both[h * head_dim : (h + 1) * head_dim], axis=0, keepdims=True)
            centre_s[h, :, place] = jnp.broadcast_to(centre, (8, WIDE))
        return 0

    lax.fori_loop(0, length // WIDE, prepare, 0)
    query_t[...] = jnp.zeros_like(query_t)
    scale = head_dim ** (-0.5)

    def one_key(j, _):
        key_place = pl.ds(pl.multiple_of(j * WIDE, WIDE), WIDE)
        keys = triple_s[key_place, here : 2 * here]
        values = triple_s[key_place, 2 * here :]
        keys_t = [key_t[h * head_dim : (h + 1) * head_dim, key_place] for h in range(heads)]

        def one_block(i, carry):
            grad_key, grad_value = carry
            place = pl.ds(pl.multiple_of(i * NARROW, NARROW), NARROW)
            same = same_doc(doc_s, key_place, doc_ref[0:1, place])
            for h in range(heads):
                query = query_s[h, place, :]
                grad = grad_s[h, place, :]
                scores = jnp.where(same, dot_t(keys, query) * (scale * LOG2E), -jnp.inf)
                weight = jnp.exp2(scores - log_ref[h, 0:1, place])
                grad_weight = dot_t(values, grad)
                grad_score = (weight * (grad_weight - centre_s[h, 0:1, place])).astype(BF)
                grad_value = grad_value + dot(weight.astype(BF), grad)
                grad_key = grad_key + dot(grad_score, query)
                query_t[h * head_dim : (h + 1) * head_dim, place] += dot(keys_t[h], grad_score)
            return grad_key, grad_value

        zero = jnp.zeros((WIDE, here), F32)
        grad_key, grad_value = lax.fori_loop(
            low_ref[m, j], high_ref[m, j], one_block, (zero, zero)
        )
        triple_s[key_place, here : 2 * here] = (grad_key * scale).astype(BF)
        triple_s[key_place, 2 * here :] = grad_value.astype(BF)
        return 0

    lax.fori_loop(0, length // WIDE, one_key, 0)

    def finish(i, _):
        place = pl.ds(pl.multiple_of(i * WIDE, WIDE), WIDE)
        triple_s[place, 0:here] = (query_t[:, place].T * scale).astype(BF)
        return 0

    lax.fori_loop(0, length // WIDE, finish, 0)
    for k in range(parts):
        place = pl.ds(pl.multiple_of((me_ref[0] ^ k) * rows, rows), rows)
        outs[k][...] = triple_s[place, :]


def attend_back(pieces, mixes, grads, me, low, high, doc, m, log_total, heads, head_dim):
    parts = len(pieces)
    rows, width = pieces[0].shape
    here = width // 3
    length = rows * parts
    return pl.pallas_call(
        partial(attend_back_kernel, parts, heads, head_dim, m),
        name="attend_back",
        out_shape=[jax.ShapeDtypeStruct((rows, width), BF)] * parts,
        in_specs=[SM, SM, SM, VM, VM] + [VM] * (3 * parts),
        out_specs=[VM] * parts,
        scratch_shapes=[
            pltpu.VMEM((length, width), BF),
            pltpu.VMEM((length, here), BF),
            pltpu.VMEM((length, here), BF),
            pltpu.VMEM((heads, length, here), BF),
            pltpu.VMEM((here, length), BF),
            pltpu.VMEM((heads, length, here), BF),
            pltpu.VMEM((heads, 8, length), F32),
            pltpu.VMEM((length, 128), F32),
            pltpu.VMEM((here, length), F32),
        ],
        compiler_params=params(),
        cost_estimate=cost(12),
    )(me, low, high, doc, log_total, *pieces, *mixes, *grads)


CHUNK = 512


def feed_kernel(parts, has_old, me_ref, tokens_ref, embed_ref, cot_ref, vec_ref, bias_ref, *refs):
    mixes = refs[:parts]
    w_out, w_up, w_down = refs[parts : parts + 3]
    refs = refs[parts + 3 + has_old :]
    out_ref, act_ref, pre_ref, hidden_ref, branch_ref, middle_ref, sums_ref = refs[:7]
    grads = refs[7 : 7 + parts]
    total_s, back_s = refs[7 + parts :]
    me = me_ref[0]
    here = mixes[0].shape[1]
    middle = tokens_ref[0].astype(F32) + embed_ref[0].astype(F32)
    for k in range(parts):
        place = pl.ds(pl.multiple_of((me ^ k) * here, here), here)
        middle = middle + dot(mixes[k][...], w_out[place, :])
    scaled, inverse = norm_parts(middle)
    hidden_ref[0] = (scaled * vec_ref[2:3] + vec_ref[3:4]).astype(BF)
    middle_ref[...] = middle
    total_s[...] = jnp.zeros_like(total_s)
    back_s[...] = jnp.zeros_like(back_s)
    root = 0.7978845608028654

    def one_chunk(f, _):
        place = pl.ds(pl.multiple_of(f * CHUNK, CHUNK), CHUNK)
        value = dot(hidden_ref[0], w_up[:, place]) + bias_ref[f]
        square = value * value
        bend = jnp.tanh(root * (value + 0.044715 * (value * square)))
        half = 0.5 * (1.0 + bend)
        act = (value * half).astype(BF)
        slope = half + (0.5 * root) * value * (1.0 - bend * bend) * (1.0 + 0.134145 * square)
        act_ref[0, :, place] = act
        total_s[...] += dot(act, w_down[place, :])
        grad_pre = (dot_t(cot_ref[0], w_down[place, :]) * slope).astype(BF)
        pre_ref[0, :, place] = grad_pre
        back_s[...] += dot_t(grad_pre, w_up[:, place])
        return 0

    lax.fori_loop(0, w_up.shape[1] // CHUNK, one_chunk, 0)
    middle = middle_ref[...]
    out_ref[0] = (middle + total_s[...] + vec_ref[4:5]).astype(BF)
    scaled, inverse = norm_parts(middle)
    grad_hidden = back_s[...]
    sums_ref[0:1] = jnp.sum(grad_hidden * scaled, axis=0, keepdims=True)
    sums_ref[1:2] = jnp.sum(grad_hidden, axis=0, keepdims=True)
    cot = cot_ref[0].astype(F32)
    sums_ref[2:3] = jnp.sum(cot, axis=0, keepdims=True)
    sums_ref[3:8] = jnp.zeros((5, sums_ref.shape[1]), F32)
    grad_middle = cot + norm_back(grad_hidden, scaled, inverse, vec_ref[2:3])
    middle_ref[...] = grad_middle
    branch = grad_middle.astype(BF)
    branch_ref[0] = branch
    for k in range(parts):
        place = pl.ds(pl.multiple_of((me ^ k) * here, here), here)
        grads[k][...] = dot_t(branch, w_out[place, :]).astype(BF)


def feed(tokens, embed, cot, micro_index, mixes, vec, bias, w_out, w_up, w_down, old, me):
    micro, rows, model = tokens.shape
    parts = len(mixes)
    here = mixes[0].shape[1]
    hidden = w_up.shape[1]
    row_spec = pl.BlockSpec((1, rows, model), lambda i: (micro_index, 0, 0))
    whole = lambda shape: pl.BlockSpec(shape, lambda i: (0,) * len(shape))
    wide_spec = pl.BlockSpec((1, rows, hidden), lambda i: (micro_index, 0, 0))
    old_args = [] if old is None else list(old)
    found = pl.pallas_call(
        partial(feed_kernel, parts, len(old_args)),
        name="feed",
        grid=(1,),
        out_shape=[
            jax.ShapeDtypeStruct((micro, rows, model), BF),
            jax.ShapeDtypeStruct((micro, rows, hidden), BF),
            jax.ShapeDtypeStruct((micro, rows, hidden), BF),
            jax.ShapeDtypeStruct((micro, rows, model), BF),
            jax.ShapeDtypeStruct((micro, rows, model), BF),
            jax.ShapeDtypeStruct((rows, model), F32),
            jax.ShapeDtypeStruct((8, model), F32),
        ]
        + [jax.ShapeDtypeStruct((rows, here), BF)] * parts,
        in_specs=[SM, row_spec, row_spec, row_spec, whole(vec.shape), whole(bias.shape)]
        + [whole((rows, here))] * parts
        + [whole(w_out.shape), whole(w_up.shape), whole(w_down.shape)]
        + [pl.BlockSpec(memory_space=pl.ANY)] * len(old_args),
        out_specs=[
            row_spec,
            wide_spec,
            wide_spec,
            row_spec,
            row_spec,
            whole((rows, model)),
            whole((8, model)),
        ]
        + [whole((rows, here))] * parts,
        scratch_shapes=[pltpu.VMEM((rows, model), F32)] * 2,
        input_output_aliases={9 + parts + t: t for t in range(len(old_args))},
        compiler_params=params(20 * 1024 * 1024),
        cost_estimate=cost(8),
    )(me, tokens, embed, cot, vec, bias, *mixes, w_out, w_up, w_down, *old_args)
    return found[:7], found[7:]


def rest_grads_kernel(micro, parts, count, me_s, me_f, act_ref, pre_ref, hidden_ref, branch_ref,
                      cot_ref, *refs):
    mixes = refs[: micro * parts]
    keep_ref, send_ref, bias_ref = refs[micro * parts : micro * parts + 3]
    hidden_t, cot_t, mixed_t, up_s, down_s, out_s = refs[micro * parts + 3 :]
    targets = (keep_ref, send_ref)
    rows, model = hidden_ref.shape[1:]
    here = mixes[0].shape[1]
    share = model // count
    chunk = pl.program_id(0)
    owners, _, down_lanes = down_s.shape
    down_rows = model // parts
    up_rows, down_height, out_groups, _ = rest_layout(model, pl.num_programs(0) * model, parts, count)

    @pl.when(chunk == 0)
    def _():
        for m in range(micro):
            hidden_t[m] = hidden_ref[m].astype(F32).T.astype(BF)
            cot_t[m] = cot_ref[m].astype(F32).T.astype(BF)
            for k in range(parts):
                place = pl.ds(pl.multiple_of((me_s[0] ^ k) * here, here), here)
                mixed_t[m, place, :] = mixes[m * parts + k][...].astype(F32).T.astype(BF)
        found = sum(dot(mixed_t[m], branch_ref[m]) for m in range(micro)).astype(BF)
        for d in range(parts):
            out_s[d] = found[:, d * down_rows : (d + 1) * down_rows]
        tall = share // out_groups
        top = up_rows + down_height

        def out_pair(s, _):
            for p in range(2):
                base = (me_f[0] ^ (2 * s + p)) * share
                for k in range(parts):
                    for g in range(out_groups):
                        place = pl.ds(pl.multiple_of(base + g * tall, tall), tall)
                        targets[p][
                            k, s, top : top + tall, g * down_rows : (g + 1) * down_rows
                        ] = out_s[me_s[0] ^ k, place, :]
            return 0

        lax.fori_loop(0, count // 2, out_pair, 0)

    found = sum(dot(hidden_t[m], pre_ref[m]) for m in range(micro)).astype(BF)
    for q in range(model // PACK):
        up_s[q] = found[:, q * PACK : (q + 1) * PACK]

    def up_pair(s, _):
        for p in range(2):
            place = pl.ds(pl.multiple_of((me_f[0] ^ (2 * s + p)) * share, share), share)
            for q in range(model // PACK):
                block = chunk * (model // PACK) + q
                groups = up_rows // share
                dest = me_s[0] ^ (block // groups)
                top = (q % groups) * share
                targets[p][dest, s, top : top + share, :] = up_s[q, place, :]
        return 0

    lax.fori_loop(0, count // 2, up_pair, 0)

    found = sum(dot(cot_t[m], act_ref[m]) for m in range(micro)).astype(BF)
    for o in range(owners):
        down_s[o] = found[:, o * down_lanes : (o + 1) * down_lanes]
    groups = PACK // down_lanes
    tall = down_rows // groups
    for low in range(owners):
        owner = low ^ (me_f[0] % owners)
        slot = ((chunk ^ (me_f[0] // owners)) * owners + low) // 2
        for k in range(parts):
            for g in range(groups):
                place = pl.ds(pl.multiple_of((me_s[0] ^ k) * down_rows + g * tall, tall), tall)
                targets[low % 2][
                    k, slot, up_rows : up_rows + tall, g * down_lanes : (g + 1) * down_lanes
                ] = down_s[owner, place, :]

    ones = jnp.ones((8, rows), BF)
    bias_ref[...] = sum(dot(ones, pre_ref[m]) for m in range(micro))


def rest_layout(model, hidden, parts, count):
    share = model // count
    up_rows = share * (hidden // parts) // PACK
    down_rows = (model // parts) * (hidden // count) // PACK
    groups = PACK // (model // parts)
    if share % (16 * groups):
        groups = 1
    return up_rows, down_rows, groups, up_rows + down_rows + share // groups


def rest_grads(acts, pres, hiddens, branches, cot, mixes, me_s, me_f, count):
    micro, rows, model = cot.shape
    parts = len(mixes[0])
    hidden = acts.shape[2]
    height = rest_layout(model, hidden, parts, count)[3]
    half = (parts, count // 2, height, PACK)
    flat = [item for group in mixes for item in group]
    lanes = hidden // count
    whole = lambda shape: pl.BlockSpec(shape, lambda t: (0,) * len(shape))
    chunk = pl.BlockSpec((micro, rows, model), lambda t: (0, 0, t))
    return pl.pallas_call(
        partial(rest_grads_kernel, micro, parts, count),
        name="rest_grads",
        grid=(hidden // model,),
        out_shape=(
            jax.ShapeDtypeStruct(half, BF),
            jax.ShapeDtypeStruct(half, BF),
            jax.ShapeDtypeStruct((8, hidden), F32),
        ),
        in_specs=[SM, SM, chunk, chunk]
        + [whole(cot.shape)] * 3
        + [whole(flat[0].shape)] * len(flat),
        out_specs=(whole(half), whole(half), pl.BlockSpec((8, model), lambda t: (0, t))),
        scratch_shapes=[pltpu.VMEM((micro, model, rows), BF)] * 3
        + [
            pltpu.VMEM((model // PACK, model, PACK), BF),
            pltpu.VMEM((model // lanes, model, lanes), BF),
            pltpu.VMEM((parts, model, model // parts), BF),
        ],
        compiler_params=params(26 * 1024 * 1024),
        cost_estimate=cost(12),
    )(me_s, me_f, acts, pres, hiddens, branches, cot, *flat)


def finish_rest_kernel(parts, me_ref, *refs):
    pieces = refs[:parts]
    out_ref, up_ref, down_ref, out_s, down_s = refs[parts:]
    share, hidden = up_ref.shape
    down_lanes, model = down_ref.shape
    up_rows, down_height, out_groups, _ = rest_layout(model, hidden, parts, model // share)
    down_rows = model // parts
    cols = hidden // parts
    for k in range(parts):
        dest = me_ref[0] ^ k
        for g in range(cols // PACK):
            place = pl.ds(pl.multiple_of(dest * cols + g * PACK, PACK), PACK)
            up_ref[:, place] = pieces[k][g * share : (g + 1) * share, :].astype(F32)
        groups = PACK // down_lanes
        tall = down_rows // groups
        for g in range(groups):
            place = pl.ds(pl.multiple_of(dest * down_rows + g * tall, tall), tall)
            down_s[place, :] = pieces[k][
                up_rows : up_rows + tall, g * down_lanes : (g + 1) * down_lanes
            ].astype(F32)
        tall = share // out_groups
        top = up_rows + down_height
        for g in range(out_groups):
            out_s[dest, g * tall : (g + 1) * tall, :] = pieces[k][
                top : top + tall, g * down_rows : (g + 1) * down_rows
            ].astype(F32)
    down_ref[...] = down_s[...].T
    for d in range(parts):
        out_ref[:, d * down_rows : (d + 1) * down_rows] = out_s[d]


def finish_rest(pieces, me, model, hidden, count):
    parts = len(pieces)
    share, lanes = model // count, hidden // count
    return pl.pallas_call(
        partial(finish_rest_kernel, parts),
        name="finish_rest",
        out_shape=(
            jax.ShapeDtypeStruct((share, model), F32),
            jax.ShapeDtypeStruct((share, hidden), F32),
            jax.ShapeDtypeStruct((lanes, model), F32),
        ),
        in_specs=[SM] + [VM] * parts,
        out_specs=(VM, VM, VM),
        scratch_shapes=[
            pltpu.VMEM((parts, share, model // parts), F32),
            pltpu.VMEM((model, lanes), F32),
        ],
        compiler_params=params(),
        cost_estimate=cost(1),
    )(me, *pieces)


def finish_qkv_kernel(parts, ratio, me_ref, *refs):
    pieces = refs[:parts]
    out_ref, vector_ref, piece_s = refs[parts:]
    share = out_ref.shape[0]
    here = pieces[0].shape[1] // 3
    model = here * parts
    each = vector_rows(parts, ratio)
    for k in range(parts):
        piece_s[me_ref[0] ^ k] = pieces[k][...].astype(F32)
    for d in range(parts):
        for t in range(3):
            lane = t * model + d * here
            out_ref[:, lane : lane + here] = piece_s[d, 0:share, t * here : (t + 1) * here]
    for r in range(5 + ratio):
        row = share + r % each
        vector_ref[r : r + 1, :] = piece_s[r // each, row : row + 1, 0:share]


def finish_qkv(pieces, ratio, me):
    parts = len(pieces)
    height, width = pieces[0].shape
    share = height - EXTRA
    return pl.pallas_call(
        partial(finish_qkv_kernel, parts, ratio),
        name="finish_qkv",
        out_shape=(
            jax.ShapeDtypeStruct((share, parts * width), F32),
            jax.ShapeDtypeStruct((5 + ratio, share), F32),
        ),
        in_specs=[SM] + [VM] * parts,
        out_specs=(VM, VM),
        scratch_shapes=[pltpu.VMEM((parts, height, width), F32)],
        compiler_params=params(),
        cost_estimate=cost(1),
    )(me, *pieces)


def input_kernel(parts, has_old, me_ref, tokens_ref, embed_ref, middle_ref, wq_ref, vec_ref, *refs):
    pieces = refs[:parts]
    out_ref, sums_ref = refs[parts + has_old :]
    half = middle_ref.shape[0] // 2
    sums_ref[...] = jnp.zeros_like(sums_ref)

    def one(i, _):
        place = pl.ds(pl.multiple_of(i * half, half), half)
        grad_hidden = dot_t(pieces[0][place, :], wq_ref[me_ref[0]])
        for k in range(1, parts):
            grad_hidden = grad_hidden + dot_t(pieces[k][place, :], wq_ref[me_ref[0] ^ k])
        rows = tokens_ref[0, place, :].astype(F32) + embed_ref[0, place, :].astype(F32)
        scaled, inverse = norm_parts(rows)
        sums_ref[0:1] += jnp.sum(grad_hidden * scaled, axis=0, keepdims=True)
        sums_ref[1:2] += jnp.sum(grad_hidden, axis=0, keepdims=True)
        back = norm_back(grad_hidden, scaled, inverse, vec_ref[0:1])
        out_ref[0, place, :] = middle_ref[place, :] + back
        return 0

    lax.fori_loop(0, 2, one, 0)


def input_gradient(tokens, embed, micro_index, grad_middle, pieces, wq, vec, old, me):
    micro, rows, model = tokens.shape
    parts = len(pieces)
    width = pieces[0].shape[1]
    row_spec = pl.BlockSpec((1, rows, model), lambda i: (micro_index, 0, 0))
    whole = lambda shape: pl.BlockSpec(shape, lambda i: (0,) * len(shape))
    old_args = [] if old is None else [old]
    return pl.pallas_call(
        partial(input_kernel, parts, len(old_args)),
        name="input_gradient",
        grid=(1,),
        out_shape=(
            jax.ShapeDtypeStruct((micro, rows, model), F32),
            jax.ShapeDtypeStruct((8, model), F32),
        ),
        in_specs=[SM, row_spec, row_spec, whole((rows, model)), whole(wq.shape), whole(vec.shape)]
        + [whole((rows, width))] * parts
        + [pl.BlockSpec(memory_space=pl.ANY)] * len(old_args),
        out_specs=(row_spec, whole((8, model))),
        input_output_aliases={6 + parts: 0} if old_args else {},
        compiler_params=params(),
        cost_estimate=cost(2.5),
    )(me, tokens, embed, grad_middle, wq, vec, *pieces, *old_args)


def qkv_first_kernel(micro, parts, count, me_f, *refs):
    hiddens = refs[:micro]
    pieces = refs[micro : micro + micro * parts]
    out_ref, hidden_t = refs[micro + micro * parts :]
    share = hiddens[0].shape[1] // count
    for m in range(micro):
        hidden_t[m] = hiddens[m][...].astype(F32).T.astype(BF)

    def one(j, _):
        place = pl.ds(pl.multiple_of((me_f[0] ^ j) * share, share), share)
        for k in range(parts):
            out_ref[k, j] = sum(
                dot(hidden_t[m, place, :], pieces[m * parts + k][...]) for m in range(micro)
            )
        return 0

    lax.fori_loop(0, count, one, 0)


EXTRA = 8


def vector_rows(parts, ratio):
    return -(-(5 + ratio) // parts)


def qkv_last_kernel(parts, count, micro, me_s, me_f, first_ref, hidden_ref, *refs):
    pieces, refs = refs[:parts], refs[parts:]
    once, twice, bias_ref = refs[:micro], refs[micro : 2 * micro], refs[2 * micro]
    keep_ref, send_ref, hidden_t, vector_s = refs[2 * micro + 1 :]
    model = hidden_ref.shape[1]
    share = model // count
    ratio = bias_ref.shape[1] // model
    each = vector_rows(parts, ratio)
    hidden_t[...] = hidden_ref[...].astype(F32).T.astype(BF)
    ones = total([item[0:2] for item in once], F32)
    twos = total([item[0:3] for item in twice], F32)
    vector_s[...] = jnp.zeros_like(vector_s)
    for o in range(count):
        for r in range(5 + ratio):
            if r < 2:
                value = ones[r : r + 1, o * share : (o + 1) * share]
            elif r < 5:
                value = twos[r - 2 : r - 1, o * share : (o + 1) * share]
            else:
                lane = (o * ratio + r - 5) * share
                value = bias_ref[0:1, lane : lane + share]
            vector_s[o, r // each, r % each : r % each + 1, 0:share] = value

    def one_pair(s, _):
        for j, target in ((2 * s, keep_ref), (2 * s + 1, send_ref)):
            owner = me_f[0] ^ j
            place = pl.ds(pl.multiple_of(owner * share, share), share)
            for k in range(parts):
                found = first_ref[k, j] + dot(hidden_t[place, :], pieces[k][...])
                target[k, s, 0:share, :] = found.astype(BF)
                target[k, s, share:, :] = vector_s[owner, me_s[0] ^ k].astype(BF)
        return 0

    lax.fori_loop(0, count // 2, one_pair, 0)


def qkv_first(hiddens, pieces, me_f, count):
    micro = len(hiddens)
    rows, model = hiddens[0].shape
    parts = len(pieces[0])
    width = pieces[0][0].shape[1]
    flat = [item for group in pieces for item in group]
    return pl.pallas_call(
        partial(qkv_first_kernel, micro, parts, count),
        name="qkv_first",
        out_shape=jax.ShapeDtypeStruct((parts, count, model // count, width), F32),
        in_specs=[SM] + [VM] * (micro + micro * parts),
        out_specs=VM,
        scratch_shapes=[pltpu.VMEM((micro, model, rows), BF)],
        compiler_params=params(),
        cost_estimate=cost(5),
    )(me_f, *hiddens, *flat)


def qkv_last(first, hidden, pieces, once, twice, bias, me_s, me_f, count):
    rows, model = hidden.shape
    parts = len(pieces)
    width = pieces[0].shape[1]
    half = jax.ShapeDtypeStruct((parts, count // 2, model // count + EXTRA, width), BF)
    return pl.pallas_call(
        partial(qkv_last_kernel, parts, count, len(once)),
        name="qkv_last",
        out_shape=(half, half),
        in_specs=[SM, SM] + [VM] * (3 + parts + 2 * len(once)),
        out_specs=(VM, VM),
        scratch_shapes=[
            pltpu.VMEM((model, rows), BF),
            pltpu.VMEM((count, parts, EXTRA, width), F32),
        ],
        compiler_params=params(),
        cost_estimate=cost(4),
    )(me_s, me_f, first, hidden, *pieces, *once, *twice, bias)


def total(items, dtype):
    found = items[0].astype(F32)
    for item in items[1:]:
        found = found + item.astype(F32)
    return found.astype(dtype)


def small_call(kernel, outs, *args):
    return pl.pallas_call(
        kernel,
        out_shape=outs,
        in_specs=[VM] * len(args),
        out_specs=jax.tree.map(lambda _: VM, outs),
        compiler_params=params(),
        cost_estimate=cost(0.5),
    )(*args)


def add_parts(keep, found):
    def kernel(keep_ref, found_ref, *outs):
        for k, out in enumerate(outs):
            out[...] = total([keep_ref[k], found_ref[k]], out.dtype)

    out = jax.ShapeDtypeStruct(keep.shape[1:], keep.dtype)
    return small_call(kernel, [out] * keep.shape[0], keep, found)


def add_all(*items):
    def kernel(*refs):
        refs[-1][...] = total([item[...] for item in refs[:-1]], refs[-1].dtype)

    return small_call(kernel, jax.ShapeDtypeStruct(items[0].shape, items[0].dtype), *items)


def reduce_early(keep, send):
    parts, slots = keep.shape[:2]
    found = swap(send, "fsdp", 1)

    def by_slot(keep_ref, found_ref, *outs):
        for k in range(parts):
            for s in range(slots):
                outs[s][k] = total([keep_ref[k, s], found_ref[k, s]], BF)

    out = jax.ShapeDtypeStruct(keep.shape[:1] + keep.shape[2:], BF)
    shares = small_call(by_slot, [out] * slots, keep, found)
    yield shares
    shares = far_exchange(shares)

    def by_part(*refs):
        for k in range(parts):
            refs[slots + k][...] = total([item[k] for item in refs[:slots]], BF)

    out = jax.ShapeDtypeStruct(keep.shape[2:], BF)
    pieces = small_call(by_part, [out] * parts, *shares)
    yield pieces
    pieces = exchange(pieces, "seq")
    final = add_all(*pieces)
    yield final
    yield gather_pieces(final, "seq")


def far_exchange(shares):
    return [shares[0]] + [swap(shares[s], "fsdp", 2 * s) for s in range(1, len(shares))]


def reduce_last(keep, send):
    slots = keep.shape[1]
    found = swap(send, "fsdp", 1)
    pieces = add_parts(keep, found)
    pieces = exchange(pieces, "seq")

    def by_slot(*refs):
        for s in range(slots):
            refs[s - slots][...] = total([item[s] for item in refs[:-slots]], BF)

    out = jax.ShapeDtypeStruct(keep.shape[2:], BF)
    shares = small_call(by_slot, [out] * slots, *pieces)
    shares = far_exchange(shares)
    final = add_all(*shares)
    return gather_pieces(final, "seq")


def layer(
    tokens,
    time_embed,
    doc_ids,
    out_grad,
    norm1_gain,
    norm1_shift,
    qkv_weight,
    out_weight,
    norm2_gain,
    norm2_shift,
    up_weight,
    up_bias,
    down_weight,
    down_bias,
):
    micro, _, _, model = tokens.shape
    parts = lax.axis_size("seq")
    count = lax.axis_size("fsdp")
    hidden = up_weight.shape[1]
    ratio = hidden // model
    head_dim = model // HEADS
    heads = HEADS // parts
    share = model // count
    seq_index = lax.axis_index("seq").astype(jnp.int32)
    fsdp_index = lax.axis_index("fsdp").astype(jnp.int32)
    me_s = seq_index.reshape(1)
    me_f = fsdp_index.reshape(1)
    tokens = tokens[:, 0]
    embed = time_embed[:, 0]
    cot = out_grad[:, 0]

    pieces = gather_pairs(qkv_weight, "fsdp")
    small = [norm1_gain, norm1_shift, norm2_gain, norm2_shift, down_bias]
    small = [item.reshape(1, share) for item in small] + [up_bias.reshape(ratio, share)]
    small = gather_pairs(jnp.concatenate(small), "fsdp")
    docs = gather_pieces(doc_ids, "seq")
    doc, low, high = assemble_docs(docs, me_s)
    wq, vec, bias = assemble_qkv(pieces, small, me_f, model, parts, hidden)
    rest = pack_rest(out_weight, up_weight, down_weight)
    rest = gather_pairs(rest, "fsdp")

    hiddens, triples, mixes, logs = [], [], [], []
    for m in range(micro):
        found = project(tokens, embed, m, wq, vec, me_s)
        hiddens.append(found[0])
        outs = after(found[1:], triples[-1]) if m else found[1:]
        triples.append(exchange(outs, "seq"))
    sent = []
    for m in range(micro):
        triple = after(triples[m], logs[-1]) if m else triples[m]
        outs, log_total = attend(triple, me_s, low, high, doc, m, heads, head_dim)
        sent.append(outs)
        logs.append(log_total)
        mixes.append(exchange(outs, "seq"))
    w_out, w_up, w_down = assemble_rest(rest, me_f, model, hidden)
    stacked = None
    middles, sums, heads_grads = [], [], []
    for m in range(micro):
        mixed = mixes[m] if m else after(mixes[m], logs[-1])
        found, grads = feed(
            tokens, embed, cot, m, mixed, vec, bias, w_out, w_up, w_down, stacked, me_s
        )
        stacked = found[:5]
        middles.append(found[5])
        sums.append(found[6])
        heads_grads.append(exchange(grads, "seq"))
    layer_output, acts, pres, seconds, branches = stacked
    keep, send, bias_sum = rest_grads(acts, pres, seconds, branches, cot, mixes, me_s, me_f, count)
    hops = reduce_early(keep, send)
    backs = []
    for m in range(micro):
        token = bias_sum if m == 0 else (outs, next(hops)) if m == 1 else outs
        grads = after(heads_grads[m], token)
        outs = attend_back(
            triples[m],
            sent[m],
            grads,
            me_s,
            low,
            high,
            doc,
            m,
            logs[m],
            heads,
            head_dim,
        )
        backs.append(exchange(outs, "seq"))
    input_grad = None
    first_sums = []
    for m in range(micro - 1):
        pieces = after(backs[m], outs) if m == 0 else backs[m]
        input_grad, sum_one = input_gradient(
            tokens, embed, m, middles[m], pieces, wq, vec, input_grad, me_s
        )
        first_sums.append(sum_one)
    first = qkv_first(hiddens[:-1], after(backs[:-1], input_grad), me_f, count)
    last = after(backs[-1], first)
    input_grad, sum_one = input_gradient(
        tokens, embed, micro - 1, middles[-1], last, wq, vec, input_grad, me_s
    )
    first_sums.append(sum_one)
    keep, send = qkv_last(first, hiddens[-1], last, first_sums, sums, bias_sum, me_s, me_f, count)
    pieces = reduce_last(keep, send)
    grad_qkv, vectors = finish_qkv(pieces, ratio, me_s)
    *_, pieces = hops
    grad_out, grad_up, grad_down = finish_rest(pieces, me_s, model, hidden, count)
    return (
        layer_output[:, None],
        input_grad[:, None],
        vectors[0],
        vectors[1],
        grad_qkv,
        grad_out,
        vectors[2],
        vectors[3],
        grad_up,
        vectors[5:].reshape(hidden // count),
        grad_down,
        vectors[4],
    )


def solution(mesh):
    rows = P(None, "fsdp", "seq", None)
    vector = P("fsdp")
    matrix = P("fsdp", None)
    return jax.shard_map(
        layer,
        mesh=mesh,
        in_specs=(
            rows,
            rows,
            P(None, "fsdp", "seq"),
            rows,
            vector,
            vector,
            matrix,
            matrix,
            vector,
            vector,
            matrix,
            vector,
            matrix,
            vector,
        ),
        out_specs=(
            rows,
            rows,
            vector,
            vector,
            matrix,
            matrix,
            vector,
            vector,
            matrix,
            vector,
            matrix,
            vector,
        ),
        check_vma=False,
    )
```
